32 devices in a mesh: fsdp: 32 (over z, y, x, core).
Axes of the slice: x: 2, y: 2, z: 4, core: 2. Of those that a mesh axis runs over, the one named last changes fastest.
Arguments:
- tokens: bfloat16 [2, 4096, 1024], P(None, 'fsdp'), may hold values from -6 to 6
- cotangent: bfloat16 [2, 4096, 1024], P(None, 'fsdp'), may hold values from -6 to 6
- seq_lengths: int32 [2, 2], replicated, may hold values from 512 to 2048, as said below
- slot_block: int32 [2, 2], replicated, may hold values from 0 to 1, each once within a row
- w_query: bfloat16 [1024, 1024], P('fsdp'), may hold values from -0.1875 to 0.1875
- w_key: bfloat16 [1024, 1024], P('fsdp'), may hold values from -0.1875 to 0.1875
- w_value: bfloat16 [1024, 1024], P('fsdp'), may hold values from -0.1875 to 0.1875
- w_output: bfloat16 [1024, 1024], P('fsdp'), may hold values from -4 to 4
- w_in: bfloat16 [1024, 4096], P('fsdp'), may hold values from -0.1875 to 0.1875
- w_out: bfloat16 [4096, 1024], P('fsdp'), may hold values from -0.09375 to 0.09375
- b_query: bfloat16 [1024], P('fsdp'), may hold values from -3 to 3
- b_value: bfloat16 [1024], P('fsdp'), may hold values from -3 to 3
- b_output: bfloat16 [1024], P('fsdp'), may hold values from -3 to 3
- b_in: bfloat16 [4096], P('fsdp'), may hold values from -3 to 3
- b_out: bfloat16 [1024], P('fsdp'), may hold values from -3 to 3
- ln1_gain: bfloat16 [1024], P('fsdp'), may hold values from 0.25 to 1.75
- ln1_bias: bfloat16 [1024], P('fsdp'), may hold values from -3 to 3
- ln2_gain: bfloat16 [1024], P('fsdp'), may hold values from 0.25 to 1.75
- ln2_bias: bfloat16 [1024], P('fsdp'), may hold values from -3 to 3
Outputs:
- layer_out: bfloat16 [2, 4096, 1024], P(None, 'fsdp')
- grad_tokens: bfloat16 [2, 4096, 1024], P(None, 'fsdp')
- grad_w_query: float32 [1024, 1024], P('fsdp')
- grad_w_key: float32 [1024, 1024], P('fsdp')
- grad_w_value: float32 [1024, 1024], P('fsdp')
- grad_w_output: float32 [1024, 1024], P('fsdp')
- grad_w_in: float32 [1024, 4096], P('fsdp')
- grad_w_out: float32 [4096, 1024], P('fsdp')
- grad_b_query: float32 [1024], P('fsdp')
- grad_b_value: float32 [1024], P('fsdp')
- grad_b_output: float32 [1024], P('fsdp')
- grad_b_in: float32 [4096], P('fsdp')
- grad_b_out: float32 [1024], P('fsdp')
- grad_ln1_gain: float32 [1024], P('fsdp')
- grad_ln1_bias: float32 [1024], P('fsdp')
- grad_ln2_gain: float32 [1024], P('fsdp')
- grad_ln2_bias: float32 [1024], P('fsdp')
The draws below stay inside these ranges and needn't reach their ends.
Inputs may be any that keep to these rules, and one draw needn't show every extreme that they name: `seq_lengths`: every sequence has 512 tokens or more, and in each micro-batch at least one fills its slot of 2048 tokens. `slot_block`: each row is a permutation of the 2 token blocks.
All inputs are finite; a program needn't handle non-finite values.
Results may differ from the reference program's by a relative error of at most 0.015.
Values may be sent and summed in bfloat16 or wider, within the bound.
A program may use at most 192 MiB of HBM per device.

```python
import jax
import jax.numpy as jnp
from jax import lax

D = 1024
HEADS = 16
HEAD_DIM = 64
FF = 4096
MB = 2
SLOT = 2048
SLOTS = 2
TOKENS = 4096


def draw_seq_lengths(key, part):
    first_key = jax.random.fold_in(key, 11)
    second_key = jax.random.fold_in(key, 23)
    random_lengths = jax.random.randint(first_key, (MB, SLOTS), SLOT // 4, SLOT + 1)
    chosen_slot = jax.random.randint(second_key, (MB, 1), 0, SLOTS)
    filled = jnp.arange(SLOTS)[None, :] == chosen_slot
    return jnp.where(filled, SLOT, random_lengths).astype(jnp.int32)


def spiked(drawn, key, source, target, shards_of, factor):
    def block_of(position):
        return (jnp.arange(drawn.shape[position]) // (drawn.shape[position] // shards_of)).reshape((-1,) + (1,) * (drawn.ndim - 1 - position))

    one_side = jax.random.permutation(key, shards_of)[block_of(target)]
    other_side = (block_of(target) + shards_of // 2) % shards_of
    return jnp.where((block_of(source) == one_side) | (block_of(source) == other_side), factor * drawn, drawn)


def levels(rng, shape, cuts, smallest, largest):
    def one(position, blocks):
        steps = jax.random.uniform(jax.random.fold_in(jax.random.fold_in(rng, 6), position), (blocks,), jnp.float32, smallest / len(cuts), largest / len(cuts))
        return jnp.repeat(jnp.exp(steps), shape[position] // blocks).reshape((-1,) + (1,) * (len(shape) - position - 1))

    factor_of = one(*cuts[0])
    for cut in cuts[1:]:
        factor_of = factor_of * one(*cut)
    return factor_of


def noise(stream_key, dims, width, most, shards=(), held_as=jnp.bfloat16):
    factor_of = levels(stream_key, dims, shards, -0.22, 0.18) if shards else 1.0
    entries = jax.random.normal(stream_key, dims, jnp.float32) * width * factor_of
    return jnp.minimum(jnp.maximum(entries, -most), most).astype(held_as)


def noise_with(key, shape, width, most, split, heavy, held_as=jnp.bfloat16):
    values = width * jax.random.normal(key, shape, jnp.float32)
    if split:
        values = values * levels(key, shape, split, -0.22, 0.18)
    return jnp.clip(spiked(values, jax.random.fold_in(key, 3), *heavy), -most, most).astype(held_as)


def setup_inputs(seed: int = 0) -> dict:
    arg_keys = jax.random.split(jax.random.key(seed), 20)
    tokens = noise_with(arg_keys[0], (MB, TOKENS, D), 1.0, 6.0, ((1, 32),), (1, 2, 32, 2.75))
    cotangent = noise(arg_keys[1], (MB, TOKENS, D), 1.0, 6.0, ((1, 32),))
    seq_lengths = draw_seq_lengths(jax.random.fold_in(arg_keys[19], 71), 0)
    slot_block = jax.vmap(lambda own: jax.random.permutation(own, SLOTS))(jax.random.split(arg_keys[3], MB)).reshape((MB, SLOTS)).astype(jnp.int32)
    w_query = noise(arg_keys[4], (D, D), D ** -0.5, 0.1875, ((0, 32),))
    w_key = noise(arg_keys[5], (D, D), D ** -0.5, 0.1875, ((0, 32),))
    w_value = noise(arg_keys[6], (D, D), D ** -0.5, 0.1875, ((0, 32),))
    w_output = noise(arg_keys[7], (D, D), (max(1, D // 512)) ** -0.5, 4.0, ((0, 32),))
    w_in = noise(arg_keys[8], (D, FF), D ** -0.5, 0.1875, ((0, 32),))
    w_out = noise(arg_keys[9], (FF, D), FF ** -0.5, 0.09375, ((0, 32),))
    b_query = noise(arg_keys[10], (D,), 0.5, 3.0, ((0, 32),))
    b_value = noise(arg_keys[11], (D,), 0.5, 3.0, ((0, 32),))
    b_output = noise(arg_keys[12], (D,), 0.5, 3.0, ((0, 32),))
    b_in = noise(arg_keys[13], (FF,), 0.5, 3.0, ((0, 32),))
    b_out = noise(arg_keys[14], (D,), 0.5, 3.0, ((0, 32),))
    ln1_gain = jnp.clip(1.0 + 0.15 * jax.random.normal(arg_keys[15], (D,), jnp.float32), 0.25, 1.75).astype(jnp.bfloat16)
    ln1_bias = noise(arg_keys[16], (D,), 0.5, 3.0, ((0, 32),))
    ln2_gain = jnp.clip(1.0 + 0.15 * jax.random.normal(arg_keys[17], (D,), jnp.float32), 0.25, 1.75).astype(jnp.bfloat16)
    ln2_bias = noise(arg_keys[18], (D,), 0.5, 3.0, ((0, 32),))
    return {"tokens": tokens, "cotangent": cotangent, "seq_lengths": seq_lengths, "slot_block": slot_block, "w_query": w_query, "w_key": w_key, "w_value": w_value, "w_output": w_output, "w_in": w_in, "w_out": w_out, "b_query": b_query, "b_value": b_value, "b_output": b_output, "b_in": b_in, "b_out": b_out, "ln1_gain": ln1_gain, "ln1_bias": ln1_bias, "ln2_gain": ln2_gain, "ln2_bias": ln2_bias}


@jax.custom_vjp
def low(v):
    return lax.optimization_barrier(v.astype(jnp.bfloat16)).astype(jnp.float32)

@jax.custom_vjp
def low_back(v):
    return v

def low_keep(v):
    return (low(v), None)

def low_pass(kept, grad):
    return (grad,)

def back_keep(v):
    return (v, None)

def back_low(kept, grad):
    return (low(grad),)
low.defvjp(low_keep, low_pass)
low_back.defvjp(back_keep, back_low)

def project(left_rows, matrix):
    return jnp.dot(left_rows, matrix, precision=lax.Precision.HIGHEST)

def layer_norm(hidden, gain_vector, shift_vector):
    center = hidden - lax.optimization_barrier(jnp.mean(hidden, axis=-1, keepdims=True))
    spread = lax.optimization_barrier(jnp.mean(center * center, axis=-1, keepdims=True))
    return center * lax.rsqrt(spread + 1e-05) * gain_vector + shift_vector

def attend_block(query_block, key_seq, value_seq, key_live):
    scores = jnp.einsum('qhd,khd->hqk', query_block, key_seq, precision=lax.Precision.HIGHEST)
    scores = jnp.where(key_live[None, None, :], low_back(scores), -1e+30)
    top_score = lax.optimization_barrier(jnp.max(scores, axis=-1, keepdims=True))
    weights_exp = jnp.exp(scores - top_score)
    totals = lax.optimization_barrier(jnp.sum(weights_exp, axis=-1, keepdims=True))
    soft_weights = low(weights_exp / totals)
    return jnp.einsum('hqk,khd->qhd', soft_weights, value_seq, precision=lax.Precision.HIGHEST)

def reference(tokens, cotangent, seq_lengths, slot_block, w_query, w_key, w_value, w_output, w_in, w_out, b_query, b_value, b_output, b_in, b_out, ln1_gain, ln1_bias, ln2_gain, ln2_bias):
    owner = slot_block[:, :, None] == jnp.arange(SLOTS, dtype=jnp.int32)[None, None, :]
    block_len = lax.optimization_barrier(jnp.sum(jnp.where(owner, seq_lengths[:, :, None], 0), axis=1)).astype(jnp.int32)
    row_live = (jnp.arange(SLOT, dtype=jnp.int32)[None, None, :] < block_len[:, :, None]).reshape(MB, TOKENS)
    scale_factor = HEAD_DIM ** (-0.5)
    block_rows = min(512, SLOT)
    seq_count = MB * SLOTS
    flat_len = block_len.reshape(seq_count)
    checked_block = jax.checkpoint(attend_block)

    def forward(inputs, whole_query, whole_key, whole_value, whole_output, whole_in, whole_out, bias_query, bias_value, bias_output, bias_in, bias_out, gain_one, shift_one, gain_two, shift_two):
        rows_all = inputs.reshape(MB * TOKENS, D)
        queries = low(low_back((project(rows_all, whole_query) + bias_query) * scale_factor))
        keys_all = low(low_back(project(rows_all, whole_key)))
        values_all = low(low_back(project(rows_all, whole_value) + bias_value))
        query_seqs = queries.reshape(seq_count, SLOT // block_rows, block_rows, HEADS, HEAD_DIM)
        key_seqs = keys_all.reshape(seq_count, SLOT, HEADS, HEAD_DIM)
        value_seqs = values_all.reshape(seq_count, SLOT, HEADS, HEAD_DIM)

        def per_sequence(operands):
            query_seq, key_seq, value_seq, seq_len = operands
            key_live = jnp.arange(SLOT, dtype=jnp.int32) < seq_len
            return lax.map(lambda query_block: checked_block(query_block, key_seq, value_seq, key_live), query_seq)
        mixed_heads = lax.map(per_sequence, (query_seqs, key_seqs, value_seqs, flat_len)).reshape(MB * TOKENS, D)
        mixed_heads = low(low_back(mixed_heads))
        middle = low_back(project(mixed_heads, whole_output) + bias_output)
        normed = layer_norm(rows_all + middle, gain_one, shift_one)
        hidden_pre = low_back(project(low(normed), whole_in) + bias_in)
        activated = low(jax.nn.gelu(hidden_pre, approximate=False))
        branch = low_back(project(activated, whole_out) + bias_out)
        return layer_norm(normed + branch, gain_two, shift_two).reshape(MB, TOKENS, D)
    float_params = [weight_array.astype(jnp.float32) for weight_array in (w_query, w_key, w_value, w_output, w_in, w_out, b_query, b_value, b_output, b_in, b_out, ln1_gain, ln1_bias, ln2_gain, ln2_bias)]
    layer_out, pull_back = jax.vjp(forward, tokens.astype(jnp.float32), *float_params)
    seed_grad = cotangent.astype(jnp.float32) * row_live[:, :, None].astype(jnp.float32)
    gradients = pull_back(seed_grad)
    return (layer_out.astype(jnp.bfloat16), gradients[0].astype(jnp.bfloat16), gradients[1], gradients[2], gradients[3], gradients[4], gradients[5], gradients[6], gradients[7], gradients[8], gradients[9], gradients[10], gradients[11], gradients[12], gradients[13], gradients[14], gradients[15])
```

```python
import functools

import jax
import jax.numpy as jnp
from jax import lax
from jax.experimental import pallas as pl
from jax.experimental.pallas import tpu as pltpu
from jax.sharding import PartitionSpec as P

HEAD_DIM = 64
BLOCK_DEVS = 16
CUBE = BLOCK_DEVS // 2
PAIR = 2 * HEAD_DIM
HALF = 512
MESH = pl.DeviceIdType.MESH
VMEM = pl.BlockSpec(memory_space=pltpu.VMEM)
SMEM = pl.BlockSpec(memory_space=pltpu.SMEM)
ANY = pl.BlockSpec(memory_space=pl.ANY)
F32 = jnp.float32
BF16 = jnp.bfloat16


def dot(a, b, ca=1, cb=0):
    return lax.dot_general(a, b, (((ca,), (cb,)), ((), ())), preferred_element_type=F32)


def send(src, dst, send_sem, recv_sem, device):
    copy = pltpu.make_async_remote_copy(
        src_ref=src,
        dst_ref=dst,
        send_sem=send_sem,
        recv_sem=recv_sem,
        device_id=(device,),
        device_id_type=MESH,
    )
    copy.start()
    return copy


def greet(devices):
    barrier = pltpu.get_barrier_semaphore()
    for device in devices:
        pl.semaphore_signal(barrier, inc=1, device_id=(device,), device_id_type=MESH)
    pl.semaphore_wait(barrier, len(devices))


def where_am_i(n):
    me = lax.axis_index("fsdp")
    chip = me // 2
    return dict(
        me=me,
        core=me % 2,
        chip=chip,
        cube=chip % CUBE,
        rank=me % BLOCK_DEVS,
        high=chip // 4,
        l1=chip // 2 % 2,
        l0=chip % 2,
        n=n,
        chips=n // 2,
        highs=n // 8,
    )


CUBE_ORDERS = ((0, 1, 2), (1, 2, 0), (2, 0, 1))


def cube_rows(total):
    first = total // 3 // 16 * 16
    last = total - 2 * first
    return ((0, last), (last, first), (last + first, first))


def gather_kernel(n, tok, pieces, w_loc, in_loc, x_all, p_all, w_all,
                  tok_s, tok_r, cube_s, cube_r, pc_s, pc_r, sw_s, sw_r, loc_s, wi_s, wi_r,
                  hi_s, hi_r, ab_s, ab_r):
    w = where_am_i(n)
    me, core, chip, high, l1, l0 = w["me"], w["core"], w["chip"], w["high"], w["l1"], w["l0"]
    rows = tok.shape[1]
    partner = me ^ 1
    others = [me ^ (2 * m) for m in range(1, w["chips"])]
    greet([partner] + others)
    bits = (w["cube"] // 4, w["cube"] // 2 % 2, w["cube"] % 2)

    def mine(s=slice(None)):
        return x_all.at[bits[0], bits[1], bits[2], s]

    own_rows = pl.ds(pl.multiple_of(core * rows, rows), rows)
    locals_ = []
    locals_.append(pltpu.make_async_copy(tok.at[core], mine(own_rows), loc_s.at[0]))
    locals_[-1].start()
    swap = send(tok.at[1 - core], mine(own_rows), tok_s, tok_r, partner)
    items = w_all.shape[0]
    ff = (items - 1) // 2
    here = lambda item, s: w_all.at[item, high, l1, l0, s]
    swap_in = send(in_loc.at[1 - core], w_all.at[pl.ds(1, ff), high, l1, l0, core], wi_s, wi_r, partner)
    locals_.append(pltpu.make_async_copy(in_loc.at[core], w_all.at[pl.ds(1, ff), high, l1, l0, core], loc_s.at[1]))
    locals_[-1].start()
    locals_.append(pltpu.make_async_copy(w_loc.at[pl.ds(0, 1)], w_all.at[pl.ds(0, 1), high, l1, l0], loc_s.at[2]))
    locals_[-1].start()
    locals_.append(pltpu.make_async_copy(w_loc.at[pl.ds(1, ff)], w_all.at[pl.ds(1 + ff, ff), high, l1, l0], loc_s.at[3]))
    locals_[-1].start()
    locals_.append(pltpu.make_async_copy(pieces.at[w["cube"]], p_all.at[chip, core], loc_s.at[4]))
    locals_[-1].start()
    piece_copies = []
    for m in range(1, w["chips"]):
        there = (chip ^ m) % CUBE
        piece_copies.append(send(pieces.at[there], p_all.at[chip, core], pc_s.at[m], pc_r.at[m], others[m - 1]))
    for copy in locals_:
        copy.wait()
    swap.wait()
    spans = cube_rows(2 * rows)
    masks = (8, 4, 2)
    live = []
    for phase in range(3):
        for copy in live:
            copy.wait()
        live = []
        for s, order in enumerate(CUBE_ORDERS):
            index = [bits[0], bits[1], bits[2]]
            for done in order[:phase]:
                index[done] = slice(None)
            region = x_all.at[index[0], index[1], index[2], pl.ds(*spans[s])]
            live.append(send(region, region, cube_s.at[phase, s], cube_r.at[phase, s], me ^ masks[order[phase]]))
    swap_in.wait()
    for copy in piece_copies:
        copy.wait()
    region = p_all.at[:, core]
    swap_p = send(region, region, sw_s, sw_r, partner)
    for copy in live:
        copy.wait()
    swap_p.wait()
    groups = [(0, 1)] + [(1 + j, None) for j in range(ff)]

    def group(g, *index):
        if g == 0:
            return [w_all.at[(pl.ds(0, 1),) + index]]
        return [w_all.at[(pl.ds(g, 1),) + index], w_all.at[(pl.ds(g + ff, 1),) + index]]

    def high_phase(g):
        out = []
        for m in range(1, w["highs"]):
            for i, region in enumerate(group(g, high, l1, l0)):
                out.append(send(region, region, hi_s.at[g, m, i], hi_r.at[g, m, i], me ^ (8 * m)))
        return out

    def low_phase(g, phase):
        out = []
        for s in range(2):
            if phase == 0:
                index = (slice(None), l1, l0, s)
                to = me ^ (2 if s == 0 else 4)
            elif s == 0:
                index = (slice(None), l1, slice(None), s)
                to = me ^ 4
            else:
                index = (slice(None), slice(None), l0, s)
                to = me ^ 2
            for i, region in enumerate(group(g, *index)):
                out.append(send(region, region, ab_s.at[g, phase, s, i], ab_r.at[g, phase, s, i], to))
        return out

    def settle(copies):
        for copy in copies:
            copy.wait()

    waiting = {}
    count = len(groups)
    for step in range(count + 2):
        if step < count:
            waiting[step, 0] = high_phase(step)
        if 0 <= step - 1 < count:
            settle(waiting.pop((step - 1, 0)))
            waiting[step - 1, 1] = low_phase(step - 1, 0)
        if 0 <= step - 2 < count:
            settle(waiting.pop((step - 2, 1)))
            waiting[step - 2, 2] = low_phase(step - 2, 1)
    for copies in waiting.values():
        settle(copies)


def gather(n, tok, pieces, w_loc, in_loc):
    rows, width = tok.shape[1:]
    wr = in_loc.shape[2]
    ff = in_loc.shape[1]
    items = 1 + 2 * ff
    chips, highs = n // 2, n // 8
    dma = pltpu.SemaphoreType.DMA
    return pl.pallas_call(
        functools.partial(gather_kernel, n),
        name="gather",
        out_shape=(
            jax.ShapeDtypeStruct((2, 2, 2, 2 * rows, width), BF16),
            jax.ShapeDtypeStruct((chips, 2) + pieces.shape[1:], BF16),
            jax.ShapeDtypeStruct((items, highs, 2, 2, 2, wr, HALF), BF16),
        ),
        in_specs=[ANY] * 4,
        out_specs=(ANY, ANY, ANY),
        scratch_shapes=[
            dma, dma, dma((3, 3)), dma((3, 3)), dma((chips,)), dma((chips,)), dma, dma, dma((5,)), dma, dma,
            dma((ff + 1, highs, 2)), dma((ff + 1, highs, 2)), dma((ff + 1, 2, 2, 2)), dma((ff + 1, 2, 2, 2)),
        ],
        compiler_params=pltpu.CompilerParams(collective_id=0, has_side_effects=True),
    )(tok, pieces, w_loc, in_loc)


def attend_kernel(live, x, w, bq, bv, q, k, v, o, low, lse):
    rows = x.shape[0]
    tile = 256

    def project(i, _):
        at = pl.ds(pl.multiple_of(i * tile, tile), tile)
        y = dot(x[at, :], w[...])
        q[at, :] = ((y[:, :PAIR] + bq[...]) * HEAD_DIM ** (-0.5)).astype(BF16)
        k[at, :] = y[:, PAIR : 2 * PAIR].astype(BF16)
        v[at, :] = (y[:, 2 * PAIR :] + bv[...]).astype(BF16)
        return 0

    lax.fori_loop(0, rows // tile, project, 0)
    length = live[0]

    def step(i, _):
        at = pl.ds(pl.multiple_of(i * tile, tile), tile)
        outs, logs = [], []
        for h in range(2):
            c = slice(h * HEAD_DIM, (h + 1) * HEAD_DIM)
            s = dot(q[at, c], k[:, c], 1, 1)
            place = lax.broadcasted_iota(jnp.int32, s.shape, 1)
            s = jnp.where(place < length, s, -1e30)
            top = jnp.max(s, axis=1, keepdims=True)
            e = jnp.exp(s - top)
            total = jnp.sum(e, axis=1, keepdims=True)
            mixed = dot(e.astype(BF16), v[:, c])
            outs.append(mixed / total)
            logs.append(jnp.broadcast_to(top + jnp.log(total), (tile, HEAD_DIM)))
        out = jnp.concatenate(outs, axis=1)
        o[at, :] = out
        low[at, :] = out.astype(BF16)
        lse[at, :] = jnp.concatenate(logs, axis=1)
        return 0

    lax.fori_loop(0, rows // tile, step, 0)


def attend(live, x, w, bq, bv):
    rows = x.shape[0]
    low = jax.ShapeDtypeStruct((rows, PAIR), BF16)
    wide = jax.ShapeDtypeStruct((rows, PAIR), F32)
    return pl.pallas_call(
        attend_kernel,
        name="attend",
        out_shape=(low, low, low, wide, low, wide),
        in_specs=[SMEM, VMEM, VMEM, VMEM, VMEM],
        out_specs=(VMEM,) * 6,
        compiler_params=pltpu.CompilerParams(vmem_limit_bytes=56 << 20),
    )(live, x, w, bq, bv)


def to_rows_kernel(n, low, out, ss, rs, ls):
    w = where_am_i(n)
    me, core, cube, rank = w["me"], w["core"], w["cube"], w["rank"]
    greet([me ^ m for m in range(1, BLOCK_DEVS)])
    there = out.at[core, :, pl.ds(pl.multiple_of(cube * PAIR, PAIR), PAIR)]
    own = pltpu.make_async_copy(low.at[rank], there, ls)
    own.start()
    copies = [send(low.at[rank ^ m], there, ss.at[m], rs.at[m], me ^ m) for m in range(1, BLOCK_DEVS)]
    own.wait()
    for copy in copies:
        copy.wait()


def to_heads_kernel(n, grad, out, ss, rs, ls):
    w = where_am_i(n)
    me, core, cube, rank = w["me"], w["core"], w["cube"], w["rank"]
    greet([me ^ m for m in range(1, BLOCK_DEVS)])

    def piece(m):
        return grad.at[core ^ (m % 2), :, pl.ds(pl.multiple_of((cube ^ (m // 2)) * PAIR, PAIR), PAIR)]

    own = pltpu.make_async_copy(piece(0), out.at[rank], ls)
    own.start()
    copies = [send(piece(m), out.at[rank], ss.at[m], rs.at[m], me ^ m) for m in range(1, BLOCK_DEVS)]
    own.wait()
    for copy in copies:
        copy.wait()


def exchange(kernel, n, value, shape, name, ident):
    dma = pltpu.SemaphoreType.DMA
    return pl.pallas_call(
        functools.partial(kernel, n),
        name=name,
        out_shape=jax.ShapeDtypeStruct(shape, BF16),
        in_specs=[ANY],
        out_specs=ANY,
        scratch_shapes=[dma((BLOCK_DEVS,)), dma((BLOCK_DEVS,)), dma],
        compiler_params=pltpu.CompilerParams(collective_id=ident, has_side_effects=True),
    )(value)


def norm_forward(h):
    center = h - jnp.mean(h, axis=1, keepdims=True)
    rs = lax.rsqrt(jnp.mean(center * center, axis=1, keepdims=True) + 1e-05)
    return center * rs, rs


def norm_back(e, n, rs, gain):
    eg = e * gain
    return (eg - jnp.mean(eg, axis=1, keepdims=True) - n * jnp.mean(eg * n, axis=1, keepdims=True)) * rs


def total_rows(value):
    return jnp.sum(value, axis=0, keepdims=True)


def rows_kernel(n, live, attn, tok, cot, w_all, small, b_in,
                out, dh, dattn, g_in, g_out, g_o, g_small, g_bin,
                w_o, x1, n1, r1, x1_low, slope, act, part, got, df2, got2,
                wo_s, wo_r, x_s, x_r, h_s, h_r, d_s, d_r, e_s, e_r, lo_s):
    w = where_am_i(n)
    me, core, rank = w["me"], w["core"], w["rank"]
    partner = me ^ 1
    greet([partner])
    rows, width = tok.shape[1:]
    own = 2 * rows
    ff = (w_all.shape[0] - 1) // 2
    swap = send(w_all.at[0], w_o.at[:, :, :, core], wo_s, wo_r, partner)
    keep = pltpu.make_async_copy(w_all.at[0], w_o.at[:, :, :, core], lo_s)
    keep.start()
    keep.wait()
    swap.wait()

    def wo(s):
        return w_o[:, :, :, :, s].reshape(width, HALF)

    names = ("bq", "bv", "bo", "bout", "g1", "s1", "g2", "s2")
    param = {name: small[i : i + 1, :].astype(F32) for i, name in enumerate(names)}
    for m in range(2):
        at = slice(m * rows, (m + 1) * rows)
        a = attn[m]
        mid = jnp.concatenate([dot(a, wo(0)), dot(a, wo(1))], axis=1)
        h = tok[m].astype(F32) + mid + param["bo"]
        nn, rs = norm_forward(h)
        n1[at, :] = nn
        r1[at, :] = jnp.broadcast_to(rs, (rows, 128))
        y = nn * param["g1"] + param["s1"]
        x1[at, :] = y
        x1_low[at, :] = y.astype(BF16)
    swap = send(x1_low.at[pl.ds(0, own)], x1_low.at[pl.ds(own, own)], x_s, x_r, partner)
    swap.wait()
    for j in range(ff):
        w_in = w_all[1 + j].reshape(width, HALF)
        u = dot(x1_low[...], w_in) + b_in[j : j + 1, :].astype(F32)
        phi = 0.5 + 0.5 * lax.erf(u * 0.7071067811865476)
        slope[j] = phi + u * (0.3989422804014327 * jnp.exp(-0.5 * u * u))
        a = (u * phi).astype(BF16)
        act[j] = a
        for s in range(2):
            w_out = w_all[1 + ff + j, :, :, :, s].reshape(HALF, HALF)
            c = slice(s * HALF, (s + 1) * HALF)
            if j == 0:
                part[:, c] = dot(a, w_out)
            else:
                part[:, c] += dot(a, w_out)
    swap = send(part.at[pl.ds(own, own)], got, h_s, h_r, partner)
    swap.wait()
    bout = param["bout"]
    sums = {name: jnp.zeros((1, width), F32) for name in ("bo", "bout", "g1", "s1", "g2", "s2")}
    for m in range(2):
        at = slice(m * rows, (m + 1) * rows)
        h = x1[at, :] + part[at, :] + got[at, :] + bout
        nn, rs = norm_forward(h)
        out[m] = (nn * param["g2"] + param["s2"]).astype(BF16)
        place = rank * rows + lax.broadcasted_iota(jnp.int32, (rows, 1), 0)
        dy = jnp.where(place < live[m], cot[m].astype(F32), 0.0)
        sums["g2"] += total_rows(dy * nn)
        sums["s2"] += total_rows(dy)
        d = norm_back(dy, nn, rs, param["g2"])
        x1[at, :] = d
        low = d.astype(BF16)
        df2[at, :] = low
        sums["bout"] += total_rows(low.astype(F32))
    swap = send(df2.at[pl.ds(0, own)], df2.at[pl.ds(own, own)], d_s, d_r, partner)
    swap.wait()
    for j in range(ff):
        w_in = w_all[1 + j].reshape(width, HALF)
        da = None
        for s in range(2):
            w_out = w_all[1 + ff + j, :, :, :, s].reshape(HALF, HALF)
            c = slice(s * HALF, (s + 1) * HALF)
            term = dot(df2[:, c], w_out, 1, 1)
            da = term if da is None else da + term
            g_out[j, s] = dot(act[j], df2[:, c], 0, 0).astype(BF16)
        du = (da * slope[j]).astype(BF16)
        g_bin[j : j + 1, :] = total_rows(du.astype(F32))
        g_in[j] = dot(x1_low[...], du, 0, 0).astype(BF16)
        back = dot(du, w_in, 1, 1)
        if j == 0:
            part[...] = back
        else:
            part[...] += back
    swap = send(part.at[pl.ds(own, own)], got2, e_s, e_r, partner)
    swap.wait()
    for m in range(2):
        at = slice(m * rows, (m + 1) * rows)
        e = x1[at, :] + part[at, :] + got2[at, :]
        nn, rs = n1[at, :], r1[at, 0:1]
        sums["g1"] += total_rows(e * nn)
        sums["s1"] += total_rows(e)
        d = norm_back(e, nn, rs, param["g1"])
        dh[m] = d
        low = d.astype(BF16)
        df2[at, :] = low
        sums["bo"] += total_rows(low.astype(F32))
        dattn[m] = (dot(low[:, :HALF], wo(0), 1, 1) + dot(low[:, HALF:], wo(1), 1, 1)).astype(BF16)
    for s in range(2):
        c = slice(s * HALF, (s + 1) * HALF)
        g_o[s] = sum(dot(attn[m], df2[m * rows : (m + 1) * rows, c], 0, 0) for m in range(2)).astype(BF16)
    g_small[0:2, :] = jnp.zeros((2, width), F32)
    for i, name in enumerate(names[2:]):
        g_small[2 + i : 3 + i, :] = sums[name]


def rows_call(n, live, attn, tok, cot, w_all, small, b_in):
    _, rows, width = tok.shape
    items, highs = w_all.shape[:2]
    wr = w_all.shape[5]
    ff = (items - 1) // 2
    own = 2 * rows
    dma = pltpu.SemaphoreType.DMA
    s = jax.ShapeDtypeStruct
    return pl.pallas_call(
        functools.partial(rows_kernel, n),
        name="rows",
        out_shape=(
            s((2, rows, width), BF16),
            s((2, rows, width), F32),
            s((2, rows, width), BF16),
            s((ff, width, HALF), BF16),
            s((ff, 2, HALF, HALF), BF16),
            s((2, width, HALF), BF16),
            s((8, width), F32),
            s((ff, HALF), F32),
        ),
        in_specs=[SMEM] + [VMEM] * 6,
        out_specs=(VMEM,) * 8,
        scratch_shapes=[
            pltpu.VMEM((highs, 2, 2, 2, 2, wr, HALF), BF16),
            pltpu.VMEM((own, width), F32),
            pltpu.VMEM((own, width), F32),
            pltpu.VMEM((own, 128), F32),
            pltpu.VMEM((2 * own, width), BF16),
            pltpu.VMEM((ff, 2 * own, HALF), F32),
            pltpu.VMEM((ff, 2 * own, HALF), BF16),
            pltpu.VMEM((2 * own, width), F32),
            pltpu.VMEM((own, width), F32),
            pltpu.VMEM((2 * own, width), BF16),
            pltpu.VMEM((own, width), F32),
        ]
        + [dma] * 11,
        compiler_params=pltpu.CompilerParams(collective_id=3, has_side_effects=True, vmem_limit_bytes=60 << 20),
    )(live, attn, tok, cot, w_all, small, b_in)


def attend_back_kernel(live, q, k, v, o, lse, do, x, w, dx, dw, db, g, dk, dv):
    rows = q.shape[0]
    tile = 256
    length = live[0]
    scale = HEAD_DIM ** (-0.5)
    dk[...] = jnp.zeros_like(dk)
    dv[...] = jnp.zeros_like(dv)

    def step(i, _):
        at = pl.ds(pl.multiple_of(i * tile, tile), tile)
        outs = []
        for h in range(2):
            c = slice(h * HEAD_DIM, (h + 1) * HEAD_DIM)
            s = dot(q[at, c], k[:, c], 1, 1)
            place = lax.broadcasted_iota(jnp.int32, s.shape, 1)
            p = jnp.where(place < length, jnp.exp(s - lse[at, h * HEAD_DIM : h * HEAD_DIM + 1]), 0.0)
            d = do[at, c]
            dp = dot(d, v[:, c], 1, 1)
            inner = jnp.sum(d.astype(F32) * o[at, c], axis=1, keepdims=True)
            ds = (p * (dp - inner)).astype(BF16)
            outs.append(dot(ds, k[:, c]))
            dk[h] += dot(ds, q[at, c], 0, 0)
            dv[h] += dot(p.astype(BF16), d, 0, 0)
        g[at, 0:PAIR] = (jnp.concatenate(outs, axis=1).astype(BF16).astype(F32) * scale).astype(BF16)
        return 0

    lax.fori_loop(0, rows // tile, step, 0)
    g[:, PAIR : 2 * PAIR] = jnp.concatenate([dk[0], dk[1]], axis=1).astype(BF16)
    g[:, 2 * PAIR :] = jnp.concatenate([dv[0], dv[1]], axis=1).astype(BF16)

    def spread(i, _):
        at = pl.ds(pl.multiple_of(i * tile, tile), tile)
        dx[at, :] = dot(g[at, :], w[...], 1, 1).astype(BF16)
        return 0

    lax.fori_loop(0, rows // tile, spread, 0)
    dw[...] = dot(x[...], g[...], 0, 0)
    db[...] = jnp.broadcast_to(total_rows(g[...].astype(F32)), db.shape)


def attend_back(live, q, k, v, o, lse, do, x, w):
    rows, width = x.shape
    s = jax.ShapeDtypeStruct
    return pl.pallas_call(
        attend_back_kernel,
        name="attend_back",
        out_shape=(s((rows, width), BF16), s((width, 3 * PAIR), F32), s((8, 3 * PAIR), F32)),
        in_specs=[SMEM] + [VMEM] * 8,
        out_specs=(VMEM,) * 3,
        scratch_shapes=[
            pltpu.VMEM((rows, 3 * PAIR), BF16),
            pltpu.VMEM((2, rows, HEAD_DIM), F32),
            pltpu.VMEM((2, rows, HEAD_DIM), F32),
        ],
        compiler_params=pltpu.CompilerParams(vmem_limit_bytes=60 << 20),
    )(live, q, k, v, o, lse, do, x, w)


def add_into(target, *terms):
    total = target[...].astype(F32)
    for term in terms:
        total = total + term[...].astype(F32)
    target[...] = total.astype(target.dtype)


def scatter_w_kernel(n, g_in, one, out, out_in, g, r1a, r1b, r2, r3,
                     o_s, o_r, a_s, a_r, b_s, b_r, h_s, h_r, i_s, i_r, k_s):
    w = where_am_i(n)
    me, core, high, l1, l0 = w["me"], w["core"], w["high"], w["l1"], w["l0"]
    highs = w["highs"]
    partner = me ^ 1
    greet([partner, me ^ 2, me ^ 4] + [me ^ (8 * m) for m in range(1, highs)])
    items = g.shape[0]
    ff = (items - 1) // 2
    swap = send(one.at[1 - core], g.at[0], o_s, o_r, partner)
    fill = pltpu.make_async_copy(g_in, g.at[pl.ds(1, 2 * ff)], k_s)
    fill.start()
    fill.wait()
    swap.wait()

    def fold(i, _):
        g[0, i] = (g[0, i].astype(F32) + one[core, i].astype(F32)).astype(BF16)
        return 0

    lax.fori_loop(0, highs, fold, 0)
    first = [
        send(g.at[:, :, 1 - l1, :, 0], r1a, a_s.at[0], a_r.at[0], me ^ 4),
        send(g.at[:, :, :, 1 - l0, 1], r1b, a_s.at[1], a_r.at[1], me ^ 2),
    ]
    for copy in first:
        copy.wait()

    def add1(i, _):
        for h in range(highs):
            for b in range(2):
                g[i, h, l1, b, 0] = (g[i, h, l1, b, 0].astype(F32) + r1a[i, h, b].astype(F32)).astype(BF16)
                g[i, h, b, l0, 1] = (g[i, h, b, l0, 1].astype(F32) + r1b[i, h, b].astype(F32)).astype(BF16)
        return 0

    lax.fori_loop(0, items, add1, 0)
    second = [
        send(g.at[:, :, l1, 1 - l0, 0], r2.at[0], b_s.at[0], b_r.at[0], me ^ 2),
        send(g.at[:, :, 1 - l1, l0, 1], r2.at[1], b_s.at[1], b_r.at[1], me ^ 4),
    ]
    for copy in second:
        copy.wait()

    def add2(i, _):
        for h in range(highs):
            for s in range(2):
                g[i, h, l1, l0, s] = (g[i, h, l1, l0, s].astype(F32) + r2[s, i, h].astype(F32)).astype(BF16)
        return 0

    lax.fori_loop(0, items, add2, 0)
    third = [
        send(g.at[:, high ^ m, l1, l0], r3.at[m - 1], h_s.at[m], h_r.at[m], me ^ (8 * m)) for m in range(1, highs)
    ]
    for copy in third:
        copy.wait()

    def add3(i, _):
        for s in range(2):
            total = g[i, high, l1, l0, s].astype(F32)
            for m in range(1, highs):
                total = total + r3[m - 1, i, s].astype(F32)
            out[i, s] = total
        return 0

    lax.fori_loop(0, items, add3, 0)
    keep = pltpu.make_async_copy(out.at[pl.ds(1, ff), core], out_in.at[core], k_s)
    keep.start()
    swap = send(out.at[pl.ds(1, ff), 1 - core], out_in.at[core], i_s, i_r, partner)
    keep.wait()
    swap.wait()


def scatter_w(n, g, one):
    items, highs = g.shape[0] + 1, g.shape[1]
    wr = g.shape[5]
    ff = (items - 1) // 2
    dma = pltpu.SemaphoreType.DMA
    s = jax.ShapeDtypeStruct
    unit = (wr, HALF)
    return pl.pallas_call(
        functools.partial(scatter_w_kernel, n),
        name="scatter_w",
        out_shape=(s((items, 2) + unit, F32), s((2, ff) + unit, F32)),
        in_specs=[ANY, VMEM],
        out_specs=(VMEM, VMEM),
        scratch_shapes=[
            pltpu.VMEM((items, highs, 2, 2, 2) + unit, BF16),
            pltpu.VMEM((items, highs, 2) + unit, BF16),
            pltpu.VMEM((items, highs, 2) + unit, BF16),
            pltpu.VMEM((2, items, highs) + unit, BF16),
            pltpu.VMEM((highs - 1, items, 2) + unit, BF16),
            dma, dma, dma((2,)), dma((2,)), dma((2,)), dma((2,)), dma((highs,)), dma((highs,)), dma, dma, dma,
        ],
        compiler_params=pltpu.CompilerParams(collective_id=4, has_side_effects=True, vmem_limit_bytes=60 << 20),
    )(g, one)


def scatter_x_kernel(n, dx_in, dh, pieces_in, gtok, red, dx, g, psum, pgot, *rest):
    ra, rb, rc = rest[0:3], rest[3:6], rest[6:9]
    mine, theirs, c_s, c_r, t_s, t_r, w_s, w_r, p_s, p_r, k_s = rest[9:]
    w = where_am_i(n)
    me, core, chip = w["me"], w["core"], w["chip"]
    partner = me ^ 1
    chips = w["chips"]
    greet([partner] + [me ^ (2 * m) for m in range(1, chips)])
    rows = dh.shape[1]
    swap_p = send(pieces_in.at[:, 1 - core], pgot, w_s, w_r, partner)
    fills = [
        pltpu.make_async_copy(dx_in, dx, k_s.at[0]),
        pltpu.make_async_copy(pieces_in.at[:, core], psum, k_s.at[1]),
    ]
    for copy in fills:
        copy.start()
    for copy in fills:
        copy.wait()
    bits = (w["cube"] // 4, w["cube"] // 2 % 2, w["cube"] % 2)
    masks = (8, 4, 2)
    spans = cube_rows(2 * rows)

    def region(s, order, phase, far):
        index = [slice(None)] * 3
        for done in order[:phase]:
            index[done] = bits[done]
        axis = order[phase]
        index[axis] = 1 - bits[axis] if far else bits[axis]
        return tuple(index) + (pl.ds(*spans[s]),)

    def launch(phase):
        bufs = (ra, rb, rc)[phase]
        return [
            send(dx.at[region(s, order, phase, True)], bufs[s], c_s.at[phase, s], c_r.at[phase, s], me ^ masks[order[phase]])
            for s, order in enumerate(CUBE_ORDERS)
        ]

    def fold(phase):
        bufs = (ra, rb, rc)[phase]
        for s, order in enumerate(CUBE_ORDERS):
            at = region(s, order, phase, False)
            dx[at] = (dx[at].astype(F32) + bufs[s][...].astype(F32)).astype(BF16)

    live = launch(0)
    swap_p.wait()
    psum[...] = (psum[...].astype(F32) + pgot[...].astype(F32)).astype(BF16)
    copies = [send(psum.at[chip ^ m], g.at[m], p_s.at[m], p_r.at[m], me ^ (2 * m)) for m in range(1, chips)]
    own = pltpu.make_async_copy(psum.at[chip], g.at[0], k_s.at[2])
    own.start()
    for phase in range(3):
        for copy in live:
            copy.wait()
        fold(phase)
        if phase < 2:
            live = launch(phase + 1)
    here = (bits[0], bits[1], bits[2])
    theirs_at = pl.ds(pl.multiple_of((1 - core) * rows, rows), rows)
    own_at = pl.ds(pl.multiple_of(core * rows, rows), rows)
    swap = send(dx.at[here + (theirs_at,)], theirs, t_s, t_r, partner)
    gtok[core] = (dh[core] + dx[here + (own_at,)].astype(F32)).astype(BF16)
    own.wait()
    for copy in copies:
        copy.wait()
    for m in range(chips):
        term = g[m].astype(F32)
        if m < CUBE:
            red[m] = term
        else:
            red[m % CUBE] += term
    swap.wait()
    gtok[1 - core] = (dh[1 - core] + theirs[...].astype(F32)).astype(BF16)


def scatter_x(n, dx, dh, pieces):
    _, rows, width = dh.shape
    chips = n // 2
    unit = pieces.shape[2:]
    dma = pltpu.SemaphoreType.DMA
    s = jax.ShapeDtypeStruct
    spans = cube_rows(2 * rows)
    bufs = [pltpu.VMEM(lead + (spans[i][1], width), BF16) for lead in ((2, 2), (2,), ()) for i in range(3)]
    return pl.pallas_call(
        functools.partial(scatter_x_kernel, n),
        name="scatter_x",
        out_shape=(s((2, rows, width), BF16), s((CUBE,) + unit, F32)),
        in_specs=[ANY, VMEM, ANY],
        out_specs=(VMEM, VMEM),
        scratch_shapes=[
            pltpu.VMEM(dx.shape, BF16),
            pltpu.VMEM((chips,) + unit, BF16),
            pltpu.VMEM((chips,) + unit, BF16),
            pltpu.VMEM((chips,) + unit, BF16),
        ]
        + bufs
        + [
            pltpu.VMEM((rows, width), BF16),
            pltpu.VMEM((rows, width), BF16),
            dma((3, 3)), dma((3, 3)), dma, dma, dma, dma, dma((chips,)), dma((chips,)), dma((3,)),
        ],
        compiler_params=pltpu.CompilerParams(collective_id=5, has_side_effects=True, vmem_limit_bytes=60 << 20),
    )(dx, dh, pieces)


def on_device(
    n, tokens, cotangent, seq_lengths, slot_block, w_query, w_key, w_value, w_output, w_in, w_out,
    b_query, b_value, b_output, b_in, b_out, ln1_gain, ln1_bias, ln2_gain, ln2_bias,
):
    _, rows, width = tokens.shape
    wr = w_query.shape[0]
    fr = w_out.shape[0]
    ff = fr // wr
    chips = n // 2
    highs = n // 8
    device = lax.axis_index("fsdp")
    core, chip = device % 2, device // 2
    cube = chip % CUBE
    lengths = jnp.sum(jnp.where(slot_block == device // BLOCK_DEVS, seq_lengths, 0), axis=1).astype(jnp.int32)
    live = lax.dynamic_slice(lengths, (core,), (1,))
    pad = -(-(wr + 1) // 16) * 16
    cols = jnp.stack([w_query, w_key, w_value]).reshape(3, wr, CUBE, PAIR).transpose(2, 1, 0, 3)
    cols = cols.reshape(CUBE, wr, 3 * PAIR)
    line = jnp.concatenate([b_query, b_value, b_output, b_out, ln1_gain, ln1_bias, ln2_gain, ln2_bias, b_in])
    line = jnp.pad(line, (0, 3 * PAIR - line.shape[0]))
    tail = jnp.pad(line[None], ((0, pad - wr - 1), (0, 0)))
    pieces = jnp.concatenate([cols, jnp.broadcast_to(tail, (CUBE,) + tail.shape)], axis=1)
    in_loc = w_in.reshape(wr, chips, 2, ff, wr).transpose(2, 3, 0, 1, 4).reshape(2, ff, wr, HALF)
    w_loc = jnp.concatenate([w_output, w_out]).reshape(ff + 1, wr, 2, HALF).transpose(0, 2, 1, 3)
    x_all, p_all, w_all = gather(n, tokens, pieces, w_loc, in_loc)
    x = x_all.reshape(BLOCK_DEVS * rows, width)
    w_qkv = p_all[:, :, :wr].reshape(width, 3 * PAIR)
    lines = p_all[:, :, wr].reshape(n, 3 * PAIR)
    small = lines[:, : 8 * wr].reshape(n, 8, wr).transpose(1, 0, 2).reshape(8, width)
    bias_in = lax.dynamic_index_in_dim(lines.reshape(chips, 2, 3 * PAIR), core, 1, keepdims=False)
    bias_in = bias_in[:, 8 * wr : 8 * wr + fr].reshape(chips, ff, wr).transpose(1, 0, 2).reshape(ff, HALF)
    bias_qv = lax.dynamic_slice(small, (0, cube * PAIR), (2, PAIR)).astype(F32)
    q, k, v, o, low, lse = attend(live, x, w_qkv, bias_qv[0:1], bias_qv[1:2])
    attn = exchange(to_rows_kernel, n, low.reshape(BLOCK_DEVS, rows, PAIR), (2, rows, width), "to_rows", 1)
    out, dh, dattn, g_in, g_out, g_o, g_small, g_bin = rows_call(
        n, lengths, attn, tokens, cotangent, w_all, small, bias_in
    )
    do = exchange(to_heads_kernel, n, dattn, (BLOCK_DEVS, rows, PAIR), "to_heads", 2).reshape(-1, PAIR)
    dx, dw, db = attend_back(live, q, k, v, o, lse, do, x, w_qkv)
    unit = (wr, HALF)
    g = jnp.concatenate(
        [
            g_in.reshape((ff, highs, 2, 2, 2) + unit),
            g_out.reshape((ff, 2, highs, 2, 2) + unit).transpose(0, 2, 3, 4, 1, 5, 6),
        ]
    )
    one = g_o.reshape((2, highs, 2, 2, 2) + unit).transpose(4, 1, 2, 3, 0, 5, 6)
    r_w, r_in = scatter_w(n, g, one)
    wide = jnp.zeros((2, width), F32)
    wide = lax.dynamic_update_slice(wide, jnp.stack([db[0, :PAIR], db[0, 2 * PAIR :]]), (0, cube * PAIR))
    lines = (g_small + jnp.pad(wide, ((0, 6), (0, 0)))).reshape(8, n, wr).transpose(1, 0, 2).reshape(n, 8 * wr)
    hidden = g_bin.reshape(ff, chips, wr).transpose(1, 0, 2).reshape(chips, 1, fr)
    hidden = jnp.where(jnp.arange(2)[None, :, None] == core, hidden, 0.0).reshape(n, fr)
    lines = jnp.concatenate([lines, hidden], axis=1)
    lines = jnp.pad(lines, ((0, 0), (0, 3 * PAIR - lines.shape[1])))[:, None]
    parts = jnp.concatenate([dw.reshape(n, wr, 3 * PAIR), lines, jnp.zeros((n, pad - wr - 1, 3 * PAIR), F32)], axis=1)
    parts = parts.astype(BF16).reshape(chips, 2, pad, 3 * PAIR)
    gtok, red = scatter_x(n, dx.reshape(2, 2, 2, 2 * rows, width), dh, parts)
    red = jnp.stack([lax.dynamic_index_in_dim(red, cube ^ m, 0, keepdims=False) for m in range(CUBE)])
    g_qkv = red[:, :wr].reshape(CUBE, wr, 3, PAIR).transpose(2, 1, 0, 3).reshape(3, wr, width)
    line = jnp.sum(red[:, wr], axis=0)
    g_w_in = r_in.reshape(2, ff, wr, chips, wr).transpose(2, 3, 0, 1, 4).reshape(wr, fr * n)
    flat = r_w.transpose(0, 2, 1, 3).reshape(ff * 2 + 1, wr, width)
    biases = [line[i * wr : (i + 1) * wr] for i in range(8)]
    bq, bv, bo, bout, gain1, shift1, gain2, shift2 = biases
    return (
        out, gtok, g_qkv[0], g_qkv[1], g_qkv[2], flat[0], g_w_in, flat[1 + ff :].reshape(fr, width),
        bq, bv, bo, line[8 * wr : 8 * wr + fr], bout, gain1, shift1, gain2, shift2,
    )


def solution(mesh):
    n = mesh.shape["fsdp"]
    rows, vector, whole = P(None, "fsdp", None), P("fsdp"), P()
    matrix = P("fsdp", None)
    return jax.shard_map(
        functools.partial(on_device, n),
        mesh=mesh,
        in_specs=(rows, rows, whole, whole) + (matrix,) * 6 + (vector,) * 9,
        out_specs=(rows, rows) + (matrix,) * 6 + (vector,) * 9,
        check_vma=False,
    )
```

```python
import functools

import jax
import jax.numpy as jnp
from jax import lax
from jax.experimental import pallas as pl
from jax.experimental.pallas import tpu as pltpu
from jax.sharding import PartitionSpec as P

HEAD_DIM = 64
BLOCK_DEVS = 16
CUBE = BLOCK_DEVS // 2
PAIR = 2 * HEAD_DIM
HALF = 512
MESH = pl.DeviceIdType.MESH
VMEM = pl.BlockSpec(memory_space=pltpu.VMEM)
SMEM = pl.BlockSpec(memory_space=pltpu.SMEM)
ANY = pl.BlockSpec(memory_space=pl.ANY)
F32 = jnp.float32
BF16 = jnp.bfloat16


def dot(a, b, ca=1, cb=0):
    return lax.dot_general(a, b, (((ca,), (cb,)), ((), ())), preferred_element_type=F32)


def send(src, dst, send_sem, recv_sem, device):
    copy = pltpu.make_async_remote_copy(
        src_ref=src,
        dst_ref=dst,
        send_sem=send_sem,
        recv_sem=recv_sem,
        device_id=(device,),
        device_id_type=MESH,
    )
    copy.start()
    return copy


def greet(devices):
    barrier = pltpu.get_barrier_semaphore()
    for device in devices:
        pl.semaphore_signal(barrier, inc=1, device_id=(device,), device_id_type=MESH)
    pl.semaphore_wait(barrier, len(devices))


def where_am_i(n):
    me = lax.axis_index("fsdp")
    chip = me // 2
    return dict(
        me=me,
        core=me % 2,
        chip=chip,
        cube=chip % CUBE,
        rank=me % BLOCK_DEVS,
        high=chip // 4,
        l1=chip // 2 % 2,
        l0=chip % 2,
        n=n,
        chips=n // 2,
        highs=n // 8,
    )


CUBE_ORDERS = ((0, 1, 2), (1, 2, 0), (2, 0, 1))


def cube_rows(total):
    first = total // 3 // 16 * 16
    last = total - 2 * first
    return ((0, last), (last, first), (last + first, first))


def gather_kernel(n, tok, pieces, w_loc, in_loc, x_all, p_all, w_all,
                  tok_s, tok_r, cube_s, cube_r, pc_s, pc_r, sw_s, sw_r, loc_s, wi_s, wi_r,
                  hi_s, hi_r, ab_s, ab_r):
    w = where_am_i(n)
    me, core, chip, high, l1, l0 = w["me"], w["core"], w["chip"], w["high"], w["l1"], w["l0"]
    rows = tok.shape[1]
    partner = me ^ 1
    others = [me ^ (2 * m) for m in range(1, w["chips"])]
    greet([partner] + others)
    bits = (w["cube"] // 4, w["cube"] // 2 % 2, w["cube"] % 2)

    def mine(s=slice(None)):
        return x_all.at[bits[0], bits[1], bits[2], s]

    own_rows = pl.ds(pl.multiple_of(core * rows, rows), rows)
    locals_ = []
    locals_.append(pltpu.make_async_copy(tok.at[core], mine(own_rows), loc_s.at[0]))
    locals_[-1].start()
    swap = send(tok.at[1 - core], mine(own_rows), tok_s, tok_r, partner)
    items = w_all.shape[0]
    ff = (items - 1) // 2
    here = lambda item, s: w_all.at[item, high, l1, l0, s]
    swap_in = send(in_loc.at[1 - core], w_all.at[pl.ds(1, ff), high, l1, l0, core], wi_s, wi_r, partner)
    locals_.append(pltpu.make_async_copy(in_loc.at[core], w_all.at[pl.ds(1, ff), high, l1, l0, core], loc_s.at[1]))
    locals_[-1].start()
    locals_.append(pltpu.make_async_copy(w_loc.at[pl.ds(0, 1)], w_all.at[pl.ds(0, 1), high, l1, l0], loc_s.at[2]))
    locals_[-1].start()
    locals_.append(pltpu.make_async_copy(w_loc.at[pl.ds(1, ff)], w_all.at[pl.ds(1 + ff, ff), high, l1, l0], loc_s.at[3]))
    locals_[-1].start()
    locals_.append(pltpu.make_async_copy(pieces.at[w["cube"]], p_all.at[chip, core], loc_s.at[4]))
    locals_[-1].start()
    piece_copies = []
    for m in range(1, w["chips"]):
        there = (chip ^ m) % CUBE
        piece_copies.append(send(pieces.at[there], p_all.at[chip, core], pc_s.at[m], pc_r.at[m], others[m - 1]))
    for copy in locals_:
        copy.wait()
    swap.wait()
    spans = cube_rows(2 * rows)
    masks = (8, 4, 2)
    live = []
    for phase in range(3):
        for copy in live:
            copy.wait()
        live = []
        for s, order in enumerate(CUBE_ORDERS):
            index = [bits[0], bits[1], bits[2]]
            for done in order[:phase]:
                index[done] = slice(None)
            region = x_all.at[index[0], index[1], index[2], pl.ds(*spans[s])]
            live.append(send(region, region, cube_s.at[phase, s], cube_r.at[phase, s], me ^ masks[order[phase]]))
    swap_in.wait()
    for copy in piece_copies:
        copy.wait()
    region = p_all.at[:, core]
    swap_p = send(region, region, sw_s, sw_r, partner)
    for copy in live:
        copy.wait()
    swap_p.wait()
    groups = [(0, 1)] + [(1 + j, None) for j in range(ff)]

    def group(g, *index):
        if g == 0:
            return [w_all.at[(pl.ds(0, 1),) + index]]
        return [w_all.at[(pl.ds(g, 1),) + index], w_all.at[(pl.ds(g + ff, 1),) + index]]

    def high_phase(g):
        out = []
        for m in range(1, w["highs"]):
            for i, region in enumerate(group(g, high, l1, l0)):
                out.append(send(region, region, hi_s.at[g, m, i], hi_r.at[g, m, i], me ^ (8 * m)))
        return out

    def low_phase(g, phase):
        out = []
        for s in range(2):
            if phase == 0:
                index = (slice(None), l1, l0, s)
                to = me ^ (2 if s == 0 else 4)
            elif s == 0:
                index = (slice(None), l1, slice(None), s)
                to = me ^ 4
            else:
                index = (slice(None), slice(None), l0, s)
                to = me ^ 2
            for i, region in enumerate(group(g, *index)):
                out.append(send(region, region, ab_s.at[g, phase, s, i], ab_r.at[g, phase, s, i], to))
        return out

    def settle(copies):
        for copy in copies:
            copy.wait()

    waiting = {}
    count = len(groups)
    for step in range(count + 2):
        if step < count:
            waiting[step, 0] = high_phase(step)
        if 0 <= step - 1 < count:
            settle(waiting.pop((step - 1, 0)))
            waiting[step - 1, 1] = low_phase(step - 1, 0)
        if 0 <= step - 2 < count:
            settle(waiting.pop((step - 2, 1)))
            waiting[step - 2, 2] = low_phase(step - 2, 1)
    for copies in waiting.values():
        settle(copies)


def gather(n, tok, pieces, w_loc, in_loc):
    rows, width = tok.shape[1:]
    wr = in_loc.shape[2]
    ff = in_loc.shape[1]
    items = 1 + 2 * ff
    chips, highs = n // 2, n // 8
    dma = pltpu.SemaphoreType.DMA
    return pl.pallas_call(
        functools.partial(gather_kernel, n),
        name="gather",
        out_shape=(
            jax.ShapeDtypeStruct((2, 2, 2, 2 * rows, width), BF16),
            jax.ShapeDtypeStruct((chips, 2) + pieces.shape[1:], BF16),
            jax.ShapeDtypeStruct((items, highs, 2, 2, 2, wr, HALF), BF16),
        ),
        in_specs=[ANY] * 4,
        out_specs=(ANY, ANY, ANY),
        scratch_shapes=[
            dma, dma, dma((3, 3)), dma((3, 3)), dma((chips,)), dma((chips,)), dma, dma, dma((5,)), dma, dma,
            dma((ff + 1, highs, 2)), dma((ff + 1, highs, 2)), dma((ff + 1, 2, 2, 2)), dma((ff + 1, 2, 2, 2)),
        ],
        compiler_params=pltpu.CompilerParams(collective_id=0, has_side_effects=True),
    )(tok, pieces, w_loc, in_loc)


def attend_kernel(live, x, w, bq, bv, q, k, v, o, low, lse):
    rows = x.shape[0]
    tile = 256

    def project(i, _):
        at = pl.ds(pl.multiple_of(i * tile, tile), tile)
        y = dot(x[at, :], w[...])
        q[at, :] = ((y[:, :PAIR] + bq[...]) * HEAD_DIM ** (-0.5)).astype(BF16)
        k[at, :] = y[:, PAIR : 2 * PAIR].astype(BF16)
        v[at, :] = (y[:, 2 * PAIR :] + bv[...]).astype(BF16)
        return 0

    lax.fori_loop(0, rows // tile, project, 0)
    length = live[0]

    def step(i, _):
        at = pl.ds(pl.multiple_of(i * tile, tile), tile)
        outs, logs = [], []
        for h in range(2):
            c = slice(h * HEAD_DIM, (h + 1) * HEAD_DIM)
            s = dot(q[at, c], k[:, c], 1, 1)
            place = lax.broadcasted_iota(jnp.int32, s.shape, 1)
            s = jnp.where(place < length, s, -1e30)
            top = jnp.max(s, axis=1, keepdims=True)
            e = jnp.exp(s - top)
            total = jnp.sum(e, axis=1, keepdims=True)
            mixed = dot(e.astype(BF16), v[:, c])
            outs.append(mixed / total)
            logs.append(jnp.broadcast_to(top + jnp.log(total), (tile, HEAD_DIM)))
        out = jnp.concatenate(outs, axis=1)
        o[at, :] = out
        low[at, :] = out.astype(BF16)
        lse[at, :] = jnp.concatenate(logs, axis=1)
        return 0

    lax.fori_loop(0, rows // tile, step, 0)


def attend(live, x, w, bq, bv):
    rows = x.shape[0]
    low = jax.ShapeDtypeStruct((rows, PAIR), BF16)
    wide = jax.ShapeDtypeStruct((rows, PAIR), F32)
    return pl.pallas_call(
        attend_kernel,
        name="attend",
        out_shape=(low, low, low, wide, low, wide),
        in_specs=[SMEM, VMEM, VMEM, VMEM, VMEM],
        out_specs=(VMEM,) * 6,
        compiler_params=pltpu.CompilerParams(vmem_limit_bytes=56 << 20),
    )(live, x, w, bq, bv)


def to_rows_kernel(n, low, out, ss, rs, ls):
    w = where_am_i(n)
    me, core, cube, rank = w["me"], w["core"], w["cube"], w["rank"]
    greet([me ^ m for m in range(1, BLOCK_DEVS)])
    there = out.at[core, :, pl.ds(pl.multiple_of(cube * PAIR, PAIR), PAIR)]
    own = pltpu.make_async_copy(low.at[rank], there, ls)
    own.start()
    copies = [send(low.at[rank ^ m], there, ss.at[m], rs.at[m], me ^ m) for m in range(1, BLOCK_DEVS)]
    own.wait()
    for copy in copies:
        copy.wait()


def to_heads_kernel(n, grad, out, ss, rs, ls):
    w = where_am_i(n)
    me, core, cube, rank = w["me"], w["core"], w["cube"], w["rank"]
    greet([me ^ m for m in range(1, BLOCK_DEVS)])

    def piece(m):
        return grad.at[core ^ (m % 2), :, pl.ds(pl.multiple_of((cube ^ (m // 2)) * PAIR, PAIR), PAIR)]

    own = pltpu.make_async_copy(piece(0), out.at[rank], ls)
    own.start()
    copies = [send(piece(m), out.at[rank], ss.at[m], rs.at[m], me ^ m) for m in range(1, BLOCK_DEVS)]
    own.wait()
    for copy in copies:
        copy.wait()


def exchange(kernel, n, value, shape, name, ident):
    dma = pltpu.SemaphoreType.DMA
    return pl.pallas_call(
        functools.partial(kernel, n),
        name=name,
        out_shape=jax.ShapeDtypeStruct(shape, BF16),
        in_specs=[ANY],
        out_specs=ANY,
        scratch_shapes=[dma((BLOCK_DEVS,)), dma((BLOCK_DEVS,)), dma],
        compiler_params=pltpu.CompilerParams(collective_id=ident, has_side_effects=True),
    )(value)


def norm_forward(h):
    center = h - jnp.mean(h, axis=1, keepdims=True)
    rs = lax.rsqrt(jnp.mean(center * center, axis=1, keepdims=True) + 1e-05)
    return center * rs, rs


def norm_back(e, n, rs, gain):
    eg = e * gain
    return (eg - jnp.mean(eg, axis=1, keepdims=True) - n * jnp.mean(eg * n, axis=1, keepdims=True)) * rs


def total_rows(value):
    return jnp.sum(value, axis=0, keepdims=True)


def rows_kernel(n, live, attn, tok, cot, w_all, small, b_in,
                out, dh, dattn, g_in, g_out, g_o, g_small, g_bin,
                w_o, x1, n1, r1, x1_low, slope, act, part, got, df2, got2,
                wo_s, wo_r, x_s, x_r, h_s, h_r, d_s, d_r, e_s, e_r, lo_s):
    w = where_am_i(n)
    me, core, rank = w["me"], w["core"], w["rank"]
    partner = me ^ 1
    greet([partner])
    rows, width = tok.shape[1:]
    own = 2 * rows
    ff = (w_all.shape[0] - 1) // 2
    swap = send(w_all.at[0], w_o.at[:, :, :, core], wo_s, wo_r, partner)
    keep = pltpu.make_async_copy(w_all.at[0], w_o.at[:, :, :, core], lo_s)
    keep.start()
    keep.wait()
    swap.wait()

    def wo(s):
        return w_o[:, :, :, :, s].reshape(width, HALF)

    names = ("bq", "bv", "bo", "bout", "g1", "s1", "g2", "s2")
    param = {name: small[i : i + 1, :].astype(F32) for i, name in enumerate(names)}
    for m in range(2):
        at = slice(m * rows, (m + 1) * rows)
        a = attn[m]
        mid = jnp.concatenate([dot(a, wo(0)), dot(a, wo(1))], axis=1)
        h = tok[m].astype(F32) + mid + param["bo"]
        nn, rs = norm_forward(h)
        n1[at, :] = nn
        r1[at, :] = jnp.broadcast_to(rs, (rows, 128))
        y = nn * param["g1"] + param["s1"]
        x1[at, :] = y
        x1_low[at, :] = y.astype(BF16)
    swap = send(x1_low.at[pl.ds(0, own)], x1_low.at[pl.ds(own, own)], x_s, x_r, partner)
    swap.wait()
    for j in range(ff):
        w_in = w_all[1 + j].reshape(width, HALF)
        u = dot(x1_low[...], w_in) + b_in[j : j + 1, :].astype(F32)
        phi = 0.5 + 0.5 * lax.erf(u * 0.7071067811865476)
        slope[j] = phi + u * (0.3989422804014327 * jnp.exp(-0.5 * u * u))
        a = (u * phi).astype(BF16)
        act[j] = a
        for s in range(2):
            w_out = w_all[1 + ff + j, :, :, :, s].reshape(HALF, HALF)
            c = slice(s * HALF, (s + 1) * HALF)
            if j == 0:
                part[:, c] = dot(a, w_out)
            else:
                part[:, c] += dot(a, w_out)
    swap = send(part.at[pl.ds(own, own)], got, h_s, h_r, partner)
    swap.wait()
    bout = param["bout"]
    sums = {name: jnp.zeros((1, width), F32) for name in ("bo", "bout", "g1", "s1", "g2", "s2")}
    for m in range(2):
        at = slice(m * rows, (m + 1) * rows)
        h = x1[at, :] + part[at, :] + got[at, :] + bout
        nn, rs = norm_forward(h)
        out[m] = (nn * param["g2"] + param["s2"]).astype(BF16)
        place = rank * rows + lax.broadcasted_iota(jnp.int32, (rows, 1), 0)
        dy = jnp.where(place < live[m], cot[m].astype(F32), 0.0)
        sums["g2"] += total_rows(dy * nn)
        sums["s2"] += total_rows(dy)
        d = norm_back(dy, nn, rs, param["g2"])
        x1[at, :] = d
        low = d.astype(BF16)
        df2[at, :] = low
        sums["bout"] += total_rows(low.astype(F32))
    swap = send(df2.at[pl.ds(0, own)], df2.at[pl.ds(own, own)], d_s, d_r, partner)
    swap.wait()
    for j in range(ff):
        w_in = w_all[1 + j].reshape(width, HALF)
        da = None
        for s in range(2):
            w_out = w_all[1 + ff + j, :, :, :, s].reshape(HALF, HALF)
            c = slice(s * HALF, (s + 1) * HALF)
            term = dot(df2[:, c], w_out, 1, 1)
            da = term if da is None else da + term
            g_out[j, s] = dot(act[j], df2[:, c], 0, 0).astype(BF16)
        du = (da * slope[j]).astype(BF16)
        g_bin[j : j + 1, :] = total_rows(du.astype(F32))
        g_in[j] = dot(x1_low[...], du, 0, 0).astype(BF16)
        back = dot(du, w_in, 1, 1)
        if j == 0:
            part[...] = back
        else:
            part[...] += back
    swap = send(part.at[pl.ds(own, own)], got2, e_s, e_r, partner)
    swap.wait()
    for m in range(2):
        at = slice(m * rows, (m + 1) * rows)
        e = x1[at, :] + part[at, :] + got2[at, :]
        nn, rs = n1[at, :], r1[at, 0:1]
        sums["g1"] += total_rows(e * nn)
        sums["s1"] += total_rows(e)
        d = norm_back(e, nn, rs, param["g1"])
        dh[m] = d
        low = d.astype(BF16)
        df2[at, :] = low
        sums["bo"] += total_rows(low.astype(F32))
        dattn[m] = (dot(low[:, :HALF], wo(0), 1, 1) + dot(low[:, HALF:], wo(1), 1, 1)).astype(BF16)
    for s in range(2):
        c = slice(s * HALF, (s + 1) * HALF)
        g_o[s] = sum(dot(attn[m], df2[m * rows : (m + 1) * rows, c], 0, 0) for m in range(2)).astype(BF16)
    g_small[0:2, :] = jnp.zeros((2, width), F32)
    for i, name in enumerate(names[2:]):
        g_small[2 + i : 3 + i, :] = sums[name]


def rows_call(n, live, attn, tok, cot, w_all, small, b_in):
    _, rows, width = tok.shape
    items, highs = w_all.shape[:2]
    wr = w_all.shape[5]
    ff = (items - 1) // 2
    own = 2 * rows
    dma = pltpu.SemaphoreType.DMA
    s = jax.ShapeDtypeStruct
    return pl.pallas_call(
        functools.partial(rows_kernel, n),
        name="rows",
        out_shape=(
            s((2, rows, width), BF16),
            s((2, rows, width), F32),
            s((2, rows, width), BF16),
            s((ff, width, HALF), BF16),
            s((ff, 2, HALF, HALF), BF16),
            s((2, width, HALF), BF16),
            s((8, width), F32),
            s((ff, HALF), F32),
        ),
        in_specs=[SMEM] + [VMEM] * 6,
        out_specs=(VMEM,) * 8,
        scratch_shapes=[
            pltpu.VMEM((highs, 2, 2, 2, 2, wr, HALF), BF16),
            pltpu.VMEM((own, width), F32),
            pltpu.VMEM((own, width), F32),
            pltpu.VMEM((own, 128), F32),
            pltpu.VMEM((2 * own, width), BF16),
            pltpu.VMEM((ff, 2 * own, HALF), F32),
            pltpu.VMEM((ff, 2 * own, HALF), BF16),
            pltpu.VMEM((2 * own, width), F32),
            pltpu.VMEM((own, width), F32),
            pltpu.VMEM((2 * own, width), BF16),
            pltpu.VMEM((own, width), F32),
        ]
        + [dma] * 11,
        compiler_params=pltpu.CompilerParams(collective_id=3, has_side_effects=True, vmem_limit_bytes=60 << 20),
    )(live, attn, tok, cot, w_all, small, b_in)


def attend_back_kernel(live, q, k, v, o, lse, do, x, w, dx, dw, db, g, dk, dv):
    rows = q.shape[0]
    tile = 256
    length = live[0]
    scale = HEAD_DIM ** (-0.5)
    dk[...] = jnp.zeros_like(dk)
    dv[...] = jnp.zeros_like(dv)

    def step(i, _):
        at = pl.ds(pl.multiple_of(i * tile, tile), tile)
        outs = []
        for h in range(2):
            c = slice(h * HEAD_DIM, (h + 1) * HEAD_DIM)
            s = dot(q[at, c], k[:, c], 1, 1)
            place = lax.broadcasted_iota(jnp.int32, s.shape, 1)
            p = jnp.where(place < length, jnp.exp(s - lse[at, h * HEAD_DIM : h * HEAD_DIM + 1]), 0.0)
            d = do[at, c]
            dp = dot(d, v[:, c], 1, 1)
            inner = jnp.sum(d.astype(F32) * o[at, c], axis=1, keepdims=True)
            ds = (p * (dp - inner)).astype(BF16)
            outs.append(dot(ds, k[:, c]))
            dk[h] += dot(ds, q[at, c], 0, 0)
            dv[h] += dot(p.astype(BF16), d, 0, 0)
        g[at, 0:PAIR] = (jnp.concatenate(outs, axis=1).astype(BF16).astype(F32) * scale).astype(BF16)
        return 0

    lax.fori_loop(0, rows // tile, step, 0)
    g[:, PAIR : 2 * PAIR] = jnp.concatenate([dk[0], dk[1]], axis=1).astype(BF16)
    g[:, 2 * PAIR :] = jnp.concatenate([dv[0], dv[1]], axis=1).astype(BF16)

    def spread(i, _):
        at = pl.ds(pl.multiple_of(i * tile, tile), tile)
        dx[at, :] = dot(g[at, :], w[...], 1, 1).astype(BF16)
        return 0

    lax.fori_loop(0, rows // tile, spread, 0)
    dw[...] = dot(x[...], g[...], 0, 0)
    db[...] = jnp.broadcast_to(total_rows(g[...].astype(F32)), db.shape)


def attend_back(live, q, k, v, o, lse, do, x, w):
    rows, width = x.shape
    s = jax.ShapeDtypeStruct
    return pl.pallas_call(
        attend_back_kernel,
        name="attend_back",
        out_shape=(s((rows, width), BF16), s((width, 3 * PAIR), F32), s((8, 3 * PAIR), F32)),
        in_specs=[SMEM] + [VMEM] * 8,
        out_specs=(VMEM,) * 3,
        scratch_shapes=[
            pltpu.VMEM((rows, 3 * PAIR), BF16),
            pltpu.VMEM((2, rows, HEAD_DIM), F32),
            pltpu.VMEM((2, rows, HEAD_DIM), F32),
        ],
        compiler_params=pltpu.CompilerParams(vmem_limit_bytes=60 << 20),
    )(live, q, k, v, o, lse, do, x, w)


def add_into(target, *terms):
    total = target[...].astype(F32)
    for term in terms:
        total = total + term[...].astype(F32)
    target[...] = total.astype(target.dtype)


def scatter_w_kernel(n, g_in, one, out, out_in, g, r1a, r1b, r2, r3,
                     o_s, o_r, a_s, a_r, b_s, b_r, h_s, h_r, i_s, i_r, k_s):
    w = where_am_i(n)
    me, core, high, l1, l0 = w["me"], w["core"], w["high"], w["l1"], w["l0"]
    highs = w["highs"]
    partner = me ^ 1
    greet([partner, me ^ 2, me ^ 4] + [me ^ (8 * m) for m in range(1, highs)])
    items = g.shape[0]
    ff = (items - 1) // 2
    swap = send(one.at[1 - core], g.at[0], o_s, o_r, partner)
    fill = pltpu.make_async_copy(g_in, g.at[pl.ds(1, 2 * ff)], k_s)
    fill.start()
    fill.wait()
    swap.wait()

    def fold(i, _):
        g[0, i] = (g[0, i].astype(F32) + one[core, i].astype(F32)).astype(BF16)
        return 0

    lax.fori_loop(0, highs, fold, 0)
    first = [
        send(g.at[:, :, 1 - l1, :, 0], r1a, a_s.at[0], a_r.at[0], me ^ 4),
        send(g.at[:, :, :, 1 - l0, 1], r1b, a_s.at[1], a_r.at[1], me ^ 2),
    ]
    for copy in first:
        copy.wait()

    def add1(i, _):
        for h in range(highs):
            for b in range(2):
                g[i, h, l1, b, 0] = (g[i, h, l1, b, 0].astype(F32) + r1a[i, h, b].astype(F32)).astype(BF16)
                g[i, h, b, l0, 1] = (g[i, h, b, l0, 1].astype(F32) + r1b[i, h, b].astype(F32)).astype(BF16)
        return 0

    lax.fori_loop(0, items, add1, 0)
    second = [
        send(g.at[:, :, l1, 1 - l0, 0], r2.at[0], b_s.at[0], b_r.at[0], me ^ 2),
        send(g.at[:, :, 1 - l1, l0, 1], r2.at[1], b_s.at[1], b_r.at[1], me ^ 4),
    ]
    for copy in second:
        copy.wait()

    def add2(i, _):
        for h in range(highs):
            for s in range(2):
                g[i, h, l1, l0, s] = (g[i, h, l1, l0, s].astype(F32) + r2[s, i, h].astype(F32)).astype(BF16)
        return 0

    lax.fori_loop(0, items, add2, 0)
    third = [
        send(g.at[:, high ^ m, l1, l0], r3.at[m - 1], h_s.at[m], h_r.at[m], me ^ (8 * m)) for m in range(1, highs)
    ]
    for copy in third:
        copy.wait()

    def add3(i, _):
        for s in range(2):
            total = g[i, high, l1, l0, s].astype(F32)
            for m in range(1, highs):
                total = total + r3[m - 1, i, s].astype(F32)
            out[i, s] = total
        return 0

    lax.fori_loop(0, items, add3, 0)
    keep = pltpu.make_async_copy(out.at[pl.ds(1, ff), core], out_in.at[core], k_s)
    keep.start()
    swap = send(out.at[pl.ds(1, ff), 1 - core], out_in.at[core], i_s, i_r, partner)
    keep.wait()
    swap.wait()


def scatter_w(n, g, one):
    items, highs = g.shape[0] + 1, g.shape[1]
    wr = g.shape[5]
    ff = (items - 1) // 2
    dma = pltpu.SemaphoreType.DMA
    s = jax.ShapeDtypeStruct
    unit = (wr, HALF)
    return pl.pallas_call(
        functools.partial(scatter_w_kernel, n),
        name="scatter_w",
        out_shape=(s((items, 2) + unit, F32), s((2, ff) + unit, F32)),
        in_specs=[ANY, VMEM],
        out_specs=(VMEM, VMEM),
        scratch_shapes=[
            pltpu.VMEM((items, highs, 2, 2, 2) + unit, BF16),
            pltpu.VMEM((items, highs, 2) + unit, BF16),
            pltpu.VMEM((items, highs, 2) + unit, BF16),
            pltpu.VMEM((2, items, highs) + unit, BF16),
            pltpu.VMEM((highs - 1, items, 2) + unit, BF16),
            dma, dma, dma((2,)), dma((2,)), dma((2,)), dma((2,)), dma((highs,)), dma((highs,)), dma, dma, dma,
        ],
        compiler_params=pltpu.CompilerParams(collective_id=4, has_side_effects=True, vmem_limit_bytes=60 << 20),
    )(g, one)


def scatter_x_kernel(n, dx_in, dh, pieces_in, gtok, red, dx, g, psum, pgot, *rest):
    ra, rb, rc = rest[0:3], rest[3:6], rest[6:9]
    mine, theirs, c_s, c_r, t_s, t_r, w_s, w_r, p_s, p_r, k_s = rest[9:]
    w = where_am_i(n)
    me, core, chip = w["me"], w["core"], w["chip"]
    partner = me ^ 1
    chips = w["chips"]
    greet([partner] + [me ^ (2 * m) for m in range(1, chips)])
    rows = dh.shape[1]
    swap_p = send(pieces_in.at[:, 1 - core], pgot, w_s, w_r, partner)
    fills = [
        pltpu.make_async_copy(dx_in, dx, k_s.at[0]),
        pltpu.make_async_copy(pieces_in.at[:, core], psum, k_s.at[1]),
    ]
    for copy in fills:
        copy.start()
    for copy in fills:
        copy.wait()
    bits = (w["cube"] // 4, w["cube"] // 2 % 2, w["cube"] % 2)
    masks = (8, 4, 2)
    spans = cube_rows(2 * rows)

    def region(s, order, phase, far):
        index = [slice(None)] * 3
        for done in order[:phase]:
            index[done] = bits[done]
        axis = order[phase]
        index[axis] = 1 - bits[axis] if far else bits[axis]
        return tuple(index) + (pl.ds(*spans[s]),)

    def launch(phase):
        bufs = (ra, rb, rc)[phase]
        return [
            send(dx.at[region(s, order, phase, True)], bufs[s], c_s.at[phase, s], c_r.at[phase, s], me ^ masks[order[phase]])
            for s, order in enumerate(CUBE_ORDERS)
        ]

    def fold(phase):
        bufs = (ra, rb, rc)[phase]
        for s, order in enumerate(CUBE_ORDERS):
            at = region(s, order, phase, False)
            dx[at] = (dx[at].astype(F32) + bufs[s][...].astype(F32)).astype(BF16)

    live = launch(0)
    swap_p.wait()
    psum[...] = (psum[...].astype(F32) + pgot[...].astype(F32)).astype(BF16)
    copies = [send(psum.at[chip ^ m], g.at[m], p_s.at[m], p_r.at[m], me ^ (2 * m)) for m in range(1, chips)]
    own = pltpu.make_async_copy(psum.at[chip], g.at[0], k_s.at[2])
    own.start()
    for phase in range(3):
        for copy in live:
            copy.wait()
        fold(phase)
        if phase < 2:
            live = launch(phase + 1)
    here = (bits[0], bits[1], bits[2])
    theirs_at = pl.ds(pl.multiple_of((1 - core) * rows, rows), rows)
    own_at = pl.ds(pl.multiple_of(core * rows, rows), rows)
    swap = send(dx.at[here + (theirs_at,)], theirs, t_s, t_r, partner)
    gtok[core] = (dh[core] + dx[here + (own_at,)].astype(F32)).astype(BF16)
    own.wait()
    for copy in copies:
        copy.wait()
    for m in range(chips):
        term = g[m].astype(F32)
        if m < CUBE:
            red[m] = term
        else:
            red[m % CUBE] += term
    swap.wait()
    gtok[1 - core] = (dh[1 - core] + theirs[...].astype(F32)).astype(BF16)


def scatter_x(n, dx, dh, pieces):
    _, rows, width = dh.shape
    chips = n // 2
    unit = pieces.shape[2:]
    dma = pltpu.SemaphoreType.DMA
    s = jax.ShapeDtypeStruct
    spans = cube_rows(2 * rows)
    bufs = [pltpu.VMEM(lead + (spans[i][1], width), BF16) for lead in ((2, 2), (2,), ()) for i in range(3)]
    return pl.pallas_call(
        functools.partial(scatter_x_kernel, n),
        name="scatter_x",
        out_shape=(s((2, rows, width), BF16), s((CUBE,) + unit, F32)),
        in_specs=[ANY, VMEM, ANY],
        out_specs=(VMEM, VMEM),
        scratch_shapes=[
            pltpu.VMEM(dx.shape, BF16),
            pltpu.VMEM((chips,) + unit, BF16),
            pltpu.VMEM((chips,) + unit, BF16),
            pltpu.VMEM((chips,) + unit, BF16),
        ]
        + bufs
        + [
            pltpu.VMEM((rows, width), BF16),
            pltpu.VMEM((rows, width), BF16),
            dma((3, 3)), dma((3, 3)), dma, dma, dma, dma, dma((chips,)), dma((chips,)), dma((3,)),
        ],
        compiler_params=pltpu.CompilerParams(collective_id=5, has_side_effects=True, vmem_limit_bytes=60 << 20),
    )(dx, dh, pieces)


def start(copies):
    for copy in copies:
        copy.start()


def wait(copies):
    for copy in copies:
        copy.wait()


def remote(src, dst, sems, index, device):
    send_sem, recv_sem = sems
    return pltpu.make_async_remote_copy(
        src_ref=src,
        dst_ref=dst,
        send_sem=send_sem.at[index],
        recv_sem=recv_sem.at[index],
        device_id=(device,),
        device_id_type=MESH,
    )


def add_rows(dst, at, src, src_at):
    dst[at] = (dst[at].astype(F32) + src[src_at].astype(F32)).astype(dst.dtype)


COLS = 256


def layer_kernel(n, shapes, seq_len, slot, tok, cot, wq, wk, wv, wo, w_in, w_out, line,
                 out, gtok, gq, gk, gv, gwo, gwin, gwout, gline, *scratch):
    s = dict(zip(shapes, scratch, strict=True))
    here = where_am_i(n)
    me, core, chip, cube, rank = (here[name] for name in ("me", "core", "chip", "cube", "rank"))
    high, l1, l0, chips, highs = (here[name] for name in ("high", "l1", "l0", "chips", "highs"))
    partner = me ^ 1
    _, rows, width = tok.shape
    own = 2 * rows
    wr, fr = wo.shape[0], w_out.shape[0]
    half = fr * chips
    chunk = half // highs
    pad = s["pieces"].shape[1]
    bits = (cube // 4, cube // 2 % 2, cube % 2)
    x_all, p_all, w_o, w_i, w_u = s["x_all"], s["p_all"], s["w_o"], s["w_i"], s["w_u"]

    def sems(name):
        return s[name + "_s"], s[name + "_r"]

    met = sorted({m for m in range(1, BLOCK_DEVS)} | {2 * m for m in range(1, chips)})
    barrier = pltpu.get_barrier_semaphore()
    for m in met:
        pl.semaphore_signal(barrier, inc=1, device_id=(me ^ m,), device_id_type=MESH)

    lengths = []
    for m in range(2):
        length = jnp.int32(0)
        for i in range(slot.shape[1]):
            length = length + jnp.where(slot[m, i] == me // BLOCK_DEVS, seq_len[m, i], 0)
        lengths.append(length)

    pieces, w_loc = s["pieces"], s["w_loc"]
    for k in range(CUBE):
        for i, ref in enumerate((wq, wk, wv)):
            pieces[k, 0:wr, i * PAIR : (i + 1) * PAIR] = ref[:, k * PAIR : (k + 1) * PAIR]
        pieces[k, wr:pad, :] = jnp.broadcast_to(line[...], (pad - wr, 3 * PAIR))
    for i in range(chips):
        for q in range(2):
            at = (2 * i + q) * fr
            w_loc[q, :, i * fr : (i + 1) * fr] = w_in[:, at : at + fr]
    pl.semaphore_wait(barrier, len(met))

    own_rows = pl.ds(pl.multiple_of(core * rows, rows), rows)
    swap_tok = remote(tok.at[1 - core], x_all.at[bits[0], bits[1], bits[2], own_rows], sems("swap"), 0, partner)
    swap_tok.start()
    swap_in = remote(w_loc.at[1 - core], w_i.at[high, l1, l0, core], sems("swap"), 1, partner)
    piece_copies = [
        remote(pieces.at[(chip ^ m) % CUBE], p_all.at[chip, core], sems("piece"), m, me ^ (2 * m))
        for m in range(1, chips)
    ]
    x_all[bits[0], bits[1], bits[2], own_rows] = tok[core]
    p_all[chip, core] = pieces[cube]
    w_i[high, l1, l0, core] = w_loc[core]
    w_o[high, l1, l0, core] = wo[...]
    w_u[high, l1, l0] = w_out[...]
    swap_tok.wait()

    spans = cube_rows(own)
    masks = (8, 4, 2)

    def cube_phase(phase):
        out_ = []
        for i, order in enumerate(CUBE_ORDERS):
            index = list(bits)
            for done in order[:phase]:
                index[done] = slice(None)
            region = x_all.at[index[0], index[1], index[2], pl.ds(*spans[i])]
            out_.append(remote(region, region, (s["cube_s"].at[phase], s["cube_r"].at[phase]), i, me ^ masks[order[phase]]))
        return out_

    outs = width // COLS
    groups = 1 + highs + outs

    def part_of(g, index):
        h_, a_, b_, t = index
        if g == 0:
            c = slice(None) if t is None else pl.ds(t * HALF, HALF)
            return w_o.at[h_, a_, b_, core, :, c]
        if g <= highs:
            c = pl.ds((g - 1) * chunk, chunk)
            return w_i.at[h_, a_, b_, slice(None) if t is None else t, :, c]
        c = pl.ds((g - 1 - highs) * COLS, COLS)
        r = slice(None) if t is None else pl.ds(t * fr // 2, fr // 2)
        return w_u.at[h_, a_, b_, r, c]

    def high_copies(g):
        region = part_of(g, (high, l1, l0, None))
        return [
            remote(region, region, (s["hi_s"].at[g], s["hi_r"].at[g]), m, me ^ (8 * m)) for m in range(1, highs)
        ]

    every = slice(None)

    def low_copies(g, phase):
        ab = (s["ab_s"].at[g, phase], s["ab_r"].at[g, phase])
        if phase == 0:
            first, second = (every, l1, l0, 0), (every, l1, l0, 1)
            to = (me ^ 2, me ^ 4)
        else:
            first, second = (every, l1, every, 0), (every, every, l0, 1)
            to = (me ^ 4, me ^ 2)
        a, b = part_of(g, first), part_of(g, second)
        return [remote(a, a, ab, 0, to[0]), remote(b, b, ab, 1, to[1])]

    def gather_beat(b):
        if 0 <= b - 1 < groups:
            wait(high_copies(b - 1))
            start(low_copies(b - 1, 0))
        if 0 <= b - 2 < groups:
            wait(low_copies(b - 2, 0))
            start(low_copies(b - 2, 1))
        if 0 <= b + 1 < groups:
            start(high_copies(b + 1))

    start(cube_phase(0))
    swap_in.start()
    start(piece_copies)
    wait(cube_phase(0))
    start(cube_phase(1))
    wait(piece_copies)
    swap_p = remote(p_all.at[:, core], p_all.at[:, core], sems("swap"), 2, partner)
    swap_p.start()
    wait(cube_phase(1))
    start(cube_phase(2))
    swap_in.wait()
    start(high_copies(0))
    start(high_copies(1))
    swap_p.wait()

    param, b_in = s["param"], s["b_in"]
    tail = p_all[:, :, wr:pad, :].reshape(n * (pad - wr), 3 * PAIR)
    pick = (
        lax.broadcasted_iota(jnp.int32, (n, n * (pad - wr)), 0) * (pad - wr)
        == lax.broadcasted_iota(jnp.int32, (n, n * (pad - wr)), 1)
    )
    lines = dot(pick.astype(BF16), tail).astype(BF16)
    lane = lax.broadcasted_iota(jnp.int32, (3 * PAIR, width), 1)
    column = lax.broadcasted_iota(jnp.int32, (3 * PAIR, width), 0)
    owner = lax.broadcasted_iota(jnp.int32, (n, width), 1) // wr == lax.broadcasted_iota(jnp.int32, (n, width), 0)

    def selector(i):
        return (column == i * wr + lane % wr).astype(BF16)

    for i in range(8):
        spread = dot(lines, selector(i))
        param[i : i + 1, :] = jnp.sum(jnp.where(owner, spread, 0.0), axis=0, keepdims=True)
    half_pick = (
        (2 * lax.broadcasted_iota(jnp.int32, (chips, n), 0) + core) == lax.broadcasted_iota(jnp.int32, (chips, n), 1)
    )
    mine = dot(half_pick.astype(BF16), lines)[:, 8 * wr : 8 * wr + fr]
    for i in range(chips):
        b_in[0:1, i * fr : (i + 1) * fr] = mine[i : i + 1, :]
    wait(cube_phase(2))

    q, k, v, o, low, lse = (s[name] for name in ("q", "k", "v", "o", "low", "lse"))
    tile = own
    pair_at = pl.ds(pl.multiple_of(cube * PAIR, PAIR), PAIR)
    bq, bv = param[0:1, pair_at], param[1:2, pair_at]
    length = jnp.where(core == 0, lengths[0], lengths[1])

    def w_qkv():
        return p_all[:, :, 0:wr, :].reshape(width, 3 * PAIR)

    def project(i, _):
        at = pl.ds(pl.multiple_of(i * tile, tile), tile)
        y = dot(x_all[i // 4, i // 2 % 2, i % 2], w_qkv())
        q[at, :] = ((y[:, :PAIR] + bq) * HEAD_DIM ** (-0.5)).astype(BF16)
        k[at, :] = y[:, PAIR : 2 * PAIR].astype(BF16)
        v[at, :] = (y[:, 2 * PAIR :] + bv).astype(BF16)
        return 0

    lax.fori_loop(0, CUBE, project, 0)
    gather_beat(1)

    attn = s["attn"]
    low_dst = attn.at[core, :, pair_at]

    def row_copy(m):
        at = pl.ds(pl.multiple_of((rank ^ m) * rows, rows), rows)
        return remote(low.at[at], low_dst, sems("torow"), m, me ^ m)

    def attend_step(step, _):
        i = cube ^ step
        at = pl.ds(pl.multiple_of(i * tile, tile), tile)
        outs_, logs = [], []
        for h in range(2):
            c = slice(h * HEAD_DIM, (h + 1) * HEAD_DIM)
            sc = dot(q[at, c], k[:, c], 1, 1)
            place = lax.broadcasted_iota(jnp.int32, sc.shape, 1)
            sc = jnp.where(place < length, sc, -1e30)
            top = jnp.max(sc, axis=1, keepdims=True)
            e = jnp.exp(sc - top)
            total = jnp.sum(e, axis=1, keepdims=True)
            outs_.append(dot(e.astype(BF16), v[:, c]) / total)
            logs.append(jnp.broadcast_to(top + jnp.log(total), (tile, HEAD_DIM)))
        mixed = jnp.concatenate(outs_, axis=1)
        o[at, :] = mixed
        low[at, :] = mixed.astype(BF16)
        lse[at, :] = jnp.concatenate(logs, axis=1)

        @pl.when(step > 0)
        def _():
            row_copy(2 * step).start()

        row_copy(2 * step + 1).start()
        for at_step, beat in GATHER_BEATS:

            @pl.when(step == at_step)
            def _():
                gather_beat(beat)

        return 0

    lax.fori_loop(0, CUBE, attend_step, 0)
    attn[core, :, pair_at] = low[pl.ds(pl.multiple_of(rank * rows, rows), rows), :]
    beat = GATHER_BEATS[-1][1] + 1
    wait(low_copies(0, 1))
    swap_o = remote(w_o.at[:, :, :, core], w_o.at[:, :, :, core], sems("swap"), 3, partner)
    swap_o.start()
    gather_beat(beat)
    wait([row_copy(m) for m in range(1, BLOCK_DEVS)])
    swap_o.wait()

    x1, n1, r1, x1_low, slope, act = (s[name] for name in ("x1", "n1", "r1", "x1_low", "slope", "act"))
    part, got, df2 = (s[name] for name in ("part", "got", "df2"))
    sums = s["sums"]

    def whole_o():
        return w_o[...].reshape(width, width)

    for m in range(2):
        at = slice(m * rows, (m + 1) * rows)
        part[at, :] = dot(attn[m], whole_o())
    for m in range(2):
        at = slice(m * rows, (m + 1) * rows)
        nn, rs = norm_forward(tok[m].astype(F32) + part[at, :] + param[2:3, :])
        n1[at, :] = nn
        r1[at, :] = jnp.broadcast_to(rs, (rows, 128))
        y = nn * param[4:5, :] + param[5:6, :]
        x1[at, :] = y
        x1_low[at, :] = y.astype(BF16)
    swap_x = remote(x1_low.at[pl.ds(0, own)], x1_low.at[pl.ds(own, own)], sems("swap"), 4, partner)
    swap_x.start()
    beat += 1
    gather_beat(beat)
    swap_x.wait()

    for j in range(highs):
        wait(low_copies(1 + j, 1))
        cols = slice(j * chunk, (j + 1) * chunk)
        slope[j] = dot(x1_low[...], w_i[:, :, :, :, :, cols].reshape(width, chunk)) + b_in[0:1, cols]

        def gelu_step(i, _):
            at = pl.ds(pl.multiple_of(i * 64, 64), 64)
            u = slope[j, at, :]
            phi = 0.5 + 0.5 * lax.erf(u * 0.7071067811865476)
            slope[j, at, :] = phi + u * (0.3989422804014327 * jnp.exp(-0.5 * u * u))
            act[at, cols] = (u * phi).astype(BF16)
            return 0

        lax.fori_loop(0, 2 * own // 64, gelu_step, 0)
        beat += 1
        gather_beat(beat)
    while beat < groups + 1:
        beat += 1
        gather_beat(beat)

    def half_copy(j):
        at = pl.ds(j * COLS, COLS)
        return remote(part.at[pl.ds(own, own), at], got.at[:, at], sems("halves"), j, partner)

    for j in range(outs):
        wait(low_copies(1 + highs + j, 1))
        cols = slice(j * COLS, (j + 1) * COLS)
        part[:, cols] = dot(act[...], w_u[:, :, :, :, cols].reshape(half, COLS))
        half_copy(j).start()
    wait([half_copy(j) for j in range(outs)])

    for i in range(8):
        sums[i : i + 1, :] = jnp.zeros((1, width), F32)
    for m in range(2):
        at = slice(m * rows, (m + 1) * rows)
        nn, rs = norm_forward(x1[at, :] + part[at, :] + got[at, :] + param[3:4, :])
        out[m] = (nn * param[6:7, :] + param[7:8, :]).astype(BF16)
        place = rank * rows + lax.broadcasted_iota(jnp.int32, (rows, 1), 0)
        dy = jnp.where(place < lengths[m], cot[m].astype(F32), 0.0)
        sums[6:7, :] += total_rows(dy * nn)
        sums[7:8, :] += total_rows(dy)
        d = norm_back(dy, nn, rs, param[6:7, :])
        x1[at, :] = d
        d_low = d.astype(BF16)
        df2[at, :] = d_low
        sums[3:4, :] += total_rows(d_low.astype(F32))
    swap_d = remote(df2.at[pl.ds(0, own)], df2.at[pl.ds(own, own)], sems("swap"), 5, partner)
    swap_d.start()

    fin = s["fin"]

    def grad_part(r, index):
        g = r + 1 if r < highs + outs else 0
        return part_of(g, index)

    def buf(name, r, t):
        if r < highs:
            return s[name + "i"].at[r, t]
        if r < highs + outs:
            return s[name + "u"].at[r - highs, t]
        return s[name + "o"].at[t]

    def reduce_copies(r, phase):
        if phase == 0:
            sem = (s["ra_s"].at[r], s["ra_r"].at[r])
            return [
                remote(grad_part(r, (every, 1 - l1, every, 0)), buf("ra", r, 0), sem, 0, me ^ 4),
                remote(grad_part(r, (every, every, 1 - l0, 1)), buf("ra", r, 1), sem, 1, me ^ 2),
            ]
        if phase == 1:
            sem = (s["rb_s"].at[r], s["rb_r"].at[r])
            return [
                remote(grad_part(r, (every, l1, 1 - l0, 0)), buf("rb", r, 0), sem, 0, me ^ 2),
                remote(grad_part(r, (every, 1 - l1, l0, 1)), buf("rb", r, 1), sem, 1, me ^ 4),
            ]
        sem = (s["rc_s"].at[r], s["rc_r"].at[r])
        return [
            remote(grad_part(r, (high ^ m, l1, l0, None)), buf("rc", r, m - 1), sem, m, me ^ (8 * m))
            for m in range(1, highs)
        ]

    def reduce_add(r, phase):
        if phase == 0:
            pairs = [
                (grad_part(r, (h, l1, b, 0)), buf("ra", r, 0).at[h, b]) for h in range(highs) for b in range(2)
            ] + [(grad_part(r, (h, b, l0, 1)), buf("ra", r, 1).at[h, b]) for h in range(highs) for b in range(2)]
        else:
            pairs = [(grad_part(r, (h, l1, l0, t)), buf("rb", r, t).at[h]) for h in range(highs) for t in range(2)]
        for mine_, theirs_ in pairs:
            mine_[...] = (mine_[...].astype(F32) + theirs_[...].astype(F32)).astype(BF16)

    def reduce_last(r):
        total = grad_part(r, (high, l1, l0, None))[...].astype(F32)
        for m in range(1, highs):
            total = total + buf("rc", r, m - 1)[...].astype(F32)
        if r < highs:
            fin[:, :, r * chunk : (r + 1) * chunk] = total
            fin_copy(r).start()
        elif r < highs + outs:
            gwout[:, (r - highs) * COLS : (r - highs + 1) * COLS] = total
        else:
            gwo[...] = total

    def fin_copy(r):
        at = pl.ds(r * chunk, chunk)
        return remote(fin.at[1 - core, :, at], s["fin_got"].at[:, at], sems("fin"), r, partner)

    def reduce_beat(b):
        if 0 <= b - 1 < groups:
            wait(reduce_copies(b - 1, 0))
            reduce_add(b - 1, 0)
            start(reduce_copies(b - 1, 1))
        if 0 <= b + 1 < groups:
            start(reduce_copies(b + 1, 0))
        if 0 <= b - 2 < groups:
            wait(reduce_copies(b - 2, 1))
            reduce_add(b - 2, 1)
            start(reduce_copies(b - 2, 2))
        if 0 <= b - 3 < groups:
            wait(reduce_copies(b - 3, 2))
            reduce_last(b - 3)

    swap_d.wait()
    du_ref, gbin = s["du"], s["gbin"]
    for j in range(highs):
        cols = slice(j * chunk, (j + 1) * chunk)
        da = dot(df2[...], w_u[j].reshape(chunk, width), 1, 1)
        du = (da * slope[j]).astype(BF16)
        du_ref[...] = du
        gbin[0:1, cols] = total_rows(du.astype(F32))
        back = dot(du, w_i[:, :, :, :, :, cols].reshape(width, chunk), 1, 1)
        if j == 0:
            part[...] = back
        else:
            part[...] += back
        if j == highs - 1:
            swap_e = remote(part.at[pl.ds(own, own)], got, sems("swap"), 6, partner)
            swap_e.start()
        w_i[:, :, :, :, :, cols] = dot(x1_low[...], du_ref[...], 0, 0).astype(BF16).reshape(highs, 2, 2, 2, wr, chunk)
        w_u[j] = dot(act[:, cols], df2[...], 0, 0).astype(BF16).reshape(2, 2, fr, width)
        if j == 1:
            start(reduce_copies(0, 0))
            start(reduce_copies(1, 0))
    reduce_beat(1)
    swap_e.wait()

    dattn = s["dattn"]
    for m in range(2):
        at = slice(m * rows, (m + 1) * rows)
        e = x1[at, :] + part[at, :] + got[at, :]
        nn, rs = n1[at, :], r1[at, 0:1]
        sums[4:5, :] += total_rows(e * nn)
        sums[5:6, :] += total_rows(e)
        d = norm_back(e, nn, rs, param[4:5, :])
        x1[at, :] = d
        d_low = d.astype(BF16)
        df2[at, :] = d_low
        sums[2:3, :] += total_rows(d_low.astype(F32))
    for m in range(2):
        dattn[m] = dot(df2[m * rows : (m + 1) * rows, :], whole_o(), 1, 1).astype(BF16)
    do = s["do"]

    def head_piece(m):
        at = pl.ds(pl.multiple_of((cube ^ (m // 2)) * PAIR, PAIR), PAIR)
        return dattn.at[core ^ (m % 2), :, at]

    def head_copy(m):
        return remote(head_piece(m), do.at[rank], sems("tohead"), m, me ^ m)

    start([head_copy(m) for m in range(1, BLOCK_DEVS)])
    do[rank] = dattn[core, :, pair_at]
    g_o = dot(attn[0], df2[0:rows, :], 0, 0) + dot(attn[1], df2[rows:own, :], 0, 0)
    w_o[...] = g_o.astype(BF16).reshape(highs, 2, 2, 2, wr, width)
    swap_g = remote(w_o.at[:, :, :, 1 - core], s["o_got"], sems("swap"), 7, partner)
    swap_g.start()
    reduce_beat(2)
    swap_g.wait()
    for h in range(highs):
        w_o[h, :, :, core] = (w_o[h, :, :, core].astype(F32) + s["o_got"][h].astype(F32)).astype(BF16)
    wait([head_copy(m) for m in range(1, BLOCK_DEVS)])

    acc, g = slope, s["g"]
    acc[...] = jnp.zeros_like(acc)
    scale = HEAD_DIM ** (-0.5)
    block = acc.shape[1]

    def back_step(i, _):
        at = pl.ds(pl.multiple_of(i * tile, tile), tile)
        outs_ = []
        d2 = do[pl.ds(2 * i, 2)].reshape(tile, PAIR)
        for h in range(2):
            c = slice(h * HEAD_DIM, (h + 1) * HEAD_DIM)
            d = d2[:, c]
            inner = jnp.sum(d.astype(F32) * o[at, c], axis=1, keepdims=True)
            norm = lse[at, h * HEAD_DIM : h * HEAD_DIM + 1]
            dq = None
            for b in range(acc.shape[0]):
                keys = slice(b * block, (b + 1) * block)
                sc = dot(q[at, c], k[keys, c], 1, 1)
                place = b * block + lax.broadcasted_iota(jnp.int32, sc.shape, 1)
                p = jnp.where(place < length, jnp.exp(sc - norm), 0.0)
                dp = dot(d, v[keys, c], 1, 1)
                ds = (p * (dp - inner)).astype(BF16)
                term = dot(ds, k[keys, c])
                dq = term if dq is None else dq + term
                acc[b, :, h * HEAD_DIM : (h + 1) * HEAD_DIM] += dot(ds, q[at, c], 0, 0)
                acc[b, :, PAIR + h * HEAD_DIM : PAIR + (h + 1) * HEAD_DIM] += dot(p.astype(BF16), d, 0, 0)
            outs_.append(dq)
        g[at, 0:PAIR] = (jnp.concatenate(outs_, axis=1).astype(BF16).astype(F32) * scale).astype(BF16)
        for at_step, beat_ in REDUCE_BEATS:

            @pl.when(i == at_step)
            def _():
                reduce_beat(beat_)

        return 0

    lax.fori_loop(0, CUBE, back_step, 0)
    for b in range(acc.shape[0]):
        lines_ = slice(b * block, (b + 1) * block)
        g[lines_, PAIR : 3 * PAIR] = acc[b, :, 0 : 2 * PAIR].astype(BF16)

    pg, pgot, pslot = s["pg"], s["pgot"], s["pslot"]
    step_width = width // highs

    def weight_step(i, _):
        cols = pl.ds(pl.multiple_of(i * step_width, step_width), step_width)
        block_ = dot(x_all[:, :, :, :, cols].reshape(CUBE * own, step_width), g[...], 0, 0).astype(BF16)
        pg[pl.ds(i * 4, 4), :, 0:wr, :] = block_.reshape(4, 2, wr, 3 * PAIR)
        return 0

    lax.fori_loop(0, highs, weight_step, 0)
    db = total_rows(g[...].astype(F32))
    sums[0:1, pair_at] = db[:, 0:PAIR]
    sums[1:2, pair_at] = db[:, 2 * PAIR :]
    sent = jnp.zeros((n, 3 * PAIR), F32)
    for i in range(8):
        placed = jnp.where(owner, sums[i : i + 1, :], 0.0).astype(BF16)
        sent = sent + dot(placed, selector(i), 1, 1)
    hidden = jnp.concatenate([gbin[0:1, i * fr : (i + 1) * fr] for i in range(chips)], axis=0)
    back_pick = (
        (2 * lax.broadcasted_iota(jnp.int32, (n, chips), 1) + core) == lax.broadcasted_iota(jnp.int32, (n, chips), 0)
    )
    hidden = dot(back_pick.astype(BF16), hidden.astype(BF16))
    sent = jnp.concatenate([sent[:, : 8 * wr], hidden], axis=1).astype(BF16)
    wide_pick = (
        lax.broadcasted_iota(jnp.int32, (n * (pad - wr), n), 1) * (pad - wr)
        == lax.broadcasted_iota(jnp.int32, (n * (pad - wr), n), 0)
    )
    pg[:, :, wr:pad, :] = dot(wide_pick.astype(BF16), sent).astype(BF16).reshape(chips, 2, pad - wr, 3 * PAIR)
    swap_g = remote(pg.at[:, 1 - core], pgot, sems("swap"), 8, partner)
    swap_g.start()

    def spread_rows(i, _):
        at = pl.ds(pl.multiple_of(i * tile, tile), tile)
        x_all[i // 4, i // 2 % 2, i % 2] = dot(g[at, :], w_qkv(), 1, 1).astype(BF16)
        return 0

    lax.fori_loop(0, CUBE, spread_rows, 0)
    bufs = [[s[f"x{phase}{i}"] for i in range(3)] for phase in range(3)]

    def region(i, order, phase, far):
        index = [slice(None)] * 3
        for done in order[:phase]:
            index[done] = bits[done]
        axis = order[phase]
        index[axis] = 1 - bits[axis] if far else bits[axis]
        return tuple(index) + (pl.ds(*spans[i]),)

    def row_sums(phase):
        sem = (s["xr_s"].at[phase], s["xr_r"].at[phase])
        return [
            remote(x_all.at[region(i, order, phase, True)], bufs[phase][i], sem, i, me ^ masks[order[phase]])
            for i, order in enumerate(CUBE_ORDERS)
        ]

    def row_fold(phase):
        for i, order in enumerate(CUBE_ORDERS):
            at = region(i, order, phase, False)
            x_all[at] = (x_all[at].astype(F32) + bufs[phase][i][...].astype(F32)).astype(BF16)

    start(row_sums(0))
    beat = REDUCE_BEATS[-1][1]
    swap_g.wait()
    for i in range(chips):
        pg[i, core] = (pg[i, core].astype(F32) + pgot[i].astype(F32)).astype(BF16)
    piece_sums = [
        remote(pg.at[chip ^ m, core], pslot.at[m], sems("psum"), m, me ^ (2 * m)) for m in range(1, chips)
    ]
    start(piece_sums)
    for phase in range(3):
        wait(row_sums(phase))
        row_fold(phase)
        if phase < 2:
            start(row_sums(phase + 1))
        beat += 1
        reduce_beat(beat)
    theirs_at = pl.ds(pl.multiple_of((1 - core) * rows, rows), rows)
    last = remote(x_all.at[bits[0], bits[1], bits[2], theirs_at], gtok.at[core], sems("swap"), 9, partner)
    last.start()
    mine_at = pl.ds(pl.multiple_of(core * rows, rows), rows)
    gtok[core] = (x1[mine_at, :] + x_all[bits[0], bits[1], bits[2], mine_at].astype(F32)).astype(BF16)
    while beat < groups + 2:
        beat += 1
        reduce_beat(beat)
    wait(piece_sums)
    gsum = jnp.zeros((1, 3 * PAIR), F32)
    for m in range(chips):
        term = pg[chip, core].astype(F32) if m == 0 else pslot[m].astype(F32)
        gsum = gsum + term[wr : wr + 1, :]
        at = pl.ds(pl.multiple_of((cube ^ (m % CUBE)) * PAIR, PAIR), PAIR)
        for i, ref in enumerate((gq, gk, gv)):
            value = term[0:wr, i * PAIR : (i + 1) * PAIR]
            if m < CUBE:
                ref[:, at] = value
            else:
                ref[:, at] += value
    gline[...] = gsum
    last.wait()
    yours_at = pl.ds(pl.multiple_of((1 - core) * rows, rows), rows)
    gtok[1 - core] = (x1[yours_at, :] + gtok[1 - core].astype(F32)).astype(BF16)
    wait([fin_copy(r) for r in range(highs)])
    for i in range(chips):
        at = slice(i * fr, (i + 1) * fr)
        gwin[:, pl.ds(pl.multiple_of((2 * i + core) * fr, fr), fr)] = fin[core, :, at]
        gwin[:, pl.ds(pl.multiple_of((2 * i + 1 - core) * fr, fr), fr)] = s["fin_got"][:, at]


GATHER_BEATS = ((1, 2), (4, 3), (7, 4))
REDUCE_BEATS = ((0, 3), (2, 4), (4, 5), (6, 6), (7, 7))


def layer(n, seq_len, slot, tok, cot, wq, wk, wv, wo, w_in, w_out, line):
    _, rows, width = tok.shape
    wr, fr = wo.shape[0], w_out.shape[0]
    chips, highs = n // 2, n // 8
    own, total = 2 * rows, BLOCK_DEVS * rows
    half = fr * chips
    chunk = half // highs
    outs = width // COLS
    groups = 1 + highs + outs
    pad = wr + 16
    spans = cube_rows(own)
    vm = pltpu.VMEM
    dma = pltpu.SemaphoreType.DMA
    shapes = {
        "x_all": vm((2, 2, 2, own, width), BF16),
        "p_all": vm((chips, 2, pad, 3 * PAIR), BF16),
        "w_o": vm((highs, 2, 2, 2, wr, width), BF16),
        "w_i": vm((highs, 2, 2, 2, wr, half), BF16),
        "w_u": vm((highs, 2, 2, fr, width), BF16),
        "pieces": vm((CUBE, pad, 3 * PAIR), BF16),
        "w_loc": vm((2, wr, half), BF16),
        "param": vm((8, width), F32),
        "b_in": vm((8, half), F32),
        "gbin": vm((8, half), F32),
        "sums": vm((8, width), F32),
        "q": vm((total, PAIR), BF16),
        "k": vm((total, PAIR), BF16),
        "v": vm((total, PAIR), BF16),
        "o": vm((total, PAIR), F32),
        "low": vm((total, PAIR), BF16),
        "lse": vm((total, PAIR), F32),
        "attn": vm((2, rows, width), BF16),
        "x1": vm((own, width), F32),
        "n1": vm((own, width), F32),
        "r1": vm((own, 128), F32),
        "x1_low": vm((2 * own, width), BF16),
        "slope": vm((highs, 2 * own, chunk), F32),
        "act": vm((2 * own, half), BF16),
        "part": vm((2 * own, width), F32),
        "got": vm((own, width), F32),
        "df2": vm((2 * own, width), BF16),
        "du": vm((2 * own, chunk), BF16),
        "dattn": vm((2, rows, width), BF16),
        "do": vm((BLOCK_DEVS, rows, PAIR), BF16),
        "g": vm((total, 3 * PAIR), BF16),
        "o_got": vm((highs, 2, 2, wr, width), BF16),
        "rai": vm((highs, 2, highs, 2, wr, chunk), BF16),
        "rau": vm((outs, 2, highs, 2, fr // 2, COLS), BF16),
        "rao": vm((2, highs, 2, wr, HALF), BF16),
        "rbi": vm((highs, 2, highs, wr, chunk), BF16),
        "rbu": vm((outs, 2, highs, fr // 2, COLS), BF16),
        "rbo": vm((2, highs, wr, HALF), BF16),
        "rci": vm((highs, highs - 1, 2, wr, chunk), BF16),
        "rcu": vm((outs, highs - 1, fr, COLS), BF16),
        "rco": vm((highs - 1, wr, width), BF16),
        "fin": vm((2, wr, half), F32),
        "fin_got": vm((wr, half), F32),
        "pg": vm((chips, 2, pad, 3 * PAIR), BF16),
        "pgot": vm((chips, pad, 3 * PAIR), BF16),
        "pslot": vm((chips, pad, 3 * PAIR), BF16),
    }
    for phase, lead in enumerate(((2, 2), (2,), ())):
        for i in range(3):
            shapes[f"x{phase}{i}"] = vm(lead + (spans[i][1], width), BF16)
    counts = {
        "swap": (10,), "piece": (chips,), "cube": (3, 3), "hi": (groups, highs), "ab": (groups, 2, 2),
        "torow": (BLOCK_DEVS,), "halves": (outs,), "tohead": (BLOCK_DEVS,), "ra": (groups, 2), "rb": (groups, 2),
        "rc": (groups, highs), "fin": (highs,), "xr": (3, 3), "psum": (chips,),
    }
    for name, count in counts.items():
        shapes[name + "_s"] = dma(count)
        shapes[name + "_r"] = dma(count)
    s = jax.ShapeDtypeStruct
    return pl.pallas_call(
        functools.partial(layer_kernel, n, tuple(shapes)),
        name="layer",
        out_shape=(
            s((2, rows, width), BF16),
            s((2, rows, width), BF16),
            s((wr, width), F32),
            s((wr, width), F32),
            s((wr, width), F32),
            s((wr, width), F32),
            s((wr, fr * n), F32),
            s((fr, width), F32),
            s((1, 3 * PAIR), F32),
        ),
        in_specs=[SMEM, SMEM] + [VMEM] * 9,
        out_specs=(VMEM,) * 9,
        scratch_shapes=list(shapes.values()),
        compiler_params=pltpu.CompilerParams(collective_id=6, has_side_effects=True, vmem_limit_bytes=64 << 20),
    )(seq_len, slot, tok, cot, wq, wk, wv, wo, w_in, w_out, line)


def on_device(
    n, tokens, cotangent, seq_lengths, slot_block, w_query, w_key, w_value, w_output, w_in, w_out,
    b_query, b_value, b_output, b_in, b_out, ln1_gain, ln1_bias, ln2_gain, ln2_bias,
):
    _, rows, width = tokens.shape
    wr = w_query.shape[0]
    fr = w_out.shape[0]
    ff = fr // wr
    chips = n // 2
    highs = n // 8
    device = lax.axis_index("fsdp")
    core, chip = device % 2, device // 2
    cube = chip % CUBE
    line = jnp.concatenate([b_query, b_value, b_output, b_out, ln1_gain, ln1_bias, ln2_gain, ln2_bias, b_in])
    if wr % 16 == 0 and 8 * wr + fr == 3 * PAIR:
        out, gtok, gq, gk, gv, gwo, gwin, gwout, line = layer(
            n, seq_lengths, slot_block, tokens, cotangent, w_query, w_key, w_value, w_output, w_in, w_out, line[None]
        )
        line = line[0]
        biases = [line[i * wr : (i + 1) * wr] for i in range(8)]
        bq, bv, bo, bout, gain1, shift1, gain2, shift2 = biases
        return (
            out, gtok, gq, gk, gv, gwo, gwin, gwout,
            bq, bv, bo, line[8 * wr :], bout, gain1, shift1, gain2, shift2,
        )
    lengths = jnp.sum(jnp.where(slot_block == device // BLOCK_DEVS, seq_lengths, 0), axis=1).astype(jnp.int32)
    live = lax.dynamic_slice(lengths, (core,), (1,))
    pad = -(-(wr + 1) // 16) * 16
    cols = jnp.stack([w_query, w_key, w_value]).reshape(3, wr, CUBE, PAIR).transpose(2, 1, 0, 3)
    cols = cols.reshape(CUBE, wr, 3 * PAIR)
    line = jnp.pad(line, (0, 3 * PAIR - line.shape[0]))
    tail = jnp.pad(line[None], ((0, pad - wr - 1), (0, 0)))
    pieces = jnp.concatenate([cols, jnp.broadcast_to(tail, (CUBE,) + tail.shape)], axis=1)
    in_loc = w_in.reshape(wr, chips, 2, ff, wr).transpose(2, 3, 0, 1, 4).reshape(2, ff, wr, HALF)
    w_loc = jnp.concatenate([w_output, w_out]).reshape(ff + 1, wr, 2, HALF).transpose(0, 2, 1, 3)
    x_all, p_all, w_all = gather(n, tokens, pieces, w_loc, in_loc)
    x = x_all.reshape(BLOCK_DEVS * rows, width)
    w_qkv = p_all[:, :, :wr].reshape(width, 3 * PAIR)
    lines = p_all[:, :, wr].reshape(n, 3 * PAIR)
    small = lines[:, : 8 * wr].reshape(n, 8, wr).transpose(1, 0, 2).reshape(8, width)
    bias_in = lax.dynamic_index_in_dim(lines.reshape(chips, 2, 3 * PAIR), core, 1, keepdims=False)
    bias_in = bias_in[:, 8 * wr : 8 * wr + fr].reshape(chips, ff, wr).transpose(1, 0, 2).reshape(ff, HALF)
    bias_qv = lax.dynamic_slice(small, (0, cube * PAIR), (2, PAIR)).astype(F32)
    q, k, v, o, low, lse = attend(live, x, w_qkv, bias_qv[0:1], bias_qv[1:2])
    attn = exchange(to_rows_kernel, n, low.reshape(BLOCK_DEVS, rows, PAIR), (2, rows, width), "to_rows", 1)
    out, dh, dattn, g_in, g_out, g_o, g_small, g_bin = rows_call(
        n, lengths, attn, tokens, cotangent, w_all, small, bias_in
    )
    do = exchange(to_heads_kernel, n, dattn, (BLOCK_DEVS, rows, PAIR), "to_heads", 2).reshape(-1, PAIR)
    dx, dw, db = attend_back(live, q, k, v, o, lse, do, x, w_qkv)
    unit = (wr, HALF)
    g = jnp.concatenate(
        [
            g_in.reshape((ff, highs, 2, 2, 2) + unit),
            g_out.reshape((ff, 2, highs, 2, 2) + unit).transpose(0, 2, 3, 4, 1, 5, 6),
        ]
    )
    one = g_o.reshape((2, highs, 2, 2, 2) + unit).transpose(4, 1, 2, 3, 0, 5, 6)
    r_w, r_in = scatter_w(n, g, one)
    wide = jnp.zeros((2, width), F32)
    wide = lax.dynamic_update_slice(wide, jnp.stack([db[0, :PAIR], db[0, 2 * PAIR :]]), (0, cube * PAIR))
    lines = (g_small + jnp.pad(wide, ((0, 6), (0, 0)))).reshape(8, n, wr).transpose(1, 0, 2).reshape(n, 8 * wr)
    hidden = g_bin.reshape(ff, chips, wr).transpose(1, 0, 2).reshape(chips, 1, fr)
    hidden = jnp.where(jnp.arange(2)[None, :, None] == core, hidden, 0.0).reshape(n, fr)
    lines = jnp.concatenate([lines, hidden], axis=1)
    lines = jnp.pad(lines, ((0, 0), (0, 3 * PAIR - lines.shape[1])))[:, None]
    parts = jnp.concatenate([dw.reshape(n, wr, 3 * PAIR), lines, jnp.zeros((n, pad - wr - 1, 3 * PAIR), F32)], axis=1)
    parts = parts.astype(BF16).reshape(chips, 2, pad, 3 * PAIR)
    gtok, red = scatter_x(n, dx.reshape(2, 2, 2, 2 * rows, width), dh, parts)
    red = jnp.stack([lax.dynamic_index_in_dim(red, cube ^ m, 0, keepdims=False) for m in range(CUBE)])
    g_qkv = red[:, :wr].reshape(CUBE, wr, 3, PAIR).transpose(2, 1, 0, 3).reshape(3, wr, width)
    line = jnp.sum(red[:, wr], axis=0)
    g_w_in = r_in.reshape(2, ff, wr, chips, wr).transpose(2, 3, 0, 1, 4).reshape(wr, fr * n)
    flat = r_w.transpose(0, 2, 1, 3).reshape(ff * 2 + 1, wr, width)
    biases = [line[i * wr : (i + 1) * wr] for i in range(8)]
    bq, bv, bo, bout, gain1, shift1, gain2, shift2 = biases
    return (
        out, gtok, g_qkv[0], g_qkv[1], g_qkv[2], flat[0], g_w_in, flat[1 + ff :].reshape(fr, width),
        bq, bv, bo, line[8 * wr : 8 * wr + fr], bout, gain1, shift1, gain2, shift2,
    )


def solution(mesh):
    n = mesh.shape["fsdp"]
    rows, vector, whole = P(None, "fsdp", None), P("fsdp"), P()
    matrix = P("fsdp", None)
    return jax.shard_map(
        functools.partial(on_device, n),
        mesh=mesh,
        in_specs=(rows, rows, whole, whole) + (matrix,) * 6 + (vector,) * 9,
        out_specs=(rows, rows) + (matrix,) * 6 + (vector,) * 9,
        check_vma=False,
    )
```

```python
import functools

import jax
import jax.numpy as jnp
from jax import lax
from jax.experimental import pallas as pl
from jax.experimental.pallas import tpu as pltpu
from jax.sharding import PartitionSpec as P

HEAD_DIM = 64
BLOCK_DEVS = 16
CUBE = BLOCK_DEVS // 2
PAIR = 2 * HEAD_DIM
HALF = 512
MESH = pl.DeviceIdType.MESH
VMEM = pl.BlockSpec(memory_space=pltpu.VMEM)
SMEM = pl.BlockSpec(memory_space=pltpu.SMEM)
ANY = pl.BlockSpec(memory_space=pl.ANY)
F32 = jnp.float32
BF16 = jnp.bfloat16


def dot(a, b, ca=1, cb=0):
    return lax.dot_general(a, b, (((ca,), (cb,)), ((), ())), preferred_element_type=F32)


def send(src, dst, send_sem, recv_sem, device):
    copy = pltpu.make_async_remote_copy(
        src_ref=src,
        dst_ref=dst,
        send_sem=send_sem,
        recv_sem=recv_sem,
        device_id=(device,),
        device_id_type=MESH,
    )
    copy.start()
    return copy


def greet(devices):
    barrier = pltpu.get_barrier_semaphore()
    for device in devices:
        pl.semaphore_signal(barrier, inc=1, device_id=(device,), device_id_type=MESH)
    pl.semaphore_wait(barrier, len(devices))


def where_am_i(n):
    me = lax.axis_index("fsdp")
    chip = me // 2
    return dict(
        me=me,
        core=me % 2,
        chip=chip,
        cube=chip % CUBE,
        rank=me % BLOCK_DEVS,
        high=chip // 4,
        l1=chip // 2 % 2,
        l0=chip % 2,
        n=n,
        chips=n // 2,
        highs=n // 8,
    )


CUBE_ORDERS = ((0, 1, 2), (1, 2, 0), (2, 0, 1))


def cube_rows(total):
    first = total // 3 // 16 * 16
    last = total - 2 * first
    return ((0, last), (last, first), (last + first, first))


def gather_kernel(n, tok, pieces, w_loc, in_loc, x_all, p_all, w_all,
                  tok_s, tok_r, cube_s, cube_r, pc_s, pc_r, sw_s, sw_r, loc_s, wi_s, wi_r,
                  hi_s, hi_r, ab_s, ab_r):
    w = where_am_i(n)
    me, core, chip, high, l1, l0 = w["me"], w["core"], w["chip"], w["high"], w["l1"], w["l0"]
    rows = tok.shape[1]
    partner = me ^ 1
    others = [me ^ (2 * m) for m in range(1, w["chips"])]
    greet([partner] + others)
    bits = (w["cube"] // 4, w["cube"] // 2 % 2, w["cube"] % 2)

    def mine(s=slice(None)):
        return x_all.at[bits[0], bits[1], bits[2], s]

    own_rows = pl.ds(pl.multiple_of(core * rows, rows), rows)
    locals_ = []
    locals_.append(pltpu.make_async_copy(tok.at[core], mine(own_rows), loc_s.at[0]))
    locals_[-1].start()
    swap = send(tok.at[1 - core], mine(own_rows), tok_s, tok_r, partner)
    items = w_all.shape[0]
    ff = (items - 1) // 2
    here = lambda item, s: w_all.at[item, high, l1, l0, s]
    swap_in = send(in_loc.at[1 - core], w_all.at[pl.ds(1, ff), high, l1, l0, core], wi_s, wi_r, partner)
    locals_.append(pltpu.make_async_copy(in_loc.at[core], w_all.at[pl.ds(1, ff), high, l1, l0, core], loc_s.at[1]))
    locals_[-1].start()
    locals_.append(pltpu.make_async_copy(w_loc.at[pl.ds(0, 1)], w_all.at[pl.ds(0, 1), high, l1, l0], loc_s.at[2]))
    locals_[-1].start()
    locals_.append(pltpu.make_async_copy(w_loc.at[pl.ds(1, ff)], w_all.at[pl.ds(1 + ff, ff), high, l1, l0], loc_s.at[3]))
    locals_[-1].start()
    locals_.append(pltpu.make_async_copy(pieces.at[w["cube"]], p_all.at[chip, core], loc_s.at[4]))
    locals_[-1].start()
    piece_copies = []
    for m in range(1, w["chips"]):
        there = (chip ^ m) % CUBE
        piece_copies.append(send(pieces.at[there], p_all.at[chip, core], pc_s.at[m], pc_r.at[m], others[m - 1]))
    for copy in locals_:
        copy.wait()
    swap.wait()
    spans = cube_rows(2 * rows)
    masks = (8, 4, 2)
    live = []
    for phase in range(3):
        for copy in live:
            copy.wait()
        live = []
        for s, order in enumerate(CUBE_ORDERS):
            index = [bits[0], bits[1], bits[2]]
            for done in order[:phase]:
                index[done] = slice(None)
            region = x_all.at[index[0], index[1], index[2], pl.ds(*spans[s])]
            live.append(send(region, region, cube_s.at[phase, s], cube_r.at[phase, s], me ^ masks[order[phase]]))
    swap_in.wait()
    for copy in piece_copies:
        copy.wait()
    region = p_all.at[:, core]
    swap_p = send(region, region, sw_s, sw_r, partner)
    for copy in live:
        copy.wait()
    swap_p.wait()
    groups = [(0, 1)] + [(1 + j, None) for j in range(ff)]

    def group(g, *index):
        if g == 0:
            return [w_all.at[(pl.ds(0, 1),) + index]]
        return [w_all.at[(pl.ds(g, 1),) + index], w_all.at[(pl.ds(g + ff, 1),) + index]]

    def high_phase(g):
        out = []
        for m in range(1, w["highs"]):
            for i, region in enumerate(group(g, high, l1, l0)):
                out.append(send(region, region, hi_s.at[g, m, i], hi_r.at[g, m, i], me ^ (8 * m)))
        return out

    def low_phase(g, phase):
        out = []
        for s in range(2):
            if phase == 0:
                index = (slice(None), l1, l0, s)
                to = me ^ (2 if s == 0 else 4)
            elif s == 0:
                index = (slice(None), l1, slice(None), s)
                to = me ^ 4
            else:
                index = (slice(None), slice(None), l0, s)
                to = me ^ 2
            for i, region in enumerate(group(g, *index)):
                out.append(send(region, region, ab_s.at[g, phase, s, i], ab_r.at[g, phase, s, i], to))
        return out

    def settle(copies):
        for copy in copies:
            copy.wait()

    waiting = {}
    count = len(groups)
    for step in range(count + 2):
        if step < count:
            waiting[step, 0] = high_phase(step)
        if 0 <= step - 1 < count:
            settle(waiting.pop((step - 1, 0)))
            waiting[step - 1, 1] = low_phase(step - 1, 0)
        if 0 <= step - 2 < count:
            settle(waiting.pop((step - 2, 1)))
            waiting[step - 2, 2] = low_phase(step - 2, 1)
    for copies in waiting.values():
        settle(copies)


def gather(n, tok, pieces, w_loc, in_loc):
    rows, width = tok.shape[1:]
    wr = in_loc.shape[2]
    ff = in_loc.shape[1]
    items = 1 + 2 * ff
    chips, highs = n // 2, n // 8
    dma = pltpu.SemaphoreType.DMA
    return pl.pallas_call(
        functools.partial(gather_kernel, n),
        name="gather",
        out_shape=(
            jax.ShapeDtypeStruct((2, 2, 2, 2 * rows, width), BF16),
            jax.ShapeDtypeStruct((chips, 2) + pieces.shape[1:], BF16),
            jax.ShapeDtypeStruct((items, highs, 2, 2, 2, wr, HALF), BF16),
        ),
        in_specs=[ANY] * 4,
        out_specs=(ANY, ANY, ANY),
        scratch_shapes=[
            dma, dma, dma((3, 3)), dma((3, 3)), dma((chips,)), dma((chips,)), dma, dma, dma((5,)), dma, dma,
            dma((ff + 1, highs, 2)), dma((ff + 1, highs, 2)), dma((ff + 1, 2, 2, 2)), dma((ff + 1, 2, 2, 2)),
        ],
        compiler_params=pltpu.CompilerParams(collective_id=0, has_side_effects=True),
    )(tok, pieces, w_loc, in_loc)


def attend_kernel(live, x, w, bq, bv, q, k, v, o, low, lse):
    rows = x.shape[0]
    tile = 256

    def project(i, _):
        at = pl.ds(pl.multiple_of(i * tile, tile), tile)
        y = dot(x[at, :], w[...])
        q[at, :] = ((y[:, :PAIR] + bq[...]) * HEAD_DIM ** (-0.5)).astype(BF16)
        k[at, :] = y[:, PAIR : 2 * PAIR].astype(BF16)
        v[at, :] = (y[:, 2 * PAIR :] + bv[...]).astype(BF16)
        return 0

    lax.fori_loop(0, rows // tile, project, 0)
    length = live[0]

    def step(i, _):
        at = pl.ds(pl.multiple_of(i * tile, tile), tile)
        outs, logs = [], []
        for h in range(2):
            c = slice(h * HEAD_DIM, (h + 1) * HEAD_DIM)
            s = dot(q[at, c], k[:, c], 1, 1)
            place = lax.broadcasted_iota(jnp.int32, s.shape, 1)
            s = jnp.where(place < length, s, -1e30)
            top = jnp.max(s, axis=1, keepdims=True)
            e = jnp.exp(s - top)
            total = jnp.sum(e, axis=1, keepdims=True)
            mixed = dot(e.astype(BF16), v[:, c])
            outs.append(mixed / total)
            logs.append(jnp.broadcast_to(top + jnp.log(total), (tile, HEAD_DIM)))
        out = jnp.concatenate(outs, axis=1)
        o[at, :] = out
        low[at, :] = out.astype(BF16)
        lse[at, :] = jnp.concatenate(logs, axis=1)
        return 0

    lax.fori_loop(0, rows // tile, step, 0)


def attend(live, x, w, bq, bv):
    rows = x.shape[0]
    low = jax.ShapeDtypeStruct((rows, PAIR), BF16)
    wide = jax.ShapeDtypeStruct((rows, PAIR), F32)
    return pl.pallas_call(
        attend_kernel,
        name="attend",
        out_shape=(low, low, low, wide, low, wide),
        in_specs=[SMEM, VMEM, VMEM, VMEM, VMEM],
        out_specs=(VMEM,) * 6,
        compiler_params=pltpu.CompilerParams(vmem_limit_bytes=56 << 20),
    )(live, x, w, bq, bv)


def to_rows_kernel(n, low, out, ss, rs, ls):
    w = where_am_i(n)
    me, core, cube, rank = w["me"], w["core"], w["cube"], w["rank"]
    greet([me ^ m for m in range(1, BLOCK_DEVS)])
    there = out.at[core, :, pl.ds(pl.multiple_of(cube * PAIR, PAIR), PAIR)]
    own = pltpu.make_async_copy(low.at[rank], there, ls)
    own.start()
    copies = [send(low.at[rank ^ m], there, ss.at[m], rs.at[m], me ^ m) for m in range(1, BLOCK_DEVS)]
    own.wait()
    for copy in copies:
        copy.wait()


def to_heads_kernel(n, grad, out, ss, rs, ls):
    w = where_am_i(n)
    me, core, cube, rank = w["me"], w["core"], w["cube"], w["rank"]
    greet([me ^ m for m in range(1, BLOCK_DEVS)])

    def piece(m):
        return grad.at[core ^ (m % 2), :, pl.ds(pl.multiple_of((cube ^ (m // 2)) * PAIR, PAIR), PAIR)]

    own = pltpu.make_async_copy(piece(0), out.at[rank], ls)
    own.start()
    copies = [send(piece(m), out.at[rank], ss.at[m], rs.at[m], me ^ m) for m in range(1, BLOCK_DEVS)]
    own.wait()
    for copy in copies:
        copy.wait()


def exchange(kernel, n, value, shape, name, ident):
    dma = pltpu.SemaphoreType.DMA
    return pl.pallas_call(
        functools.partial(kernel, n),
        name=name,
        out_shape=jax.ShapeDtypeStruct(shape, BF16),
        in_specs=[ANY],
        out_specs=ANY,
        scratch_shapes=[dma((BLOCK_DEVS,)), dma((BLOCK_DEVS,)), dma],
        compiler_params=pltpu.CompilerParams(collective_id=ident, has_side_effects=True),
    )(value)


def norm_forward(h):
    center = h - jnp.mean(h, axis=1, keepdims=True)
    rs = lax.rsqrt(jnp.mean(center * center, axis=1, keepdims=True) + 1e-05)
    return center * rs, rs


def norm_back(e, n, rs, gain):
    eg = e * gain
    return (eg - jnp.mean(eg, axis=1, keepdims=True) - n * jnp.mean(eg * n, axis=1, keepdims=True)) * rs


def total_rows(value):
    return jnp.sum(value, axis=0, keepdims=True)


def rows_kernel(n, live, attn, tok, cot, w_all, small, b_in,
                out, dh, dattn, g_in, g_out, g_o, g_small, g_bin,
                w_o, x1, n1, r1, x1_low, slope, act, part, got, df2, got2,
                wo_s, wo_r, x_s, x_r, h_s, h_r, d_s, d_r, e_s, e_r, lo_s):
    w = where_am_i(n)
    me, core, rank = w["me"], w["core"], w["rank"]
    partner = me ^ 1
    greet([partner])
    rows, width = tok.shape[1:]
    own = 2 * rows
    ff = (w_all.shape[0] - 1) // 2
    swap = send(w_all.at[0], w_o.at[:, :, :, core], wo_s, wo_r, partner)
    keep = pltpu.make_async_copy(w_all.at[0], w_o.at[:, :, :, core], lo_s)
    keep.start()
    keep.wait()
    swap.wait()

    def wo(s):
        return w_o[:, :, :, :, s].reshape(width, HALF)

    names = ("bq", "bv", "bo", "bout", "g1", "s1", "g2", "s2")
    param = {name: small[i : i + 1, :].astype(F32) for i, name in enumerate(names)}
    for m in range(2):
        at = slice(m * rows, (m + 1) * rows)
        a = attn[m]
        mid = jnp.concatenate([dot(a, wo(0)), dot(a, wo(1))], axis=1)
        h = tok[m].astype(F32) + mid + param["bo"]
        nn, rs = norm_forward(h)
        n1[at, :] = nn
        r1[at, :] = jnp.broadcast_to(rs, (rows, 128))
        y = nn * param["g1"] + param["s1"]
        x1[at, :] = y
        x1_low[at, :] = y.astype(BF16)
    swap = send(x1_low.at[pl.ds(0, own)], x1_low.at[pl.ds(own, own)], x_s, x_r, partner)
    swap.wait()
    for j in range(ff):
        w_in = w_all[1 + j].reshape(width, HALF)
        u = dot(x1_low[...], w_in) + b_in[j : j + 1, :].astype(F32)
        phi = 0.5 + 0.5 * lax.erf(u * 0.7071067811865476)
        slope[j] = phi + u * (0.3989422804014327 * jnp.exp(-0.5 * u * u))
        a = (u * phi).astype(BF16)
        act[j] = a
        for s in range(2):
            w_out = w_all[1 + ff + j, :, :, :, s].reshape(HALF, HALF)
            c = slice(s * HALF, (s + 1) * HALF)
            if j == 0:
                part[:, c] = dot(a, w_out)
            else:
                part[:, c] += dot(a, w_out)
    swap = send(part.at[pl.ds(own, own)], got, h_s, h_r, partner)
    swap.wait()
    bout = param["bout"]
    sums = {name: jnp.zeros((1, width), F32) for name in ("bo", "bout", "g1", "s1", "g2", "s2")}
    for m in range(2):
        at = slice(m * rows, (m + 1) * rows)
        h = x1[at, :] + part[at, :] + got[at, :] + bout
        nn, rs = norm_forward(h)
        out[m] = (nn * param["g2"] + param["s2"]).astype(BF16)
        place = rank * rows + lax.broadcasted_iota(jnp.int32, (rows, 1), 0)
        dy = jnp.where(place < live[m], cot[m].astype(F32), 0.0)
        sums["g2"] += total_rows(dy * nn)
        sums["s2"] += total_rows(dy)
        d = norm_back(dy, nn, rs, param["g2"])
        x1[at, :] = d
        low = d.astype(BF16)
        df2[at, :] = low
        sums["bout"] += total_rows(low.astype(F32))
    swap = send(df2.at[pl.ds(0, own)], df2.at[pl.ds(own, own)], d_s, d_r, partner)
    swap.wait()
    for j in range(ff):
        w_in = w_all[1 + j].reshape(width, HALF)
        da = None
        for s in range(2):
            w_out = w_all[1 + ff + j, :, :, :, s].reshape(HALF, HALF)
            c = slice(s * HALF, (s + 1) * HALF)
            term = dot(df2[:, c], w_out, 1, 1)
            da = term if da is None else da + term
            g_out[j, s] = dot(act[j], df2[:, c], 0, 0).astype(BF16)
        du = (da * slope[j]).astype(BF16)
        g_bin[j : j + 1, :] = total_rows(du.astype(F32))
        g_in[j] = dot(x1_low[...], du, 0, 0).astype(BF16)
        back = dot(du, w_in, 1, 1)
        if j == 0:
            part[...] = back
        else:
            part[...] += back
    swap = send(part.at[pl.ds(own, own)], got2, e_s, e_r, partner)
    swap.wait()
    for m in range(2):
        at = slice(m * rows, (m + 1) * rows)
        e = x1[at, :] + part[at, :] + got2[at, :]
        nn, rs = n1[at, :], r1[at, 0:1]
        sums["g1"] += total_rows(e * nn)
        sums["s1"] += total_rows(e)
        d = norm_back(e, nn, rs, param["g1"])
        dh[m] = d
        low = d.astype(BF16)
        df2[at, :] = low
        sums["bo"] += total_rows(low.astype(F32))
        dattn[m] = (dot(low[:, :HALF], wo(0), 1, 1) + dot(low[:, HALF:], wo(1), 1, 1)).astype(BF16)
    for s in range(2):
        c = slice(s * HALF, (s + 1) * HALF)
        g_o[s] = sum(dot(attn[m], df2[m * rows : (m + 1) * rows, c], 0, 0) for m in range(2)).astype(BF16)
    g_small[0:2, :] = jnp.zeros((2, width), F32)
    for i, name in enumerate(names[2:]):
        g_small[2 + i : 3 + i, :] = sums[name]


def rows_call(n, live, attn, tok, cot, w_all, small, b_in):
    _, rows, width = tok.shape
    items, highs = w_all.shape[:2]
    wr = w_all.shape[5]
    ff = (items - 1) // 2
    own = 2 * rows
    dma = pltpu.SemaphoreType.DMA
    s = jax.ShapeDtypeStruct
    return pl.pallas_call(
        functools.partial(rows_kernel, n),
        name="rows",
        out_shape=(
            s((2, rows, width), BF16),
            s((2, rows, width), F32),
            s((2, rows, width), BF16),
            s((ff, width, HALF), BF16),
            s((ff, 2, HALF, HALF), BF16),
            s((2, width, HALF), BF16),
            s((8, width), F32),
            s((ff, HALF), F32),
        ),
        in_specs=[SMEM] + [VMEM] * 6,
        out_specs=(VMEM,) * 8,
        scratch_shapes=[
            pltpu.VMEM((highs, 2, 2, 2, 2, wr, HALF), BF16),
            pltpu.VMEM((own, width), F32),
            pltpu.VMEM((own, width), F32),
            pltpu.VMEM((own, 128), F32),
            pltpu.VMEM((2 * own, width), BF16),
            pltpu.VMEM((ff, 2 * own, HALF), F32),
            pltpu.VMEM((ff, 2 * own, HALF), BF16),
            pltpu.VMEM((2 * own, width), F32),
            pltpu.VMEM((own, width), F32),
            pltpu.VMEM((2 * own, width), BF16),
            pltpu.VMEM((own, width), F32),
        ]
        + [dma] * 11,
        compiler_params=pltpu.CompilerParams(collective_id=3, has_side_effects=True, vmem_limit_bytes=60 << 20),
    )(live, attn, tok, cot, w_all, small, b_in)


def attend_back_kernel(live, q, k, v, o, lse, do, x, w, dx, dw, db, g, dk, dv):
    rows = q.shape[0]
    tile = 256
    length = live[0]
    scale = HEAD_DIM ** (-0.5)
    dk[...] = jnp.zeros_like(dk)
    dv[...] = jnp.zeros_like(dv)

    def step(i, _):
        at = pl.ds(pl.multiple_of(i * tile, tile), tile)
        outs = []
        for h in range(2):
            c = slice(h * HEAD_DIM, (h + 1) * HEAD_DIM)
            s = dot(q[at, c], k[:, c], 1, 1)
            place = lax.broadcasted_iota(jnp.int32, s.shape, 1)
            p = jnp.where(place < length, jnp.exp(s - lse[at, h * HEAD_DIM : h * HEAD_DIM + 1]), 0.0)
            d = do[at, c]
            dp = dot(d, v[:, c], 1, 1)
            inner = jnp.sum(d.astype(F32) * o[at, c], axis=1, keepdims=True)
            ds = (p * (dp - inner)).astype(BF16)
            outs.append(dot(ds, k[:, c]))
            dk[h] += dot(ds, q[at, c], 0, 0)
            dv[h] += dot(p.astype(BF16), d, 0, 0)
        g[at, 0:PAIR] = (jnp.concatenate(outs, axis=1).astype(BF16).astype(F32) * scale).astype(BF16)
        return 0

    lax.fori_loop(0, rows // tile, step, 0)
    g[:, PAIR : 2 * PAIR] = jnp.concatenate([dk[0], dk[1]], axis=1).astype(BF16)
    g[:, 2 * PAIR :] = jnp.concatenate([dv[0], dv[1]], axis=1).astype(BF16)

    def spread(i, _):
        at = pl.ds(pl.multiple_of(i * tile, tile), tile)
        dx[at, :] = dot(g[at, :], w[...], 1, 1).astype(BF16)
        return 0

    lax.fori_loop(0, rows // tile, spread, 0)
    dw[...] = dot(x[...], g[...], 0, 0)
    db[...] = jnp.broadcast_to(total_rows(g[...].astype(F32)), db.shape)


def attend_back(live, q, k, v, o, lse, do, x, w):
    rows, width = x.shape
    s = jax.ShapeDtypeStruct
    return pl.pallas_call(
        attend_back_kernel,
        name="attend_back",
        out_shape=(s((rows, width), BF16), s((width, 3 * PAIR), F32), s((8, 3 * PAIR), F32)),
        in_specs=[SMEM] + [VMEM] * 8,
        out_specs=(VMEM,) * 3,
        scratch_shapes=[
            pltpu.VMEM((rows, 3 * PAIR), BF16),
            pltpu.VMEM((2, rows, HEAD_DIM), F32),
            pltpu.VMEM((2, rows, HEAD_DIM), F32),
        ],
        compiler_params=pltpu.CompilerParams(vmem_limit_bytes=60 << 20),
    )(live, q, k, v, o, lse, do, x, w)


def add_into(target, *terms):
    total = target[...].astype(F32)
    for term in terms:
        total = total + term[...].astype(F32)
    target[...] = total.astype(target.dtype)


def scatter_w_kernel(n, g_in, one, out, out_in, g, r1a, r1b, r2, r3,
                     o_s, o_r, a_s, a_r, b_s, b_r, h_s, h_r, i_s, i_r, k_s):
    w = where_am_i(n)
    me, core, high, l1, l0 = w["me"], w["core"], w["high"], w["l1"], w["l0"]
    highs = w["highs"]
    partner = me ^ 1
    greet([partner, me ^ 2, me ^ 4] + [me ^ (8 * m) for m in range(1, highs)])
    items = g.shape[0]
    ff = (items - 1) // 2
    swap = send(one.at[1 - core], g.at[0], o_s, o_r, partner)
    fill = pltpu.make_async_copy(g_in, g.at[pl.ds(1, 2 * ff)], k_s)
    fill.start()
    fill.wait()
    swap.wait()

    def fold(i, _):
        g[0, i] = (g[0, i].astype(F32) + one[core, i].astype(F32)).astype(BF16)
        return 0

    lax.fori_loop(0, highs, fold, 0)
    first = [
        send(g.at[:, :, 1 - l1, :, 0], r1a, a_s.at[0], a_r.at[0], me ^ 4),
        send(g.at[:, :, :, 1 - l0, 1], r1b, a_s.at[1], a_r.at[1], me ^ 2),
    ]
    for copy in first:
        copy.wait()

    def add1(i, _):
        for h in range(highs):
            for b in range(2):
                g[i, h, l1, b, 0] = (g[i, h, l1, b, 0].astype(F32) + r1a[i, h, b].astype(F32)).astype(BF16)
                g[i, h, b, l0, 1] = (g[i, h, b, l0, 1].astype(F32) + r1b[i, h, b].astype(F32)).astype(BF16)
        return 0

    lax.fori_loop(0, items, add1, 0)
    second = [
        send(g.at[:, :, l1, 1 - l0, 0], r2.at[0], b_s.at[0], b_r.at[0], me ^ 2),
        send(g.at[:, :, 1 - l1, l0, 1], r2.at[1], b_s.at[1], b_r.at[1], me ^ 4),
    ]
    for copy in second:
        copy.wait()

    def add2(i, _):
        for h in range(highs):
            for s in range(2):
                g[i, h, l1, l0, s] = (g[i, h, l1, l0, s].astype(F32) + r2[s, i, h].astype(F32)).astype(BF16)
        return 0

    lax.fori_loop(0, items, add2, 0)
    third = [
        send(g.at[:, high ^ m, l1, l0], r3.at[m - 1], h_s.at[m], h_r.at[m], me ^ (8 * m)) for m in range(1, highs)
    ]
    for copy in third:
        copy.wait()

    def add3(i, _):
        for s in range(2):
            total = g[i, high, l1, l0, s].astype(F32)
            for m in range(1, highs):
                total = total + r3[m - 1, i, s].astype(F32)
            out[i, s] = total
        return 0

    lax.fori_loop(0, items, add3, 0)
    keep = pltpu.make_async_copy(out.at[pl.ds(1, ff), core], out_in.at[core], k_s)
    keep.start()
    swap = send(out.at[pl.ds(1, ff), 1 - core], out_in.at[core], i_s, i_r, partner)
    keep.wait()
    swap.wait()


def scatter_w(n, g, one):
    items, highs = g.shape[0] + 1, g.shape[1]
    wr = g.shape[5]
    ff = (items - 1) // 2
    dma = pltpu.SemaphoreType.DMA
    s = jax.ShapeDtypeStruct
    unit = (wr, HALF)
    return pl.pallas_call(
        functools.partial(scatter_w_kernel, n),
        name="scatter_w",
        out_shape=(s((items, 2) + unit, F32), s((2, ff) + unit, F32)),
        in_specs=[ANY, VMEM],
        out_specs=(VMEM, VMEM),
        scratch_shapes=[
            pltpu.VMEM((items, highs, 2, 2, 2) + unit, BF16),
            pltpu.VMEM((items, highs, 2) + unit, BF16),
            pltpu.VMEM((items, highs, 2) + unit, BF16),
            pltpu.VMEM((2, items, highs) + unit, BF16),
            pltpu.VMEM((highs - 1, items, 2) + unit, BF16),
            dma, dma, dma((2,)), dma((2,)), dma((2,)), dma((2,)), dma((highs,)), dma((highs,)), dma, dma, dma,
        ],
        compiler_params=pltpu.CompilerParams(collective_id=4, has_side_effects=True, vmem_limit_bytes=60 << 20),
    )(g, one)


def scatter_x_kernel(n, dx_in, dh, pieces_in, gtok, red, dx, g, psum, pgot, *rest):
    ra, rb, rc = rest[0:3], rest[3:6], rest[6:9]
    mine, theirs, c_s, c_r, t_s, t_r, w_s, w_r, p_s, p_r, k_s = rest[9:]
    w = where_am_i(n)
    me, core, chip = w["me"], w["core"], w["chip"]
    partner = me ^ 1
    chips = w["chips"]
    greet([partner] + [me ^ (2 * m) for m in range(1, chips)])
    rows = dh.shape[1]
    swap_p = send(pieces_in.at[:, 1 - core], pgot, w_s, w_r, partner)
    fills = [
        pltpu.make_async_copy(dx_in, dx, k_s.at[0]),
        pltpu.make_async_copy(pieces_in.at[:, core], psum, k_s.at[1]),
    ]
    for copy in fills:
        copy.start()
    for copy in fills:
        copy.wait()
    bits = (w["cube"] // 4, w["cube"] // 2 % 2, w["cube"] % 2)
    masks = (8, 4, 2)
    spans = cube_rows(2 * rows)

    def region(s, order, phase, far):
        index = [slice(None)] * 3
        for done in order[:phase]:
            index[done] = bits[done]
        axis = order[phase]
        index[axis] = 1 - bits[axis] if far else bits[axis]
        return tuple(index) + (pl.ds(*spans[s]),)

    def launch(phase):
        bufs = (ra, rb, rc)[phase]
        return [
            send(dx.at[region(s, order, phase, True)], bufs[s], c_s.at[phase, s], c_r.at[phase, s], me ^ masks[order[phase]])
            for s, order in enumerate(CUBE_ORDERS)
        ]

    def fold(phase):
        bufs = (ra, rb, rc)[phase]
        for s, order in enumerate(CUBE_ORDERS):
            at = region(s, order, phase, False)
            dx[at] = (dx[at].astype(F32) + bufs[s][...].astype(F32)).astype(BF16)

    live = launch(0)
    swap_p.wait()
    psum[...] = (psum[...].astype(F32) + pgot[...].astype(F32)).astype(BF16)
    copies = [send(psum.at[chip ^ m], g.at[m], p_s.at[m], p_r.at[m], me ^ (2 * m)) for m in range(1, chips)]
    own = pltpu.make_async_copy(psum.at[chip], g.at[0], k_s.at[2])
    own.start()
    for phase in range(3):
        for copy in live:
            copy.wait()
        fold(phase)
        if phase < 2:
            live = launch(phase + 1)
    here = (bits[0], bits[1], bits[2])
    theirs_at = pl.ds(pl.multiple_of((1 - core) * rows, rows), rows)
    own_at = pl.ds(pl.multiple_of(core * rows, rows), rows)
    swap = send(dx.at[here + (theirs_at,)], theirs, t_s, t_r, partner)
    gtok[core] = (dh[core] + dx[here + (own_at,)].astype(F32)).astype(BF16)
    own.wait()
    for copy in copies:
        copy.wait()
    for m in range(chips):
        term = g[m].astype(F32)
        if m < CUBE:
            red[m] = term
        else:
            red[m % CUBE] += term
    swap.wait()
    gtok[1 - core] = (dh[1 - core] + theirs[...].astype(F32)).astype(BF16)


def scatter_x(n, dx, dh, pieces):
    _, rows, width = dh.shape
    chips = n // 2
    unit = pieces.shape[2:]
    dma = pltpu.SemaphoreType.DMA
    s = jax.ShapeDtypeStruct
    spans = cube_rows(2 * rows)
    bufs = [pltpu.VMEM(lead + (spans[i][1], width), BF16) for lead in ((2, 2), (2,), ()) for i in range(3)]
    return pl.pallas_call(
        functools.partial(scatter_x_kernel, n),
        name="scatter_x",
        out_shape=(s((2, rows, width), BF16), s((CUBE,) + unit, F32)),
        in_specs=[ANY, VMEM, ANY],
        out_specs=(VMEM, VMEM),
        scratch_shapes=[
            pltpu.VMEM(dx.shape, BF16),
            pltpu.VMEM((chips,) + unit, BF16),
            pltpu.VMEM((chips,) + unit, BF16),
            pltpu.VMEM((chips,) + unit, BF16),
        ]
        + bufs
        + [
            pltpu.VMEM((rows, width), BF16),
            pltpu.VMEM((rows, width), BF16),
            dma((3, 3)), dma((3, 3)), dma, dma, dma, dma, dma((chips,)), dma((chips,)), dma((3,)),
        ],
        compiler_params=pltpu.CompilerParams(collective_id=5, has_side_effects=True, vmem_limit_bytes=60 << 20),
    )(dx, dh, pieces)


def start(copies):
    for copy in copies:
        copy.start()


def wait(copies):
    for copy in copies:
        copy.wait()


def remote(src, dst, sems, index, device):
    send_sem, recv_sem = sems
    return pltpu.make_async_remote_copy(
        src_ref=src,
        dst_ref=dst,
        send_sem=send_sem.at[index],
        recv_sem=recv_sem.at[index],
        device_id=(device,),
        device_id_type=MESH,
    )


def add_rows(dst, at, src, src_at):
    dst[at] = (dst[at].astype(F32) + src[src_at].astype(F32)).astype(dst.dtype)


COLS = 256


def layer_kernel(n, shapes, seq_len, slot, tok_h, cot_h, wq_h, wk_h, wv_h, wo, w_in_h, w_out, line,
                 out_h, gtok_h, gq_h, gk_h, gv_h, gwo_h, gwin_h, gwout_h, gline_h, *scratch):
    s = dict(zip(shapes, scratch, strict=True))
    here = where_am_i(n)
    me, core, chip, cube, rank = (here[name] for name in ("me", "core", "chip", "cube", "rank"))
    high, l1, l0, chips, highs = (here[name] for name in ("high", "l1", "l0", "chips", "highs"))
    partner = me ^ 1
    tok, cot, out, gtok = (s[name] for name in ("tok", "cot", "out", "gtok"))
    gqkv, gwo, gwin, gwout, gline = (s[name] for name in ("gqkv", "gwo", "gwin", "gwout", "gline"))
    wqkv, w_in = s["wqkv"], s["w_in"]
    _, rows, width = tok.shape
    own = 2 * rows
    wr, fr = wo.shape[0], w_out.shape[0]
    half = fr * chips
    chunk = half // highs
    bits = (cube // 4, cube // 2 % 2, cube % 2)

    def sems(name):
        return s[name + "_s"], s[name + "_r"]

    own_rows = pl.ds(pl.multiple_of(core * rows, rows), rows)
    x_all, p_all, w_o, w_i, w_u = s["x_all"], s["p_all"], s["w_o"], s["w_i"], s["w_u"]

    def load(src, dst, i):
        copy = pltpu.make_async_copy(src, dst, s["load"].at[i])
        copy.start()
        return copy

    loads = [load(ref, wqkv.at[i], i) for i, ref in enumerate((wq_h, wk_h, wv_h))]
    loads.append(load(w_in_h, w_in, 3))
    load_o = load(wo, w_o.at[high, l1, l0, core], 4)
    load_u = load(w_out, w_u.at[high, l1, l0], 5)
    load_x = load(tok_h.at[core], x_all.at[bits[0], bits[1], bits[2], own_rows], 6)
    load_t = load(tok_h, tok, 7)
    load_c = load(cot_h, cot, 8)

    met = sorted({m for m in range(1, BLOCK_DEVS)} | {2 * m for m in range(1, chips)})
    barrier = pltpu.get_barrier_semaphore()
    for m in met:
        pl.semaphore_signal(barrier, inc=1, device_id=(me ^ m,), device_id_type=MESH)

    lengths = []
    for m in range(2):
        length = jnp.int32(0)
        for i in range(slot.shape[1]):
            length = length + jnp.where(slot[m, i] == me // BLOCK_DEVS, seq_len[m, i], 0)
        lengths.append(length)

    pieces, w_loc, line_at, lines_all = s["pieces"], s["w_loc"], s["line"], s["lines"]
    wait(loads)
    for k in range(CUBE):
        for i in range(3):
            pieces[k, :, i * PAIR : (i + 1) * PAIR] = wqkv[i, :, k * PAIR : (k + 1) * PAIR]
    value = line[...]
    line_at[...] = jnp.concatenate(
        [value[:, i * PAIR : (i + 1) * PAIR] for i in range(3)] + [jnp.zeros((13, PAIR), F32)], axis=0
    ).astype(BF16)
    for i in range(chips):
        for q in range(2):
            at = (2 * i + q) * fr
            w_loc[q, :, i * fr : (i + 1) * fr] = w_in[:, at : at + fr]
    pl.semaphore_wait(barrier, len(met))

    swap_tok = remote(tok_h.at[1 - core], x_all.at[bits[0], bits[1], bits[2], own_rows], sems("swap"), 0, partner)
    swap_tok.start()
    swap_in = remote(w_loc.at[1 - core], w_i.at[high, l1, l0, core], sems("swap"), 1, partner)
    swap_in.start()
    piece_copies = [
        remote(pieces.at[(chip ^ m) % CUBE], p_all.at[chip, core], sems("piece"), m, me ^ (2 * m))
        for m in range(1, chips)
    ]
    line_copies = [
        remote(line_at, lines_all.at[chip, core], sems("line"), m, me ^ (2 * m)) for m in range(1, chips)
    ]

    masks = (8, 4, 2)
    set_at = (core * rows, (1 - core) * rows)

    def rows_of(t, i):
        first, count = SPANS[t][i]
        return pl.ds(pl.multiple_of(set_at[t] + first, 16), count)

    def cube_phase(t, phase):
        out_ = []
        for i, order in enumerate(CUBE_ORDERS):
            index = list(bits)
            for done in order[:phase]:
                index[done] = slice(None)
            region = x_all.at[index[0], index[1], index[2], rows_of(t, i)]
            sem = (s["cube_s"].at[t, phase], s["cube_r"].at[t, phase])
            out_.append(remote(region, region, sem, i, me ^ masks[order[phase]]))
        return out_

    outs = width // COLS
    groups = 1 + highs + outs
    every = slice(None)

    def part_of(g, index):
        h_, a_, b_, t = index
        if g == 0:
            c = slice(None) if t is None else pl.ds(t * HALF, HALF)
            return w_o.at[h_, a_, b_, core, :, c]
        if g <= highs:
            c = pl.ds((g - 1) * chunk, chunk)
            return w_i.at[h_, a_, b_, slice(None) if t is None else t, :, c]
        c = pl.ds((g - 1 - highs) * COLS, COLS)
        r = slice(None) if t is None else pl.ds(t * fr // 2, fr // 2)
        return w_u.at[h_, a_, b_, r, c]

    def high_copies(g):
        region = part_of(g, (high, every, every, None) if g in LAST_HIGH else (high, l1, l0, None))
        return [
            remote(region, region, (s["hi_s"].at[g], s["hi_r"].at[g]), m, me ^ (8 * m)) for m in range(1, highs)
        ]

    def low_copies(g, phase):
        ab = (s["ab_s"].at[g, phase], s["ab_r"].at[g, phase])
        up = high if g in LAST_HIGH else every
        if phase == 0:
            first, second = (up, l1, l0, 0), (up, l1, l0, 1)
            to = (me ^ 2, me ^ 4)
        else:
            first, second = (up, l1, every, 0), (up, every, l0, 1)
            to = (me ^ 4, me ^ 2)
        a, b = part_of(g, first), part_of(g, second)
        return [remote(a, a, ab, 0, to[0]), remote(b, b, ab, 1, to[1])]

    def gather_event(kind, g):
        late = g in LAST_HIGH
        if kind == "h":
            if late:
                wait(low_copies(g, 1))
            start(high_copies(g))
        elif kind == "a":
            if not late:
                wait(high_copies(g))
            start(low_copies(g, 0))
        else:
            wait(low_copies(g, 0))
            start(low_copies(g, 1))

    def gather_events(name):
        for kind, g in GATHER.get(name, ()):
            gather_event(kind, g)

    def gather_end(g):
        wait(high_copies(g) if g in LAST_HIGH else low_copies(g, 1))

    load_x.wait()
    start(cube_phase(0, 0))
    p_all[chip, core] = pieces[cube]
    lines_all[chip, core] = line_at[...]
    w_i[high, l1, l0, core] = w_loc[core]
    load_o.wait()
    load_u.wait()
    swap_tok.wait()
    start(cube_phase(1, 0))
    start(piece_copies)
    start(line_copies)
    swap_in.wait()
    gather_events("t0")
    wait(cube_phase(0, 0))
    start(cube_phase(0, 1))
    wait(cube_phase(1, 0))
    start(cube_phase(1, 1))
    gather_events("t1")
    wait(piece_copies)
    wait(line_copies)
    swap_p = remote(p_all.at[:, core], p_all.at[:, core], sems("swap"), 2, partner)
    swap_p.start()
    swap_l = remote(lines_all.at[:, core], lines_all.at[:, core], sems("swap"), 10, partner)
    swap_l.start()
    wait(cube_phase(0, 1))
    start(cube_phase(0, 2))
    wait(cube_phase(1, 1))
    start(cube_phase(1, 2))
    gather_events("t2")
    swap_p.wait()
    swap_l.wait()

    param, b_in = s["param"], s["b_in"]
    tail = lines_all[...].reshape(n * 16, PAIR)
    at_row = lax.broadcasted_iota(jnp.int32, (n, n * 16), 1) - 16 * lax.broadcasted_iota(jnp.int32, (n, n * 16), 0)
    lines = [dot((at_row == i).astype(BF16), tail).astype(BF16) for i in range(3)]
    lane = lax.broadcasted_iota(jnp.int32, (PAIR, width), 1)
    column = lax.broadcasted_iota(jnp.int32, (PAIR, width), 0)
    owner = lax.broadcasted_iota(jnp.int32, (n, width), 1) // wr == lax.broadcasted_iota(jnp.int32, (n, width), 0)

    def selector(i):
        return (column == i % 4 * wr + lane % wr).astype(BF16)

    for i in range(8):
        spread = dot(lines[i // 4], selector(i))
        param[i : i + 1, :] = jnp.sum(jnp.where(owner, spread, 0.0), axis=0, keepdims=True)
    half_pick = (
        (2 * lax.broadcasted_iota(jnp.int32, (chips, n), 0) + core) == lax.broadcasted_iota(jnp.int32, (chips, n), 1)
    )
    mine = dot(half_pick.astype(BF16), lines[2])
    for i in range(chips):
        b_in[0:1, i * fr : (i + 1) * fr] = mine[i : i + 1, :]
    wait(cube_phase(0, 2))
    wait(cube_phase(1, 2))

    q, k, v, o, low, lse = (s[name] for name in ("q", "k", "v", "o", "low", "lse"))
    tile = own
    pair_at = pl.ds(pl.multiple_of(cube * PAIR, PAIR), PAIR)
    bq, bv = param[0:1, pair_at], param[1:2, pair_at]
    length = jnp.where(core == 0, lengths[0], lengths[1])

    def w_qkv():
        return p_all[...].reshape(width, 3 * PAIR)

    def project(i, _):
        at = pl.ds(pl.multiple_of(i * tile, tile), tile)
        y = dot(x_all[i // 4, i // 2 % 2, i % 2], w_qkv())
        q[at, :] = ((y[:, :PAIR] + bq) * HEAD_DIM ** (-0.5)).astype(BF16)
        k[at, :] = y[:, PAIR : 2 * PAIR].astype(BF16)
        v[at, :] = (y[:, 2 * PAIR :] + bv).astype(BF16)
        return 0

    lax.fori_loop(0, CUBE, project, 0)
    gather_events("p")

    attn = s["attn"]
    low_dst = attn.at[core, :, pair_at]

    def row_copy(m):
        at = pl.ds(pl.multiple_of((rank ^ m) * rows, rows), rows)
        return remote(low.at[at], low_dst, sems("torow"), m, me ^ m)

    def attend_step(step, _):
        i = cube ^ step
        at = pl.ds(pl.multiple_of(i * tile, tile), tile)
        outs_, logs = [], []
        for h in range(2):
            c = slice(h * HEAD_DIM, (h + 1) * HEAD_DIM)
            sc = dot(q[at, c], k[:, c], 1, 1)
            place = lax.broadcasted_iota(jnp.int32, sc.shape, 1)
            sc = jnp.where(place < length, sc, -1e30)
            top = jnp.max(sc, axis=1, keepdims=True)
            e = jnp.exp(sc - top)
            total = jnp.sum(e, axis=1, keepdims=True)
            outs_.append(dot(e.astype(BF16), v[:, c]) / total)
            logs.append(jnp.broadcast_to(top + jnp.log(total), (tile, HEAD_DIM)))
        mixed = jnp.concatenate(outs_, axis=1)
        o[at, :] = mixed
        low[at, :] = mixed.astype(BF16)
        lse[at, :] = jnp.concatenate(logs, axis=1)

        @pl.when(step > 0)
        def _():
            row_copy(2 * step).start()

        row_copy(2 * step + 1).start()
        for at_step in range(CUBE):
            if at_step in GATHER:

                @pl.when(step == at_step)
                def _():
                    gather_events(at_step)

        return 0

    lax.fori_loop(0, CUBE, attend_step, 0)
    attn[core, :, pair_at] = low[pl.ds(pl.multiple_of(rank * rows, rows), rows), :]
    gather_end(0)
    swap_o = remote(w_o.at[:, :, :, core], w_o.at[:, :, :, core], sems("swap"), 3, partner)
    swap_o.start()
    gather_events("r")
    wait([row_copy(m) for m in range(1, BLOCK_DEVS)])
    swap_o.wait()

    x1, n1, r1, x1_low, slope, act = (s[name] for name in ("x1", "n1", "r1", "x1_low", "slope", "act"))
    part, got, df2 = (s[name] for name in ("part", "got", "df2"))
    sums = s["sums"]

    def whole_o():
        return w_o[...].reshape(width, width)

    for m in range(2):
        at = slice(m * rows, (m + 1) * rows)
        part[at, :] = dot(attn[m], whole_o())
    load_t.wait()
    for m in range(2):
        at = slice(m * rows, (m + 1) * rows)
        nn, rs = norm_forward(tok[m].astype(F32) + part[at, :] + param[2:3, :])
        n1[at, :] = nn
        r1[at, :] = jnp.broadcast_to(rs, (rows, 128))
        y = nn * param[4:5, :] + param[5:6, :]
        x1[at, :] = y
        x1_low[at, :] = y.astype(BF16)
    swap_x = remote(x1_low.at[pl.ds(0, own)], x1_low.at[pl.ds(own, own)], sems("swap"), 4, partner)
    swap_x.start()
    gather_events("x")
    swap_x.wait()

    for j in range(highs):
        gather_end(1 + j)
        cols = slice(j * chunk, (j + 1) * chunk)
        slope[j] = dot(x1_low[...], w_i[:, :, :, :, :, cols].reshape(width, chunk)) + b_in[0:1, cols]

        def gelu_step(i, _):
            at = pl.ds(pl.multiple_of(i * 64, 64), 64)
            u = slope[j, at, :]
            phi = 0.5 + 0.5 * lax.erf(u * 0.7071067811865476)
            slope[j, at, :] = phi + u * (0.3989422804014327 * jnp.exp(-0.5 * u * u))
            act[at, cols] = (u * phi).astype(BF16)
            return 0

        lax.fori_loop(0, 2 * own // 64, gelu_step, 0)
        gather_events(f"i{j}")

    def half_copy(j):
        at = pl.ds(j * COLS, COLS)
        return remote(part.at[pl.ds(own, own), at], got.at[:, at], sems("halves"), j, partner)

    for j in range(outs):
        gather_end(1 + highs + j)
        cols = slice(j * COLS, (j + 1) * COLS)
        part[:, cols] = dot(act[...], w_u[:, :, :, :, cols].reshape(half, COLS))
        half_copy(j).start()
    wait([half_copy(j) for j in range(outs)])

    for i in range(8):
        sums[i : i + 1, :] = jnp.zeros((1, width), F32)
    load_c.wait()
    for m in range(2):
        at = slice(m * rows, (m + 1) * rows)
        nn, rs = norm_forward(x1[at, :] + part[at, :] + got[at, :] + param[3:4, :])
        out[m] = (nn * param[6:7, :] + param[7:8, :]).astype(BF16)
        place = rank * rows + lax.broadcasted_iota(jnp.int32, (rows, 1), 0)
        dy = jnp.where(place < lengths[m], cot[m].astype(F32), 0.0)
        sums[6:7, :] += total_rows(dy * nn)
        sums[7:8, :] += total_rows(dy)
        d = norm_back(dy, nn, rs, param[6:7, :])
        x1[at, :] = d
        d_low = d.astype(BF16)
        df2[at, :] = d_low
        sums[3:4, :] += total_rows(d_low.astype(F32))
    swap_d = remote(df2.at[pl.ds(0, own)], df2.at[pl.ds(own, own)], sems("swap"), 5, partner)
    swap_d.start()
    stores = [load(out, out_h, 9)]

    fin = s["fin"]

    def grad_part(r, index):
        g = r + 1 if r < highs + outs else 0
        return part_of(g, index)

    def buf(name, r, t):
        if r < FIRST_HIGH:
            return s[name + "f"].at[r, t]
        if r < highs:
            return s[name + "i"].at[r - FIRST_HIGH, t]
        if r < highs + outs:
            return s[name + "u"].at[r - highs, t]
        return s[name + "o"].at[t]

    def reduce_copies(r, phase):
        name = ("ra", "rb", "rc")[phase]
        sem = (s[name + "_s"].at[r], s[name + "_r"].at[r])
        early = r < FIRST_HIGH
        if phase == (0 if early else 2):
            index = (every, every) if early else (l1, l0)
            return [
                remote(grad_part(r, (high ^ m,) + index + (None,)), buf(name, r, m - 1), sem, m, me ^ (8 * m))
                for m in range(1, highs)
            ]
        up = high if early else every
        if phase == (1 if early else 0):
            regions = (up, 1 - l1, every, 0), (up, every, 1 - l0, 1)
            to = (me ^ 4, me ^ 2)
        else:
            regions = (up, l1, 1 - l0, 0), (up, 1 - l1, l0, 1)
            to = (me ^ 2, me ^ 4)
        return [remote(grad_part(r, regions[t]), buf(name, r, t), sem, t, to[t]) for t in range(2)]

    def add_all(target, terms):
        total = target[...].astype(F32)
        for term in terms:
            total = total + term[...].astype(F32)
        target[...] = total.astype(BF16)

    def reduce_add(r, phase):
        name = ("ra", "rb", "rc")[phase]
        early = r < FIRST_HIGH
        if early and phase == 0:
            for a_ in range(2):
                for b_ in range(2):
                    add_all(
                        grad_part(r, (high, a_, b_, None)), [buf(name, r, m - 1).at[a_, b_] for m in range(1, highs)]
                    )
        elif early:
            for b_ in range(2):
                add_all(grad_part(r, (high, l1, b_, 0)), [buf(name, r, 0).at[b_]])
                add_all(grad_part(r, (high, b_, l0, 1)), [buf(name, r, 1).at[b_]])
        elif phase == 0:
            for h in range(highs):
                for b_ in range(2):
                    add_all(grad_part(r, (h, l1, b_, 0)), [buf(name, r, 0).at[h, b_]])
                    add_all(grad_part(r, (h, b_, l0, 1)), [buf(name, r, 1).at[h, b_]])
        else:
            for h in range(highs):
                for t in range(2):
                    add_all(grad_part(r, (h, l1, l0, t)), [buf(name, r, t).at[h]])

    def reduce_last(r):
        if r < FIRST_HIGH:
            for t in range(2):
                fin[t, :, r * chunk : (r + 1) * chunk] = grad_part(r, (high, l1, l0, t))[...].astype(F32) + buf(
                    "rc", r, t
                )[...].astype(F32)
            fin_copy(r).start()
            return
        total = grad_part(r, (high, l1, l0, None))[...].astype(F32)
        for m in range(1, highs):
            total = total + buf("rc", r, m - 1)[...].astype(F32)
        if r < highs:
            fin[:, :, r * chunk : (r + 1) * chunk] = total
            fin_copy(r).start()
        elif r < highs + outs:
            gwout[:, (r - highs) * COLS : (r - highs + 1) * COLS] = total
        else:
            gwo[...] = total

    def fin_copy(r):
        at = pl.ds(r * chunk, chunk)
        return remote(fin.at[1 - core, :, at], s["fin_got"].at[:, at], sems("fin"), r, partner)

    def reduce_events(name):
        for phase, r in REDUCE.get(name, ()):
            if phase > 0:
                wait(reduce_copies(r, phase - 1))
            if phase in (1, 2):
                reduce_add(r, phase - 1)
            if phase == 3:
                reduce_last(r)
            else:
                start(reduce_copies(r, phase))

    swap_d.wait()
    du_ref, gbin = s["du"], s["gbin"]
    for j in range(highs):
        cols = slice(j * chunk, (j + 1) * chunk)
        da = dot(df2[...], w_u[j].reshape(chunk, width), 1, 1)
        du = (da * slope[j]).astype(BF16)
        du_ref[...] = du
        gbin[0:1, cols] = total_rows(du.astype(F32))
        back = dot(du, w_i[:, :, :, :, :, cols].reshape(width, chunk), 1, 1)
        if j == 0:
            part[...] = back
        else:
            part[...] += back
        if j == highs - 1:
            swap_e = remote(part.at[pl.ds(own, own)], got, sems("swap"), 6, partner)
            swap_e.start()
        w_i[:, :, :, :, :, cols] = dot(x1_low[...], du_ref[...], 0, 0).astype(BF16).reshape(highs, 2, 2, 2, wr, chunk)
        w_u[j] = dot(act[:, cols], df2[...], 0, 0).astype(BF16).reshape(2, 2, fr, width)
        reduce_events(f"i{j}")
    swap_e.wait()

    dattn = s["dattn"]
    for m in range(2):
        at = slice(m * rows, (m + 1) * rows)
        e = x1[at, :] + part[at, :] + got[at, :]
        nn, rs = n1[at, :], r1[at, 0:1]
        sums[4:5, :] += total_rows(e * nn)
        sums[5:6, :] += total_rows(e)
        d = norm_back(e, nn, rs, param[4:5, :])
        x1[at, :] = d
        d_low = d.astype(BF16)
        df2[at, :] = d_low
        sums[2:3, :] += total_rows(d_low.astype(F32))
    for m in range(2):
        dattn[m] = dot(df2[m * rows : (m + 1) * rows, :], whole_o(), 1, 1).astype(BF16)
    do = s["do"]

    def head_piece(m):
        at = pl.ds(pl.multiple_of((cube ^ (m // 2)) * PAIR, PAIR), PAIR)
        return dattn.at[core ^ (m % 2), :, at]

    def head_copy(m):
        return remote(head_piece(m), do.at[rank], sems("tohead"), m, me ^ m)

    start([head_copy(m) for m in range(1, BLOCK_DEVS)])
    do[rank] = dattn[core, :, pair_at]
    g_o = dot(attn[0], df2[0:rows, :], 0, 0) + dot(attn[1], df2[rows:own, :], 0, 0)
    w_o[...] = g_o.astype(BF16).reshape(highs, 2, 2, 2, wr, width)
    swap_g = remote(w_o.at[:, :, :, 1 - core], s["o_got"], sems("swap"), 7, partner)
    swap_g.start()
    reduce_events("x")
    swap_g.wait()
    for h in range(highs):
        w_o[h, :, :, core] = (w_o[h, :, :, core].astype(F32) + s["o_got"][h].astype(F32)).astype(BF16)
    wait([head_copy(m) for m in range(1, BLOCK_DEVS)])

    acc, g = slope, s["g"]
    acc[...] = jnp.zeros_like(acc)
    scale = HEAD_DIM ** (-0.5)
    block = acc.shape[1]

    def back_step(i, _):
        at = pl.ds(pl.multiple_of(i * tile, tile), tile)
        outs_ = []
        d2 = do[pl.ds(2 * i, 2)].reshape(tile, PAIR)
        for h in range(2):
            c = slice(h * HEAD_DIM, (h + 1) * HEAD_DIM)
            d = d2[:, c]
            inner = jnp.sum(d.astype(F32) * o[at, c], axis=1, keepdims=True)
            norm = lse[at, h * HEAD_DIM : h * HEAD_DIM + 1]
            dq = None
            for b in range(acc.shape[0]):
                keys = slice(b * block, (b + 1) * block)
                sc = dot(q[at, c], k[keys, c], 1, 1)
                place = b * block + lax.broadcasted_iota(jnp.int32, sc.shape, 1)
                p = jnp.where(place < length, jnp.exp(sc - norm), 0.0)
                dp = dot(d, v[keys, c], 1, 1)
                ds = (p * (dp - inner)).astype(BF16)
                term = dot(ds, k[keys, c])
                dq = term if dq is None else dq + term
                acc[b, :, h * HEAD_DIM : (h + 1) * HEAD_DIM] += dot(ds, q[at, c], 0, 0)
                acc[b, :, PAIR + h * HEAD_DIM : PAIR + (h + 1) * HEAD_DIM] += dot(p.astype(BF16), d, 0, 0)
            outs_.append(dq)
        g[at, 0:PAIR] = (jnp.concatenate(outs_, axis=1).astype(BF16).astype(F32) * scale).astype(BF16)
        for at_step in range(CUBE):
            if at_step in REDUCE:

                @pl.when(i == at_step)
                def _():
                    reduce_events(at_step)

        return 0

    lax.fori_loop(0, CUBE, back_step, 0)
    for b in range(acc.shape[0]):
        lines_ = slice(b * block, (b + 1) * block)
        g[lines_, PAIR : 3 * PAIR] = acc[b, :, 0 : 2 * PAIR].astype(BF16)

    pg, pgot, pslot = s["pg"], s["pgot"], s["pslot"]
    step_width = width // highs

    def weight_step(i, _):
        cols = pl.ds(pl.multiple_of(i * step_width, step_width), step_width)
        block_ = dot(x_all[:, :, :, :, cols].reshape(CUBE * own, step_width), g[...], 0, 0).astype(BF16)
        pg[pl.ds(i * 4, 4)] = block_.reshape(4, 2, wr, 3 * PAIR)
        return 0

    lax.fori_loop(0, highs, weight_step, 0)
    swap_g = remote(pg.at[:, 1 - core], pgot, sems("swap"), 8, partner)
    swap_g.start()

    def spread_rows(i, _):
        at = pl.ds(pl.multiple_of(i * tile, tile), tile)
        x_all[i // 4, i // 2 % 2, i % 2] = dot(g[at, :], w_qkv(), 1, 1).astype(BF16)
        return 0

    lax.fori_loop(0, CUBE, spread_rows, 0)

    def region(t, i, phase, far):
        order = CUBE_ORDERS[i]
        index = [slice(None)] * 3
        for done in order[:phase]:
            index[done] = bits[done]
        axis = order[phase]
        index[axis] = 1 - bits[axis] if far else bits[axis]
        return tuple(index) + (rows_of(t, i),)

    def row_sums(t, phase):
        sem = (s["xr_s"].at[t, phase], s["xr_r"].at[t, phase])
        return [
            remote(x_all.at[region(t, i, phase, True)], s[f"x{t}{phase}{i}"], sem, i, me ^ masks[order[phase]])
            for i, order in enumerate(CUBE_ORDERS)
        ]

    def row_fold(t, phase):
        for i in range(3):
            at = region(t, i, phase, False)
            x_all[at] = (x_all[at].astype(F32) + s[f"x{t}{phase}{i}"][...].astype(F32)).astype(BF16)

    start(row_sums(1, 0))
    start(row_sums(0, 0))

    db = total_rows(g[...].astype(F32))
    sums[0:1, pair_at] = db[:, 0:PAIR]
    sums[1:2, pair_at] = db[:, 2 * PAIR :]
    sent = []
    for a_ in range(2):
        line_sum = jnp.zeros((n, PAIR), F32)
        for i in range(4 * a_, 4 * a_ + 4):
            placed = jnp.where(owner, sums[i : i + 1, :], 0.0).astype(BF16)
            line_sum = line_sum + dot(placed, selector(i), 1, 1)
        sent.append(line_sum.astype(BF16))
    hidden = jnp.concatenate([gbin[0:1, i * fr : (i + 1) * fr] for i in range(chips)], axis=0)
    back_pick = (
        (2 * lax.broadcasted_iota(jnp.int32, (n, chips), 1) + core) == lax.broadcasted_iota(jnp.int32, (n, chips), 0)
    )
    sent.append(dot(back_pick.astype(BF16), hidden.astype(BF16)).astype(BF16))
    at_line = lax.broadcasted_iota(jnp.int32, (n * 16, n), 0) - 16 * lax.broadcasted_iota(jnp.int32, (n * 16, n), 1)
    wide = jnp.zeros((n * 16, PAIR), F32)
    for a_ in range(3):
        wide = wide + dot((at_line == a_).astype(BF16), sent[a_])
    lines_all[...] = wide.astype(BF16).reshape(chips, 2, 16, PAIR)
    swap_l = remote(lines_all.at[:, 1 - core], s["line_got"], sems("swap"), 11, partner)
    swap_l.start()
    swap_g.wait()
    for i in range(chips):
        pg[i, core] = (pg[i, core].astype(F32) + pgot[i].astype(F32)).astype(BF16)
    piece_sums = [
        remote(pg.at[chip ^ m, core], pslot.at[m], sems("psum"), m, me ^ (2 * m)) for m in range(1, chips)
    ]
    start(piece_sums)
    swap_l.wait()
    for i in range(chips):
        lines_all[i, core] = (lines_all[i, core].astype(F32) + s["line_got"][i].astype(F32)).astype(BF16)
    line_sums = [
        remote(lines_all.at[chip ^ m, core], s["line_slot"].at[m], sems("lsum"), m, me ^ (2 * m))
        for m in range(1, chips)
    ]
    start(line_sums)

    theirs_at = pl.ds(pl.multiple_of((1 - core) * rows, rows), rows)
    last = remote(x_all.at[bits[0], bits[1], bits[2], theirs_at], gtok.at[core], sems("swap"), 9, partner)
    for phase in range(3):
        for t in (1, 0):
            wait(row_sums(t, phase))
            row_fold(t, phase)
            if phase < 2:
                start(row_sums(t, phase + 1))
            elif t == 1:
                last.start()
            reduce_events(f"d{phase}{t}")
    gtok[core] = (x1[own_rows, :] + x_all[bits[0], bits[1], bits[2], own_rows].astype(F32)).astype(BF16)
    reduce_events("e")
    wait(piece_sums)
    for m in range(chips):
        term = pg[chip, core].astype(F32) if m == 0 else pslot[m].astype(F32)
        at = pl.ds(pl.multiple_of((cube ^ (m % CUBE)) * PAIR, PAIR), PAIR)
        for i in range(3):
            value = term[:, i * PAIR : (i + 1) * PAIR]
            if m < CUBE:
                gqkv[i, :, at] = value
            else:
                gqkv[i, :, at] += value
    wait(line_sums)
    line_total = lines_all[chip, core].astype(F32)
    for m in range(1, chips):
        line_total = line_total + s["line_slot"][m].astype(F32)
    gline[...] = jnp.concatenate([line_total[i : i + 1, :] for i in range(3)], axis=1)
    wait([fin_copy(r) for r in range(highs)])
    for i in range(chips):
        at = slice(i * fr, (i + 1) * fr)
        gwin[:, pl.ds(pl.multiple_of((2 * i + core) * fr, fr), fr)] = fin[core, :, at]
        gwin[:, pl.ds(pl.multiple_of((2 * i + 1 - core) * fr, fr), fr)] = s["fin_got"][:, at]
    stores += [load(gqkv.at[i], ref, 10 + i) for i, ref in enumerate((gq_h, gk_h, gv_h))]
    stores += [load(gwo, gwo_h, 13), load(gwin, gwin_h, 14), load(gwout, gwout_h, 15), load(gline, gline_h, 16)]
    last.wait()
    gtok[1 - core] = (x1[theirs_at, :] + gtok[1 - core].astype(F32)).astype(BF16)
    stores.append(load(gtok, gtok_h, 17))
    wait(stores)


SPANS = (((0, 48), (48, 48), (96, 32)), ((0, 48), (48, 32), (80, 48)))
LAST_HIGH = (8,)
FIRST_HIGH = 1
GATHER = {
    "t0": (("h", 0), ("a", 8)),
    "t1": (("a", 0), ("h", 1), ("b", 8)),
    "t2": (("a", 1), ("h", 2), ("b", 0)),
    "p": (("a", 2), ("h", 3), ("b", 1)),
    2: (("a", 3), ("h", 4), ("b", 2)),
    5: (("a", 4), ("h", 5), ("b", 3)),
    "r": (("a", 5), ("h", 6), ("b", 4), ("h", 8)),
    "x": (("a", 6), ("h", 7), ("b", 5)),
    "i0": (("a", 7), ("b", 6)),
    "i3": (("b", 7),),
}
REDUCE = {
    "i0": ((0, 0),),
    "i1": ((0, 1),),
    "i2": ((0, 2),),
    "x": ((1, 1), (0, 3)),
    0: ((1, 2), (0, 4), (2, 1)),
    2: ((1, 3), (0, 5), (2, 2), (3, 1)),
    3: ((1, 0), (1, 4), (0, 6), (2, 3), (3, 2)),
    5: ((1, 5), (0, 7), (2, 4), (3, 3), (2, 0)),
    7: ((1, 6), (0, 8), (2, 5), (3, 4), (3, 0)),
    "d01": ((1, 7), (2, 6), (3, 5)),
    "d00": ((1, 8), (2, 7), (3, 6)),
    "d11": ((2, 8), (3, 7)),
    "d10": ((3, 8),),
}


def layer(n, seq_len, slot, tok, cot, wq, wk, wv, wo, w_in, w_out, line):
    _, rows, width = tok.shape
    wr, fr = wo.shape[0], w_out.shape[0]
    chips, highs = n // 2, n // 8
    own, total = 2 * rows, BLOCK_DEVS * rows
    half = fr * chips
    chunk = half // highs
    outs = width // COLS
    groups = 1 + highs + outs
    late = highs - FIRST_HIGH
    vm = pltpu.VMEM
    dma = pltpu.SemaphoreType.DMA
    shapes = {
        "x_all": vm((2, 2, 2, own, width), BF16),
        "p_all": vm((chips, 2, wr, 3 * PAIR), BF16),
        "w_o": vm((highs, 2, 2, 2, wr, width), BF16),
        "w_i": vm((highs, 2, 2, 2, wr, half), BF16),
        "w_u": vm((highs, 2, 2, fr, width), BF16),
        "pieces": vm((CUBE, wr, 3 * PAIR), BF16),
        "w_loc": vm((2, wr, half), BF16),
        "param": vm((8, width), F32),
        "b_in": vm((8, half), F32),
        "gbin": vm((8, half), F32),
        "sums": vm((8, width), F32),
        "q": vm((total, PAIR), BF16),
        "k": vm((total, PAIR), BF16),
        "v": vm((total, PAIR), BF16),
        "o": vm((total, PAIR), F32),
        "low": vm((total, PAIR), BF16),
        "lse": vm((total, PAIR), F32),
        "attn": vm((2, rows, width), BF16),
        "x1": vm((own, width), F32),
        "n1": vm((own, width), F32),
        "r1": vm((own, 128), F32),
        "x1_low": vm((2 * own, width), BF16),
        "slope": vm((highs, 2 * own, chunk), F32),
        "act": vm((2 * own, half), BF16),
        "part": vm((2 * own, width), F32),
        "got": vm((own, width), F32),
        "df2": vm((2 * own, width), BF16),
        "du": vm((2 * own, chunk), BF16),
        "dattn": vm((2, rows, width), BF16),
        "do": vm((BLOCK_DEVS, rows, PAIR), BF16),
        "g": vm((total, 3 * PAIR), BF16),
        "o_got": vm((highs, 2, 2, wr, width), BF16),
        "rai": vm((late, 2, highs, 2, wr, chunk), BF16),
        "rau": vm((outs, 2, highs, 2, fr // 2, COLS), BF16),
        "rao": vm((2, highs, 2, wr, HALF), BF16),
        "rbi": vm((late, 2, highs, wr, chunk), BF16),
        "rbu": vm((outs, 2, highs, fr // 2, COLS), BF16),
        "rbo": vm((2, highs, wr, HALF), BF16),
        "rci": vm((late, highs - 1, 2, wr, chunk), BF16),
        "rcu": vm((outs, highs - 1, fr, COLS), BF16),
        "rco": vm((highs - 1, wr, width), BF16),
        "raf": vm((FIRST_HIGH, highs - 1, 2, 2, 2, wr, chunk), BF16),
        "rbf": vm((FIRST_HIGH, 2, 2, wr, chunk), BF16),
        "rcf": vm((FIRST_HIGH, 2, wr, chunk), BF16),
        "line": vm((16, PAIR), BF16),
        "lines": vm((chips, 2, 16, PAIR), BF16),
        "line_got": vm((chips, 16, PAIR), BF16),
        "line_slot": vm((chips, 16, PAIR), BF16),
        "tok": vm((2, rows, width), BF16),
        "cot": vm((2, rows, width), BF16),
        "out": vm((2, rows, width), BF16),
        "gtok": vm((2, rows, width), BF16),
        "wqkv": vm((3, wr, width), BF16),
        "w_in": vm((wr, fr * n), BF16),
        "gqkv": vm((3, wr, width), F32),
        "gwo": vm((wr, width), F32),
        "gwin": vm((wr, fr * n), F32),
        "gwout": vm((fr, width), F32),
        "gline": vm((1, 3 * PAIR), F32),
        "fin": vm((2, wr, half), F32),
        "fin_got": vm((wr, half), F32),
        "pg": vm((chips, 2, wr, 3 * PAIR), BF16),
        "pgot": vm((chips, wr, 3 * PAIR), BF16),
        "pslot": vm((chips, wr, 3 * PAIR), BF16),
    }
    for t in range(2):
        for phase, lead in enumerate(((2, 2), (2,), ())):
            for i in range(3):
                shapes[f"x{t}{phase}{i}"] = vm(lead + (SPANS[t][i][1], width), BF16)
    counts = {
        "swap": (12,), "piece": (chips,), "line": (chips,), "lsum": (chips,), "cube": (2, 3, 3), "hi": (groups, highs), "ab": (groups, 2, 2),
        "torow": (BLOCK_DEVS,), "halves": (outs,), "tohead": (BLOCK_DEVS,), "ra": (groups, highs), "rb": (groups, 2),
        "rc": (groups, highs), "fin": (highs,), "xr": (2, 3, 3), "psum": (chips,),
    }
    for name, count in counts.items():
        shapes[name + "_s"] = dma(count)
        shapes[name + "_r"] = dma(count)
    shapes["load"] = dma((18,))
    s = jax.ShapeDtypeStruct
    return pl.pallas_call(
        functools.partial(layer_kernel, n, tuple(shapes)),
        name="layer",
        out_shape=(
            s((2, rows, width), BF16),
            s((2, rows, width), BF16),
            s((wr, width), F32),
            s((wr, width), F32),
            s((wr, width), F32),
            s((wr, width), F32),
            s((wr, fr * n), F32),
            s((fr, width), F32),
            s((1, 3 * PAIR), F32),
        ),
        in_specs=[SMEM, SMEM] + [ANY] * 8 + [VMEM],
        out_specs=(ANY,) * 9,
        scratch_shapes=list(shapes.values()),
        compiler_params=pltpu.CompilerParams(collective_id=6, has_side_effects=True, vmem_limit_bytes=64 << 20),
    )(seq_len, slot, tok, cot, wq, wk, wv, wo, w_in, w_out, line)


def finish_kernel(wr, *refs):
    big, lines, outs, small = refs[:8], refs[8], refs[9:17], refs[17:26]
    held, sem = refs[26:34], refs[34]
    ins = [pltpu.make_async_copy(a, b, sem.at[0, i]) for i, (a, b) in enumerate(zip(big, held))]
    start(ins)
    copies = [pltpu.make_async_copy(a, b, sem.at[1, i]) for i, (a, b) in enumerate(zip(held, outs))]
    for i, ref in enumerate(small):
        ref[...] = lines[0, i * wr : i * wr + ref.shape[0]]
    for one, other in zip(ins, copies):
        one.wait()
        other.start()
    wait(copies)


def finish(wr, fr, *values):
    s = jax.ShapeDtypeStruct
    return pl.pallas_call(
        functools.partial(finish_kernel, wr),
        name="finish",
        out_shape=tuple(s(value.shape, value.dtype) for value in values[:8])
        + (s((wr,), F32),) * 8
        + (s((fr,), F32),),
        in_specs=[ANY] * 8 + [VMEM],
        out_specs=(ANY,) * 8 + (VMEM,) * 9,
        scratch_shapes=[pltpu.VMEM(value.shape, value.dtype) for value in values[:8]]
        + [pltpu.SemaphoreType.DMA((2, 8))],
    )(*values)


def on_device(
    n, tokens, cotangent, seq_lengths, slot_block, w_query, w_key, w_value, w_output, w_in, w_out,
    b_query, b_value, b_output, b_in, b_out, ln1_gain, ln1_bias, ln2_gain, ln2_bias,
):
    _, rows, width = tokens.shape
    wr = w_query.shape[0]
    fr = w_out.shape[0]
    ff = fr // wr
    chips = n // 2
    highs = n // 8
    device = lax.axis_index("fsdp")
    core, chip = device % 2, device // 2
    cube = chip % CUBE
    vectors = (b_query, b_value, b_output, b_out, ln1_gain, ln1_bias, ln2_gain, ln2_bias, b_in)
    if wr % 16 == 0 and 8 * wr + fr == 3 * PAIR and fr == PAIR:
        total = 3 * PAIR
        line = sum(
            jnp.pad(value.astype(F32)[None], ((0, 0), (i * wr, total - i * wr - value.shape[0])))
            for i, value in enumerate(vectors)
        )
        values = layer(
            n, seq_lengths, slot_block, tokens, cotangent, w_query, w_key, w_value, w_output, w_in, w_out, line
        )
        results = finish(wr, fr, *values)
        bq, bv, bo, bout, gain1, shift1, gain2, shift2, bin_ = results[8:]
        return results[:8] + (bq, bv, bo, bin_, bout, gain1, shift1, gain2, shift2)
    line = jnp.concatenate(vectors)
    lengths = jnp.sum(jnp.where(slot_block == device // BLOCK_DEVS, seq_lengths, 0), axis=1).astype(jnp.int32)
    live = lax.dynamic_slice(lengths, (core,), (1,))
    pad = -(-(wr + 1) // 16) * 16
    cols = jnp.stack([w_query, w_key, w_value]).reshape(3, wr, CUBE, PAIR).transpose(2, 1, 0, 3)
    cols = cols.reshape(CUBE, wr, 3 * PAIR)
    line = jnp.pad(line, (0, 3 * PAIR - line.shape[0]))
    tail = jnp.pad(line[None], ((0, pad - wr - 1), (0, 0)))
    pieces = jnp.concatenate([cols, jnp.broadcast_to(tail, (CUBE,) + tail.shape)], axis=1)
    in_loc = w_in.reshape(wr, chips, 2, ff, wr).transpose(2, 3, 0, 1, 4).reshape(2, ff, wr, HALF)
    w_loc = jnp.concatenate([w_output, w_out]).reshape(ff + 1, wr, 2, HALF).transpose(0, 2, 1, 3)
    x_all, p_all, w_all = gather(n, tokens, pieces, w_loc, in_loc)
    x = x_all.reshape(BLOCK_DEVS * rows, width)
    w_qkv = p_all[:, :, :wr].reshape(width, 3 * PAIR)
    lines = p_all[:, :, wr].reshape(n, 3 * PAIR)
    small = lines[:, : 8 * wr].reshape(n, 8, wr).transpose(1, 0, 2).reshape(8, width)
    bias_in = lax.dynamic_index_in_dim(lines.reshape(chips, 2, 3 * PAIR), core, 1, keepdims=False)
    bias_in = bias_in[:, 8 * wr : 8 * wr + fr].reshape(chips, ff, wr).transpose(1, 0, 2).reshape(ff, HALF)
    bias_qv = lax.dynamic_slice(small, (0, cube * PAIR), (2, PAIR)).astype(F32)
    q, k, v, o, low, lse = attend(live, x, w_qkv, bias_qv[0:1], bias_qv[1:2])
    attn = exchange(to_rows_kernel, n, low.reshape(BLOCK_DEVS, rows, PAIR), (2, rows, width), "to_rows", 1)
    out, dh, dattn, g_in, g_out, g_o, g_small, g_bin = rows_call(
        n, lengths, attn, tokens, cotangent, w_all, small, bias_in
    )
    do = exchange(to_heads_kernel, n, dattn, (BLOCK_DEVS, rows, PAIR), "to_heads", 2).reshape(-1, PAIR)
    dx, dw, db = attend_back(live, q, k, v, o, lse, do, x, w_qkv)
    unit = (wr, HALF)
    g = jnp.concatenate(
        [
            g_in.reshape((ff, highs, 2, 2, 2) + unit),
            g_out.reshape((ff, 2, highs, 2, 2) + unit).transpose(0, 2, 3, 4, 1, 5, 6),
        ]
    )
    one = g_o.reshape((2, highs, 2, 2, 2) + unit).transpose(4, 1, 2, 3, 0, 5, 6)
    r_w, r_in = scatter_w(n, g, one)
    wide = jnp.zeros((2, width), F32)
    wide = lax.dynamic_update_slice(wide, jnp.stack([db[0, :PAIR], db[0, 2 * PAIR :]]), (0, cube * PAIR))
    lines = (g_small + jnp.pad(wide, ((0, 6), (0, 0)))).reshape(8, n, wr).transpose(1, 0, 2).reshape(n, 8 * wr)
    hidden = g_bin.reshape(ff, chips, wr).transpose(1, 0, 2).reshape(chips, 1, fr)
    hidden = jnp.where(jnp.arange(2)[None, :, None] == core, hidden, 0.0).reshape(n, fr)
    lines = jnp.concatenate([lines, hidden], axis=1)
    lines = jnp.pad(lines, ((0, 0), (0, 3 * PAIR - lines.shape[1])))[:, None]
    parts = jnp.concatenate([dw.reshape(n, wr, 3 * PAIR), lines, jnp.zeros((n, pad - wr - 1, 3 * PAIR), F32)], axis=1)
    parts = parts.astype(BF16).reshape(chips, 2, pad, 3 * PAIR)
    gtok, red = scatter_x(n, dx.reshape(2, 2, 2, 2 * rows, width), dh, parts)
    red = jnp.stack([lax.dynamic_index_in_dim(red, cube ^ m, 0, keepdims=False) for m in range(CUBE)])
    g_qkv = red[:, :wr].reshape(CUBE, wr, 3, PAIR).transpose(2, 1, 0, 3).reshape(3, wr, width)
    line = jnp.sum(red[:, wr], axis=0)
    g_w_in = r_in.reshape(2, ff, wr, chips, wr).transpose(2, 3, 0, 1, 4).reshape(wr, fr * n)
    flat = r_w.transpose(0, 2, 1, 3).reshape(ff * 2 + 1, wr, width)
    biases = [line[i * wr : (i + 1) * wr] for i in range(8)]
    bq, bv, bo, bout, gain1, shift1, gain2, shift2 = biases
    return (
        out, gtok, g_qkv[0], g_qkv[1], g_qkv[2], flat[0], g_w_in, flat[1 + ff :].reshape(fr, width),
        bq, bv, bo, line[8 * wr : 8 * wr + fr], bout, gain1, shift1, gain2, shift2,
    )


def solution(mesh):
    n = mesh.shape["fsdp"]
    rows, vector, whole = P(None, "fsdp", None), P("fsdp"), P()
    matrix = P("fsdp", None)
    return jax.shard_map(
        functools.partial(on_device, n),
        mesh=mesh,
        in_specs=(rows, rows, whole, whole) + (matrix,) * 6 + (vector,) * 9,
        out_specs=(rows, rows) + (matrix,) * 6 + (vector,) * 9,
        check_vma=False,
    )
```

```python
import functools

import jax
import jax.numpy as jnp
from jax import lax
from jax.experimental import pallas as pl
from jax.experimental.pallas import tpu as pltpu
from jax.sharding import PartitionSpec as P

HEAD_DIM = 64
BLOCK_DEVS = 16
CUBE = BLOCK_DEVS // 2
PAIR = 2 * HEAD_DIM
HALF = 512
MESH = pl.DeviceIdType.MESH
VMEM = pl.BlockSpec(memory_space=pltpu.VMEM)
SMEM = pl.BlockSpec(memory_space=pltpu.SMEM)
ANY = pl.BlockSpec(memory_space=pl.ANY)
F32 = jnp.float32
BF16 = jnp.bfloat16


def dot(a, b, ca=1, cb=0):
    return lax.dot_general(a, b, (((ca,), (cb,)), ((), ())), preferred_element_type=F32)


def send(src, dst, send_sem, recv_sem, device):
    copy = pltpu.make_async_remote_copy(
        src_ref=src,
        dst_ref=dst,
        send_sem=send_sem,
        recv_sem=recv_sem,
        device_id=(device,),
        device_id_type=MESH,
    )
    copy.start()
    return copy


def greet(devices):
    barrier = pltpu.get_barrier_semaphore()
    for device in devices:
        pl.semaphore_signal(barrier, inc=1, device_id=(device,), device_id_type=MESH)
    pl.semaphore_wait(barrier, len(devices))


def where_am_i(n):
    me = lax.axis_index("fsdp")
    chip = me // 2
    return dict(
        me=me,
        core=me % 2,
        chip=chip,
        cube=chip % CUBE,
        rank=me % BLOCK_DEVS,
        high=chip // 4,
        l1=chip // 2 % 2,
        l0=chip % 2,
        n=n,
        chips=n // 2,
        highs=n // 8,
    )


CUBE_ORDERS = ((0, 1, 2), (1, 2, 0), (2, 0, 1))


def cube_rows(total):
    first = total // 3 // 16 * 16
    last = total - 2 * first
    return ((0, last), (last, first), (last + first, first))


def gather_kernel(n, tok, pieces, w_loc, in_loc, x_all, p_all, w_all,
                  tok_s, tok_r, cube_s, cube_r, pc_s, pc_r, sw_s, sw_r, loc_s, wi_s, wi_r,
                  hi_s, hi_r, ab_s, ab_r):
    w = where_am_i(n)
    me, core, chip, high, l1, l0 = w["me"], w["core"], w["chip"], w["high"], w["l1"], w["l0"]
    rows = tok.shape[1]
    partner = me ^ 1
    others = [me ^ (2 * m) for m in range(1, w["chips"])]
    greet([partner] + others)
    bits = (w["cube"] // 4, w["cube"] // 2 % 2, w["cube"] % 2)

    def mine(s=slice(None)):
        return x_all.at[bits[0], bits[1], bits[2], s]

    own_rows = pl.ds(pl.multiple_of(core * rows, rows), rows)
    locals_ = []
    locals_.append(pltpu.make_async_copy(tok.at[core], mine(own_rows), loc_s.at[0]))
    locals_[-1].start()
    swap = send(tok.at[1 - core], mine(own_rows), tok_s, tok_r, partner)
    items = w_all.shape[0]
    ff = (items - 1) // 2
    here = lambda item, s: w_all.at[item, high, l1, l0, s]
    swap_in = send(in_loc.at[1 - core], w_all.at[pl.ds(1, ff), high, l1, l0, core], wi_s, wi_r, partner)
    locals_.append(pltpu.make_async_copy(in_loc.at[core], w_all.at[pl.ds(1, ff), high, l1, l0, core], loc_s.at[1]))
    locals_[-1].start()
    locals_.append(pltpu.make_async_copy(w_loc.at[pl.ds(0, 1)], w_all.at[pl.ds(0, 1), high, l1, l0], loc_s.at[2]))
    locals_[-1].start()
    locals_.append(pltpu.make_async_copy(w_loc.at[pl.ds(1, ff)], w_all.at[pl.ds(1 + ff, ff), high, l1, l0], loc_s.at[3]))
    locals_[-1].start()
    locals_.append(pltpu.make_async_copy(pieces.at[w["cube"]], p_all.at[chip, core], loc_s.at[4]))
    locals_[-1].start()
    piece_copies = []
    for m in range(1, w["chips"]):
        there = (chip ^ m) % CUBE
        piece_copies.append(send(pieces.at[there], p_all.at[chip, core], pc_s.at[m], pc_r.at[m], others[m - 1]))
    for copy in locals_:
        copy.wait()
    swap.wait()
    spans = cube_rows(2 * rows)
    masks = (8, 4, 2)
    live = []
    for phase in range(3):
        for copy in live:
            copy.wait()
        live = []
        for s, order in enumerate(CUBE_ORDERS):
            index = [bits[0], bits[1], bits[2]]
            for done in order[:phase]:
                index[done] = slice(None)
            region = x_all.at[index[0], index[1], index[2], pl.ds(*spans[s])]
            live.append(send(region, region, cube_s.at[phase, s], cube_r.at[phase, s], me ^ masks[order[phase]]))
    swap_in.wait()
    for copy in piece_copies:
        copy.wait()
    region = p_all.at[:, core]
    swap_p = send(region, region, sw_s, sw_r, partner)
    for copy in live:
        copy.wait()
    swap_p.wait()
    groups = [(0, 1)] + [(1 + j, None) for j in range(ff)]

    def group(g, *index):
        if g == 0:
            return [w_all.at[(pl.ds(0, 1),) + index]]
        return [w_all.at[(pl.ds(g, 1),) + index], w_all.at[(pl.ds(g + ff, 1),) + index]]

    def high_phase(g):
        out = []
        for m in range(1, w["highs"]):
            for i, region in enumerate(group(g, high, l1, l0)):
                out.append(send(region, region, hi_s.at[g, m, i], hi_r.at[g, m, i], me ^ (8 * m)))
        return out

    def low_phase(g, phase):
        out = []
        for s in range(2):
            if phase == 0:
                index = (slice(None), l1, l0, s)
                to = me ^ (2 if s == 0 else 4)
            elif s == 0:
                index = (slice(None), l1, slice(None), s)
                to = me ^ 4
            else:
                index = (slice(None), slice(None), l0, s)
                to = me ^ 2
            for i, region in enumerate(group(g, *index)):
                out.append(send(region, region, ab_s.at[g, phase, s, i], ab_r.at[g, phase, s, i], to))
        return out

    def settle(copies):
        for copy in copies:
            copy.wait()

    waiting = {}
    count = len(groups)
    for step in range(count + 2):
        if step < count:
            waiting[step, 0] = high_phase(step)
        if 0 <= step - 1 < count:
            settle(waiting.pop((step - 1, 0)))
            waiting[step - 1, 1] = low_phase(step - 1, 0)
        if 0 <= step - 2 < count:
            settle(waiting.pop((step - 2, 1)))
            waiting[step - 2, 2] = low_phase(step - 2, 1)
    for copies in waiting.values():
        settle(copies)


def gather(n, tok, pieces, w_loc, in_loc):
    rows, width = tok.shape[1:]
    wr = in_loc.shape[2]
    ff = in_loc.shape[1]
    items = 1 + 2 * ff
    chips, highs = n // 2, n // 8
    dma = pltpu.SemaphoreType.DMA
    return pl.pallas_call(
        functools.partial(gather_kernel, n),
        name="gather",
        out_shape=(
            jax.ShapeDtypeStruct((2, 2, 2, 2 * rows, width), BF16),
            jax.ShapeDtypeStruct((chips, 2) + pieces.shape[1:], BF16),
            jax.ShapeDtypeStruct((items, highs, 2, 2, 2, wr, HALF), BF16),
        ),
        in_specs=[ANY] * 4,
        out_specs=(ANY, ANY, ANY),
        scratch_shapes=[
            dma, dma, dma((3, 3)), dma((3, 3)), dma((chips,)), dma((chips,)), dma, dma, dma((5,)), dma, dma,
            dma((ff + 1, highs, 2)), dma((ff + 1, highs, 2)), dma((ff + 1, 2, 2, 2)), dma((ff + 1, 2, 2, 2)),
        ],
        compiler_params=pltpu.CompilerParams(collective_id=0, has_side_effects=True),
    )(tok, pieces, w_loc, in_loc)


def attend_kernel(live, x, w, bq, bv, q, k, v, o, low, lse):
    rows = x.shape[0]
    tile = 256

    def project(i, _):
        at = pl.ds(pl.multiple_of(i * tile, tile), tile)
        y = dot(x[at, :], w[...])
        q[at, :] = ((y[:, :PAIR] + bq[...]) * HEAD_DIM ** (-0.5)).astype(BF16)
        k[at, :] = y[:, PAIR : 2 * PAIR].astype(BF16)
        v[at, :] = (y[:, 2 * PAIR :] + bv[...]).astype(BF16)
        return 0

    lax.fori_loop(0, rows // tile, project, 0)
    length = live[0]

    def step(i, _):
        at = pl.ds(pl.multiple_of(i * tile, tile), tile)
        outs, logs = [], []
        for h in range(2):
            c = slice(h * HEAD_DIM, (h + 1) * HEAD_DIM)
            s = dot(q[at, c], k[:, c], 1, 1)
            place = lax.broadcasted_iota(jnp.int32, s.shape, 1)
            s = jnp.where(place < length, s, -1e30)
            top = jnp.max(s, axis=1, keepdims=True)
            e = jnp.exp(s - top)
            total = jnp.sum(e, axis=1, keepdims=True)
            mixed = dot(e.astype(BF16), v[:, c])
            outs.append(mixed / total)
            logs.append(jnp.broadcast_to(top + jnp.log(total), (tile, HEAD_DIM)))
        out = jnp.concatenate(outs, axis=1)
        o[at, :] = out
        low[at, :] = out.astype(BF16)
        lse[at, :] = jnp.concatenate(logs, axis=1)
        return 0

    lax.fori_loop(0, rows // tile, step, 0)


def attend(live, x, w, bq, bv):
    rows = x.shape[0]
    low = jax.ShapeDtypeStruct((rows, PAIR), BF16)
    wide = jax.ShapeDtypeStruct((rows, PAIR), F32)
    return pl.pallas_call(
        attend_kernel,
        name="attend",
        out_shape=(low, low, low, wide, low, wide),
        in_specs=[SMEM, VMEM, VMEM, VMEM, VMEM],
        out_specs=(VMEM,) * 6,
        compiler_params=pltpu.CompilerParams(vmem_limit_bytes=56 << 20),
    )(live, x, w, bq, bv)


def to_rows_kernel(n, low, out, ss, rs, ls):
    w = where_am_i(n)
    me, core, cube, rank = w["me"], w["core"], w["cube"], w["rank"]
    greet([me ^ m for m in range(1, BLOCK_DEVS)])
    there = out.at[core, :, pl.ds(pl.multiple_of(cube * PAIR, PAIR), PAIR)]
    own = pltpu.make_async_copy(low.at[rank], there, ls)
    own.start()
    copies = [send(low.at[rank ^ m], there, ss.at[m], rs.at[m], me ^ m) for m in range(1, BLOCK_DEVS)]
    own.wait()
    for copy in copies:
        copy.wait()


def to_heads_kernel(n, grad, out, ss, rs, ls):
    w = where_am_i(n)
    me, core, cube, rank = w["me"], w["core"], w["cube"], w["rank"]
    greet([me ^ m for m in range(1, BLOCK_DEVS)])

    def piece(m):
        return grad.at[core ^ (m % 2), :, pl.ds(pl.multiple_of((cube ^ (m // 2)) * PAIR, PAIR), PAIR)]

    own = pltpu.make_async_copy(piece(0), out.at[rank], ls)
    own.start()
    copies = [send(piece(m), out.at[rank], ss.at[m], rs.at[m], me ^ m) for m in range(1, BLOCK_DEVS)]
    own.wait()
    for copy in copies:
        copy.wait()


def exchange(kernel, n, value, shape, name, ident):
    dma = pltpu.SemaphoreType.DMA
    return pl.pallas_call(
        functools.partial(kernel, n),
        name=name,
        out_shape=jax.ShapeDtypeStruct(shape, BF16),
        in_specs=[ANY],
        out_specs=ANY,
        scratch_shapes=[dma((BLOCK_DEVS,)), dma((BLOCK_DEVS,)), dma],
        compiler_params=pltpu.CompilerParams(collective_id=ident, has_side_effects=True),
    )(value)


def norm_forward(h):
    center = h - jnp.mean(h, axis=1, keepdims=True)
    rs = lax.rsqrt(jnp.mean(center * center, axis=1, keepdims=True) + 1e-05)
    return center * rs, rs


def norm_back(e, n, rs, gain):
    eg = e * gain
    return (eg - jnp.mean(eg, axis=1, keepdims=True) - n * jnp.mean(eg * n, axis=1, keepdims=True)) * rs


def total_rows(value):
    return jnp.sum(value, axis=0, keepdims=True)


def rows_kernel(n, live, attn, tok, cot, w_all, small, b_in,
                out, dh, dattn, g_in, g_out, g_o, g_small, g_bin,
                w_o, x1, n1, r1, x1_low, slope, act, part, got, df2, got2,
                wo_s, wo_r, x_s, x_r, h_s, h_r, d_s, d_r, e_s, e_r, lo_s):
    w = where_am_i(n)
    me, core, rank = w["me"], w["core"], w["rank"]
    partner = me ^ 1
    greet([partner])
    rows, width = tok.shape[1:]
    own = 2 * rows
    ff = (w_all.shape[0] - 1) // 2
    swap = send(w_all.at[0], w_o.at[:, :, :, core], wo_s, wo_r, partner)
    keep = pltpu.make_async_copy(w_all.at[0], w_o.at[:, :, :, core], lo_s)
    keep.start()
    keep.wait()
    swap.wait()

    def wo(s):
        return w_o[:, :, :, :, s].reshape(width, HALF)

    names = ("bq", "bv", "bo", "bout", "g1", "s1", "g2", "s2")
    param = {name: small[i : i + 1, :].astype(F32) for i, name in enumerate(names)}
    for m in range(2):
        at = slice(m * rows, (m + 1) * rows)
        a = attn[m]
        mid = jnp.concatenate([dot(a, wo(0)), dot(a, wo(1))], axis=1)
        h = tok[m].astype(F32) + mid + param["bo"]
        nn, rs = norm_forward(h)
        n1[at, :] = nn
        r1[at, :] = jnp.broadcast_to(rs, (rows, 128))
        y = nn * param["g1"] + param["s1"]
        x1[at, :] = y
        x1_low[at, :] = y.astype(BF16)
    swap = send(x1_low.at[pl.ds(0, own)], x1_low.at[pl.ds(own, own)], x_s, x_r, partner)
    swap.wait()
    for j in range(ff):
        w_in = w_all[1 + j].reshape(width, HALF)
        u = dot(x1_low[...], w_in) + b_in[j : j + 1, :].astype(F32)
        phi = 0.5 + 0.5 * lax.erf(u * 0.7071067811865476)
        slope[j] = phi + u * (0.3989422804014327 * jnp.exp(-0.5 * u * u))
        a = (u * phi).astype(BF16)
        act[j] = a
        for s in range(2):
            w_out = w_all[1 + ff + j, :, :, :, s].reshape(HALF, HALF)
            c = slice(s * HALF, (s + 1) * HALF)
            if j == 0:
                part[:, c] = dot(a, w_out)
            else:
                part[:, c] += dot(a, w_out)
    swap = send(part.at[pl.ds(own, own)], got, h_s, h_r, partner)
    swap.wait()
    bout = param["bout"]
    sums = {name: jnp.zeros((1, width), F32) for name in ("bo", "bout", "g1", "s1", "g2", "s2")}
    for m in range(2):
        at = slice(m * rows, (m + 1) * rows)
        h = x1[at, :] + part[at, :] + got[at, :] + bout
        nn, rs = norm_forward(h)
        out[m] = (nn * param["g2"] + param["s2"]).astype(BF16)
        place = rank * rows + lax.broadcasted_iota(jnp.int32, (rows, 1), 0)
        dy = jnp.where(place < live[m], cot[m].astype(F32), 0.0)
        sums["g2"] += total_rows(dy * nn)
        sums["s2"] += total_rows(dy)
        d = norm_back(dy, nn, rs, param["g2"])
        x1[at, :] = d
        low = d.astype(BF16)
        df2[at, :] = low
        sums["bout"] += total_rows(low.astype(F32))
    swap = send(df2.at[pl.ds(0, own)], df2.at[pl.ds(own, own)], d_s, d_r, partner)
    swap.wait()
    for j in range(ff):
        w_in = w_all[1 + j].reshape(width, HALF)
        da = None
        for s in range(2):
            w_out = w_all[1 + ff + j, :, :, :, s].reshape(HALF, HALF)
            c = slice(s * HALF, (s + 1) * HALF)
            term = dot(df2[:, c], w_out, 1, 1)
            da = term if da is None else da + term
            g_out[j, s] = dot(act[j], df2[:, c], 0, 0).astype(BF16)
        du = (da * slope[j]).astype(BF16)
        g_bin[j : j + 1, :] = total_rows(du.astype(F32))
        g_in[j] = dot(x1_low[...], du, 0, 0).astype(BF16)
        back = dot(du, w_in, 1, 1)
        if j == 0:
            part[...] = back
        else:
            part[...] += back
    swap = send(part.at[pl.ds(own, own)], got2, e_s, e_r, partner)
    swap.wait()
    for m in range(2):
        at = slice(m * rows, (m + 1) * rows)
        e = x1[at, :] + part[at, :] + got2[at, :]
        nn, rs = n1[at, :], r1[at, 0:1]
        sums["g1"] += total_rows(e * nn)
        sums["s1"] += total_rows(e)
        d = norm_back(e, nn, rs, param["g1"])
        dh[m] = d
        low = d.astype(BF16)
        df2[at, :] = low
        sums["bo"] += total_rows(low.astype(F32))
        dattn[m] = (dot(low[:, :HALF], wo(0), 1, 1) + dot(low[:, HALF:], wo(1), 1, 1)).astype(BF16)
    for s in range(2):
        c = slice(s * HALF, (s + 1) * HALF)
        g_o[s] = sum(dot(attn[m], df2[m * rows : (m + 1) * rows, c], 0, 0) for m in range(2)).astype(BF16)
    g_small[0:2, :] = jnp.zeros((2, width), F32)
    for i, name in enumerate(names[2:]):
        g_small[2 + i : 3 + i, :] = sums[name]


def rows_call(n, live, attn, tok, cot, w_all, small, b_in):
    _, rows, width = tok.shape
    items, highs = w_all.shape[:2]
    wr = w_all.shape[5]
    ff = (items - 1) // 2
    own = 2 * rows
    dma = pltpu.SemaphoreType.DMA
    s = jax.ShapeDtypeStruct
    return pl.pallas_call(
        functools.partial(rows_kernel, n),
        name="rows",
        out_shape=(
            s((2, rows, width), BF16),
            s((2, rows, width), F32),
            s((2, rows, width), BF16),
            s((ff, width, HALF), BF16),
            s((ff, 2, HALF, HALF), BF16),
            s((2, width, HALF), BF16),
            s((8, width), F32),
            s((ff, HALF), F32),
        ),
        in_specs=[SMEM] + [VMEM] * 6,
        out_specs=(VMEM,) * 8,
        scratch_shapes=[
            pltpu.VMEM((highs, 2, 2, 2, 2, wr, HALF), BF16),
            pltpu.VMEM((own, width), F32),
            pltpu.VMEM((own, width), F32),
            pltpu.VMEM((own, 128), F32),
            pltpu.VMEM((2 * own, width), BF16),
            pltpu.VMEM((ff, 2 * own, HALF), F32),
            pltpu.VMEM((ff, 2 * own, HALF), BF16),
            pltpu.VMEM((2 * own, width), F32),
            pltpu.VMEM((own, width), F32),
            pltpu.VMEM((2 * own, width), BF16),
            pltpu.VMEM((own, width), F32),
        ]
        + [dma] * 11,
        compiler_params=pltpu.CompilerParams(collective_id=3, has_side_effects=True, vmem_limit_bytes=60 << 20),
    )(live, attn, tok, cot, w_all, small, b_in)


def attend_back_kernel(live, q, k, v, o, lse, do, x, w, dx, dw, db, g, dk, dv):
    rows = q.shape[0]
    tile = 256
    length = live[0]
    scale = HEAD_DIM ** (-0.5)
    dk[...] = jnp.zeros_like(dk)
    dv[...] = jnp.zeros_like(dv)

    def step(i, _):
        at = pl.ds(pl.multiple_of(i * tile, tile), tile)
        outs = []
        for h in range(2):
            c = slice(h * HEAD_DIM, (h + 1) * HEAD_DIM)
            s = dot(q[at, c], k[:, c], 1, 1)
            place = lax.broadcasted_iota(jnp.int32, s.shape, 1)
            p = jnp.where(place < length, jnp.exp(s - lse[at, h * HEAD_DIM : h * HEAD_DIM + 1]), 0.0)
            d = do[at, c]
            dp = dot(d, v[:, c], 1, 1)
            inner = jnp.sum(d.astype(F32) * o[at, c], axis=1, keepdims=True)
            ds = (p * (dp - inner)).astype(BF16)
            outs.append(dot(ds, k[:, c]))
            dk[h] += dot(ds, q[at, c], 0, 0)
            dv[h] += dot(p.astype(BF16), d, 0, 0)
        g[at, 0:PAIR] = (jnp.concatenate(outs, axis=1).astype(BF16).astype(F32) * scale).astype(BF16)
        return 0

    lax.fori_loop(0, rows // tile, step, 0)
    g[:, PAIR : 2 * PAIR] = jnp.concatenate([dk[0], dk[1]], axis=1).astype(BF16)
    g[:, 2 * PAIR :] = jnp.concatenate([dv[0], dv[1]], axis=1).astype(BF16)

    def spread(i, _):
        at = pl.ds(pl.multiple_of(i * tile, tile), tile)
        dx[at, :] = dot(g[at, :], w[...], 1, 1).astype(BF16)
        return 0

    lax.fori_loop(0, rows // tile, spread, 0)
    dw[...] = dot(x[...], g[...], 0, 0)
    db[...] = jnp.broadcast_to(total_rows(g[...].astype(F32)), db.shape)


def attend_back(live, q, k, v, o, lse, do, x, w):
    rows, width = x.shape
    s = jax.ShapeDtypeStruct
    return pl.pallas_call(
        attend_back_kernel,
        name="attend_back",
        out_shape=(s((rows, width), BF16), s((width, 3 * PAIR), F32), s((8, 3 * PAIR), F32)),
        in_specs=[SMEM] + [VMEM] * 8,
        out_specs=(VMEM,) * 3,
        scratch_shapes=[
            pltpu.VMEM((rows, 3 * PAIR), BF16),
            pltpu.VMEM((2, rows, HEAD_DIM), F32),
            pltpu.VMEM((2, rows, HEAD_DIM), F32),
        ],
        compiler_params=pltpu.CompilerParams(vmem_limit_bytes=60 << 20),
    )(live, q, k, v, o, lse, do, x, w)


def add_into(target, *terms):
    total = target[...].astype(F32)
    for term in terms:
        total = total + term[...].astype(F32)
    target[...] = total.astype(target.dtype)


def scatter_w_kernel(n, g_in, one, out, out_in, g, r1a, r1b, r2, r3,
                     o_s, o_r, a_s, a_r, b_s, b_r, h_s, h_r, i_s, i_r, k_s):
    w = where_am_i(n)
    me, core, high, l1, l0 = w["me"], w["core"], w["high"], w["l1"], w["l0"]
    highs = w["highs"]
    partner = me ^ 1
    greet([partner, me ^ 2, me ^ 4] + [me ^ (8 * m) for m in range(1, highs)])
    items = g.shape[0]
    ff = (items - 1) // 2
    swap = send(one.at[1 - core], g.at[0], o_s, o_r, partner)
    fill = pltpu.make_async_copy(g_in, g.at[pl.ds(1, 2 * ff)], k_s)
    fill.start()
    fill.wait()
    swap.wait()

    def fold(i, _):
        g[0, i] = (g[0, i].astype(F32) + one[core, i].astype(F32)).astype(BF16)
        return 0

    lax.fori_loop(0, highs, fold, 0)
    first = [
        send(g.at[:, :, 1 - l1, :, 0], r1a, a_s.at[0], a_r.at[0], me ^ 4),
        send(g.at[:, :, :, 1 - l0, 1], r1b, a_s.at[1], a_r.at[1], me ^ 2),
    ]
    for copy in first:
        copy.wait()

    def add1(i, _):
        for h in range(highs):
            for b in range(2):
                g[i, h, l1, b, 0] = (g[i, h, l1, b, 0].astype(F32) + r1a[i, h, b].astype(F32)).astype(BF16)
                g[i, h, b, l0, 1] = (g[i, h, b, l0, 1].astype(F32) + r1b[i, h, b].astype(F32)).astype(BF16)
        return 0

    lax.fori_loop(0, items, add1, 0)
    second = [
        send(g.at[:, :, l1, 1 - l0, 0], r2.at[0], b_s.at[0], b_r.at[0], me ^ 2),
        send(g.at[:, :, 1 - l1, l0, 1], r2.at[1], b_s.at[1], b_r.at[1], me ^ 4),
    ]
    for copy in second:
        copy.wait()

    def add2(i, _):
        for h in range(highs):
            for s in range(2):
                g[i, h, l1, l0, s] = (g[i, h, l1, l0, s].astype(F32) + r2[s, i, h].astype(F32)).astype(BF16)
        return 0

    lax.fori_loop(0, items, add2, 0)
    third = [
        send(g.at[:, high ^ m, l1, l0], r3.at[m - 1], h_s.at[m], h_r.at[m], me ^ (8 * m)) for m in range(1, highs)
    ]
    for copy in third:
        copy.wait()

    def add3(i, _):
        for s in range(2):
            total = g[i, high, l1, l0, s].astype(F32)
            for m in range(1, highs):
                total = total + r3[m - 1, i, s].astype(F32)
            out[i, s] = total
        return 0

    lax.fori_loop(0, items, add3, 0)
    keep = pltpu.make_async_copy(out.at[pl.ds(1, ff), core], out_in.at[core], k_s)
    keep.start()
    swap = send(out.at[pl.ds(1, ff), 1 - core], out_in.at[core], i_s, i_r, partner)
    keep.wait()
    swap.wait()


def scatter_w(n, g, one):
    items, highs = g.shape[0] + 1, g.shape[1]
    wr = g.shape[5]
    ff = (items - 1) // 2
    dma = pltpu.SemaphoreType.DMA
    s = jax.ShapeDtypeStruct
    unit = (wr, HALF)
    return pl.pallas_call(
        functools.partial(scatter_w_kernel, n),
        name="scatter_w",
        out_shape=(s((items, 2) + unit, F32), s((2, ff) + unit, F32)),
        in_specs=[ANY, VMEM],
        out_specs=(VMEM, VMEM),
        scratch_shapes=[
            pltpu.VMEM((items, highs, 2, 2, 2) + unit, BF16),
            pltpu.VMEM((items, highs, 2) + unit, BF16),
            pltpu.VMEM((items, highs, 2) + unit, BF16),
            pltpu.VMEM((2, items, highs) + unit, BF16),
            pltpu.VMEM((highs - 1, items, 2) + unit, BF16),
            dma, dma, dma((2,)), dma((2,)), dma((2,)), dma((2,)), dma((highs,)), dma((highs,)), dma, dma, dma,
        ],
        compiler_params=pltpu.CompilerParams(collective_id=4, has_side_effects=True, vmem_limit_bytes=60 << 20),
    )(g, one)


def scatter_x_kernel(n, dx_in, dh, pieces_in, gtok, red, dx, g, psum, pgot, *rest):
    ra, rb, rc = rest[0:3], rest[3:6], rest[6:9]
    mine, theirs, c_s, c_r, t_s, t_r, w_s, w_r, p_s, p_r, k_s = rest[9:]
    w = where_am_i(n)
    me, core, chip = w["me"], w["core"], w["chip"]
    partner = me ^ 1
    chips = w["chips"]
    greet([partner] + [me ^ (2 * m) for m in range(1, chips)])
    rows = dh.shape[1]
    swap_p = send(pieces_in.at[:, 1 - core], pgot, w_s, w_r, partner)
    fills = [
        pltpu.make_async_copy(dx_in, dx, k_s.at[0]),
        pltpu.make_async_copy(pieces_in.at[:, core], psum, k_s.at[1]),
    ]
    for copy in fills:
        copy.start()
    for copy in fills:
        copy.wait()
    bits = (w["cube"] // 4, w["cube"] // 2 % 2, w["cube"] % 2)
    masks = (8, 4, 2)
    spans = cube_rows(2 * rows)

    def region(s, order, phase, far):
        index = [slice(None)] * 3
        for done in order[:phase]:
            index[done] = bits[done]
        axis = order[phase]
        index[axis] = 1 - bits[axis] if far else bits[axis]
        return tuple(index) + (pl.ds(*spans[s]),)

    def launch(phase):
        bufs = (ra, rb, rc)[phase]
        return [
            send(dx.at[region(s, order, phase, True)], bufs[s], c_s.at[phase, s], c_r.at[phase, s], me ^ masks[order[phase]])
            for s, order in enumerate(CUBE_ORDERS)
        ]

    def fold(phase):
        bufs = (ra, rb, rc)[phase]
        for s, order in enumerate(CUBE_ORDERS):
            at = region(s, order, phase, False)
            dx[at] = (dx[at].astype(F32) + bufs[s][...].astype(F32)).astype(BF16)

    live = launch(0)
    swap_p.wait()
    psum[...] = (psum[...].astype(F32) + pgot[...].astype(F32)).astype(BF16)
    copies = [send(psum.at[chip ^ m], g.at[m], p_s.at[m], p_r.at[m], me ^ (2 * m)) for m in range(1, chips)]
    own = pltpu.make_async_copy(psum.at[chip], g.at[0], k_s.at[2])
    own.start()
    for phase in range(3):
        for copy in live:
            copy.wait()
        fold(phase)
        if phase < 2:
            live = launch(phase + 1)
    here = (bits[0], bits[1], bits[2])
    theirs_at = pl.ds(pl.multiple_of((1 - core) * rows, rows), rows)
    own_at = pl.ds(pl.multiple_of(core * rows, rows), rows)
    swap = send(dx.at[here + (theirs_at,)], theirs, t_s, t_r, partner)
    gtok[core] = (dh[core] + dx[here + (own_at,)].astype(F32)).astype(BF16)
    own.wait()
    for copy in copies:
        copy.wait()
    for m in range(chips):
        term = g[m].astype(F32)
        if m < CUBE:
            red[m] = term
        else:
            red[m % CUBE] += term
    swap.wait()
    gtok[1 - core] = (dh[1 - core] + theirs[...].astype(F32)).astype(BF16)


def scatter_x(n, dx, dh, pieces):
    _, rows, width = dh.shape
    chips = n // 2
    unit = pieces.shape[2:]
    dma = pltpu.SemaphoreType.DMA
    s = jax.ShapeDtypeStruct
    spans = cube_rows(2 * rows)
    bufs = [pltpu.VMEM(lead + (spans[i][1], width), BF16) for lead in ((2, 2), (2,), ()) for i in range(3)]
    return pl.pallas_call(
        functools.partial(scatter_x_kernel, n),
        name="scatter_x",
        out_shape=(s((2, rows, width), BF16), s((CUBE,) + unit, F32)),
        in_specs=[ANY, VMEM, ANY],
        out_specs=(VMEM, VMEM),
        scratch_shapes=[
            pltpu.VMEM(dx.shape, BF16),
            pltpu.VMEM((chips,) + unit, BF16),
            pltpu.VMEM((chips,) + unit, BF16),
            pltpu.VMEM((chips,) + unit, BF16),
        ]
        + bufs
        + [
            pltpu.VMEM((rows, width), BF16),
            pltpu.VMEM((rows, width), BF16),
            dma((3, 3)), dma((3, 3)), dma, dma, dma, dma, dma((chips,)), dma((chips,)), dma((3,)),
        ],
        compiler_params=pltpu.CompilerParams(collective_id=5, has_side_effects=True, vmem_limit_bytes=60 << 20),
    )(dx, dh, pieces)


def start(copies):
    for copy in copies:
        copy.start()


def wait(copies):
    for copy in copies:
        copy.wait()


def remote(src, dst, sems, index, device):
    send_sem, recv_sem = sems
    return pltpu.make_async_remote_copy(
        src_ref=src,
        dst_ref=dst,
        send_sem=send_sem.at[index],
        recv_sem=recv_sem.at[index],
        device_id=(device,),
        device_id_type=MESH,
    )


def add_rows(dst, at, src, src_at):
    dst[at] = (dst[at].astype(F32) + src[src_at].astype(F32)).astype(dst.dtype)


COLS = 256
QUAD = 4
FAR = 8


def mate(m):
    return m % 2 + m // 2 * FAR


def device_of(quad, spot):
    return quad // 4 * 16 + spot // 2 * FAR + quad % 4 * 2 + spot % 2


def layer_kernel(n, shapes, seq_len, slot, tok_h, cot_h, wq_h, wk_h, wv_h, wo, w_in_h, w_out, line,
                 out_h, gtok_h, gq_h, gk_h, gv_h, gwo_h, gwin_h, gwout_h, gline_h, *scratch):
    s = dict(zip(shapes, scratch, strict=True))
    here = where_am_i(n)
    me, core, chip, cube, rank = (here[name] for name in ("me", "core", "chip", "cube", "rank"))
    high, l1, l0, chips, highs = (here[name] for name in ("high", "l1", "l0", "chips", "highs"))
    partner = me ^ 1
    tok, cot, out, gtok = (s[name] for name in ("tok", "cot", "out", "gtok"))
    gqkv, gwo, gwin, gwout, gline = (s[name] for name in ("gqkv", "gwo", "gwin", "gwout", "gline"))
    wqkv, w_in = s["wqkv"], s["w_in"]
    _, rows, width = tok.shape
    own = 2 * rows
    wr, fr = wo.shape[0], w_out.shape[0]
    quads = n // QUAD
    quarter = fr * quads
    chunk = quarter // 2
    spot = core + high % 2 * 2
    z1 = high // 2
    bits = (cube // 4, cube // 2 % 2, cube % 2)

    def sems(name):
        return s[name + "_s"], s[name + "_r"]

    own_rows = pl.ds(pl.multiple_of(core * rows, rows), rows)
    x_all, p_all, w_o, w_i, w_u = s["x_all"], s["p_all"], s["w_o"], s["w_i"], s["w_u"]

    def load(src, dst, i):
        copy = pltpu.make_async_copy(src, dst, s["load"].at[i])
        copy.start()
        return copy

    loads = [load(ref, wqkv.at[i], i) for i, ref in enumerate((wq_h, wk_h, wv_h))]
    loads.append(load(w_in_h, w_in, 3))
    load_o = load(wo, w_o.at[high, l1, l0, core], 4)
    load_u = load(w_out, w_u.at[me // 16, l1, l0], 5)
    load_x = load(tok_h.at[core], x_all.at[bits[0], bits[1], bits[2], own_rows], 6)
    load_t = load(tok_h, tok, 7)
    load_c = load(cot_h, cot, 8)

    met = sorted({m for m in range(1, BLOCK_DEVS)} | {2 * m for m in range(1, chips)})
    barrier = pltpu.get_barrier_semaphore()
    for m in met:
        pl.semaphore_signal(barrier, inc=1, device_id=(me ^ m,), device_id_type=MESH)

    lengths = []
    for m in range(2):
        length = jnp.int32(0)
        for i in range(slot.shape[1]):
            length = length + jnp.where(slot[m, i] == me // BLOCK_DEVS, seq_len[m, i], 0)
        lengths.append(length)

    pieces, w_loc, line_at, lines_all = s["pieces"], s["w_loc"], s["line"], s["lines"]
    wait(loads)
    for k in range(CUBE):
        for i in range(3):
            pieces[k, :, i * PAIR : (i + 1) * PAIR] = wqkv[i, :, k * PAIR : (k + 1) * PAIR]
    value = line[...]
    line_at[...] = jnp.concatenate(
        [value[:, i * PAIR : (i + 1) * PAIR] for i in range(3)] + [jnp.zeros((13, PAIR), F32)], axis=0
    ).astype(BF16)
    for i in range(quads):
        for q in range(QUAD):
            at = device_of(i, q) * fr
            w_loc[q, :, i * fr : (i + 1) * fr] = w_in[:, at : at + fr]
    pl.semaphore_wait(barrier, len(met))

    swap_tok = remote(tok_h.at[1 - core], x_all.at[bits[0], bits[1], bits[2], own_rows], sems("swap"), 0, partner)
    swap_tok.start()
    trade_in = [remote(w_loc.at[spot ^ m], w_i.at[z1, high % 2, l1, l0, core], sems("trade"), m, me ^ mate(m)) for m in range(1, QUAD)]
    start(trade_in)
    piece_copies = [
        remote(pieces.at[(chip ^ m) % CUBE], p_all.at[chip, core], sems("piece"), m, me ^ (2 * m))
        for m in range(1, chips)
    ]
    line_copies = [
        remote(line_at, lines_all.at[chip, core], sems("line"), m, me ^ (2 * m)) for m in range(1, chips)
    ]

    masks = (8, 4, 2)
    set_at = (core * rows, (1 - core) * rows)

    def rows_of(t, i):
        first, count = SPANS[t][i]
        return pl.ds(pl.multiple_of(set_at[t] + first, 16), count)

    def cube_phase(t, phase):
        out_ = []
        for i, order in enumerate(ROW_ORDERS):
            index = list(bits)
            for done in order[:phase]:
                index[done] = slice(None)
            region = x_all.at[index[0], index[1], index[2], rows_of(t, i)]
            sem = (s["cube_s"].at[t, phase], s["cube_r"].at[t, phase])
            out_.append(remote(region, region, sem, i, me ^ masks[order[phase]]))
        return out_

    groups = 5
    every = slice(None)

    def part_o(h_, a_, b_, t):
        return w_o.at[h_, a_, b_, core, :, every if t is None else pl.ds(t * HALF, HALF)]

    def part_of(g, h_, a_, b_, t):
        if g <= 2:
            return w_i.at[h_, :, a_, b_, every if t is None else t, :, pl.ds((g - 1) * chunk, chunk)]
        r_ = every if t is None else pl.ds(t * fr // 2, fr // 2)
        return w_u.at[h_, a_, b_, r_, pl.ds((g - 3) * HALF, HALF)]

    def high_copies(g):
        sem = (s["hi_s"].at[g], s["hi_r"].at[g])
        if g:
            region = part_of(g, z1, l1, l0, None)
            return [remote(region, region, sem, 0, me ^ 16)]
        region = part_o(high, l1, l0, None)
        return [remote(region, region, sem, m, me ^ (8 * m)) for m in range(1, highs)]

    def low_copies(g, phase):
        ab = (s["ab_s"].at[g, phase], s["ab_r"].at[g, phase])
        first, second = (every, l1, l0, 0), (every, l1, l0, 1)
        to = (me ^ 2, me ^ 4)
        if phase == 1:
            first, second = (every, l1, every, 0), (every, every, l0, 1)
            to = (me ^ 4, me ^ 2)
        a, b = (part_of(g, *first), part_of(g, *second)) if g else (part_o(*first), part_o(*second))
        return [remote(a, a, ab, 0, to[0]), remote(b, b, ab, 1, to[1])]

    def gather_event(kind, g):
        if kind == "h":
            start(high_copies(g))
        elif kind == "a":
            wait(high_copies(g))
            start(low_copies(g, 0))
        else:
            wait(low_copies(g, 0))
            start(low_copies(g, 1))

    def gather_events(name):
        for kind, g in GATHER.get(name, ()):
            gather_event(kind, g)

    def gather_end(g):
        wait(low_copies(g, 1))

    load_x.wait()
    start(cube_phase(0, 0))
    p_all[chip, core] = pieces[cube]
    lines_all[chip, core] = line_at[...]
    w_i[z1, high % 2, l1, l0, core] = w_loc[spot]
    load_o.wait()
    load_u.wait()
    swap_tok.wait()
    start(cube_phase(1, 0))
    start(piece_copies)
    start(line_copies)
    wait(trade_in)
    gather_events("t0")
    wait(cube_phase(0, 0))
    start(cube_phase(0, 1))
    wait(cube_phase(1, 0))
    start(cube_phase(1, 1))
    gather_events("t1")
    wait(piece_copies)
    wait(line_copies)
    swap_p = remote(p_all.at[:, core], p_all.at[:, core], sems("swap"), 2, partner)
    swap_p.start()
    swap_l = remote(lines_all.at[:, core], lines_all.at[:, core], sems("swap"), 10, partner)
    swap_l.start()
    wait(cube_phase(0, 1))
    start(cube_phase(0, 2))
    wait(cube_phase(1, 1))
    start(cube_phase(1, 2))
    gather_events("t2")
    swap_p.wait()
    swap_l.wait()

    param, b_in = s["param"], s["b_in"]
    tail = lines_all[...].reshape(n * 16, PAIR)
    at_row = lax.broadcasted_iota(jnp.int32, (n, n * 16), 1) - 16 * lax.broadcasted_iota(jnp.int32, (n, n * 16), 0)
    lines = [dot((at_row == i).astype(BF16), tail).astype(BF16) for i in range(3)]
    lane = lax.broadcasted_iota(jnp.int32, (PAIR, width), 1)
    column = lax.broadcasted_iota(jnp.int32, (PAIR, width), 0)
    owner = lax.broadcasted_iota(jnp.int32, (n, width), 1) // wr == lax.broadcasted_iota(jnp.int32, (n, width), 0)

    def selector(i):
        return (column == i % 4 * wr + lane % wr).astype(BF16)

    for i in range(8):
        spread = dot(lines[i // 4], selector(i))
        param[i : i + 1, :] = jnp.sum(jnp.where(owner, spread, 0.0), axis=0, keepdims=True)
    quarter_pick = (
        device_of(lax.broadcasted_iota(jnp.int32, (quads, n), 0), spot)
        == lax.broadcasted_iota(jnp.int32, (quads, n), 1)
    )
    mine = dot(quarter_pick.astype(BF16), lines[2])
    for i in range(quads):
        b_in[0:1, i * fr : (i + 1) * fr] = mine[i : i + 1, :]
    wait(cube_phase(0, 2))
    wait(cube_phase(1, 2))

    q, k, v, o, low, lse = (s[name] for name in ("q", "k", "v", "o", "low", "lse"))
    tile = own
    pair_at = pl.ds(pl.multiple_of(cube * PAIR, PAIR), PAIR)
    bq, bv = param[0:1, pair_at], param[1:2, pair_at]
    length = jnp.where(core == 0, lengths[0], lengths[1])

    def w_qkv():
        return p_all[...].reshape(width, 3 * PAIR)

    def project(i, _):
        at = pl.ds(pl.multiple_of(i * tile, tile), tile)
        y = dot(x_all[i // 4, i // 2 % 2, i % 2], w_qkv())
        q[at, :] = ((y[:, :PAIR] + bq) * HEAD_DIM ** (-0.5)).astype(BF16)
        k[at, :] = y[:, PAIR : 2 * PAIR].astype(BF16)
        v[at, :] = (y[:, 2 * PAIR :] + bv).astype(BF16)
        return 0

    lax.fori_loop(0, CUBE, project, 0)
    gather_events("p")

    attn = s["attn"]
    low_dst = attn.at[core, :, pair_at]

    def row_copy(m):
        at = pl.ds(pl.multiple_of((rank ^ m) * rows, rows), rows)
        return remote(low.at[at], low_dst, sems("torow"), m, me ^ m)

    def attend_step(step, _):
        i = cube ^ step
        at = pl.ds(pl.multiple_of(i * tile, tile), tile)
        outs_, logs = [], []
        for h in range(2):
            c = slice(h * HEAD_DIM, (h + 1) * HEAD_DIM)
            sc = dot(q[at, c], k[:, c], 1, 1)
            place = lax.broadcasted_iota(jnp.int32, sc.shape, 1)
            sc = jnp.where(place < length, sc, -1e30)
            top = jnp.max(sc, axis=1, keepdims=True)
            e = jnp.exp(sc - top)
            total = jnp.sum(e, axis=1, keepdims=True)
            outs_.append(dot(e.astype(BF16), v[:, c]) / total)
            logs.append(jnp.broadcast_to(top + jnp.log(total), (tile, HEAD_DIM)))
        mixed = jnp.concatenate(outs_, axis=1)
        o[at, :] = mixed
        low[at, :] = mixed.astype(BF16)
        lse[at, :] = jnp.concatenate(logs, axis=1)

        @pl.when(step > 0)
        def _():
            row_copy(2 * step).start()

        row_copy(2 * step + 1).start()
        for at_step in range(CUBE):
            if at_step in GATHER:

                @pl.when(step == at_step)
                def _():
                    gather_events(at_step)

        return 0

    lax.fori_loop(0, CUBE, attend_step, 0)
    attn[core, :, pair_at] = low[pl.ds(pl.multiple_of(rank * rows, rows), rows), :]
    gather_end(0)
    swap_o = remote(w_o.at[:, :, :, core], w_o.at[:, :, :, core], sems("swap"), 3, partner)
    swap_o.start()
    gather_events("r")
    wait([row_copy(m) for m in range(1, BLOCK_DEVS)])
    swap_o.wait()

    x1, n1, r1, x1_low, slope, act = (s[name] for name in ("x1", "n1", "r1", "x1_low", "slope", "act"))
    part, got, df2 = (s[name] for name in ("part", "got", "df2"))
    p2, p3, got2, got3 = (s[name] for name in ("p2", "p3", "got2", "got3"))
    sums = s["sums"]

    def whole_o():
        return w_o[...].reshape(width, width)

    for m in range(2):
        part[0, m * rows : (m + 1) * rows, :] = dot(attn[m], whole_o())
    def trade_rows(buf, m):
        at = pl.ds(m * rows, rows)
        return remote(buf.at[0, at], buf.at[2, at], sems("rowx"), m, me ^ FAR)

    def pass_rows(buf, m):
        at = pl.ds(m * rows, rows)
        return remote(buf.at[2, at], buf.at[3, at], sems("rowp"), m, partner)

    def swap_rows(buf, m):
        at = pl.ds(m * rows, rows)
        return remote(buf.at[0, at], buf.at[1, at], sems("rows"), m, partner)

    load_t.wait()
    for m in range(2):
        at = slice(m * rows, (m + 1) * rows)
        nn, rs = norm_forward(tok[m].astype(F32) + part[0, at, :] + param[2:3, :])
        n1[at, :] = nn
        r1[at, :] = jnp.broadcast_to(rs, (rows, 128))
        y = nn * param[4:5, :] + param[5:6, :]
        x1[at, :] = y
        x1_low[0, at, :] = y.astype(BF16)
        trade_rows(x1_low, m).start()
        swap_rows(x1_low, m).start()
    gather_events("x")

    def hidden_units(a, j):
        cols = slice(j * chunk, (j + 1) * chunk)
        lines_ = slice(a * own, (a + 2) * own)
        w_ = w_i[:, :, :, :, :, :, cols].reshape(width, chunk)
        slope[j, lines_, :] = dot(x1_low[a : a + 2].reshape(2 * own, width), w_) + b_in[0:1, cols]

        def gelu_step(i, _):
            at = pl.ds(pl.multiple_of(a * own + i * 64, 64), 64)
            u = slope[j, at, :]
            phi = 0.5 + 0.5 * lax.erf(u * 0.7071067811865476)
            slope[j, at, :] = phi + u * (0.3989422804014327 * jnp.exp(-0.5 * u * u))
            act[at, cols] = (u * phi).astype(BF16)
            return 0

        lax.fori_loop(0, 2 * own // 64, gelu_step, 0)

    def pass_on(buf, m):
        trade_rows(buf, m).wait()
        pass_rows(buf, m).start()

    wait([swap_rows(x1_low, m) for m in range(2)])
    for j in range(2):
        gather_end(1 + j)
        hidden_units(0, j)
        pass_on(x1_low, j)
    gather_events("i")
    wait([pass_rows(x1_low, m) for m in range(2)])
    for j in range(2):
        hidden_units(2, j)
    gather_events("j")

    def near_copy(i):
        at = pl.ds(i * COLS, COLS)
        return remote(part.at[1, :, at], got.at[:, at], sems("near"), i, partner)

    def side_copy(i):
        at = pl.ds(i * COLS, COLS)
        return remote(p3.at[:, at], got3.at[:, at], sems("side"), i, partner)

    def far_copy(i):
        at = pl.ds(i * COLS, COLS)
        return remote(p2.at[:, at], got2.at[:, at], sems("far"), i, me ^ FAR)

    outs = width // COLS

    def partial_sums(terms):
        def send_far(i):
            cols = slice(i * COLS, (i + 1) * COLS)
            side_copy(i).wait()
            p2[:, cols] = (part[0, :, cols] + got3[:, cols].astype(F32)).astype(BF16)
            far_copy(i).start()

        for i in range(outs):
            cols = slice(i * COLS, (i + 1) * COLS)
            y = terms(2, i)
            part[0, :, cols] = y[:own]
            p3[:, cols] = y[own:].astype(BF16)
            side_copy(i).start()
            if i:
                send_far(i - 1)
        send_far(outs - 1)
        for i in range(outs):
            cols = slice(i * COLS, (i + 1) * COLS)
            y = terms(0, i)
            part[0, :, cols] = y[:own]
            part[1, :, cols] = y[own:]
            near_copy(i).start()

    def partial_end():
        wait([near_copy(i) for i in range(outs)])
        wait([far_copy(i) for i in range(outs)])

    def forward_terms(a, i):
        if a == 2 and i % 2 == 0:
            gather_end(3 + i // 2)
        w_ = w_u[:, :, :, :, i * COLS : (i + 1) * COLS].reshape(quarter, COLS)
        return dot(act[a * own : (a + 2) * own, :], w_)

    partial_sums(forward_terms)
    partial_end()

    for i in range(8):
        sums[i : i + 1, :] = jnp.zeros((1, width), F32)
    load_c.wait()
    for m in range(2):
        at = slice(m * rows, (m + 1) * rows)
        nn, rs = norm_forward(x1[at, :] + part[0, at, :] + got[at, :] + got2[at, :].astype(F32) + param[3:4, :])
        out[m] = (nn * param[6:7, :] + param[7:8, :]).astype(BF16)
        place = rank * rows + lax.broadcasted_iota(jnp.int32, (rows, 1), 0)
        dy = jnp.where(place < lengths[m], cot[m].astype(F32), 0.0)
        sums[6:7, :] += total_rows(dy * nn)
        sums[7:8, :] += total_rows(dy)
        d = norm_back(dy, nn, rs, param[6:7, :])
        x1[at, :] = d
        d_low = d.astype(BF16)
        df2[0, at, :] = d_low
        trade_rows(df2, m).start()
        swap_rows(df2, m).start()
        sums[3:4, :] += total_rows(d_low.astype(F32))
    stores = [load(out, out_h, 9)]

    fin = s["fin"]

    def unit(r, h_, a_, b_, t):
        return part_of(r + 1, h_, a_, b_, t) if r < 4 else part_o(h_, a_, b_, t)

    def buf(name, r):
        if r == 4:
            return s[name + "o"]
        return s[name + "i"].at[r] if r < 2 else s[name + "u"].at[r - 2]

    def reduce_copies(r, phase):
        name = ("ra", "rb", "rc")[phase]
        sem = (s[name + "_s"].at[r], s[name + "_r"].at[r])
        if phase == 2:
            if r < 4:
                return [remote(unit(r, 1 - z1, l1, l0, None), buf(name, r), sem, 0, me ^ 16)]
            return [
                remote(part_o(high ^ m, l1, l0, None), s["rco"].at[m - 1], sem, m, me ^ (8 * m))
                for m in range(1, highs)
            ]
        if phase == 0:
            regions = (every, 1 - l1, every, 0), (every, every, 1 - l0, 1)
            to = (me ^ 4, me ^ 2)
        else:
            regions = (every, l1, 1 - l0, 0), (every, 1 - l1, l0, 1)
            to = (me ^ 2, me ^ 4)
        return [remote(unit(r, *regions[t]), buf(name, r).at[t], sem, t, to[t]) for t in range(2)]

    def add_all(target, term):
        target[...] = target[...] + term[...]

    def reduce_add(r, phase):
        for h in range(2 if r < 4 else highs):
            if phase == 0:
                for b_ in range(2):
                    at = (h, every, b_) if r < 2 else (h, b_)
                    add_all(unit(r, h, l1, b_, 0), buf("ra", r).at[(0,) + at])
                    add_all(unit(r, h, b_, l0, 1), buf("ra", r).at[(1,) + at])
            else:
                for t in range(2):
                    add_all(unit(r, h, l1, l0, t), buf("rb", r).at[t, h])

    def reduce_last(r):
        if r == 4:
            total = part_o(high, l1, l0, None)[...].astype(F32)
            for m in range(1, highs):
                total = total + s["rco"][m - 1].astype(F32)
            gwo[...] = total
            return
        total = unit(r, z1, l1, l0, None)[...].astype(F32) + buf("rc", r)[...].astype(F32)
        if r < 2:
            fin[:, :, r * chunk : (r + 1) * chunk] = total.astype(BF16).reshape(QUAD, wr, chunk)
            start(fin_copies(r))
        else:
            gwout[:, (r - 2) * HALF : (r - 1) * HALF] = total

    def fin_copies(r):
        at = pl.ds(r * chunk, chunk)
        return [
            remote(fin.at[spot ^ m, :, at], s["fin_got"].at[m, :, at], (s["fin_s"].at[r], s["fin_r"].at[r]), m, me ^ mate(m))
            for m in range(1, QUAD)
        ]

    def reduce_events(name):
        for phase, r in REDUCE.get(name, ()):
            if phase > 0:
                wait(reduce_copies(r, phase - 1))
            if 0 < phase < 3:
                reduce_add(r, phase - 1)
            if phase == 3:
                reduce_last(r)
            else:
                start(reduce_copies(r, phase))

    du, gbin = s["du"], s["gbin"]

    def hidden_back(a, j):
        lines_ = slice(a * own, (a + 2) * own)
        cols = slice(j * chunk, (j + 1) * chunk)
        w_ = w_u[j].reshape(chunk, width)
        da = dot(df2[a : a + 2].reshape(2 * own, width), w_, 1, 1)
        du[lines_, cols] = (da * slope[j, lines_, :]).astype(BF16)

    wait([swap_rows(df2, m) for m in range(2)])
    for j in range(2):
        hidden_back(0, j)
        pass_on(df2, j)
    wait([pass_rows(df2, m) for m in range(2)])
    for j in range(2):
        hidden_back(2, j)

    def back_terms(a, i):
        return dot(du[a * own : (a + 2) * own, :], w_i[i // 2, i % 2].reshape(COLS, quarter), 1, 1)

    partial_sums(back_terms)
    x1_rows, df2_rows = x1_low[...].reshape(4 * own, width), df2[...].reshape(4 * own, width)
    for j in range(2):
        cols = slice(j * chunk, (j + 1) * chunk)
        w_i[:, :, :, :, :, :, cols] = dot(x1_rows, du[:, cols], 0, 0).astype(BF16).reshape(2, 2, 2, 2, 2, wr, chunk)
        reduce_events(f"w{j}")
    for j in range(2):
        cols = slice(j * HALF, (j + 1) * HALF)
        w_u[:, :, :, :, cols] = dot(act[...], df2_rows[:, cols], 0, 0).astype(BF16).reshape(2, 2, 2, fr, HALF)
        reduce_events(f"w{j + 2}")
    gbin[0:1, :] = total_rows(du[...].astype(F32))
    partial_end()

    dattn, dmid = s["dattn"], s["dmid"]
    for m in range(2):
        at = slice(m * rows, (m + 1) * rows)
        e = x1[at, :] + part[0, at, :] + got[at, :] + got2[at, :].astype(F32)
        nn, rs = n1[at, :], r1[at, 0:1]
        sums[4:5, :] += total_rows(e * nn)
        sums[5:6, :] += total_rows(e)
        d = norm_back(e, nn, rs, param[4:5, :])
        x1[at, :] = d
        d_low = d.astype(BF16)
        dmid[at, :] = d_low
        sums[2:3, :] += total_rows(d_low.astype(F32))
    for m in range(2):
        dattn[m] = dot(dmid[m * rows : (m + 1) * rows, :], whole_o(), 1, 1).astype(BF16)
    do = s["do"]

    def head_piece(m):
        at = pl.ds(pl.multiple_of((cube ^ (m // 2)) * PAIR, PAIR), PAIR)
        return dattn.at[core ^ (m % 2), :, at]

    def head_copy(m):
        return remote(head_piece(m), do.at[rank], sems("tohead"), m, me ^ m)

    start([head_copy(m) for m in range(1, BLOCK_DEVS)])
    do[rank] = dattn[core, :, pair_at]
    g_o = dot(attn[0], dmid[0:rows, :], 0, 0) + dot(attn[1], dmid[rows:own, :], 0, 0)
    w_o[...] = g_o.astype(BF16).reshape(highs, 2, 2, 2, wr, width)
    swap_g = remote(w_o.at[:, :, :, 1 - core], s["o_got"], sems("swap"), 7, partner)
    swap_g.start()
    reduce_events("x")
    swap_g.wait()
    for h in range(highs):
        w_o[h, :, :, core] = (w_o[h, :, :, core].astype(F32) + s["o_got"][h].astype(F32)).astype(BF16)
    wait([head_copy(m) for m in range(1, BLOCK_DEVS)])

    acc, g = slope, s["g"]
    acc[...] = jnp.zeros_like(acc)
    scale = HEAD_DIM ** (-0.5)
    block = acc.shape[1]

    def back_step(i, _):
        at = pl.ds(pl.multiple_of(i * tile, tile), tile)
        outs_ = []
        d2 = do[pl.ds(2 * i, 2)].reshape(tile, PAIR)
        for h in range(2):
            c = slice(h * HEAD_DIM, (h + 1) * HEAD_DIM)
            d = d2[:, c]
            inner = jnp.sum(d.astype(F32) * o[at, c], axis=1, keepdims=True)
            norm = lse[at, h * HEAD_DIM : h * HEAD_DIM + 1]
            dq = None
            for b in range(acc.shape[0]):
                keys = slice(b * block, (b + 1) * block)
                sc = dot(q[at, c], k[keys, c], 1, 1)
                place = b * block + lax.broadcasted_iota(jnp.int32, sc.shape, 1)
                p = jnp.where(place < length, jnp.exp(sc - norm), 0.0)
                dp = dot(d, v[keys, c], 1, 1)
                ds = (p * (dp - inner)).astype(BF16)
                term = dot(ds, k[keys, c])
                dq = term if dq is None else dq + term
                acc[b, :, h * HEAD_DIM : (h + 1) * HEAD_DIM] += dot(ds, q[at, c], 0, 0)
                acc[b, :, PAIR + h * HEAD_DIM : PAIR + (h + 1) * HEAD_DIM] += dot(p.astype(BF16), d, 0, 0)
            outs_.append(dq)
        g[at, 0:PAIR] = (jnp.concatenate(outs_, axis=1).astype(BF16).astype(F32) * scale).astype(BF16)
        for at_step in range(CUBE):
            if at_step in REDUCE:

                @pl.when(i == at_step)
                def _():
                    reduce_events(at_step)

        return 0

    lax.fori_loop(0, CUBE, back_step, 0)
    for b in range(acc.shape[0]):
        lines_ = slice(b * block, (b + 1) * block)
        g[lines_, PAIR : 3 * PAIR] = acc[b, :, 0 : 2 * PAIR].astype(BF16)

    pg, pgot, pslot = s["pg"], s["pgot"], s["pslot"]
    step_width = width // highs

    def weight_step(i, _):
        cols = pl.ds(pl.multiple_of(i * step_width, step_width), step_width)
        block_ = dot(x_all[:, :, :, :, cols].reshape(CUBE * own, step_width), g[...], 0, 0).astype(BF16)
        pg[pl.ds(i * 4, 4)] = block_.reshape(4, 2, wr, 3 * PAIR)
        return 0

    lax.fori_loop(0, highs, weight_step, 0)
    swap_g = remote(pg.at[:, 1 - core], pgot, sems("swap"), 8, partner)
    swap_g.start()

    def spread_rows(i, _):
        at = pl.ds(pl.multiple_of(i * tile, tile), tile)
        x_all[i // 4, i // 2 % 2, i % 2] = dot(g[at, :], w_qkv(), 1, 1).astype(BF16)
        return 0

    lax.fori_loop(0, CUBE, spread_rows, 0)

    def region(t, i, phase, far):
        order = SUM_ORDERS[i]
        index = [slice(None)] * 3
        for done in order[:phase]:
            index[done] = bits[done]
        axis = order[phase]
        index[axis] = 1 - bits[axis] if far else bits[axis]
        return tuple(index) + (rows_of(t, i),)

    def row_sums(t, phase):
        sem = (s["xr_s"].at[t, phase], s["xr_r"].at[t, phase])
        return [
            remote(x_all.at[region(t, i, phase, True)], s[f"x{t}{phase}{i}"], sem, i, me ^ masks[order[phase]])
            for i, order in enumerate(SUM_ORDERS)
        ]

    def row_fold(t, phase):
        for i in range(3):
            at = region(t, i, phase, False)
            x_all[at] = x_all[at] + s[f"x{t}{phase}{i}"][...]

    start(row_sums(1, 0))
    start(row_sums(0, 0))

    db = total_rows(g[...].astype(F32))
    sums[0:1, pair_at] = db[:, 0:PAIR]
    sums[1:2, pair_at] = db[:, 2 * PAIR :]
    sent = []
    for a_ in range(2):
        line_sum = jnp.zeros((n, PAIR), F32)
        for i in range(4 * a_, 4 * a_ + 4):
            placed = jnp.where(owner, sums[i : i + 1, :], 0.0).astype(BF16)
            line_sum = line_sum + dot(placed, selector(i), 1, 1)
        sent.append(line_sum.astype(BF16))
    hidden = jnp.concatenate([gbin[0:1, i * fr : (i + 1) * fr] for i in range(quads)], axis=0)
    back_pick = (
        device_of(lax.broadcasted_iota(jnp.int32, (n, quads), 1), spot)
        == lax.broadcasted_iota(jnp.int32, (n, quads), 0)
    )
    sent.append(dot(back_pick.astype(BF16), hidden.astype(BF16)).astype(BF16))
    at_line = lax.broadcasted_iota(jnp.int32, (n * 16, n), 0) - 16 * lax.broadcasted_iota(jnp.int32, (n * 16, n), 1)
    wide = jnp.zeros((n * 16, PAIR), F32)
    for a_ in range(3):
        wide = wide + dot((at_line == a_).astype(BF16), sent[a_])
    lines_all[...] = wide.astype(BF16).reshape(chips, 2, 16, PAIR)
    swap_l = remote(lines_all.at[:, 1 - core], s["line_got"], sems("swap"), 11, partner)
    swap_l.start()
    swap_g.wait()
    for i in range(chips):
        pg[i, core] = (pg[i, core].astype(F32) + pgot[i].astype(F32)).astype(BF16)
    piece_sums = [
        remote(pg.at[chip ^ m, core], pslot.at[m], sems("psum"), m, me ^ (2 * m)) for m in range(1, chips)
    ]
    start(piece_sums)
    swap_l.wait()
    for i in range(chips):
        lines_all[i, core] = (lines_all[i, core].astype(F32) + s["line_got"][i].astype(F32)).astype(BF16)
    line_sums = [
        remote(lines_all.at[chip ^ m, core], s["line_slot"].at[m], sems("lsum"), m, me ^ (2 * m))
        for m in range(1, chips)
    ]
    start(line_sums)

    theirs_at = pl.ds(pl.multiple_of((1 - core) * rows, rows), rows)
    last = remote(x_all.at[bits[0], bits[1], bits[2], theirs_at], gtok.at[core], sems("swap"), 9, partner)
    for phase in range(3):
        for t in (1, 0):
            wait(row_sums(t, phase))
            row_fold(t, phase)
            if phase < 2:
                start(row_sums(t, phase + 1))
            elif t == 1:
                last.start()
            reduce_events(f"d{phase}{t}")
    gtok[core] = (x1[own_rows, :] + x_all[bits[0], bits[1], bits[2], own_rows].astype(F32)).astype(BF16)
    reduce_events("e")
    wait(piece_sums)
    for m in range(chips):
        term = pg[chip, core].astype(F32) if m == 0 else pslot[m].astype(F32)
        at = pl.ds(pl.multiple_of((cube ^ (m % CUBE)) * PAIR, PAIR), PAIR)
        for i in range(3):
            value = term[:, i * PAIR : (i + 1) * PAIR]
            if m < CUBE:
                gqkv[i, :, at] = value
            else:
                gqkv[i, :, at] += value
    wait(line_sums)
    line_total = lines_all[chip, core].astype(F32)
    for m in range(1, chips):
        line_total = line_total + s["line_slot"][m].astype(F32)
    gline[...] = jnp.concatenate([line_total[i : i + 1, :] for i in range(3)], axis=1)
    for r in range(2):
        wait(fin_copies(r))
    for i in range(quads):
        at = slice(i * fr, (i + 1) * fr)
        for m in range(QUAD):
            value = fin[spot, :, at] if m == 0 else s["fin_got"][m, :, at]
            gwin[:, pl.ds(pl.multiple_of(device_of(i, spot ^ m) * fr, fr), fr)] = value.astype(F32)
    stores += [load(gqkv.at[i], ref, 10 + i) for i, ref in enumerate((gq_h, gk_h, gv_h))]
    stores += [load(gwo, gwo_h, 13), load(gwin, gwin_h, 14), load(gwout, gwout_h, 15), load(gline, gline_h, 16)]
    last.wait()
    gtok[1 - core] = (x1[theirs_at, :] + gtok[1 - core].astype(F32)).astype(BF16)
    stores.append(load(gtok, gtok_h, 17))
    wait(stores)


ROW_ORDERS = ((0, 1, 2), (1, 2, 0), (2, 0, 1))
SUM_ORDERS = tuple(order[::-1] for order in ROW_ORDERS)
SPANS = (((0, 48), (48, 48), (96, 32)), ((0, 48), (48, 32), (80, 48)))
GATHER = {
    "t0": (("h", 0),),
    "t1": (("h", 1), ("h", 2)),
    "t2": (("a", 0), ("h", 3), ("h", 4)),
    "p": (("b", 0), ("a", 1), ("a", 2)),
    2: (("b", 1), ("a", 3)),
    5: (("b", 2), ("a", 4)),
    "r": (("b", 3),),
    "x": (("b", 4),),
}
REDUCE = {
    "w0": ((0, 0),),
    0: ((1, 0), (0, 1)),
    1: ((0, 2),),
    2: ((1, 1), (2, 0)),
    3: ((1, 2), (0, 3), (2, 1)),
    4: ((0, 4), (3, 0)),
    5: ((1, 3), (2, 2), (3, 1)),
    6: ((1, 4),),
    7: ((2, 3), (3, 2), (2, 4)),
    "d01": ((3, 3),),
    "d00": ((3, 4),),
}


def layer(n, seq_len, slot, tok, cot, wq, wk, wv, wo, w_in, w_out, line):
    _, rows, width = tok.shape
    wr, fr = wo.shape[0], w_out.shape[0]
    chips, highs = n // 2, n // 8
    own, total = 2 * rows, BLOCK_DEVS * rows
    quads = n // QUAD
    quarter = fr * quads
    chunk = quarter // 2
    outs = width // COLS
    groups = 5
    vm = pltpu.VMEM
    dma = pltpu.SemaphoreType.DMA
    shapes = {
        "x_all": vm((2, 2, 2, own, width), BF16),
        "p_all": vm((chips, 2, wr, 3 * PAIR), BF16),
        "w_o": vm((highs, 2, 2, 2, wr, width), BF16),
        "w_i": vm((2, 2, 2, 2, 2, wr, quarter), BF16),
        "w_u": vm((2, 2, 2, fr, width), BF16),
        "pieces": vm((CUBE, wr, 3 * PAIR), BF16),
        "w_loc": vm((QUAD, wr, quarter), BF16),
        "param": vm((8, width), F32),
        "b_in": vm((8, quarter), F32),
        "gbin": vm((8, quarter), F32),
        "sums": vm((8, width), F32),
        "q": vm((total, PAIR), BF16),
        "k": vm((total, PAIR), BF16),
        "v": vm((total, PAIR), BF16),
        "o": vm((total, PAIR), F32),
        "low": vm((total, PAIR), BF16),
        "lse": vm((total, PAIR), F32),
        "attn": vm((2, rows, width), BF16),
        "x1": vm((own, width), F32),
        "n1": vm((own, width), F32),
        "r1": vm((own, 128), F32),
        "x1_low": vm((4, own, width), BF16),
        "slope": vm((2, 4 * own, chunk), F32),
        "act": vm((4 * own, quarter), BF16),
        "part": vm((2, own, width), F32),
        "got": vm((own, width), F32),
        "df2": vm((4, own, width), BF16),
        "du": vm((4 * own, quarter), BF16),
        "dattn": vm((2, rows, width), BF16),
        "do": vm((BLOCK_DEVS, rows, PAIR), BF16),
        "g": vm((total, 3 * PAIR), BF16),
        "o_got": vm((highs, 2, 2, wr, width), BF16),
        "p2": vm((own, width), BF16),
        "p3": vm((own, width), BF16),
        "got2": vm((own, width), BF16),
        "got3": vm((own, width), BF16),
        "dmid": vm((own, width), BF16),
        "rai": vm((2, 2, 2, 2, 2, wr, chunk), BF16),
        "rau": vm((2, 2, 2, 2, fr // 2, HALF), BF16),
        "rbi": vm((2, 2, 2, 2, wr, chunk), BF16),
        "rbu": vm((2, 2, 2, fr // 2, HALF), BF16),
        "rci": vm((2, 2, 2, wr, chunk), BF16),
        "rcu": vm((2, fr, HALF), BF16),
        "rao": vm((2, highs, 2, wr, HALF), BF16),
        "rbo": vm((2, highs, wr, HALF), BF16),
        "rco": vm((highs - 1, wr, width), BF16),
        "line": vm((16, PAIR), BF16),
        "lines": vm((chips, 2, 16, PAIR), BF16),
        "line_got": vm((chips, 16, PAIR), BF16),
        "line_slot": vm((chips, 16, PAIR), BF16),
        "tok": vm((2, rows, width), BF16),
        "cot": vm((2, rows, width), BF16),
        "out": vm((2, rows, width), BF16),
        "gtok": vm((2, rows, width), BF16),
        "wqkv": vm((3, wr, width), BF16),
        "w_in": vm((wr, fr * n), BF16),
        "gqkv": vm((3, wr, width), F32),
        "gwo": vm((wr, width), F32),
        "gwin": vm((wr, fr * n), F32),
        "gwout": vm((fr, width), F32),
        "gline": vm((1, 3 * PAIR), F32),
        "fin": vm((QUAD, wr, quarter), BF16),
        "fin_got": vm((QUAD, wr, quarter), BF16),
        "pg": vm((chips, 2, wr, 3 * PAIR), BF16),
        "pgot": vm((chips, wr, 3 * PAIR), BF16),
        "pslot": vm((chips, wr, 3 * PAIR), BF16),
    }
    for t in range(2):
        for phase, lead in enumerate(((2, 2), (2,), ())):
            for i in range(3):
                shapes[f"x{t}{phase}{i}"] = vm(lead + (SPANS[t][i][1], width), BF16)
    counts = {
        "swap": (12,), "piece": (chips,), "line": (chips,), "lsum": (chips,), "cube": (2, 3, 3), "hi": (groups, highs), "ab": (groups, 2, 2),
        "torow": (BLOCK_DEVS,), "trade": (QUAD,), "rowx": (2,), "rowp": (2,), "rows": (2,), "near": (outs,), "side": (outs,),
        "far": (outs,), "tohead": (BLOCK_DEVS,), "ra": (groups, highs), "rb": (groups, highs),
        "rc": (groups, highs), "fin": (2, QUAD), "xr": (2, 3, 3), "psum": (chips,),
    }
    for name, count in counts.items():
        shapes[name + "_s"] = dma(count)
        shapes[name + "_r"] = dma(count)
    shapes["load"] = dma((18,))
    s = jax.ShapeDtypeStruct
    return pl.pallas_call(
        functools.partial(layer_kernel, n, tuple(shapes)),
        name="layer",
        out_shape=(
            s((2, rows, width), BF16),
            s((2, rows, width), BF16),
            s((wr, width), F32),
            s((wr, width), F32),
            s((wr, width), F32),
            s((wr, width), F32),
            s((wr, fr * n), F32),
            s((fr, width), F32),
            s((1, 3 * PAIR), F32),
        ),
        in_specs=[SMEM, SMEM] + [ANY] * 8 + [VMEM],
        out_specs=(ANY,) * 9,
        scratch_shapes=list(shapes.values()),
        compiler_params=pltpu.CompilerParams(collective_id=6, has_side_effects=True, vmem_limit_bytes=64 << 20),
    )(seq_len, slot, tok, cot, wq, wk, wv, wo, w_in, w_out, line)


def finish_kernel(wr, *refs):
    big, lines, outs, small = refs[:8], refs[8], refs[9:17], refs[17:26]
    held, sem = refs[26:34], refs[34]
    ins = [pltpu.make_async_copy(a, b, sem.at[0, i]) for i, (a, b) in enumerate(zip(big, held))]
    start(ins)
    copies = [pltpu.make_async_copy(a, b, sem.at[1, i]) for i, (a, b) in enumerate(zip(held, outs))]
    for i, ref in enumerate(small):
        ref[...] = lines[0, i * wr : i * wr + ref.shape[0]]
    for one, other in zip(ins, copies):
        one.wait()
        other.start()
    wait(copies)


def finish(wr, fr, *values):
    s = jax.ShapeDtypeStruct
    return pl.pallas_call(
        functools.partial(finish_kernel, wr),
        name="finish",
        out_shape=tuple(s(value.shape, value.dtype) for value in values[:8])
        + (s((wr,), F32),) * 8
        + (s((fr,), F32),),
        in_specs=[ANY] * 8 + [VMEM],
        out_specs=(ANY,) * 8 + (VMEM,) * 9,
        scratch_shapes=[pltpu.VMEM(value.shape, value.dtype) for value in values[:8]]
        + [pltpu.SemaphoreType.DMA((2, 8))],
    )(*values)


def on_device(
    n, tokens, cotangent, seq_lengths, slot_block, w_query, w_key, w_value, w_output, w_in, w_out,
    b_query, b_value, b_output, b_in, b_out, ln1_gain, ln1_bias, ln2_gain, ln2_bias,
):
    _, rows, width = tokens.shape
    wr = w_query.shape[0]
    fr = w_out.shape[0]
    ff = fr // wr
    chips = n // 2
    highs = n // 8
    device = lax.axis_index("fsdp")
    core, chip = device % 2, device // 2
    cube = chip % CUBE
    vectors = (b_query, b_value, b_output, b_out, ln1_gain, ln1_bias, ln2_gain, ln2_bias, b_in)
    if wr % 16 == 0 and 8 * wr + fr == 3 * PAIR and fr == PAIR and n == 32:
        total = 3 * PAIR
        line = sum(
            jnp.pad(value.astype(F32)[None], ((0, 0), (i * wr, total - i * wr - value.shape[0])))
            for i, value in enumerate(vectors)
        )
        values = layer(
            n, seq_lengths, slot_block, tokens, cotangent, w_query, w_key, w_value, w_output, w_in, w_out, line
        )
        results = finish(wr, fr, *values)
        bq, bv, bo, bout, gain1, shift1, gain2, shift2, bin_ = results[8:]
        return results[:8] + (bq, bv, bo, bin_, bout, gain1, shift1, gain2, shift2)
    line = jnp.concatenate(vectors)
    lengths = jnp.sum(jnp.where(slot_block == device // BLOCK_DEVS, seq_lengths, 0), axis=1).astype(jnp.int32)
    live = lax.dynamic_slice(lengths, (core,), (1,))
    pad = -(-(wr + 1) // 16) * 16
    cols = jnp.stack([w_query, w_key, w_value]).reshape(3, wr, CUBE, PAIR).transpose(2, 1, 0, 3)
    cols = cols.reshape(CUBE, wr, 3 * PAIR)
    line = jnp.pad(line, (0, 3 * PAIR - line.shape[0]))
    tail = jnp.pad(line[None], ((0, pad - wr - 1), (0, 0)))
    pieces = jnp.concatenate([cols, jnp.broadcast_to(tail, (CUBE,) + tail.shape)], axis=1)
    in_loc = w_in.reshape(wr, chips, 2, ff, wr).transpose(2, 3, 0, 1, 4).reshape(2, ff, wr, HALF)
    w_loc = jnp.concatenate([w_output, w_out]).reshape(ff + 1, wr, 2, HALF).transpose(0, 2, 1, 3)
    x_all, p_all, w_all = gather(n, tokens, pieces, w_loc, in_loc)
    x = x_all.reshape(BLOCK_DEVS * rows, width)
    w_qkv = p_all[:, :, :wr].reshape(width, 3 * PAIR)
    lines = p_all[:, :, wr].reshape(n, 3 * PAIR)
    small = lines[:, : 8 * wr].reshape(n, 8, wr).transpose(1, 0, 2).reshape(8, width)
    bias_in = lax.dynamic_index_in_dim(lines.reshape(chips, 2, 3 * PAIR), core, 1, keepdims=False)
    bias_in = bias_in[:, 8 * wr : 8 * wr + fr].reshape(chips, ff, wr).transpose(1, 0, 2).reshape(ff, HALF)
    bias_qv = lax.dynamic_slice(small, (0, cube * PAIR), (2, PAIR)).astype(F32)
    q, k, v, o, low, lse = attend(live, x, w_qkv, bias_qv[0:1], bias_qv[1:2])
    attn = exchange(to_rows_kernel, n, low.reshape(BLOCK_DEVS, rows, PAIR), (2, rows, width), "to_rows", 1)
    out, dh, dattn, g_in, g_out, g_o, g_small, g_bin = rows_call(
        n, lengths, attn, tokens, cotangent, w_all, small, bias_in
    )
    do = exchange(to_heads_kernel, n, dattn, (BLOCK_DEVS, rows, PAIR), "to_heads", 2).reshape(-1, PAIR)
    dx, dw, db = attend_back(live, q, k, v, o, lse, do, x, w_qkv)
    unit = (wr, HALF)
    g = jnp.concatenate(
        [
            g_in.reshape((ff, highs, 2, 2, 2) + unit),
            g_out.reshape((ff, 2, highs, 2, 2) + unit).transpose(0, 2, 3, 4, 1, 5, 6),
        ]
    )
    one = g_o.reshape((2, highs, 2, 2, 2) + unit).transpose(4, 1, 2, 3, 0, 5, 6)
    r_w, r_in = scatter_w(n, g, one)
    wide = jnp.zeros((2, width), F32)
    wide = lax.dynamic_update_slice(wide, jnp.stack([db[0, :PAIR], db[0, 2 * PAIR :]]), (0, cube * PAIR))
    lines = (g_small + jnp.pad(wide, ((0, 6), (0, 0)))).reshape(8, n, wr).transpose(1, 0, 2).reshape(n, 8 * wr)
    hidden = g_bin.reshape(ff, chips, wr).transpose(1, 0, 2).reshape(chips, 1, fr)
    hidden = jnp.where(jnp.arange(2)[None, :, None] == core, hidden, 0.0).reshape(n, fr)
    lines = jnp.concatenate([lines, hidden], axis=1)
    lines = jnp.pad(lines, ((0, 0), (0, 3 * PAIR - lines.shape[1])))[:, None]
    parts = jnp.concatenate([dw.reshape(n, wr, 3 * PAIR), lines, jnp.zeros((n, pad - wr - 1, 3 * PAIR), F32)], axis=1)
    parts = parts.astype(BF16).reshape(chips, 2, pad, 3 * PAIR)
    gtok, red = scatter_x(n, dx.reshape(2, 2, 2, 2 * rows, width), dh, parts)
    red = jnp.stack([lax.dynamic_index_in_dim(red, cube ^ m, 0, keepdims=False) for m in range(CUBE)])
    g_qkv = red[:, :wr].reshape(CUBE, wr, 3, PAIR).transpose(2, 1, 0, 3).reshape(3, wr, width)
    line = jnp.sum(red[:, wr], axis=0)
    g_w_in = r_in.reshape(2, ff, wr, chips, wr).transpose(2, 3, 0, 1, 4).reshape(wr, fr * n)
    flat = r_w.transpose(0, 2, 1, 3).reshape(ff * 2 + 1, wr, width)
    biases = [line[i * wr : (i + 1) * wr] for i in range(8)]
    bq, bv, bo, bout, gain1, shift1, gain2, shift2 = biases
    return (
        out, gtok, g_qkv[0], g_qkv[1], g_qkv[2], flat[0], g_w_in, flat[1 + ff :].reshape(fr, width),
        bq, bv, bo, line[8 * wr : 8 * wr + fr], bout, gain1, shift1, gain2, shift2,
    )


def solution(mesh):
    n = mesh.shape["fsdp"]
    rows, vector, whole = P(None, "fsdp", None), P("fsdp"), P()
    matrix = P("fsdp", None)
    return jax.shard_map(
        functools.partial(on_device, n),
        mesh=mesh,
        in_specs=(rows, rows, whole, whole) + (matrix,) * 6 + (vector,) * 9,
        out_specs=(rows, rows) + (matrix,) * 6 + (vector,) * 9,
        check_vma=False,
    )
```

```python
import functools

import jax
import jax.numpy as jnp
from jax import lax
from jax.experimental import pallas as pl
from jax.experimental.pallas import tpu as pltpu
from jax.sharding import PartitionSpec as P

HEAD_DIM = 64
BLOCK_DEVS = 16
CUBE = BLOCK_DEVS // 2
PAIR = 2 * HEAD_DIM
HALF = 512
MESH = pl.DeviceIdType.MESH
VMEM = pl.BlockSpec(memory_space=pltpu.VMEM)
SMEM = pl.BlockSpec(memory_space=pltpu.SMEM)
ANY = pl.BlockSpec(memory_space=pl.ANY)
F32 = jnp.float32
BF16 = jnp.bfloat16


def dot(a, b, ca=1, cb=0):
    return lax.dot_general(a, b, (((ca,), (cb,)), ((), ())), preferred_element_type=F32)


def send(src, dst, send_sem, recv_sem, device):
    copy = pltpu.make_async_remote_copy(
        src_ref=src,
        dst_ref=dst,
        send_sem=send_sem,
        recv_sem=recv_sem,
        device_id=(device,),
        device_id_type=MESH,
    )
    copy.start()
    return copy


def greet(devices):
    barrier = pltpu.get_barrier_semaphore()
    for device in devices:
        pl.semaphore_signal(barrier, inc=1, device_id=(device,), device_id_type=MESH)
    pl.semaphore_wait(barrier, len(devices))


def where_am_i(n):
    me = lax.axis_index("fsdp")
    chip = me // 2
    return dict(
        me=me,
        core=me % 2,
        chip=chip,
        cube=chip % CUBE,
        rank=me % BLOCK_DEVS,
        high=chip // 4,
        l1=chip // 2 % 2,
        l0=chip % 2,
        n=n,
        chips=n // 2,
        highs=n // 8,
    )


CUBE_ORDERS = ((0, 1, 2), (1, 2, 0), (2, 0, 1))


def cube_rows(total):
    first = total // 3 // 16 * 16
    last = total - 2 * first
    return ((0, last), (last, first), (last + first, first))


def gather_kernel(n, tok, pieces, w_loc, in_loc, x_all, p_all, w_all,
                  tok_s, tok_r, cube_s, cube_r, pc_s, pc_r, sw_s, sw_r, loc_s, wi_s, wi_r,
                  hi_s, hi_r, ab_s, ab_r):
    w = where_am_i(n)
    me, core, chip, high, l1, l0 = w["me"], w["core"], w["chip"], w["high"], w["l1"], w["l0"]
    rows = tok.shape[1]
    partner = me ^ 1
    others = [me ^ (2 * m) for m in range(1, w["chips"])]
    greet([partner] + others)
    bits = (w["cube"] // 4, w["cube"] // 2 % 2, w["cube"] % 2)

    def mine(s=slice(None)):
        return x_all.at[bits[0], bits[1], bits[2], s]

    own_rows = pl.ds(pl.multiple_of(core * rows, rows), rows)
    locals_ = []
    locals_.append(pltpu.make_async_copy(tok.at[core], mine(own_rows), loc_s.at[0]))
    locals_[-1].start()
    swap = send(tok.at[1 - core], mine(own_rows), tok_s, tok_r, partner)
    items = w_all.shape[0]
    ff = (items - 1) // 2
    here = lambda item, s: w_all.at[item, high, l1, l0, s]
    swap_in = send(in_loc.at[1 - core], w_all.at[pl.ds(1, ff), high, l1, l0, core], wi_s, wi_r, partner)
    locals_.append(pltpu.make_async_copy(in_loc.at[core], w_all.at[pl.ds(1, ff), high, l1, l0, core], loc_s.at[1]))
    locals_[-1].start()
    locals_.append(pltpu.make_async_copy(w_loc.at[pl.ds(0, 1)], w_all.at[pl.ds(0, 1), high, l1, l0], loc_s.at[2]))
    locals_[-1].start()
    locals_.append(pltpu.make_async_copy(w_loc.at[pl.ds(1, ff)], w_all.at[pl.ds(1 + ff, ff), high, l1, l0], loc_s.at[3]))
    locals_[-1].start()
    locals_.append(pltpu.make_async_copy(pieces.at[w["cube"]], p_all.at[chip, core], loc_s.at[4]))
    locals_[-1].start()
    piece_copies = []
    for m in range(1, w["chips"]):
        there = (chip ^ m) % CUBE
        piece_copies.append(send(pieces.at[there], p_all.at[chip, core], pc_s.at[m], pc_r.at[m], others[m - 1]))
    for copy in locals_:
        copy.wait()
    swap.wait()
    spans = cube_rows(2 * rows)
    masks = (8, 4, 2)
    live = []
    for phase in range(3):
        for copy in live:
            copy.wait()
        live = []
        for s, order in enumerate(CUBE_ORDERS):
            index = [bits[0], bits[1], bits[2]]
            for done in order[:phase]:
                index[done] = slice(None)
            region = x_all.at[index[0], index[1], index[2], pl.ds(*spans[s])]
            live.append(send(region, region, cube_s.at[phase, s], cube_r.at[phase, s], me ^ masks[order[phase]]))
    swap_in.wait()
    for copy in piece_copies:
        copy.wait()
    region = p_all.at[:, core]
    swap_p = send(region, region, sw_s, sw_r, partner)
    for copy in live:
        copy.wait()
    swap_p.wait()
    groups = [(0, 1)] + [(1 + j, None) for j in range(ff)]

    def group(g, *index):
        if g == 0:
            return [w_all.at[(pl.ds(0, 1),) + index]]
        return [w_all.at[(pl.ds(g, 1),) + index], w_all.at[(pl.ds(g + ff, 1),) + index]]

    def high_phase(g):
        out = []
        for m in range(1, w["highs"]):
            for i, region in enumerate(group(g, high, l1, l0)):
                out.append(send(region, region, hi_s.at[g, m, i], hi_r.at[g, m, i], me ^ (8 * m)))
        return out

    def low_phase(g, phase):
        out = []
        for s in range(2):
            if phase == 0:
                index = (slice(None), l1, l0, s)
                to = me ^ (2 if s == 0 else 4)
            elif s == 0:
                index = (slice(None), l1, slice(None), s)
                to = me ^ 4
            else:
                index = (slice(None), slice(None), l0, s)
                to = me ^ 2
            for i, region in enumerate(group(g, *index)):
                out.append(send(region, region, ab_s.at[g, phase, s, i], ab_r.at[g, phase, s, i], to))
        return out

    def settle(copies):
        for copy in copies:
            copy.wait()

    waiting = {}
    count = len(groups)
    for step in range(count + 2):
        if step < count:
            waiting[step, 0] = high_phase(step)
        if 0 <= step - 1 < count:
            settle(waiting.pop((step - 1, 0)))
            waiting[step - 1, 1] = low_phase(step - 1, 0)
        if 0 <= step - 2 < count:
            settle(waiting.pop((step - 2, 1)))
            waiting[step - 2, 2] = low_phase(step - 2, 1)
    for copies in waiting.values():
        settle(copies)


def gather(n, tok, pieces, w_loc, in_loc):
    rows, width = tok.shape[1:]
    wr = in_loc.shape[2]
    ff = in_loc.shape[1]
    items = 1 + 2 * ff
    chips, highs = n // 2, n // 8
    dma = pltpu.SemaphoreType.DMA
    return pl.pallas_call(
        functools.partial(gather_kernel, n),
        name="gather",
        out_shape=(
            jax.ShapeDtypeStruct((2, 2, 2, 2 * rows, width), BF16),
            jax.ShapeDtypeStruct((chips, 2) + pieces.shape[1:], BF16),
            jax.ShapeDtypeStruct((items, highs, 2, 2, 2, wr, HALF), BF16),
        ),
        in_specs=[ANY] * 4,
        out_specs=(ANY, ANY, ANY),
        scratch_shapes=[
            dma, dma, dma((3, 3)), dma((3, 3)), dma((chips,)), dma((chips,)), dma, dma, dma((5,)), dma, dma,
            dma((ff + 1, highs, 2)), dma((ff + 1, highs, 2)), dma((ff + 1, 2, 2, 2)), dma((ff + 1, 2, 2, 2)),
        ],
        compiler_params=pltpu.CompilerParams(collective_id=0, has_side_effects=True),
    )(tok, pieces, w_loc, in_loc)


def attend_kernel(live, x, w, bq, bv, q, k, v, o, low, lse):
    rows = x.shape[0]
    tile = 256

    def project(i, _):
        at = pl.ds(pl.multiple_of(i * tile, tile), tile)
        y = dot(x[at, :], w[...])
        q[at, :] = ((y[:, :PAIR] + bq[...]) * HEAD_DIM ** (-0.5)).astype(BF16)
        k[at, :] = y[:, PAIR : 2 * PAIR].astype(BF16)
        v[at, :] = (y[:, 2 * PAIR :] + bv[...]).astype(BF16)
        return 0

    lax.fori_loop(0, rows // tile, project, 0)
    length = live[0]

    def step(i, _):
        at = pl.ds(pl.multiple_of(i * tile, tile), tile)
        outs, logs = [], []
        for h in range(2):
            c = slice(h * HEAD_DIM, (h + 1) * HEAD_DIM)
            s = dot(q[at, c], k[:, c], 1, 1)
            place = lax.broadcasted_iota(jnp.int32, s.shape, 1)
            s = jnp.where(place < length, s, -1e30)
            top = jnp.max(s, axis=1, keepdims=True)
            e = jnp.exp(s - top)
            total = jnp.sum(e, axis=1, keepdims=True)
            mixed = dot(e.astype(BF16), v[:, c])
            outs.append(mixed / total)
            logs.append(jnp.broadcast_to(top + jnp.log(total), (tile, HEAD_DIM)))
        out = jnp.concatenate(outs, axis=1)
        o[at, :] = out
        low[at, :] = out.astype(BF16)
        lse[at, :] = jnp.concatenate(logs, axis=1)
        return 0

    lax.fori_loop(0, rows // tile, step, 0)


def attend(live, x, w, bq, bv):
    rows = x.shape[0]
    low = jax.ShapeDtypeStruct((rows, PAIR), BF16)
    wide = jax.ShapeDtypeStruct((rows, PAIR), F32)
    return pl.pallas_call(
        attend_kernel,
        name="attend",
        out_shape=(low, low, low, wide, low, wide),
        in_specs=[SMEM, VMEM, VMEM, VMEM, VMEM],
        out_specs=(VMEM,) * 6,
        compiler_params=pltpu.CompilerParams(vmem_limit_bytes=56 << 20),
    )(live, x, w, bq, bv)


def to_rows_kernel(n, low, out, ss, rs, ls):
    w = where_am_i(n)
    me, core, cube, rank = w["me"], w["core"], w["cube"], w["rank"]
    greet([me ^ m for m in range(1, BLOCK_DEVS)])
    there = out.at[core, :, pl.ds(pl.multiple_of(cube * PAIR, PAIR), PAIR)]
    own = pltpu.make_async_copy(low.at[rank], there, ls)
    own.start()
    copies = [send(low.at[rank ^ m], there, ss.at[m], rs.at[m], me ^ m) for m in range(1, BLOCK_DEVS)]
    own.wait()
    for copy in copies:
        copy.wait()


def to_heads_kernel(n, grad, out, ss, rs, ls):
    w = where_am_i(n)
    me, core, cube, rank = w["me"], w["core"], w["cube"], w["rank"]
    greet([me ^ m for m in range(1, BLOCK_DEVS)])

    def piece(m):
        return grad.at[core ^ (m % 2), :, pl.ds(pl.multiple_of((cube ^ (m // 2)) * PAIR, PAIR), PAIR)]

    own = pltpu.make_async_copy(piece(0), out.at[rank], ls)
    own.start()
    copies = [send(piece(m), out.at[rank], ss.at[m], rs.at[m], me ^ m) for m in range(1, BLOCK_DEVS)]
    own.wait()
    for copy in copies:
        copy.wait()


def exchange(kernel, n, value, shape, name, ident):
    dma = pltpu.SemaphoreType.DMA
    return pl.pallas_call(
        functools.partial(kernel, n),
        name=name,
        out_shape=jax.ShapeDtypeStruct(shape, BF16),
        in_specs=[ANY],
        out_specs=ANY,
        scratch_shapes=[dma((BLOCK_DEVS,)), dma((BLOCK_DEVS,)), dma],
        compiler_params=pltpu.CompilerParams(collective_id=ident, has_side_effects=True),
    )(value)


def norm_forward(h):
    center = h - jnp.mean(h, axis=1, keepdims=True)
    rs = lax.rsqrt(jnp.mean(center * center, axis=1, keepdims=True) + 1e-05)
    return center * rs, rs


def norm_back(e, n, rs, gain):
    eg = e * gain
    return (eg - jnp.mean(eg, axis=1, keepdims=True) - n * jnp.mean(eg * n, axis=1, keepdims=True)) * rs


def total_rows(value):
    return jnp.sum(value, axis=0, keepdims=True)


def rows_kernel(n, live, attn, tok, cot, w_all, small, b_in,
                out, dh, dattn, g_in, g_out, g_o, g_small, g_bin,
                w_o, x1, n1, r1, x1_low, slope, act, part, got, df2, got2,
                wo_s, wo_r, x_s, x_r, h_s, h_r, d_s, d_r, e_s, e_r, lo_s):
    w = where_am_i(n)
    me, core, rank = w["me"], w["core"], w["rank"]
    partner = me ^ 1
    greet([partner])
    rows, width = tok.shape[1:]
    own = 2 * rows
    ff = (w_all.shape[0] - 1) // 2
    swap = send(w_all.at[0], w_o.at[:, :, :, core], wo_s, wo_r, partner)
    keep = pltpu.make_async_copy(w_all.at[0], w_o.at[:, :, :, core], lo_s)
    keep.start()
    keep.wait()
    swap.wait()

    def wo(s):
        return w_o[:, :, :, :, s].reshape(width, HALF)

    names = ("bq", "bv", "bo", "bout", "g1", "s1", "g2", "s2")
    param = {name: small[i : i + 1, :].astype(F32) for i, name in enumerate(names)}
    for m in range(2):
        at = slice(m * rows, (m + 1) * rows)
        a = attn[m]
        mid = jnp.concatenate([dot(a, wo(0)), dot(a, wo(1))], axis=1)
        h = tok[m].astype(F32) + mid + param["bo"]
        nn, rs = norm_forward(h)
        n1[at, :] = nn
        r1[at, :] = jnp.broadcast_to(rs, (rows, 128))
        y = nn * param["g1"] + param["s1"]
        x1[at, :] = y
        x1_low[at, :] = y.astype(BF16)
    swap = send(x1_low.at[pl.ds(0, own)], x1_low.at[pl.ds(own, own)], x_s, x_r, partner)
    swap.wait()
    for j in range(ff):
        w_in = w_all[1 + j].reshape(width, HALF)
        u = dot(x1_low[...], w_in) + b_in[j : j + 1, :].astype(F32)
        phi = 0.5 + 0.5 * lax.erf(u * 0.7071067811865476)
        slope[j] = phi + u * (0.3989422804014327 * jnp.exp(-0.5 * u * u))
        a = (u * phi).astype(BF16)
        act[j] = a
        for s in range(2):
            w_out = w_all[1 + ff + j, :, :, :, s].reshape(HALF, HALF)
            c = slice(s * HALF, (s + 1) * HALF)
            if j == 0:
                part[:, c] = dot(a, w_out)
            else:
                part[:, c] += dot(a, w_out)
    swap = send(part.at[pl.ds(own, own)], got, h_s, h_r, partner)
    swap.wait()
    bout = param["bout"]
    sums = {name: jnp.zeros((1, width), F32) for name in ("bo", "bout", "g1", "s1", "g2", "s2")}
    for m in range(2):
        at = slice(m * rows, (m + 1) * rows)
        h = x1[at, :] + part[at, :] + got[at, :] + bout
        nn, rs = norm_forward(h)
        out[m] = (nn * param["g2"] + param["s2"]).astype(BF16)
        place = rank * rows + lax.broadcasted_iota(jnp.int32, (rows, 1), 0)
        dy = jnp.where(place < live[m], cot[m].astype(F32), 0.0)
        sums["g2"] += total_rows(dy * nn)
        sums["s2"] += total_rows(dy)
        d = norm_back(dy, nn, rs, param["g2"])
        x1[at, :] = d
        low = d.astype(BF16)
        df2[at, :] = low
        sums["bout"] += total_rows(low.astype(F32))
    swap = send(df2.at[pl.ds(0, own)], df2.at[pl.ds(own, own)], d_s, d_r, partner)
    swap.wait()
    for j in range(ff):
        w_in = w_all[1 + j].reshape(width, HALF)
        da = None
        for s in range(2):
            w_out = w_all[1 + ff + j, :, :, :, s].reshape(HALF, HALF)
            c = slice(s * HALF, (s + 1) * HALF)
            term = dot(df2[:, c], w_out, 1, 1)
            da = term if da is None else da + term
            g_out[j, s] = dot(act[j], df2[:, c], 0, 0).astype(BF16)
        du = (da * slope[j]).astype(BF16)
        g_bin[j : j + 1, :] = total_rows(du.astype(F32))
        g_in[j] = dot(x1_low[...], du, 0, 0).astype(BF16)
        back = dot(du, w_in, 1, 1)
        if j == 0:
            part[...] = back
        else:
            part[...] += back
    swap = send(part.at[pl.ds(own, own)], got2, e_s, e_r, partner)
    swap.wait()
    for m in range(2):
        at = slice(m * rows, (m + 1) * rows)
        e = x1[at, :] + part[at, :] + got2[at, :]
        nn, rs = n1[at, :], r1[at, 0:1]
        sums["g1"] += total_rows(e * nn)
        sums["s1"] += total_rows(e)
        d = norm_back(e, nn, rs, param["g1"])
        dh[m] = d
        low = d.astype(BF16)
        df2[at, :] = low
        sums["bo"] += total_rows(low.astype(F32))
        dattn[m] = (dot(low[:, :HALF], wo(0), 1, 1) + dot(low[:, HALF:], wo(1), 1, 1)).astype(BF16)
    for s in range(2):
        c = slice(s * HALF, (s + 1) * HALF)
        g_o[s] = sum(dot(attn[m], df2[m * rows : (m + 1) * rows, c], 0, 0) for m in range(2)).astype(BF16)
    g_small[0:2, :] = jnp.zeros((2, width), F32)
    for i, name in enumerate(names[2:]):
        g_small[2 + i : 3 + i, :] = sums[name]


def rows_call(n, live, attn, tok, cot, w_all, small, b_in):
    _, rows, width = tok.shape
    items, highs = w_all.shape[:2]
    wr = w_all.shape[5]
    ff = (items - 1) // 2
    own = 2 * rows
    dma = pltpu.SemaphoreType.DMA
    s = jax.ShapeDtypeStruct
    return pl.pallas_call(
        functools.partial(rows_kernel, n),
        name="rows",
        out_shape=(
            s((2, rows, width), BF16),
            s((2, rows, width), F32),
            s((2, rows, width), BF16),
            s((ff, width, HALF), BF16),
            s((ff, 2, HALF, HALF), BF16),
            s((2, width, HALF), BF16),
            s((8, width), F32),
            s((ff, HALF), F32),
        ),
        in_specs=[SMEM] + [VMEM] * 6,
        out_specs=(VMEM,) * 8,
        scratch_shapes=[
            pltpu.VMEM((highs, 2, 2, 2, 2, wr, HALF), BF16),
            pltpu.VMEM((own, width), F32),
            pltpu.VMEM((own, width), F32),
            pltpu.VMEM((own, 128), F32),
            pltpu.VMEM((2 * own, width), BF16),
            pltpu.VMEM((ff, 2 * own, HALF), F32),
            pltpu.VMEM((ff, 2 * own, HALF), BF16),
            pltpu.VMEM((2 * own, width), F32),
            pltpu.VMEM((own, width), F32),
            pltpu.VMEM((2 * own, width), BF16),
            pltpu.VMEM((own, width), F32),
        ]
        + [dma] * 11,
        compiler_params=pltpu.CompilerParams(collective_id=3, has_side_effects=True, vmem_limit_bytes=60 << 20),
    )(live, attn, tok, cot, w_all, small, b_in)


def attend_back_kernel(live, q, k, v, o, lse, do, x, w, dx, dw, db, g, dk, dv):
    rows = q.shape[0]
    tile = 256
    length = live[0]
    scale = HEAD_DIM ** (-0.5)
    dk[...] = jnp.zeros_like(dk)
    dv[...] = jnp.zeros_like(dv)

    def step(i, _):
        at = pl.ds(pl.multiple_of(i * tile, tile), tile)
        outs = []
        for h in range(2):
            c = slice(h * HEAD_DIM, (h + 1) * HEAD_DIM)
            s = dot(q[at, c], k[:, c], 1, 1)
            place = lax.broadcasted_iota(jnp.int32, s.shape, 1)
            p = jnp.where(place < length, jnp.exp(s - lse[at, h * HEAD_DIM : h * HEAD_DIM + 1]), 0.0)
            d = do[at, c]
            dp = dot(d, v[:, c], 1, 1)
            inner = jnp.sum(d.astype(F32) * o[at, c], axis=1, keepdims=True)
            ds = (p * (dp - inner)).astype(BF16)
            outs.append(dot(ds, k[:, c]))
            dk[h] += dot(ds, q[at, c], 0, 0)
            dv[h] += dot(p.astype(BF16), d, 0, 0)
        g[at, 0:PAIR] = (jnp.concatenate(outs, axis=1).astype(BF16).astype(F32) * scale).astype(BF16)
        return 0

    lax.fori_loop(0, rows // tile, step, 0)
    g[:, PAIR : 2 * PAIR] = jnp.concatenate([dk[0], dk[1]], axis=1).astype(BF16)
    g[:, 2 * PAIR :] = jnp.concatenate([dv[0], dv[1]], axis=1).astype(BF16)

    def spread(i, _):
        at = pl.ds(pl.multiple_of(i * tile, tile), tile)
        dx[at, :] = dot(g[at, :], w[...], 1, 1).astype(BF16)
        return 0

    lax.fori_loop(0, rows // tile, spread, 0)
    dw[...] = dot(x[...], g[...], 0, 0)
    db[...] = jnp.broadcast_to(total_rows(g[...].astype(F32)), db.shape)


def attend_back(live, q, k, v, o, lse, do, x, w):
    rows, width = x.shape
    s = jax.ShapeDtypeStruct
    return pl.pallas_call(
        attend_back_kernel,
        name="attend_back",
        out_shape=(s((rows, width), BF16), s((width, 3 * PAIR), F32), s((8, 3 * PAIR), F32)),
        in_specs=[SMEM] + [VMEM] * 8,
        out_specs=(VMEM,) * 3,
        scratch_shapes=[
            pltpu.VMEM((rows, 3 * PAIR), BF16),
            pltpu.VMEM((2, rows, HEAD_DIM), F32),
            pltpu.VMEM((2, rows, HEAD_DIM), F32),
        ],
        compiler_params=pltpu.CompilerParams(vmem_limit_bytes=60 << 20),
    )(live, q, k, v, o, lse, do, x, w)


def add_into(target, *terms):
    total = target[...].astype(F32)
    for term in terms:
        total = total + term[...].astype(F32)
    target[...] = total.astype(target.dtype)


def scatter_w_kernel(n, g_in, one, out, out_in, g, r1a, r1b, r2, r3,
                     o_s, o_r, a_s, a_r, b_s, b_r, h_s, h_r, i_s, i_r, k_s):
    w = where_am_i(n)
    me, core, high, l1, l0 = w["me"], w["core"], w["high"], w["l1"], w["l0"]
    highs = w["highs"]
    partner = me ^ 1
    greet([partner, me ^ 2, me ^ 4] + [me ^ (8 * m) for m in range(1, highs)])
    items = g.shape[0]
    ff = (items - 1) // 2
    swap = send(one.at[1 - core], g.at[0], o_s, o_r, partner)
    fill = pltpu.make_async_copy(g_in, g.at[pl.ds(1, 2 * ff)], k_s)
    fill.start()
    fill.wait()
    swap.wait()

    def fold(i, _):
        g[0, i] = (g[0, i].astype(F32) + one[core, i].astype(F32)).astype(BF16)
        return 0

    lax.fori_loop(0, highs, fold, 0)
    first = [
        send(g.at[:, :, 1 - l1, :, 0], r1a, a_s.at[0], a_r.at[0], me ^ 4),
        send(g.at[:, :, :, 1 - l0, 1], r1b, a_s.at[1], a_r.at[1], me ^ 2),
    ]
    for copy in first:
        copy.wait()

    def add1(i, _):
        for h in range(highs):
            for b in range(2):
                g[i, h, l1, b, 0] = (g[i, h, l1, b, 0].astype(F32) + r1a[i, h, b].astype(F32)).astype(BF16)
                g[i, h, b, l0, 1] = (g[i, h, b, l0, 1].astype(F32) + r1b[i, h, b].astype(F32)).astype(BF16)
        return 0

    lax.fori_loop(0, items, add1, 0)
    second = [
        send(g.at[:, :, l1, 1 - l0, 0], r2.at[0], b_s.at[0], b_r.at[0], me ^ 2),
        send(g.at[:, :, 1 - l1, l0, 1], r2.at[1], b_s.at[1], b_r.at[1], me ^ 4),
    ]
    for copy in second:
        copy.wait()

    def add2(i, _):
        for h in range(highs):
            for s in range(2):
                g[i, h, l1, l0, s] = (g[i, h, l1, l0, s].astype(F32) + r2[s, i, h].astype(F32)).astype(BF16)
        return 0

    lax.fori_loop(0, items, add2, 0)
    third = [
        send(g.at[:, high ^ m, l1, l0], r3.at[m - 1], h_s.at[m], h_r.at[m], me ^ (8 * m)) for m in range(1, highs)
    ]
    for copy in third:
        copy.wait()

    def add3(i, _):
        for s in range(2):
            total = g[i, high, l1, l0, s].astype(F32)
            for m in range(1, highs):
                total = total + r3[m - 1, i, s].astype(F32)
            out[i, s] = total
        return 0

    lax.fori_loop(0, items, add3, 0)
    keep = pltpu.make_async_copy(out.at[pl.ds(1, ff), core], out_in.at[core], k_s)
    keep.start()
    swap = send(out.at[pl.ds(1, ff), 1 - core], out_in.at[core], i_s, i_r, partner)
    keep.wait()
    swap.wait()


def scatter_w(n, g, one):
    items, highs = g.shape[0] + 1, g.shape[1]
    wr = g.shape[5]
    ff = (items - 1) // 2
    dma = pltpu.SemaphoreType.DMA
    s = jax.ShapeDtypeStruct
    unit = (wr, HALF)
    return pl.pallas_call(
        functools.partial(scatter_w_kernel, n),
        name="scatter_w",
        out_shape=(s((items, 2) + unit, F32), s((2, ff) + unit, F32)),
        in_specs=[ANY, VMEM],
        out_specs=(VMEM, VMEM),
        scratch_shapes=[
            pltpu.VMEM((items, highs, 2, 2, 2) + unit, BF16),
            pltpu.VMEM((items, highs, 2) + unit, BF16),
            pltpu.VMEM((items, highs, 2) + unit, BF16),
            pltpu.VMEM((2, items, highs) + unit, BF16),
            pltpu.VMEM((highs - 1, items, 2) + unit, BF16),
            dma, dma, dma((2,)), dma((2,)), dma((2,)), dma((2,)), dma((highs,)), dma((highs,)), dma, dma, dma,
        ],
        compiler_params=pltpu.CompilerParams(collective_id=4, has_side_effects=True, vmem_limit_bytes=60 << 20),
    )(g, one)


def scatter_x_kernel(n, dx_in, dh, pieces_in, gtok, red, dx, g, psum, pgot, *rest):
    ra, rb, rc = rest[0:3], rest[3:6], rest[6:9]
    mine, theirs, c_s, c_r, t_s, t_r, w_s, w_r, p_s, p_r, k_s = rest[9:]
    w = where_am_i(n)
    me, core, chip = w["me"], w["core"], w["chip"]
    partner = me ^ 1
    chips = w["chips"]
    greet([partner] + [me ^ (2 * m) for m in range(1, chips)])
    rows = dh.shape[1]
    swap_p = send(pieces_in.at[:, 1 - core], pgot, w_s, w_r, partner)
    fills = [
        pltpu.make_async_copy(dx_in, dx, k_s.at[0]),
        pltpu.make_async_copy(pieces_in.at[:, core], psum, k_s.at[1]),
    ]
    for copy in fills:
        copy.start()
    for copy in fills:
        copy.wait()
    bits = (w["cube"] // 4, w["cube"] // 2 % 2, w["cube"] % 2)
    masks = (8, 4, 2)
    spans = cube_rows(2 * rows)

    def region(s, order, phase, far):
        index = [slice(None)] * 3
        for done in order[:phase]:
            index[done] = bits[done]
        axis = order[phase]
        index[axis] = 1 - bits[axis] if far else bits[axis]
        return tuple(index) + (pl.ds(*spans[s]),)

    def launch(phase):
        bufs = (ra, rb, rc)[phase]
        return [
            send(dx.at[region(s, order, phase, True)], bufs[s], c_s.at[phase, s], c_r.at[phase, s], me ^ masks[order[phase]])
            for s, order in enumerate(CUBE_ORDERS)
        ]

    def fold(phase):
        bufs = (ra, rb, rc)[phase]
        for s, order in enumerate(CUBE_ORDERS):
            at = region(s, order, phase, False)
            dx[at] = (dx[at].astype(F32) + bufs[s][...].astype(F32)).astype(BF16)

    live = launch(0)
    swap_p.wait()
    psum[...] = (psum[...].astype(F32) + pgot[...].astype(F32)).astype(BF16)
    copies = [send(psum.at[chip ^ m], g.at[m], p_s.at[m], p_r.at[m], me ^ (2 * m)) for m in range(1, chips)]
    own = pltpu.make_async_copy(psum.at[chip], g.at[0], k_s.at[2])
    own.start()
    for phase in range(3):
        for copy in live:
            copy.wait()
        fold(phase)
        if phase < 2:
            live = launch(phase + 1)
    here = (bits[0], bits[1], bits[2])
    theirs_at = pl.ds(pl.multiple_of((1 - core) * rows, rows), rows)
    own_at = pl.ds(pl.multiple_of(core * rows, rows), rows)
    swap = send(dx.at[here + (theirs_at,)], theirs, t_s, t_r, partner)
    gtok[core] = (dh[core] + dx[here + (own_at,)].astype(F32)).astype(BF16)
    own.wait()
    for copy in copies:
        copy.wait()
    for m in range(chips):
        term = g[m].astype(F32)
        if m < CUBE:
            red[m] = term
        else:
            red[m % CUBE] += term
    swap.wait()
    gtok[1 - core] = (dh[1 - core] + theirs[...].astype(F32)).astype(BF16)


def scatter_x(n, dx, dh, pieces):
    _, rows, width = dh.shape
    chips = n // 2
    unit = pieces.shape[2:]
    dma = pltpu.SemaphoreType.DMA
    s = jax.ShapeDtypeStruct
    spans = cube_rows(2 * rows)
    bufs = [pltpu.VMEM(lead + (spans[i][1], width), BF16) for lead in ((2, 2), (2,), ()) for i in range(3)]
    return pl.pallas_call(
        functools.partial(scatter_x_kernel, n),
        name="scatter_x",
        out_shape=(s((2, rows, width), BF16), s((CUBE,) + unit, F32)),
        in_specs=[ANY, VMEM, ANY],
        out_specs=(VMEM, VMEM),
        scratch_shapes=[
            pltpu.VMEM(dx.shape, BF16),
            pltpu.VMEM((chips,) + unit, BF16),
            pltpu.VMEM((chips,) + unit, BF16),
            pltpu.VMEM((chips,) + unit, BF16),
        ]
        + bufs
        + [
            pltpu.VMEM((rows, width), BF16),
            pltpu.VMEM((rows, width), BF16),
            dma((3, 3)), dma((3, 3)), dma, dma, dma, dma, dma((chips,)), dma((chips,)), dma((3,)),
        ],
        compiler_params=pltpu.CompilerParams(collective_id=5, has_side_effects=True, vmem_limit_bytes=60 << 20),
    )(dx, dh, pieces)


def start(copies):
    for copy in copies:
        copy.start()


def wait(copies):
    for copy in copies:
        copy.wait()


def remote(src, dst, sems, index, device):
    send_sem, recv_sem = sems
    return pltpu.make_async_remote_copy(
        src_ref=src,
        dst_ref=dst,
        send_sem=send_sem.at[index],
        recv_sem=recv_sem.at[index],
        device_id=(device,),
        device_id_type=MESH,
    )


def add_rows(dst, at, src, src_at):
    dst[at] = (dst[at].astype(F32) + src[src_at].astype(F32)).astype(dst.dtype)


COLS = 256
QUAD = 4
FAR = 8


def mate(m):
    return m % 2 + m // 2 * FAR


def device_of(quad, spot):
    return quad // 4 * 16 + spot // 2 * FAR + quad % 4 * 2 + spot % 2


def layer_kernel(n, shapes, seq_len, slot, tok_h, cot_h, wq_h, wk_h, wv_h, wo, w_in_h, w_out, line,
                 out_h, gtok_h, gq_h, gk_h, gv_h, gwo_h, gwin_h, gwout_h, gline_h, *scratch):
    s = dict(zip(shapes, scratch, strict=True))
    here = where_am_i(n)
    me, core, chip, cube, rank = (here[name] for name in ("me", "core", "chip", "cube", "rank"))
    high, l1, l0, chips, highs = (here[name] for name in ("high", "l1", "l0", "chips", "highs"))
    partner = me ^ 1
    tok, cot, out, gtok = (s[name] for name in ("tok", "cot", "out", "gtok"))
    gqkv, gwo, gwin, gwout, gline = (s[name] for name in ("gqkv", "gwo", "gwin", "gwout", "gline"))
    wqkv, w_in = s["wqkv"], s["w_in"]
    _, rows, width = tok.shape
    own = 2 * rows
    wr, fr = wo.shape[0], w_out.shape[0]
    quads = n // QUAD
    quarter = fr * quads
    chunk = quarter // 2
    spot = core + high % 2 * 2
    z1 = high // 2
    bits = (cube // 4, cube // 2 % 2, cube % 2)

    def sems(name):
        return s[name + "_s"], s[name + "_r"]

    own_rows = pl.ds(pl.multiple_of(core * rows, rows), rows)
    x_all, p_all, w_o, w_i, w_u = s["x_all"], s["p_all"], s["w_o"], s["w_i"], s["w_u"]

    def load(src, dst, i):
        copy = pltpu.make_async_copy(src, dst, s["load"].at[i])
        copy.start()
        return copy

    loads = [load(ref, wqkv.at[i], i) for i, ref in enumerate((wq_h, wk_h, wv_h))]
    loads.append(load(w_in_h, w_in, 3))
    load_o = load(wo, w_o.at[high, l1, l0, core], 4)
    load_u = load(w_out, w_u.at[me // 16, l1, l0], 5)
    load_x = load(tok_h.at[core], x_all.at[bits[0], bits[1], bits[2], own_rows], 6)
    load_t = load(tok_h, tok, 7)
    load_c = load(cot_h, cot, 8)

    met = sorted({m for m in range(1, BLOCK_DEVS)} | {2 * m for m in range(1, chips)})
    barrier = pltpu.get_barrier_semaphore()
    for m in met:
        pl.semaphore_signal(barrier, inc=1, device_id=(me ^ m,), device_id_type=MESH)

    lengths = []
    for m in range(2):
        length = jnp.int32(0)
        for i in range(slot.shape[1]):
            length = length + jnp.where(slot[m, i] == me // BLOCK_DEVS, seq_len[m, i], 0)
        lengths.append(length)

    pieces, w_loc, line_at, lines_all = s["pieces"], s["w_loc"], s["line"], s["lines"]
    wait(loads)
    for k in range(CUBE):
        for i in range(3):
            pieces[k, :, i * PAIR : (i + 1) * PAIR] = wqkv[i, :, k * PAIR : (k + 1) * PAIR]
    value = line[...]
    line_at[...] = jnp.concatenate(
        [value[:, i * PAIR : (i + 1) * PAIR] for i in range(3)] + [jnp.zeros((13, PAIR), F32)], axis=0
    ).astype(BF16)
    for i in range(quads):
        for q in range(QUAD):
            at = device_of(i, q) * fr
            w_loc[q, :, i * fr : (i + 1) * fr] = w_in[:, at : at + fr]
    pl.semaphore_wait(barrier, len(met))

    swap_tok = remote(tok_h.at[1 - core], x_all.at[bits[0], bits[1], bits[2], own_rows], sems("swap"), 0, partner)
    swap_tok.start()
    trade_in = [remote(w_loc.at[spot ^ m], w_i.at[z1, high % 2, l1, l0, core], sems("trade"), m, me ^ mate(m)) for m in range(1, QUAD)]
    start(trade_in)
    piece_copies = [
        remote(pieces.at[(chip ^ m) % CUBE], p_all.at[chip, core], sems("piece"), m, me ^ (2 * m))
        for m in range(chips - 1, 0, -1)
    ]
    line_copies = [
        remote(line_at, lines_all.at[chip, core], sems("line"), m, me ^ (2 * m)) for m in range(1, chips)
    ]

    masks = (8, 4, 2)
    set_at = (core * rows, (1 - core) * rows)

    def rows_of(t, i):
        first, count = SPANS[t][i]
        return pl.ds(pl.multiple_of(set_at[t] + first, 16), count)

    def cube_phase(t, phase):
        out_ = []
        for i, order in enumerate(ROW_ORDERS):
            index = list(bits)
            for done in order[:phase]:
                index[done] = slice(None)
            region = x_all.at[index[0], index[1], index[2], rows_of(t, i)]
            sem = (s["cube_s"].at[t, phase], s["cube_r"].at[t, phase])
            out_.append(remote(region, region, sem, i, me ^ masks[order[phase]]))
        return out_

    groups = 5
    every = slice(None)

    def part_o(h_, a_, b_, t):
        return w_o.at[h_, a_, b_, core, :, every if t is None else pl.ds(t * HALF, HALF)]

    def part_of(g, h_, a_, b_, t):
        if g <= 2:
            return w_i.at[h_, :, a_, b_, every if t is None else t, :, pl.ds((g - 1) * chunk, chunk)]
        r_ = every if t is None else pl.ds(t * fr // 2, fr // 2)
        return w_u.at[h_, a_, b_, r_, pl.ds((g - 3) * HALF, HALF)]

    def high_copies(g):
        sem = (s["hi_s"].at[g], s["hi_r"].at[g])
        if g:
            region = part_of(g, z1, l1, l0, None)
            return [remote(region, region, sem, 0, me ^ 16)]
        region = part_o(high, l1, l0, None)
        return [remote(region, region, sem, m, me ^ (8 * m)) for m in range(1, highs)]

    def low_copies(g, phase):
        ab = (s["ab_s"].at[g, phase], s["ab_r"].at[g, phase])
        first, second = (every, l1, l0, 0), (every, l1, l0, 1)
        to = (me ^ 2, me ^ 4)
        if phase == 1:
            first, second = (every, l1, every, 0), (every, every, l0, 1)
            to = (me ^ 4, me ^ 2)
        a, b = (part_of(g, *first), part_of(g, *second)) if g else (part_o(*first), part_o(*second))
        return [remote(a, a, ab, 0, to[0]), remote(b, b, ab, 1, to[1])]

    swap_o = remote(w_o.at[:, :, :, core], w_o.at[:, :, :, core], sems("swap"), 3, partner)

    def gather_event(kind, g):
        if kind == "o":
            gather_end(g)
            swap_o.start()
        elif kind == "h":
            start(high_copies(g))
        elif kind == "a":
            wait(high_copies(g))
            start(low_copies(g, 0))
        else:
            wait(low_copies(g, 0))
            start(low_copies(g, 1))

    def gather_events(name):
        for kind, g in GATHER.get(name, ()):
            gather_event(kind, g)

    def gather_end(g):
        wait(low_copies(g, 1))

    load_x.wait()
    start(cube_phase(0, 0))
    p_all[chip, core] = pieces[cube]
    lines_all[chip, core] = line_at[...]
    w_i[z1, high % 2, l1, l0, core] = w_loc[spot]
    load_o.wait()
    load_u.wait()
    swap_tok.wait()
    start(cube_phase(1, 0))
    start(piece_copies)
    start(line_copies)
    wait(trade_in)
    gather_events("t0")
    wait(cube_phase(0, 0))
    start(cube_phase(0, 1))
    wait(cube_phase(1, 0))
    start(cube_phase(1, 1))
    gather_events("t1")
    wait(cube_phase(0, 1))
    start(cube_phase(0, 2))
    wait(cube_phase(1, 1))
    start(cube_phase(1, 2))
    gather_events("t2")
    wait(piece_copies)
    wait(line_copies)
    swap_p = remote(p_all.at[:, core], p_all.at[:, core], sems("swap"), 2, partner)
    swap_p.start()
    swap_l = remote(lines_all.at[:, core], lines_all.at[:, core], sems("swap"), 10, partner)
    swap_l.start()
    swap_p.wait()
    swap_l.wait()

    param, b_in = s["param"], s["b_in"]
    tail = lines_all[...].reshape(n * 16, PAIR)
    at_row = lax.broadcasted_iota(jnp.int32, (n, n * 16), 1) - 16 * lax.broadcasted_iota(jnp.int32, (n, n * 16), 0)
    lines = [dot((at_row == i).astype(BF16), tail).astype(BF16) for i in range(3)]
    lane = lax.broadcasted_iota(jnp.int32, (PAIR, width), 1)
    column = lax.broadcasted_iota(jnp.int32, (PAIR, width), 0)
    owner = lax.broadcasted_iota(jnp.int32, (n, width), 1) // wr == lax.broadcasted_iota(jnp.int32, (n, width), 0)

    def selector(i):
        return (column == i % 4 * wr + lane % wr).astype(BF16)

    for i in range(8):
        spread = dot(lines[i // 4], selector(i))
        param[i : i + 1, :] = jnp.sum(jnp.where(owner, spread, 0.0), axis=0, keepdims=True)
    quarter_pick = (
        device_of(lax.broadcasted_iota(jnp.int32, (quads, n), 0), spot)
        == lax.broadcasted_iota(jnp.int32, (quads, n), 1)
    )
    mine = dot(quarter_pick.astype(BF16), lines[2])
    for i in range(quads):
        b_in[0:1, i * fr : (i + 1) * fr] = mine[i : i + 1, :]
    wait(cube_phase(0, 2))
    wait(cube_phase(1, 2))

    q, k, v, o, low, lse = (s[name] for name in ("q", "k", "v", "o", "low", "lse"))
    tile = own
    pair_at = pl.ds(pl.multiple_of(cube * PAIR, PAIR), PAIR)
    bq, bv = param[0:1, pair_at], param[1:2, pair_at]
    length = jnp.where(core == 0, lengths[0], lengths[1])

    def w_qkv():
        return p_all[...].reshape(width, 3 * PAIR)

    def project(i, _):
        at = pl.ds(pl.multiple_of(i * tile, tile), tile)
        y = dot(x_all[i // 4, i // 2 % 2, i % 2], w_qkv())
        q[at, :] = ((y[:, :PAIR] + bq) * HEAD_DIM ** (-0.5)).astype(BF16)
        k[at, :] = y[:, PAIR : 2 * PAIR].astype(BF16)
        v[at, :] = (y[:, 2 * PAIR :] + bv).astype(BF16)
        return 0

    lax.fori_loop(0, CUBE, project, 0)
    gather_events("p")

    attn = s["attn"]
    low_dst = attn.at[core, :, pair_at]

    def row_copy(m):
        at = pl.ds(pl.multiple_of((rank ^ m) * rows, rows), rows)
        return remote(low.at[at], low_dst, sems("torow"), m, me ^ m)

    def attend_step(step, _):
        far = CUBE - 1 - step
        i = cube ^ far
        at = pl.ds(pl.multiple_of(i * tile, tile), tile)
        outs_, logs = [], []
        for h in range(2):
            c = slice(h * HEAD_DIM, (h + 1) * HEAD_DIM)
            sc = dot(q[at, c], k[:, c], 1, 1)
            place = lax.broadcasted_iota(jnp.int32, sc.shape, 1)
            sc = jnp.where(place < length, sc, -1e30)
            top = jnp.max(sc, axis=1, keepdims=True)
            e = jnp.exp(sc - top)
            total = jnp.sum(e, axis=1, keepdims=True)
            outs_.append(dot(e.astype(BF16), v[:, c]) / total)
            logs.append(jnp.broadcast_to(top + jnp.log(total), (tile, HEAD_DIM)))
        mixed = jnp.concatenate(outs_, axis=1)
        o[at, :] = mixed
        low[at, :] = mixed.astype(BF16)
        lse[at, :] = jnp.concatenate(logs, axis=1)

        @pl.when(far > 0)
        def _():
            row_copy(2 * far).start()

        row_copy(2 * far + 1).start()
        for at_step in range(CUBE):
            if at_step in GATHER:

                @pl.when(step == at_step)
                def _():
                    gather_events(at_step)

        return 0

    lax.fori_loop(0, CUBE, attend_step, 0)
    attn[core, :, pair_at] = low[pl.ds(pl.multiple_of(rank * rows, rows), rows), :]
    gather_events("r")
    wait([row_copy(m) for m in range(1, BLOCK_DEVS)])
    swap_o.wait()

    x1, n1, r1, x1_low, slope, act = (s[name] for name in ("x1", "n1", "r1", "x1_low", "slope", "act"))
    part, got, df2 = (s[name] for name in ("part", "got", "df2"))
    p2, p3, got2, got3 = (s[name] for name in ("p2", "p3", "got2", "got3"))
    sums = s["sums"]

    def whole_o():
        return w_o[...].reshape(width, width)

    for m in range(2):
        part[0, m * rows : (m + 1) * rows, :] = dot(attn[m], whole_o())
    def trade_rows(buf, m):
        at = pl.ds(m * rows, rows)
        return remote(buf.at[0, at], buf.at[2, at], sems("rowx"), m, me ^ FAR)

    def pass_rows(buf, m):
        at = pl.ds(m * rows, rows)
        return remote(buf.at[2, at], buf.at[3, at], sems("rowp"), m, partner)

    def swap_rows(buf, m):
        at = pl.ds(m * rows, rows)
        return remote(buf.at[0, at], buf.at[1, at], sems("rows"), m, partner)

    load_t.wait()
    for m in range(2):
        at = slice(m * rows, (m + 1) * rows)
        nn, rs = norm_forward(tok[m].astype(F32) + part[0, at, :] + param[2:3, :])
        n1[at, :] = nn
        r1[at, :] = jnp.broadcast_to(rs, (rows, 128))
        y = nn * param[4:5, :] + param[5:6, :]
        x1[at, :] = y
        x1_low[0, at, :] = y.astype(BF16)
        trade_rows(x1_low, m).start()
        swap_rows(x1_low, m).start()
    gather_events("x")

    def hidden_units(a, j):
        cols = slice(j * chunk, (j + 1) * chunk)
        lines_ = slice(a * own, (a + 2) * own)
        w_ = w_i[:, :, :, :, :, :, cols].reshape(width, chunk)
        slope[j, lines_, :] = dot(x1_low[a : a + 2].reshape(2 * own, width), w_) + b_in[0:1, cols]

        def gelu_step(i, _):
            at = pl.ds(pl.multiple_of(a * own + i * 64, 64), 64)
            u = slope[j, at, :]
            phi = 0.5 + 0.5 * lax.erf(u * 0.7071067811865476)
            slope[j, at, :] = phi + u * (0.3989422804014327 * jnp.exp(-0.5 * u * u))
            act[at, cols] = (u * phi).astype(BF16)
            return 0

        lax.fori_loop(0, 2 * own // 64, gelu_step, 0)

    def pass_on(buf, m):
        trade_rows(buf, m).wait()
        pass_rows(buf, m).start()

    wait([swap_rows(x1_low, m) for m in range(2)])
    for j in range(2):
        gather_end(1 + j)
        hidden_units(0, j)
        pass_on(x1_low, j)
    gather_events("i")
    wait([pass_rows(x1_low, m) for m in range(2)])
    for j in range(2):
        hidden_units(2, j)
    gather_events("j")

    def near_copy(i):
        at = pl.ds(i * COLS, COLS)
        return remote(part.at[1, :, at], got.at[:, at], sems("near"), i, partner)

    def side_copy(i):
        at = pl.ds(i * COLS, COLS)
        return remote(p3.at[:, at], got3.at[:, at], sems("side"), i, partner)

    def far_copy(i):
        at = pl.ds(i * COLS, COLS)
        return remote(p2.at[:, at], got2.at[:, at], sems("far"), i, me ^ FAR)

    outs = width // COLS

    def partial_sums(terms):
        def send_far(i):
            cols = slice(i * COLS, (i + 1) * COLS)
            side_copy(i).wait()
            p2[:, cols] = (part[0, :, cols] + got3[:, cols].astype(F32)).astype(BF16)
            far_copy(i).start()

        for i in range(outs):
            cols = slice(i * COLS, (i + 1) * COLS)
            y = terms(2, i)
            part[0, :, cols] = y[:own]
            p3[:, cols] = y[own:].astype(BF16)
            side_copy(i).start()
            if i:
                send_far(i - 1)
        send_far(outs - 1)
        for i in range(outs):
            cols = slice(i * COLS, (i + 1) * COLS)
            y = terms(0, i)
            part[0, :, cols] = y[:own]
            part[1, :, cols] = y[own:]
            near_copy(i).start()

    def partial_end():
        wait([near_copy(i) for i in range(outs)])
        wait([far_copy(i) for i in range(outs)])

    def forward_terms(a, i):
        if a == 2 and i % 2 == 0:
            gather_end(3 + i // 2)
        w_ = w_u[:, :, :, :, i * COLS : (i + 1) * COLS].reshape(quarter, COLS)
        return dot(act[a * own : (a + 2) * own, :], w_)

    partial_sums(forward_terms)
    partial_end()

    for i in range(8):
        sums[i : i + 1, :] = jnp.zeros((1, width), F32)
    load_c.wait()
    for m in range(2):
        at = slice(m * rows, (m + 1) * rows)
        nn, rs = norm_forward(x1[at, :] + part[0, at, :] + got[at, :] + got2[at, :].astype(F32) + param[3:4, :])
        out[m] = (nn * param[6:7, :] + param[7:8, :]).astype(BF16)
        place = rank * rows + lax.broadcasted_iota(jnp.int32, (rows, 1), 0)
        dy = jnp.where(place < lengths[m], cot[m].astype(F32), 0.0)
        sums[6:7, :] += total_rows(dy * nn)
        sums[7:8, :] += total_rows(dy)
        d = norm_back(dy, nn, rs, param[6:7, :])
        x1[at, :] = d
        d_low = d.astype(BF16)
        df2[0, at, :] = d_low
        trade_rows(df2, m).start()
        swap_rows(df2, m).start()
        sums[3:4, :] += total_rows(d_low.astype(F32))
    stores = [load(out, out_h, 9)]

    fin = s["fin"]

    def unit(r, h_, a_, b_, t):
        return part_of(r + 1, h_, a_, b_, t) if r < 4 else part_o(h_, a_, b_, t)

    def buf(name, r):
        if r == 4:
            return s[name + "o"]
        return s[name + "i"].at[r] if r < 2 else s[name + "u"].at[r - 2]

    def reduce_copies(r, phase):
        name = ("ra", "rb", "rc")[phase]
        sem = (s[name + "_s"].at[r], s[name + "_r"].at[r])
        if phase == 2:
            if r < 4:
                return [remote(unit(r, 1 - z1, l1, l0, None), buf(name, r), sem, 0, me ^ 16)]
            return [
                remote(part_o(high ^ m, l1, l0, None), s["rco"].at[m - 1], sem, m, me ^ (8 * m))
                for m in range(1, highs)
            ]
        if phase == 0:
            regions = (every, 1 - l1, every, 0), (every, every, 1 - l0, 1)
            to = (me ^ 4, me ^ 2)
        else:
            regions = (every, l1, 1 - l0, 0), (every, 1 - l1, l0, 1)
            to = (me ^ 2, me ^ 4)
        return [remote(unit(r, *regions[t]), buf(name, r).at[t], sem, t, to[t]) for t in range(2)]

    def add_all(target, term):
        target[...] = target[...] + term[...]

    def reduce_add(r, phase):
        for h in range(2 if r < 4 else highs):
            if phase == 0:
                for b_ in range(2):
                    at = (h, every, b_) if r < 2 else (h, b_)
                    add_all(unit(r, h, l1, b_, 0), buf("ra", r).at[(0,) + at])
                    add_all(unit(r, h, b_, l0, 1), buf("ra", r).at[(1,) + at])
            else:
                for t in range(2):
                    add_all(unit(r, h, l1, l0, t), buf("rb", r).at[t, h])

    def reduce_last(r):
        if r == 4:
            total = part_o(high, l1, l0, None)[...].astype(F32)
            for m in range(1, highs):
                total = total + s["rco"][m - 1].astype(F32)
            gwo[...] = total
            return
        total = unit(r, z1, l1, l0, None)[...].astype(F32) + buf("rc", r)[...].astype(F32)
        if r < 2:
            fin[:, :, r * chunk : (r + 1) * chunk] = total.astype(BF16).reshape(QUAD, wr, chunk)
            start(fin_copies(r))
        else:
            gwout[:, (r - 2) * HALF : (r - 1) * HALF] = total

    def fin_copies(r):
        at = pl.ds(r * chunk, chunk)
        return [
            remote(fin.at[spot ^ m, :, at], s["fin_got"].at[m, :, at], (s["fin_s"].at[r], s["fin_r"].at[r]), m, me ^ mate(m))
            for m in range(1, QUAD)
        ]

    def reduce_events(name):
        for phase, r in REDUCE.get(name, ()):
            if phase > 0:
                wait(reduce_copies(r, phase - 1))
            if 0 < phase < 3:
                reduce_add(r, phase - 1)
            if phase == 3:
                reduce_last(r)
            else:
                start(reduce_copies(r, phase))

    du, gbin = s["du"], s["gbin"]

    def hidden_back(a, j):
        lines_ = slice(a * own, (a + 2) * own)
        cols = slice(j * chunk, (j + 1) * chunk)
        w_ = w_u[j].reshape(chunk, width)
        da = dot(df2[a : a + 2].reshape(2 * own, width), w_, 1, 1)
        du[lines_, cols] = (da * slope[j, lines_, :]).astype(BF16)

    wait([swap_rows(df2, m) for m in range(2)])
    for j in range(2):
        hidden_back(0, j)
        pass_on(df2, j)
    wait([pass_rows(df2, m) for m in range(2)])
    for j in range(2):
        hidden_back(2, j)

    def back_terms(a, i):
        return dot(du[a * own : (a + 2) * own, :], w_i[i // 2, i % 2].reshape(COLS, quarter), 1, 1)

    partial_sums(back_terms)
    x1_rows, df2_rows = x1_low[...].reshape(4 * own, width), df2[...].reshape(4 * own, width)
    for j in range(2):
        cols = slice(j * chunk, (j + 1) * chunk)
        w_i[:, :, :, :, :, :, cols] = dot(x1_rows, du[:, cols], 0, 0).astype(BF16).reshape(2, 2, 2, 2, 2, wr, chunk)
        reduce_events(f"w{j}")
    for j in range(2):
        cols = slice(j * HALF, (j + 1) * HALF)
        w_u[:, :, :, :, cols] = dot(act[...], df2_rows[:, cols], 0, 0).astype(BF16).reshape(2, 2, 2, fr, HALF)
        reduce_events(f"w{j + 2}")
    gbin[0:1, :] = total_rows(du[...].astype(F32))
    partial_end()

    dattn, dmid = s["dattn"], s["dmid"]
    for m in range(2):
        at = slice(m * rows, (m + 1) * rows)
        e = x1[at, :] + part[0, at, :] + got[at, :] + got2[at, :].astype(F32)
        nn, rs = n1[at, :], r1[at, 0:1]
        sums[4:5, :] += total_rows(e * nn)
        sums[5:6, :] += total_rows(e)
        d = norm_back(e, nn, rs, param[4:5, :])
        x1[at, :] = d
        d_low = d.astype(BF16)
        dmid[at, :] = d_low
        sums[2:3, :] += total_rows(d_low.astype(F32))
    for m in range(2):
        dattn[m] = dot(dmid[m * rows : (m + 1) * rows, :], whole_o(), 1, 1).astype(BF16)
    do = s["do"]

    def head_piece(m):
        at = pl.ds(pl.multiple_of((cube ^ (m // 2)) * PAIR, PAIR), PAIR)
        return dattn.at[core ^ (m % 2), :, at]

    def head_copy(m):
        return remote(head_piece(m), do.at[rank], sems("tohead"), m, me ^ m)

    start([head_copy(m) for m in range(BLOCK_DEVS - 1, 0, -1)])
    do[rank] = dattn[core, :, pair_at]
    g_o = dot(attn[0], dmid[0:rows, :], 0, 0) + dot(attn[1], dmid[rows:own, :], 0, 0)
    w_o[...] = g_o.astype(BF16).reshape(highs, 2, 2, 2, wr, width)
    swap_g = remote(w_o.at[:, :, :, 1 - core], s["o_got"], sems("swap"), 7, partner)
    swap_g.start()
    reduce_events("x")
    swap_g.wait()
    for h in range(highs):
        w_o[h, :, :, core] = (w_o[h, :, :, core].astype(F32) + s["o_got"][h].astype(F32)).astype(BF16)

    acc, g = slope, s["g"]
    acc[...] = jnp.zeros_like(acc)
    scale = HEAD_DIM ** (-0.5)
    block = acc.shape[2]

    def back_step(step, _):
        i = cube ^ step

        @pl.when(step > 0)
        def _():
            head_copy(2 * step).wait()

        head_copy(2 * step + 1).wait()
        at = pl.ds(pl.multiple_of(i * tile, tile), tile)
        outs_ = []
        d2 = do[pl.ds(2 * i, 2)].reshape(tile, PAIR)
        for h in range(2):
            c = slice(h * HEAD_DIM, (h + 1) * HEAD_DIM)
            d = d2[:, c]
            inner = jnp.sum(d.astype(F32) * o[at, c], axis=1, keepdims=True)
            norm = lse[at, h * HEAD_DIM : h * HEAD_DIM + 1]
            dq = None
            for b in range(4):
                keys = slice(b * block, (b + 1) * block)
                first = b % 2 * 2 * PAIR + h * HEAD_DIM
                sc = dot(q[at, c], k[keys, c], 1, 1)
                place = b * block + lax.broadcasted_iota(jnp.int32, sc.shape, 1)
                p = jnp.where(place < length, jnp.exp(sc - norm), 0.0)
                dp = dot(d, v[keys, c], 1, 1)
                ds = (p * (dp - inner)).astype(BF16)
                term = dot(ds, k[keys, c])
                dq = term if dq is None else dq + term
                acc[b // 2, first : first + HEAD_DIM, :] += dot(q[at, c], ds, 0, 0)
                acc[b // 2, first + PAIR : first + PAIR + HEAD_DIM, :] += dot(d, p.astype(BF16), 0, 0)
            outs_.append(dq)
        g[at, 0:PAIR] = (jnp.concatenate(outs_, axis=1).astype(BF16).astype(F32) * scale).astype(BF16)
        for at_step in range(CUBE):
            if at_step in REDUCE:

                @pl.when(step == at_step)
                def _():
                    reduce_events(at_step)

        return 0

    lax.fori_loop(0, CUBE, back_step, 0)
    for b in range(4):
        lines_ = slice(b * block, (b + 1) * block)
        first = b % 2 * 2 * PAIR
        g[lines_, PAIR : 3 * PAIR] = acc[b // 2, first : first + 2 * PAIR, :].T.astype(BF16)

    pg, pgot, pslot = s["pg"], s["pgot"], s["pslot"]
    step_width = width // highs

    def weight_step(i, _):
        cols = pl.ds(pl.multiple_of(i * step_width, step_width), step_width)
        block_ = dot(x_all[:, :, :, :, cols].reshape(CUBE * own, step_width), g[...], 0, 0).astype(BF16)
        pg[pl.ds(i * 4, 4)] = block_.reshape(4, 2, wr, 3 * PAIR)
        return 0

    lax.fori_loop(0, highs, weight_step, 0)
    swap_g = remote(pg.at[:, 1 - core], pgot, sems("swap"), 8, partner)
    swap_g.start()

    def spread_rows(i, _):
        at = pl.ds(pl.multiple_of(i * tile, tile), tile)
        x_all[i // 4, i // 2 % 2, i % 2] = dot(g[at, :], w_qkv(), 1, 1).astype(BF16)
        return 0

    lax.fori_loop(0, CUBE, spread_rows, 0)

    def region(t, i, phase, far):
        order = SUM_ORDERS[i]
        index = [slice(None)] * 3
        for done in order[:phase]:
            index[done] = bits[done]
        axis = order[phase]
        index[axis] = 1 - bits[axis] if far else bits[axis]
        return tuple(index) + (rows_of(t, i),)

    def row_sums(t, phase):
        sem = (s["xr_s"].at[t, phase], s["xr_r"].at[t, phase])
        return [
            remote(x_all.at[region(t, i, phase, True)], s[f"x{t}{phase}{i}"], sem, i, me ^ masks[order[phase]])
            for i, order in enumerate(SUM_ORDERS)
        ]

    def row_fold(t, phase):
        for i in range(3):
            at = region(t, i, phase, False)
            x_all[at] = x_all[at] + s[f"x{t}{phase}{i}"][...]

    start(row_sums(1, 0))
    start(row_sums(0, 0))

    db = total_rows(g[...].astype(F32))
    sums[0:1, pair_at] = db[:, 0:PAIR]
    sums[1:2, pair_at] = db[:, 2 * PAIR :]
    sent = []
    for a_ in range(2):
        line_sum = jnp.zeros((n, PAIR), F32)
        for i in range(4 * a_, 4 * a_ + 4):
            placed = jnp.where(owner, sums[i : i + 1, :], 0.0).astype(BF16)
            line_sum = line_sum + dot(placed, selector(i), 1, 1)
        sent.append(line_sum.astype(BF16))
    hidden = jnp.concatenate([gbin[0:1, i * fr : (i + 1) * fr] for i in range(quads)], axis=0)
    back_pick = (
        device_of(lax.broadcasted_iota(jnp.int32, (n, quads), 1), spot)
        == lax.broadcasted_iota(jnp.int32, (n, quads), 0)
    )
    sent.append(dot(back_pick.astype(BF16), hidden.astype(BF16)).astype(BF16))
    at_line = lax.broadcasted_iota(jnp.int32, (n * 16, n), 0) - 16 * lax.broadcasted_iota(jnp.int32, (n * 16, n), 1)
    wide = jnp.zeros((n * 16, PAIR), F32)
    for a_ in range(3):
        wide = wide + dot((at_line == a_).astype(BF16), sent[a_])
    lines_all[...] = wide.astype(BF16).reshape(chips, 2, 16, PAIR)
    swap_l = remote(lines_all.at[:, 1 - core], s["line_got"], sems("swap"), 11, partner)
    swap_l.start()
    swap_g.wait()
    for i in range(chips):
        pg[i, core] = (pg[i, core].astype(F32) + pgot[i].astype(F32)).astype(BF16)
    piece_sums = [
        remote(pg.at[chip ^ m, core], pslot.at[m], sems("psum"), m, me ^ (2 * m)) for m in range(1, chips)
    ]
    start(piece_sums)
    swap_l.wait()
    for i in range(chips):
        lines_all[i, core] = (lines_all[i, core].astype(F32) + s["line_got"][i].astype(F32)).astype(BF16)
    line_sums = [
        remote(lines_all.at[chip ^ m, core], s["line_slot"].at[m], sems("lsum"), m, me ^ (2 * m))
        for m in range(1, chips)
    ]
    start(line_sums)

    theirs_at = pl.ds(pl.multiple_of((1 - core) * rows, rows), rows)
    last = remote(x_all.at[bits[0], bits[1], bits[2], theirs_at], gtok.at[core], sems("swap"), 9, partner)
    for phase in range(3):
        for t in (1, 0):
            wait(row_sums(t, phase))
            row_fold(t, phase)
            if phase < 2:
                start(row_sums(t, phase + 1))
            elif t == 1:
                last.start()
            reduce_events(f"d{phase}{t}")
    gtok[core] = (x1[own_rows, :] + x_all[bits[0], bits[1], bits[2], own_rows].astype(F32)).astype(BF16)
    reduce_events("e")
    wait(piece_sums)
    for m in range(chips):
        term = pg[chip, core].astype(F32) if m == 0 else pslot[m].astype(F32)
        at = pl.ds(pl.multiple_of((cube ^ (m % CUBE)) * PAIR, PAIR), PAIR)
        for i in range(3):
            value = term[:, i * PAIR : (i + 1) * PAIR]
            if m < CUBE:
                gqkv[i, :, at] = value
            else:
                gqkv[i, :, at] += value
    wait(line_sums)
    line_total = lines_all[chip, core].astype(F32)
    for m in range(1, chips):
        line_total = line_total + s["line_slot"][m].astype(F32)
    gline[...] = jnp.concatenate([line_total[i : i + 1, :] for i in range(3)], axis=1)
    for r in range(2):
        wait(fin_copies(r))
    for i in range(quads):
        at = slice(i * fr, (i + 1) * fr)
        for m in range(QUAD):
            value = fin[spot, :, at] if m == 0 else s["fin_got"][m, :, at]
            gwin[:, pl.ds(pl.multiple_of(device_of(i, spot ^ m) * fr, fr), fr)] = value.astype(F32)
    stores += [load(gqkv.at[i], ref, 10 + i) for i, ref in enumerate((gq_h, gk_h, gv_h))]
    stores += [load(gwo, gwo_h, 13), load(gwin, gwin_h, 14), load(gwout, gwout_h, 15), load(gline, gline_h, 16)]
    last.wait()
    gtok[1 - core] = (x1[theirs_at, :] + gtok[1 - core].astype(F32)).astype(BF16)
    stores.append(load(gtok, gtok_h, 17))
    wait(stores)


ROW_ORDERS = ((0, 1, 2), (1, 2, 0), (2, 0, 1))
SUM_ORDERS = tuple(order[::-1] for order in ROW_ORDERS)
SPANS = (((0, 48), (48, 48), (96, 32)), ((0, 48), (48, 32), (80, 48)))
GATHER = {
    "t1": (("h", 0),),
    "t2": (("a", 0), ("h", 1), ("h", 2), ("h", 3), ("h", 4)),
    "p": (("b", 0),),
    2: (("a", 1), ("a", 2)),
    4: (("o", 0), ("b", 1)),
    6: (("b", 2),),
    7: (("a", 3), ("a", 4)),
    "x": (("b", 3),),
    "i": (("b", 4),),
}
REDUCE = {
    "w0": ((0, 0),),
    "w1": ((0, 1),),
    0: ((1, 0), (0, 2)),
    1: ((1, 1), (2, 0)),
    2: ((0, 3), (1, 2)),
    3: ((2, 1), (0, 4)),
    4: ((1, 3), (3, 0)),
    5: ((2, 2), (1, 4)),
    6: ((3, 1), (2, 3)),
    7: ((3, 2), (2, 4)),
    "d01": ((3, 3),),
    "d00": ((3, 4),),
}


def layer(n, seq_len, slot, tok, cot, wq, wk, wv, wo, w_in, w_out, line):
    _, rows, width = tok.shape
    wr, fr = wo.shape[0], w_out.shape[0]
    chips, highs = n // 2, n // 8
    own, total = 2 * rows, BLOCK_DEVS * rows
    quads = n // QUAD
    quarter = fr * quads
    chunk = quarter // 2
    outs = width // COLS
    groups = 5
    vm = pltpu.VMEM
    dma = pltpu.SemaphoreType.DMA
    shapes = {
        "x_all": vm((2, 2, 2, own, width), BF16),
        "p_all": vm((chips, 2, wr, 3 * PAIR), BF16),
        "w_o": vm((highs, 2, 2, 2, wr, width), BF16),
        "w_i": vm((2, 2, 2, 2, 2, wr, quarter), BF16),
        "w_u": vm((2, 2, 2, fr, width), BF16),
        "pieces": vm((CUBE, wr, 3 * PAIR), BF16),
        "w_loc": vm((QUAD, wr, quarter), BF16),
        "param": vm((8, width), F32),
        "b_in": vm((8, quarter), F32),
        "gbin": vm((8, quarter), F32),
        "sums": vm((8, width), F32),
        "q": vm((total, PAIR), BF16),
        "k": vm((total, PAIR), BF16),
        "v": vm((total, PAIR), BF16),
        "o": vm((total, PAIR), F32),
        "low": vm((total, PAIR), BF16),
        "lse": vm((total, PAIR), F32),
        "attn": vm((2, rows, width), BF16),
        "x1": vm((own, width), F32),
        "n1": vm((own, width), F32),
        "r1": vm((own, 128), F32),
        "x1_low": vm((4, own, width), BF16),
        "slope": vm((2, 4 * own, chunk), F32),
        "act": vm((4 * own, quarter), BF16),
        "part": vm((2, own, width), F32),
        "got": vm((own, width), F32),
        "df2": vm((4, own, width), BF16),
        "du": vm((4 * own, quarter), BF16),
        "dattn": vm((2, rows, width), BF16),
        "do": vm((BLOCK_DEVS, rows, PAIR), BF16),
        "g": vm((total, 3 * PAIR), BF16),
        "o_got": vm((highs, 2, 2, wr, width), BF16),
        "p2": vm((own, width), BF16),
        "p3": vm((own, width), BF16),
        "got2": vm((own, width), BF16),
        "got3": vm((own, width), BF16),
        "dmid": vm((own, width), BF16),
        "rai": vm((2, 2, 2, 2, 2, wr, chunk), BF16),
        "rau": vm((2, 2, 2, 2, fr // 2, HALF), BF16),
        "rbi": vm((2, 2, 2, 2, wr, chunk), BF16),
        "rbu": vm((2, 2, 2, fr // 2, HALF), BF16),
        "rci": vm((2, 2, 2, wr, chunk), BF16),
        "rcu": vm((2, fr, HALF), BF16),
        "rao": vm((2, highs, 2, wr, HALF), BF16),
        "rbo": vm((2, highs, wr, HALF), BF16),
        "rco": vm((highs - 1, wr, width), BF16),
        "line": vm((16, PAIR), BF16),
        "lines": vm((chips, 2, 16, PAIR), BF16),
        "line_got": vm((chips, 16, PAIR), BF16),
        "line_slot": vm((chips, 16, PAIR), BF16),
        "tok": vm((2, rows, width), BF16),
        "cot": vm((2, rows, width), BF16),
        "out": vm((2, rows, width), BF16),
        "gtok": vm((2, rows, width), BF16),
        "wqkv": vm((3, wr, width), BF16),
        "w_in": vm((wr, fr * n), BF16),
        "gqkv": vm((3, wr, width), F32),
        "gwo": vm((wr, width), F32),
        "gwin": vm((wr, fr * n), F32),
        "gwout": vm((fr, width), F32),
        "gline": vm((1, 3 * PAIR), F32),
        "fin": vm((QUAD, wr, quarter), BF16),
        "fin_got": vm((QUAD, wr, quarter), BF16),
        "pg": vm((chips, 2, wr, 3 * PAIR), BF16),
        "pgot": vm((chips, wr, 3 * PAIR), BF16),
        "pslot": vm((chips, wr, 3 * PAIR), BF16),
    }
    for t in range(2):
        for phase, lead in enumerate(((2, 2), (2,), ())):
            for i in range(3):
                shapes[f"x{t}{phase}{i}"] = vm(lead + (SPANS[t][i][1], width), BF16)
    counts = {
        "swap": (12,), "piece": (chips,), "line": (chips,), "lsum": (chips,), "cube": (2, 3, 3), "hi": (groups, highs), "ab": (groups, 2, 2),
        "torow": (BLOCK_DEVS,), "trade": (QUAD,), "rowx": (2,), "rowp": (2,), "rows": (2,), "near": (outs,), "side": (outs,),
        "far": (outs,), "tohead": (BLOCK_DEVS,), "ra": (groups, highs), "rb": (groups, highs),
        "rc": (groups, highs), "fin": (2, QUAD), "xr": (2, 3, 3), "psum": (chips,),
    }
    for name, count in counts.items():
        shapes[name + "_s"] = dma(count)
        shapes[name + "_r"] = dma(count)
    shapes["load"] = dma((18,))
    s = jax.ShapeDtypeStruct
    return pl.pallas_call(
        functools.partial(layer_kernel, n, tuple(shapes)),
        name="layer",
        out_shape=(
            s((2, rows, width), BF16),
            s((2, rows, width), BF16),
            s((wr, width), F32),
            s((wr, width), F32),
            s((wr, width), F32),
            s((wr, width), F32),
            s((wr, fr * n), F32),
            s((fr, width), F32),
            s((1, 3 * PAIR), F32),
        ),
        in_specs=[SMEM, SMEM] + [ANY] * 8 + [VMEM],
        out_specs=(ANY,) * 9,
        scratch_shapes=list(shapes.values()),
        compiler_params=pltpu.CompilerParams(collective_id=6, has_side_effects=True, vmem_limit_bytes=64 << 20),
    )(seq_len, slot, tok, cot, wq, wk, wv, wo, w_in, w_out, line)


def finish_kernel(wr, *refs):
    big, lines, outs, small = refs[:8], refs[8], refs[9:17], refs[17:26]
    held, sem = refs[26:34], refs[34]
    ins = [pltpu.make_async_copy(a, b, sem.at[0, i]) for i, (a, b) in enumerate(zip(big, held))]
    start(ins)
    copies = [pltpu.make_async_copy(a, b, sem.at[1, i]) for i, (a, b) in enumerate(zip(held, outs))]
    for i, ref in enumerate(small):
        ref[...] = lines[0, i * wr : i * wr + ref.shape[0]]
    for one, other in zip(ins, copies):
        one.wait()
        other.start()
    wait(copies)


def finish(wr, fr, *values):
    s = jax.ShapeDtypeStruct
    return pl.pallas_call(
        functools.partial(finish_kernel, wr),
        name="finish",
        out_shape=tuple(s(value.shape, value.dtype) for value in values[:8])
        + (s((wr,), F32),) * 8
        + (s((fr,), F32),),
        in_specs=[ANY] * 8 + [VMEM],
        out_specs=(ANY,) * 8 + (VMEM,) * 9,
        scratch_shapes=[pltpu.VMEM(value.shape, value.dtype) for value in values[:8]]
        + [pltpu.SemaphoreType.DMA((2, 8))],
    )(*values)


def on_device(
    n, tokens, cotangent, seq_lengths, slot_block, w_query, w_key, w_value, w_output, w_in, w_out,
    b_query, b_value, b_output, b_in, b_out, ln1_gain, ln1_bias, ln2_gain, ln2_bias,
):
    _, rows, width = tokens.shape
    wr = w_query.shape[0]
    fr = w_out.shape[0]
    ff = fr // wr
    chips = n // 2
    highs = n // 8
    device = lax.axis_index("fsdp")
    core, chip = device % 2, device // 2
    cube = chip % CUBE
    vectors = (b_query, b_value, b_output, b_out, ln1_gain, ln1_bias, ln2_gain, ln2_bias, b_in)
    if wr % 16 == 0 and 8 * wr + fr == 3 * PAIR and fr == PAIR:
        total = 3 * PAIR
        line = sum(
            jnp.pad(value.astype(F32)[None], ((0, 0), (i * wr, total - i * wr - value.shape[0])))
            for i, value in enumerate(vectors)
        )
        values = layer(
            n, seq_lengths, slot_block, tokens, cotangent, w_query, w_key, w_value, w_output, w_in, w_out, line
        )
        results = finish(wr, fr, *values)
        bq, bv, bo, bout, gain1, shift1, gain2, shift2, bin_ = results[8:]
        return results[:8] + (bq, bv, bo, bin_, bout, gain1, shift1, gain2, shift2)
    line = jnp.concatenate(vectors)
    lengths = jnp.sum(jnp.where(slot_block == device // BLOCK_DEVS, seq_lengths, 0), axis=1).astype(jnp.int32)
    live = lax.dynamic_slice(lengths, (core,), (1,))
    pad = -(-(wr + 1) // 16) * 16
    cols = jnp.stack([w_query, w_key, w_value]).reshape(3, wr, CUBE, PAIR).transpose(2, 1, 0, 3)
    cols = cols.reshape(CUBE, wr, 3 * PAIR)
    line = jnp.pad(line, (0, 3 * PAIR - line.shape[0]))
    tail = jnp.pad(line[None], ((0, pad - wr - 1), (0, 0)))
    pieces = jnp.concatenate([cols, jnp.broadcast_to(tail, (CUBE,) + tail.shape)], axis=1)
    in_loc = w_in.reshape(wr, chips, 2, ff, wr).transpose(2, 3, 0, 1, 4).reshape(2, ff, wr, HALF)
    w_loc = jnp.concatenate([w_output, w_out]).reshape(ff + 1, wr, 2, HALF).transpose(0, 2, 1, 3)
    x_all, p_all, w_all = gather(n, tokens, pieces, w_loc, in_loc)
    x = x_all.reshape(BLOCK_DEVS * rows, width)
    w_qkv = p_all[:, :, :wr].reshape(width, 3 * PAIR)
    lines = p_all[:, :, wr].reshape(n, 3 * PAIR)
    small = lines[:, : 8 * wr].reshape(n, 8, wr).transpose(1, 0, 2).reshape(8, width)
    bias_in = lax.dynamic_index_in_dim(lines.reshape(chips, 2, 3 * PAIR), core, 1, keepdims=False)
    bias_in = bias_in[:, 8 * wr : 8 * wr + fr].reshape(chips, ff, wr).transpose(1, 0, 2).reshape(ff, HALF)
    bias_qv = lax.dynamic_slice(small, (0, cube * PAIR), (2, PAIR)).astype(F32)
    q, k, v, o, low, lse = attend(live, x, w_qkv, bias_qv[0:1], bias_qv[1:2])
    attn = exchange(to_rows_kernel, n, low.reshape(BLOCK_DEVS, rows, PAIR), (2, rows, width), "to_rows", 1)
    out, dh, dattn, g_in, g_out, g_o, g_small, g_bin = rows_call(
        n, lengths, attn, tokens, cotangent, w_all, small, bias_in
    )
    do = exchange(to_heads_kernel, n, dattn, (BLOCK_DEVS, rows, PAIR), "to_heads", 2).reshape(-1, PAIR)
    dx, dw, db = attend_back(live, q, k, v, o, lse, do, x, w_qkv)
    unit = (wr, HALF)
    g = jnp.concatenate(
        [
            g_in.reshape((ff, highs, 2, 2, 2) + unit),
            g_out.reshape((ff, 2, highs, 2, 2) + unit).transpose(0, 2, 3, 4, 1, 5, 6),
        ]
    )
    one = g_o.reshape((2, highs, 2, 2, 2) + unit).transpose(4, 1, 2, 3, 0, 5, 6)
    r_w, r_in = scatter_w(n, g, one)
    wide = jnp.zeros((2, width), F32)
    wide = lax.dynamic_update_slice(wide, jnp.stack([db[0, :PAIR], db[0, 2 * PAIR :]]), (0, cube * PAIR))
    lines = (g_small + jnp.pad(wide, ((0, 6), (0, 0)))).reshape(8, n, wr).transpose(1, 0, 2).reshape(n, 8 * wr)
    hidden = g_bin.reshape(ff, chips, wr).transpose(1, 0, 2).reshape(chips, 1, fr)
    hidden = jnp.where(jnp.arange(2)[None, :, None] == core, hidden, 0.0).reshape(n, fr)
    lines = jnp.concatenate([lines, hidden], axis=1)
    lines = jnp.pad(lines, ((0, 0), (0, 3 * PAIR - lines.shape[1])))[:, None]
    parts = jnp.concatenate([dw.reshape(n, wr, 3 * PAIR), lines, jnp.zeros((n, pad - wr - 1, 3 * PAIR), F32)], axis=1)
    parts = parts.astype(BF16).reshape(chips, 2, pad, 3 * PAIR)
    gtok, red = scatter_x(n, dx.reshape(2, 2, 2, 2 * rows, width), dh, parts)
    red = jnp.stack([lax.dynamic_index_in_dim(red, cube ^ m, 0, keepdims=False) for m in range(CUBE)])
    g_qkv = red[:, :wr].reshape(CUBE, wr, 3, PAIR).transpose(2, 1, 0, 3).reshape(3, wr, width)
    line = jnp.sum(red[:, wr], axis=0)
    g_w_in = r_in.reshape(2, ff, wr, chips, wr).transpose(2, 3, 0, 1, 4).reshape(wr, fr * n)
    flat = r_w.transpose(0, 2, 1, 3).reshape(ff * 2 + 1, wr, width)
    biases = [line[i * wr : (i + 1) * wr] for i in range(8)]
    bq, bv, bo, bout, gain1, shift1, gain2, shift2 = biases
    return (
        out, gtok, g_qkv[0], g_qkv[1], g_qkv[2], flat[0], g_w_in, flat[1 + ff :].reshape(fr, width),
        bq, bv, bo, line[8 * wr : 8 * wr + fr], bout, gain1, shift1, gain2, shift2,
    )


def solution(mesh):
    n = mesh.shape["fsdp"]
    rows, vector, whole = P(None, "fsdp", None), P("fsdp"), P()
    matrix = P("fsdp", None)
    return jax.shard_map(
        functools.partial(on_device, n),
        mesh=mesh,
        in_specs=(rows, rows, whole, whole) + (matrix,) * 6 + (vector,) * 9,
        out_specs=(rows, rows) + (matrix,) * 6 + (vector,) * 9,
        check_vma=False,
    )
```

```python
import functools

import jax
import jax.numpy as jnp
from jax import lax
from jax.experimental import pallas as pl
from jax.experimental.pallas import tpu as pltpu
from jax.sharding import PartitionSpec as P

HEAD_DIM = 64
BLOCK_DEVS = 16
CUBE = BLOCK_DEVS // 2
PAIR = 2 * HEAD_DIM
HALF = 512
MESH = pl.DeviceIdType.MESH
VMEM = pl.BlockSpec(memory_space=pltpu.VMEM)
SMEM = pl.BlockSpec(memory_space=pltpu.SMEM)
ANY = pl.BlockSpec(memory_space=pl.ANY)
F32 = jnp.float32
BF16 = jnp.bfloat16


def dot(a, b, ca=1, cb=0):
    return lax.dot_general(a, b, (((ca,), (cb,)), ((), ())), preferred_element_type=F32)


def send(src, dst, send_sem, recv_sem, device):
    copy = pltpu.make_async_remote_copy(
        src_ref=src,
        dst_ref=dst,
        send_sem=send_sem,
        recv_sem=recv_sem,
        device_id=(device,),
        device_id_type=MESH,
    )
    copy.start()
    return copy


def greet(devices):
    barrier = pltpu.get_barrier_semaphore()
    for device in devices:
        pl.semaphore_signal(barrier, inc=1, device_id=(device,), device_id_type=MESH)
    pl.semaphore_wait(barrier, len(devices))


def where_am_i(n):
    me = lax.axis_index("fsdp")
    chip = me // 2
    return dict(
        me=me,
        core=me % 2,
        chip=chip,
        cube=chip % CUBE,
        rank=me % BLOCK_DEVS,
        high=chip // 4,
        l1=chip // 2 % 2,
        l0=chip % 2,
        n=n,
        chips=n // 2,
        highs=n // 8,
    )


CUBE_ORDERS = ((0, 1, 2), (1, 2, 0), (2, 0, 1))


def cube_rows(total):
    first = total // 3 // 16 * 16
    last = total - 2 * first
    return ((0, last), (last, first), (last + first, first))


def gather_kernel(n, tok, pieces, w_loc, in_loc, x_all, p_all, w_all,
                  tok_s, tok_r, cube_s, cube_r, pc_s, pc_r, sw_s, sw_r, loc_s, wi_s, wi_r,
                  hi_s, hi_r, ab_s, ab_r):
    w = where_am_i(n)
    me, core, chip, high, l1, l0 = w["me"], w["core"], w["chip"], w["high"], w["l1"], w["l0"]
    rows = tok.shape[1]
    partner = me ^ 1
    others = [me ^ (2 * m) for m in range(1, w["chips"])]
    greet([partner] + others)
    bits = (w["cube"] // 4, w["cube"] // 2 % 2, w["cube"] % 2)

    def mine(s=slice(None)):
        return x_all.at[bits[0], bits[1], bits[2], s]

    own_rows = pl.ds(pl.multiple_of(core * rows, rows), rows)
    locals_ = []
    locals_.append(pltpu.make_async_copy(tok.at[core], mine(own_rows), loc_s.at[0]))
    locals_[-1].start()
    swap = send(tok.at[1 - core], mine(own_rows), tok_s, tok_r, partner)
    items = w_all.shape[0]
    ff = (items - 1) // 2
    here = lambda item, s: w_all.at[item, high, l1, l0, s]
    swap_in = send(in_loc.at[1 - core], w_all.at[pl.ds(1, ff), high, l1, l0, core], wi_s, wi_r, partner)
    locals_.append(pltpu.make_async_copy(in_loc.at[core], w_all.at[pl.ds(1, ff), high, l1, l0, core], loc_s.at[1]))
    locals_[-1].start()
    locals_.append(pltpu.make_async_copy(w_loc.at[pl.ds(0, 1)], w_all.at[pl.ds(0, 1), high, l1, l0], loc_s.at[2]))
    locals_[-1].start()
    locals_.append(pltpu.make_async_copy(w_loc.at[pl.ds(1, ff)], w_all.at[pl.ds(1 + ff, ff), high, l1, l0], loc_s.at[3]))
    locals_[-1].start()
    locals_.append(pltpu.make_async_copy(pieces.at[w["cube"]], p_all.at[chip, core], loc_s.at[4]))
    locals_[-1].start()
    piece_copies = []
    for m in range(1, w["chips"]):
        there = (chip ^ m) % CUBE
        piece_copies.append(send(pieces.at[there], p_all.at[chip, core], pc_s.at[m], pc_r.at[m], others[m - 1]))
    for copy in locals_:
        copy.wait()
    swap.wait()
    spans = cube_rows(2 * rows)
    masks = (8, 4, 2)
    live = []
    for phase in range(3):
        for copy in live:
            copy.wait()
        live = []
        for s, order in enumerate(CUBE_ORDERS):
            index = [bits[0], bits[1], bits[2]]
            for done in order[:phase]:
                index[done] = slice(None)
            region = x_all.at[index[0], index[1], index[2], pl.ds(*spans[s])]
            live.append(send(region, region, cube_s.at[phase, s], cube_r.at[phase, s], me ^ masks[order[phase]]))
    swap_in.wait()
    for copy in piece_copies:
        copy.wait()
    region = p_all.at[:, core]
    swap_p = send(region, region, sw_s, sw_r, partner)
    for copy in live:
        copy.wait()
    swap_p.wait()
    groups = [(0, 1)] + [(1 + j, None) for j in range(ff)]

    def group(g, *index):
        if g == 0:
            return [w_all.at[(pl.ds(0, 1),) + index]]
        return [w_all.at[(pl.ds(g, 1),) + index], w_all.at[(pl.ds(g + ff, 1),) + index]]

    def high_phase(g):
        out = []
        for m in range(1, w["highs"]):
            for i, region in enumerate(group(g, high, l1, l0)):
                out.append(send(region, region, hi_s.at[g, m, i], hi_r.at[g, m, i], me ^ (8 * m)))
        return out

    def low_phase(g, phase):
        out = []
        for s in range(2):
            if phase == 0:
                index = (slice(None), l1, l0, s)
                to = me ^ (2 if s == 0 else 4)
            elif s == 0:
                index = (slice(None), l1, slice(None), s)
                to = me ^ 4
            else:
                index = (slice(None), slice(None), l0, s)
                to = me ^ 2
            for i, region in enumerate(group(g, *index)):
                out.append(send(region, region, ab_s.at[g, phase, s, i], ab_r.at[g, phase, s, i], to))
        return out

    def settle(copies):
        for copy in copies:
            copy.wait()

    waiting = {}
    count = len(groups)
    for step in range(count + 2):
        if step < count:
            waiting[step, 0] = high_phase(step)
        if 0 <= step - 1 < count:
            settle(waiting.pop((step - 1, 0)))
            waiting[step - 1, 1] = low_phase(step - 1, 0)
        if 0 <= step - 2 < count:
            settle(waiting.pop((step - 2, 1)))
            waiting[step - 2, 2] = low_phase(step - 2, 1)
    for copies in waiting.values():
        settle(copies)


def gather(n, tok, pieces, w_loc, in_loc):
    rows, width = tok.shape[1:]
    wr = in_loc.shape[2]
    ff = in_loc.shape[1]
    items = 1 + 2 * ff
    chips, highs = n // 2, n // 8
    dma = pltpu.SemaphoreType.DMA
    return pl.pallas_call(
        functools.partial(gather_kernel, n),
        name="gather",
        out_shape=(
            jax.ShapeDtypeStruct((2, 2, 2, 2 * rows, width), BF16),
            jax.ShapeDtypeStruct((chips, 2) + pieces.shape[1:], BF16),
            jax.ShapeDtypeStruct((items, highs, 2, 2, 2, wr, HALF), BF16),
        ),
        in_specs=[ANY] * 4,
        out_specs=(ANY, ANY, ANY),
        scratch_shapes=[
            dma, dma, dma((3, 3)), dma((3, 3)), dma((chips,)), dma((chips,)), dma, dma, dma((5,)), dma, dma,
            dma((ff + 1, highs, 2)), dma((ff + 1, highs, 2)), dma((ff + 1, 2, 2, 2)), dma((ff + 1, 2, 2, 2)),
        ],
        compiler_params=pltpu.CompilerParams(collective_id=0, has_side_effects=True),
    )(tok, pieces, w_loc, in_loc)


def attend_kernel(live, x, w, bq, bv, q, k, v, o, low, lse):
    rows = x.shape[0]
    tile = 256

    def project(i, _):
        at = pl.ds(pl.multiple_of(i * tile, tile), tile)
        y = dot(x[at, :], w[...])
        q[at, :] = ((y[:, :PAIR] + bq[...]) * HEAD_DIM ** (-0.5)).astype(BF16)
        k[at, :] = y[:, PAIR : 2 * PAIR].astype(BF16)
        v[at, :] = (y[:, 2 * PAIR :] + bv[...]).astype(BF16)
        return 0

    lax.fori_loop(0, rows // tile, project, 0)
    length = live[0]

    def step(i, _):
        at = pl.ds(pl.multiple_of(i * tile, tile), tile)
        outs, logs = [], []
        for h in range(2):
            c = slice(h * HEAD_DIM, (h + 1) * HEAD_DIM)
            s = dot(q[at, c], k[:, c], 1, 1)
            place = lax.broadcasted_iota(jnp.int32, s.shape, 1)
            s = jnp.where(place < length, s, -1e30)
            top = jnp.max(s, axis=1, keepdims=True)
            e = jnp.exp(s - top)
            total = jnp.sum(e, axis=1, keepdims=True)
            mixed = dot(e.astype(BF16), v[:, c])
            outs.append(mixed / total)
            logs.append(jnp.broadcast_to(top + jnp.log(total), (tile, HEAD_DIM)))
        out = jnp.concatenate(outs, axis=1)
        o[at, :] = out
        low[at, :] = out.astype(BF16)
        lse[at, :] = jnp.concatenate(logs, axis=1)
        return 0

    lax.fori_loop(0, rows // tile, step, 0)


def attend(live, x, w, bq, bv):
    rows = x.shape[0]
    low = jax.ShapeDtypeStruct((rows, PAIR), BF16)
    wide = jax.ShapeDtypeStruct((rows, PAIR), F32)
    return pl.pallas_call(
        attend_kernel,
        name="attend",
        out_shape=(low, low, low, wide, low, wide),
        in_specs=[SMEM, VMEM, VMEM, VMEM, VMEM],
        out_specs=(VMEM,) * 6,
        compiler_params=pltpu.CompilerParams(vmem_limit_bytes=56 << 20),
    )(live, x, w, bq, bv)


def to_rows_kernel(n, low, out, ss, rs, ls):
    w = where_am_i(n)
    me, core, cube, rank = w["me"], w["core"], w["cube"], w["rank"]
    greet([me ^ m for m in range(1, BLOCK_DEVS)])
    there = out.at[core, :, pl.ds(pl.multiple_of(cube * PAIR, PAIR), PAIR)]
    own = pltpu.make_async_copy(low.at[rank], there, ls)
    own.start()
    copies = [send(low.at[rank ^ m], there, ss.at[m], rs.at[m], me ^ m) for m in range(1, BLOCK_DEVS)]
    own.wait()
    for copy in copies:
        copy.wait()


def to_heads_kernel(n, grad, out, ss, rs, ls):
    w = where_am_i(n)
    me, core, cube, rank = w["me"], w["core"], w["cube"], w["rank"]
    greet([me ^ m for m in range(1, BLOCK_DEVS)])

    def piece(m):
        return grad.at[core ^ (m % 2), :, pl.ds(pl.multiple_of((cube ^ (m // 2)) * PAIR, PAIR), PAIR)]

    own = pltpu.make_async_copy(piece(0), out.at[rank], ls)
    own.start()
    copies = [send(piece(m), out.at[rank], ss.at[m], rs.at[m], me ^ m) for m in range(1, BLOCK_DEVS)]
    own.wait()
    for copy in copies:
        copy.wait()


def exchange(kernel, n, value, shape, name, ident):
    dma = pltpu.SemaphoreType.DMA
    return pl.pallas_call(
        functools.partial(kernel, n),
        name=name,
        out_shape=jax.ShapeDtypeStruct(shape, BF16),
        in_specs=[ANY],
        out_specs=ANY,
        scratch_shapes=[dma((BLOCK_DEVS,)), dma((BLOCK_DEVS,)), dma],
        compiler_params=pltpu.CompilerParams(collective_id=ident, has_side_effects=True),
    )(value)


def norm_forward(h):
    center = h - jnp.mean(h, axis=1, keepdims=True)
    rs = lax.rsqrt(jnp.mean(center * center, axis=1, keepdims=True) + 1e-05)
    return center * rs, rs


def norm_back(e, n, rs, gain):
    eg = e * gain
    return (eg - jnp.mean(eg, axis=1, keepdims=True) - n * jnp.mean(eg * n, axis=1, keepdims=True)) * rs


def total_rows(value):
    return jnp.sum(value, axis=0, keepdims=True)


def rows_kernel(n, live, attn, tok, cot, w_all, small, b_in,
                out, dh, dattn, g_in, g_out, g_o, g_small, g_bin,
                w_o, x1, n1, r1, x1_low, slope, act, part, got, df2, got2,
                wo_s, wo_r, x_s, x_r, h_s, h_r, d_s, d_r, e_s, e_r, lo_s):
    w = where_am_i(n)
    me, core, rank = w["me"], w["core"], w["rank"]
    partner = me ^ 1
    greet([partner])
    rows, width = tok.shape[1:]
    own = 2 * rows
    ff = (w_all.shape[0] - 1) // 2
    swap = send(w_all.at[0], w_o.at[:, :, :, core], wo_s, wo_r, partner)
    keep = pltpu.make_async_copy(w_all.at[0], w_o.at[:, :, :, core], lo_s)
    keep.start()
    keep.wait()
    swap.wait()

    def wo(s):
        return w_o[:, :, :, :, s].reshape(width, HALF)

    names = ("bq", "bv", "bo", "bout", "g1", "s1", "g2", "s2")
    param = {name: small[i : i + 1, :].astype(F32) for i, name in enumerate(names)}
    for m in range(2):
        at = slice(m * rows, (m + 1) * rows)
        a = attn[m]
        mid = jnp.concatenate([dot(a, wo(0)), dot(a, wo(1))], axis=1)
        h = tok[m].astype(F32) + mid + param["bo"]
        nn, rs = norm_forward(h)
        n1[at, :] = nn
        r1[at, :] = jnp.broadcast_to(rs, (rows, 128))
        y = nn * param["g1"] + param["s1"]
        x1[at, :] = y
        x1_low[at, :] = y.astype(BF16)
    swap = send(x1_low.at[pl.ds(0, own)], x1_low.at[pl.ds(own, own)], x_s, x_r, partner)
    swap.wait()
    for j in range(ff):
        w_in = w_all[1 + j].reshape(width, HALF)
        u = dot(x1_low[...], w_in) + b_in[j : j + 1, :].astype(F32)
        phi = 0.5 + 0.5 * lax.erf(u * 0.7071067811865476)
        slope[j] = phi + u * (0.3989422804014327 * jnp.exp(-0.5 * u * u))
        a = (u * phi).astype(BF16)
        act[j] = a
        for s in range(2):
            w_out = w_all[1 + ff + j, :, :, :, s].reshape(HALF, HALF)
            c = slice(s * HALF, (s + 1) * HALF)
            if j == 0:
                part[:, c] = dot(a, w_out)
            else:
                part[:, c] += dot(a, w_out)
    swap = send(part.at[pl.ds(own, own)], got, h_s, h_r, partner)
    swap.wait()
    bout = param["bout"]
    sums = {name: jnp.zeros((1, width), F32) for name in ("bo", "bout", "g1", "s1", "g2", "s2")}
    for m in range(2):
        at = slice(m * rows, (m + 1) * rows)
        h = x1[at, :] + part[at, :] + got[at, :] + bout
        nn, rs = norm_forward(h)
        out[m] = (nn * param["g2"] + param["s2"]).astype(BF16)
        place = rank * rows + lax.broadcasted_iota(jnp.int32, (rows, 1), 0)
        dy = jnp.where(place < live[m], cot[m].astype(F32), 0.0)
        sums["g2"] += total_rows(dy * nn)
        sums["s2"] += total_rows(dy)
        d = norm_back(dy, nn, rs, param["g2"])
        x1[at, :] = d
        low = d.astype(BF16)
        df2[at, :] = low
        sums["bout"] += total_rows(low.astype(F32))
    swap = send(df2.at[pl.ds(0, own)], df2.at[pl.ds(own, own)], d_s, d_r, partner)
    swap.wait()
    for j in range(ff):
        w_in = w_all[1 + j].reshape(width, HALF)
        da = None
        for s in range(2):
            w_out = w_all[1 + ff + j, :, :, :, s].reshape(HALF, HALF)
            c = slice(s * HALF, (s + 1) * HALF)
            term = dot(df2[:, c], w_out, 1, 1)
            da = term if da is None else da + term
            g_out[j, s] = dot(act[j], df2[:, c], 0, 0).astype(BF16)
        du = (da * slope[j]).astype(BF16)
        g_bin[j : j + 1, :] = total_rows(du.astype(F32))
        g_in[j] = dot(x1_low[...], du, 0, 0).astype(BF16)
        back = dot(du, w_in, 1, 1)
        if j == 0:
            part[...] = back
        else:
            part[...] += back
    swap = send(part.at[pl.ds(own, own)], got2, e_s, e_r, partner)
    swap.wait()
    for m in range(2):
        at = slice(m * rows, (m + 1) * rows)
        e = x1[at, :] + part[at, :] + got2[at, :]
        nn, rs = n1[at, :], r1[at, 0:1]
        sums["g1"] += total_rows(e * nn)
        sums["s1"] += total_rows(e)
        d = norm_back(e, nn, rs, param["g1"])
        dh[m] = d
        low = d.astype(BF16)
        df2[at, :] = low
        sums["bo"] += total_rows(low.astype(F32))
        dattn[m] = (dot(low[:, :HALF], wo(0), 1, 1) + dot(low[:, HALF:], wo(1), 1, 1)).astype(BF16)
    for s in range(2):
        c = slice(s * HALF, (s + 1) * HALF)
        g_o[s] = sum(dot(attn[m], df2[m * rows : (m + 1) * rows, c], 0, 0) for m in range(2)).astype(BF16)
    g_small[0:2, :] = jnp.zeros((2, width), F32)
    for i, name in enumerate(names[2:]):
        g_small[2 + i : 3 + i, :] = sums[name]


def rows_call(n, live, attn, tok, cot, w_all, small, b_in):
    _, rows, width = tok.shape
    items, highs = w_all.shape[:2]
    wr = w_all.shape[5]
    ff = (items - 1) // 2
    own = 2 * rows
    dma = pltpu.SemaphoreType.DMA
    s = jax.ShapeDtypeStruct
    return pl.pallas_call(
        functools.partial(rows_kernel, n),
        name="rows",
        out_shape=(
            s((2, rows, width), BF16),
            s((2, rows, width), F32),
            s((2, rows, width), BF16),
            s((ff, width, HALF), BF16),
            s((ff, 2, HALF, HALF), BF16),
            s((2, width, HALF), BF16),
            s((8, width), F32),
            s((ff, HALF), F32),
        ),
        in_specs=[SMEM] + [VMEM] * 6,
        out_specs=(VMEM,) * 8,
        scratch_shapes=[
            pltpu.VMEM((highs, 2, 2, 2, 2, wr, HALF), BF16),
            pltpu.VMEM((own, width), F32),
            pltpu.VMEM((own, width), F32),
            pltpu.VMEM((own, 128), F32),
            pltpu.VMEM((2 * own, width), BF16),
            pltpu.VMEM((ff, 2 * own, HALF), F32),
            pltpu.VMEM((ff, 2 * own, HALF), BF16),
            pltpu.VMEM((2 * own, width), F32),
            pltpu.VMEM((own, width), F32),
            pltpu.VMEM((2 * own, width), BF16),
            pltpu.VMEM((own, width), F32),
        ]
        + [dma] * 11,
        compiler_params=pltpu.CompilerParams(collective_id=3, has_side_effects=True, vmem_limit_bytes=60 << 20),
    )(live, attn, tok, cot, w_all, small, b_in)


def attend_back_kernel(live, q, k, v, o, lse, do, x, w, dx, dw, db, g, dk, dv):
    rows = q.shape[0]
    tile = 256
    length = live[0]
    scale = HEAD_DIM ** (-0.5)
    dk[...] = jnp.zeros_like(dk)
    dv[...] = jnp.zeros_like(dv)

    def step(i, _):
        at = pl.ds(pl.multiple_of(i * tile, tile), tile)
        outs = []
        for h in range(2):
            c = slice(h * HEAD_DIM, (h + 1) * HEAD_DIM)
            s = dot(q[at, c], k[:, c], 1, 1)
            place = lax.broadcasted_iota(jnp.int32, s.shape, 1)
            p = jnp.where(place < length, jnp.exp(s - lse[at, h * HEAD_DIM : h * HEAD_DIM + 1]), 0.0)
            d = do[at, c]
            dp = dot(d, v[:, c], 1, 1)
            inner = jnp.sum(d.astype(F32) * o[at, c], axis=1, keepdims=True)
            ds = (p * (dp - inner)).astype(BF16)
            outs.append(dot(ds, k[:, c]))
            dk[h] += dot(ds, q[at, c], 0, 0)
            dv[h] += dot(p.astype(BF16), d, 0, 0)
        g[at, 0:PAIR] = (jnp.concatenate(outs, axis=1).astype(BF16).astype(F32) * scale).astype(BF16)
        return 0

    lax.fori_loop(0, rows // tile, step, 0)
    g[:, PAIR : 2 * PAIR] = jnp.concatenate([dk[0], dk[1]], axis=1).astype(BF16)
    g[:, 2 * PAIR :] = jnp.concatenate([dv[0], dv[1]], axis=1).astype(BF16)

    def spread(i, _):
        at = pl.ds(pl.multiple_of(i * tile, tile), tile)
        dx[at, :] = dot(g[at, :], w[...], 1, 1).astype(BF16)
        return 0

    lax.fori_loop(0, rows // tile, spread, 0)
    dw[...] = dot(x[...], g[...], 0, 0)
    db[...] = jnp.broadcast_to(total_rows(g[...].astype(F32)), db.shape)


def attend_back(live, q, k, v, o, lse, do, x, w):
    rows, width = x.shape
    s = jax.ShapeDtypeStruct
    return pl.pallas_call(
        attend_back_kernel,
        name="attend_back",
        out_shape=(s((rows, width), BF16), s((width, 3 * PAIR), F32), s((8, 3 * PAIR), F32)),
        in_specs=[SMEM] + [VMEM] * 8,
        out_specs=(VMEM,) * 3,
        scratch_shapes=[
            pltpu.VMEM((rows, 3 * PAIR), BF16),
            pltpu.VMEM((2, rows, HEAD_DIM), F32),
            pltpu.VMEM((2, rows, HEAD_DIM), F32),
        ],
        compiler_params=pltpu.CompilerParams(vmem_limit_bytes=60 << 20),
    )(live, q, k, v, o, lse, do, x, w)


def add_into(target, *terms):
    total = target[...].astype(F32)
    for term in terms:
        total = total + term[...].astype(F32)
    target[...] = total.astype(target.dtype)


def scatter_w_kernel(n, g_in, one, out, out_in, g, r1a, r1b, r2, r3,
                     o_s, o_r, a_s, a_r, b_s, b_r, h_s, h_r, i_s, i_r, k_s):
    w = where_am_i(n)
    me, core, high, l1, l0 = w["me"], w["core"], w["high"], w["l1"], w["l0"]
    highs = w["highs"]
    partner = me ^ 1
    greet([partner, me ^ 2, me ^ 4] + [me ^ (8 * m) for m in range(1, highs)])
    items = g.shape[0]
    ff = (items - 1) // 2
    swap = send(one.at[1 - core], g.at[0], o_s, o_r, partner)
    fill = pltpu.make_async_copy(g_in, g.at[pl.ds(1, 2 * ff)], k_s)
    fill.start()
    fill.wait()
    swap.wait()

    def fold(i, _):
        g[0, i] = (g[0, i].astype(F32) + one[core, i].astype(F32)).astype(BF16)
        return 0

    lax.fori_loop(0, highs, fold, 0)
    first = [
        send(g.at[:, :, 1 - l1, :, 0], r1a, a_s.at[0], a_r.at[0], me ^ 4),
        send(g.at[:, :, :, 1 - l0, 1], r1b, a_s.at[1], a_r.at[1], me ^ 2),
    ]
    for copy in first:
        copy.wait()

    def add1(i, _):
        for h in range(highs):
            for b in range(2):
                g[i, h, l1, b, 0] = (g[i, h, l1, b, 0].astype(F32) + r1a[i, h, b].astype(F32)).astype(BF16)
                g[i, h, b, l0, 1] = (g[i, h, b, l0, 1].astype(F32) + r1b[i, h, b].astype(F32)).astype(BF16)
        return 0

    lax.fori_loop(0, items, add1, 0)
    second = [
        send(g.at[:, :, l1, 1 - l0, 0], r2.at[0], b_s.at[0], b_r.at[0], me ^ 2),
        send(g.at[:, :, 1 - l1, l0, 1], r2.at[1], b_s.at[1], b_r.at[1], me ^ 4),
    ]
    for copy in second:
        copy.wait()

    def add2(i, _):
        for h in range(highs):
            for s in range(2):
                g[i, h, l1, l0, s] = (g[i, h, l1, l0, s].astype(F32) + r2[s, i, h].astype(F32)).astype(BF16)
        return 0

    lax.fori_loop(0, items, add2, 0)
    third = [
        send(g.at[:, high ^ m, l1, l0], r3.at[m - 1], h_s.at[m], h_r.at[m], me ^ (8 * m)) for m in range(1, highs)
    ]
    for copy in third:
        copy.wait()

    def add3(i, _):
        for s in range(2):
            total = g[i, high, l1, l0, s].astype(F32)
            for m in range(1, highs):
                total = total + r3[m - 1, i, s].astype(F32)
            out[i, s] = total
        return 0

    lax.fori_loop(0, items, add3, 0)
    keep = pltpu.make_async_copy(out.at[pl.ds(1, ff), core], out_in.at[core], k_s)
    keep.start()
    swap = send(out.at[pl.ds(1, ff), 1 - core], out_in.at[core], i_s, i_r, partner)
    keep.wait()
    swap.wait()


def scatter_w(n, g, one):
    items, highs = g.shape[0] + 1, g.shape[1]
    wr = g.shape[5]
    ff = (items - 1) // 2
    dma = pltpu.SemaphoreType.DMA
    s = jax.ShapeDtypeStruct
    unit = (wr, HALF)
    return pl.pallas_call(
        functools.partial(scatter_w_kernel, n),
        name="scatter_w",
        out_shape=(s((items, 2) + unit, F32), s((2, ff) + unit, F32)),
        in_specs=[ANY, VMEM],
        out_specs=(VMEM, VMEM),
        scratch_shapes=[
            pltpu.VMEM((items, highs, 2, 2, 2) + unit, BF16),
            pltpu.VMEM((items, highs, 2) + unit, BF16),
            pltpu.VMEM((items, highs, 2) + unit, BF16),
            pltpu.VMEM((2, items, highs) + unit, BF16),
            pltpu.VMEM((highs - 1, items, 2) + unit, BF16),
            dma, dma, dma((2,)), dma((2,)), dma((2,)), dma((2,)), dma((highs,)), dma((highs,)), dma, dma, dma,
        ],
        compiler_params=pltpu.CompilerParams(collective_id=4, has_side_effects=True, vmem_limit_bytes=60 << 20),
    )(g, one)


def scatter_x_kernel(n, dx_in, dh, pieces_in, gtok, red, dx, g, psum, pgot, *rest):
    ra, rb, rc = rest[0:3], rest[3:6], rest[6:9]
    mine, theirs, c_s, c_r, t_s, t_r, w_s, w_r, p_s, p_r, k_s = rest[9:]
    w = where_am_i(n)
    me, core, chip = w["me"], w["core"], w["chip"]
    partner = me ^ 1
    chips = w["chips"]
    greet([partner] + [me ^ (2 * m) for m in range(1, chips)])
    rows = dh.shape[1]
    swap_p = send(pieces_in.at[:, 1 - core], pgot, w_s, w_r, partner)
    fills = [
        pltpu.make_async_copy(dx_in, dx, k_s.at[0]),
        pltpu.make_async_copy(pieces_in.at[:, core], psum, k_s.at[1]),
    ]
    for copy in fills:
        copy.start()
    for copy in fills:
        copy.wait()
    bits = (w["cube"] // 4, w["cube"] // 2 % 2, w["cube"] % 2)
    masks = (8, 4, 2)
    spans = cube_rows(2 * rows)

    def region(s, order, phase, far):
        index = [slice(None)] * 3
        for done in order[:phase]:
            index[done] = bits[done]
        axis = order[phase]
        index[axis] = 1 - bits[axis] if far else bits[axis]
        return tuple(index) + (pl.ds(*spans[s]),)

    def launch(phase):
        bufs = (ra, rb, rc)[phase]
        return [
            send(dx.at[region(s, order, phase, True)], bufs[s], c_s.at[phase, s], c_r.at[phase, s], me ^ masks[order[phase]])
            for s, order in enumerate(CUBE_ORDERS)
        ]

    def fold(phase):
        bufs = (ra, rb, rc)[phase]
        for s, order in enumerate(CUBE_ORDERS):
            at = region(s, order, phase, False)
            dx[at] = (dx[at].astype(F32) + bufs[s][...].astype(F32)).astype(BF16)

    live = launch(0)
    swap_p.wait()
    psum[...] = (psum[...].astype(F32) + pgot[...].astype(F32)).astype(BF16)
    copies = [send(psum.at[chip ^ m], g.at[m], p_s.at[m], p_r.at[m], me ^ (2 * m)) for m in range(1, chips)]
    own = pltpu.make_async_copy(psum.at[chip], g.at[0], k_s.at[2])
    own.start()
    for phase in range(3):
        for copy in live:
            copy.wait()
        fold(phase)
        if phase < 2:
            live = launch(phase + 1)
    here = (bits[0], bits[1], bits[2])
    theirs_at = pl.ds(pl.multiple_of((1 - core) * rows, rows), rows)
    own_at = pl.ds(pl.multiple_of(core * rows, rows), rows)
    swap = send(dx.at[here + (theirs_at,)], theirs, t_s, t_r, partner)
    gtok[core] = (dh[core] + dx[here + (own_at,)].astype(F32)).astype(BF16)
    own.wait()
    for copy in copies:
        copy.wait()
    for m in range(chips):
        term = g[m].astype(F32)
        if m < CUBE:
            red[m] = term
        else:
            red[m % CUBE] += term
    swap.wait()
    gtok[1 - core] = (dh[1 - core] + theirs[...].astype(F32)).astype(BF16)


def scatter_x(n, dx, dh, pieces):
    _, rows, width = dh.shape
    chips = n // 2
    unit = pieces.shape[2:]
    dma = pltpu.SemaphoreType.DMA
    s = jax.ShapeDtypeStruct
    spans = cube_rows(2 * rows)
    bufs = [pltpu.VMEM(lead + (spans[i][1], width), BF16) for lead in ((2, 2), (2,), ()) for i in range(3)]
    return pl.pallas_call(
        functools.partial(scatter_x_kernel, n),
        name="scatter_x",
        out_shape=(s((2, rows, width), BF16), s((CUBE,) + unit, F32)),
        in_specs=[ANY, VMEM, ANY],
        out_specs=(VMEM, VMEM),
        scratch_shapes=[
            pltpu.VMEM(dx.shape, BF16),
            pltpu.VMEM((chips,) + unit, BF16),
            pltpu.VMEM((chips,) + unit, BF16),
            pltpu.VMEM((chips,) + unit, BF16),
        ]
        + bufs
        + [
            pltpu.VMEM((rows, width), BF16),
            pltpu.VMEM((rows, width), BF16),
            dma((3, 3)), dma((3, 3)), dma, dma, dma, dma, dma((chips,)), dma((chips,)), dma((3,)),
        ],
        compiler_params=pltpu.CompilerParams(collective_id=5, has_side_effects=True, vmem_limit_bytes=60 << 20),
    )(dx, dh, pieces)


def start(copies):
    for copy in copies:
        copy.start()


def wait(copies):
    for copy in copies:
        copy.wait()


def remote(src, dst, sems, index, device):
    send_sem, recv_sem = sems
    return pltpu.make_async_remote_copy(
        src_ref=src,
        dst_ref=dst,
        send_sem=send_sem.at[index],
        recv_sem=recv_sem.at[index],
        device_id=(device,),
        device_id_type=MESH,
    )


def add_rows(dst, at, src, src_at):
    dst[at] = (dst[at].astype(F32) + src[src_at].astype(F32)).astype(dst.dtype)


COLS = 256
QUAD = 4
FAR = 8


def mate(m):
    return m % 2 + m // 2 * FAR


def device_of(quad, spot):
    return quad // 4 * 16 + spot // 2 * FAR + quad % 4 * 2 + spot % 2


def layer_kernel(n, shapes, seq_len, slot, tok_h, cot_h, wq_h, wk_h, wv_h, wo, w_in_h, w_out, line,
                 out_h, gtok_h, gq_h, gk_h, gv_h, gwo_h, gwin_h, gwout_h, gline_h, *scratch):
    s = dict(zip(shapes, scratch, strict=True))
    here = where_am_i(n)
    me, core, chip, cube, rank = (here[name] for name in ("me", "core", "chip", "cube", "rank"))
    high, l1, l0, chips, highs = (here[name] for name in ("high", "l1", "l0", "chips", "highs"))
    partner = me ^ 1
    tok, cot, out, gtok = (s[name] for name in ("tok", "cot", "out", "gtok"))
    gqkv, gwo, gwin, gwout, gline = (s[name] for name in ("gqkv", "gwo", "gwin", "gwout", "gline"))
    wqkv, w_in = s["wqkv"], s["w_in"]
    _, rows, width = tok.shape
    own = 2 * rows
    wr, fr = wo.shape[0], w_out.shape[0]
    quads = n // QUAD
    quarter = fr * quads
    chunk = quarter // 2
    spot = core + high % 2 * 2
    z1 = high // 2
    bits = (cube // 4, cube // 2 % 2, cube % 2)

    def sems(name):
        return s[name + "_s"], s[name + "_r"]

    own_rows = pl.ds(pl.multiple_of(core * rows, rows), rows)
    x_all, p_all, w_o, w_i, w_u = s["x_all"], s["p_all"], s["w_o"], s["w_i"], s["w_u"]

    def load(src, dst, i):
        copy = pltpu.make_async_copy(src, dst, s["load"].at[i])
        copy.start()
        return copy

    loads = [load(ref, wqkv.at[i], i) for i, ref in enumerate((wq_h, wk_h, wv_h))]
    loads.append(load(w_in_h, w_in, 3))
    load_o = load(wo, w_o.at[high, l1, l0, core], 4)
    load_u = load(w_out, w_u.at[me // 16, l1, l0], 5)
    load_x = load(tok_h.at[core], x_all.at[bits[0], bits[1], bits[2], own_rows], 6)
    load_t = load(tok_h, tok, 7)
    load_c = load(cot_h, cot, 8)

    met = sorted({m for m in range(1, BLOCK_DEVS)} | {2 * m for m in range(1, chips)})
    barrier = pltpu.get_barrier_semaphore()
    for m in met:
        pl.semaphore_signal(barrier, inc=1, device_id=(me ^ m,), device_id_type=MESH)

    lengths = []
    for m in range(2):
        length = jnp.int32(0)
        for i in range(slot.shape[1]):
            length = length + jnp.where(slot[m, i] == me // BLOCK_DEVS, seq_len[m, i], 0)
        lengths.append(length)

    pieces, w_loc, line_at, lines_all = s["pieces"], s["w_loc"], s["line"], s["lines"]
    wait(loads)
    for k in range(CUBE):
        for i in range(3):
            pieces[k, :, i * PAIR : (i + 1) * PAIR] = wqkv[i, :, k * PAIR : (k + 1) * PAIR]
    value = line[...]
    line_at[...] = jnp.concatenate(
        [value[:, i * PAIR : (i + 1) * PAIR] for i in range(3)] + [jnp.zeros((13, PAIR), F32)], axis=0
    ).astype(BF16)
    for i in range(quads):
        for q in range(QUAD):
            at = device_of(i, q) * fr
            w_loc[q, :, i * fr : (i + 1) * fr] = w_in[:, at : at + fr]
    pl.semaphore_wait(barrier, len(met))

    swap_tok = remote(tok_h.at[1 - core], x_all.at[bits[0], bits[1], bits[2], own_rows], sems("swap"), 0, partner)
    swap_tok.start()
    trade_in = [remote(w_loc.at[spot ^ m], w_i.at[z1, high % 2, l1, l0, core], sems("trade"), m, me ^ mate(m)) for m in range(1, QUAD)]
    start(trade_in)
    piece_copies = [
        remote(pieces.at[(chip ^ m) % CUBE], p_all.at[chip, core], sems("piece"), m, me ^ (2 * m))
        for m in range(chips - 1, 0, -1)
    ]
    line_copies = [
        remote(line_at, lines_all.at[chip, core], sems("line"), m, me ^ (2 * m)) for m in range(1, chips)
    ]

    masks = (8, 4, 2)
    set_at = (core * rows, (1 - core) * rows)

    def rows_of(t, i):
        first, count = SPANS[t][i]
        return pl.ds(pl.multiple_of(set_at[t] + first, 16), count)

    def cube_phase(t, phase):
        out_ = []
        for i, order in enumerate(ROW_ORDERS):
            index = list(bits)
            for done in order[:phase]:
                index[done] = slice(None)
            region = x_all.at[index[0], index[1], index[2], rows_of(t, i)]
            sem = (s["cube_s"].at[t, phase], s["cube_r"].at[t, phase])
            out_.append(remote(region, region, sem, i, me ^ masks[order[phase]]))
        return out_

    groups = 5
    every = slice(None)

    def part_o(h_, a_, b_, t):
        return w_o.at[h_, a_, b_, core, :, every if t is None else pl.ds(t * HALF, HALF)]

    def part_of(g, h_, a_, b_, t):
        if g <= 2:
            return w_i.at[h_, :, a_, b_, every if t is None else t, :, pl.ds((g - 1) * chunk, chunk)]
        r_ = every if t is None else pl.ds(t * fr // 2, fr // 2)
        return w_u.at[h_, a_, b_, r_, pl.ds((g - 3) * HALF, HALF)]

    def high_copies(g):
        sem = (s["hi_s"].at[g], s["hi_r"].at[g])
        if g:
            region = part_of(g, z1, l1, l0, None)
            return [remote(region, region, sem, 0, me ^ 16)]
        region = part_o(high, l1, l0, None)
        return [remote(region, region, sem, m, me ^ (8 * m)) for m in range(1, highs)]

    def low_copies(g, phase):
        ab = (s["ab_s"].at[g, phase], s["ab_r"].at[g, phase])
        first, second = (every, l1, l0, 0), (every, l1, l0, 1)
        to = (me ^ 2, me ^ 4)
        if phase == 1:
            first, second = (every, l1, every, 0), (every, every, l0, 1)
            to = (me ^ 4, me ^ 2)
        a, b = (part_of(g, *first), part_of(g, *second)) if g else (part_o(*first), part_o(*second))
        return [remote(a, a, ab, 0, to[0]), remote(b, b, ab, 1, to[1])]

    swap_o = remote(w_o.at[:, :, :, core], w_o.at[:, :, :, core], sems("swap"), 3, partner)

    def gather_event(kind, g):
        if kind == "o":
            gather_end(g)
            swap_o.start()
        elif kind == "h":
            start(high_copies(g))
        elif kind == "a":
            wait(high_copies(g))
            start(low_copies(g, 0))
        else:
            wait(low_copies(g, 0))
            start(low_copies(g, 1))

    def gather_events(name):
        for kind, g in GATHER.get(name, ()):
            gather_event(kind, g)

    def gather_end(g):
        wait(low_copies(g, 1))

    load_x.wait()
    start(cube_phase(0, 0))
    p_all[chip, core] = pieces[cube]
    lines_all[chip, core] = line_at[...]
    w_i[z1, high % 2, l1, l0, core] = w_loc[spot]
    load_o.wait()
    load_u.wait()
    swap_tok.wait()
    start(cube_phase(1, 0))
    start(piece_copies)
    start(line_copies)
    wait(trade_in)
    gather_events("t0")
    wait(cube_phase(0, 0))
    start(cube_phase(0, 1))
    wait(cube_phase(1, 0))
    start(cube_phase(1, 1))
    gather_events("t1")
    wait(cube_phase(0, 1))
    start(cube_phase(0, 2))
    wait(cube_phase(1, 1))
    start(cube_phase(1, 2))
    gather_events("t2")
    wait(piece_copies)
    wait(line_copies)
    swap_p = remote(p_all.at[:, core], p_all.at[:, core], sems("swap"), 2, partner)
    swap_p.start()
    swap_l = remote(lines_all.at[:, core], lines_all.at[:, core], sems("swap"), 10, partner)
    swap_l.start()
    swap_p.wait()
    swap_l.wait()

    param, b_in = s["param"], s["b_in"]
    tail = lines_all[...].reshape(n * 16, PAIR)
    at_row = lax.broadcasted_iota(jnp.int32, (n, n * 16), 1) - 16 * lax.broadcasted_iota(jnp.int32, (n, n * 16), 0)
    lines = [dot((at_row == i).astype(BF16), tail).astype(BF16) for i in range(3)]
    lane = lax.broadcasted_iota(jnp.int32, (PAIR, width), 1)
    column = lax.broadcasted_iota(jnp.int32, (PAIR, width), 0)
    owner = lax.broadcasted_iota(jnp.int32, (n, width), 1) // wr == lax.broadcasted_iota(jnp.int32, (n, width), 0)

    def selector(i):
        return (column == i % 4 * wr + lane % wr).astype(BF16)

    for i in range(8):
        spread = dot(lines[i // 4], selector(i))
        param[i : i + 1, :] = jnp.sum(jnp.where(owner, spread, 0.0), axis=0, keepdims=True)
    quarter_pick = (
        device_of(lax.broadcasted_iota(jnp.int32, (quads, n), 0), spot)
        == lax.broadcasted_iota(jnp.int32, (quads, n), 1)
    )
    mine = dot(quarter_pick.astype(BF16), lines[2])
    for i in range(quads):
        b_in[0:1, i * fr : (i + 1) * fr] = mine[i : i + 1, :]
    wait(cube_phase(0, 2))
    wait(cube_phase(1, 2))

    q, k, v, o, low, lse = (s[name] for name in ("q", "k", "v", "o", "low", "lse"))
    tile = own
    pair_at = pl.ds(pl.multiple_of(cube * PAIR, PAIR), PAIR)
    bq, bv = param[0:1, pair_at], param[1:2, pair_at]
    length = jnp.where(core == 0, lengths[0], lengths[1])

    def w_qkv():
        return p_all[...].reshape(width, 3 * PAIR)

    def project(i, _):
        at = pl.ds(pl.multiple_of(i * tile, tile), tile)
        y = dot(x_all[i // 4, i // 2 % 2, i % 2], w_qkv())
        q[at, :] = ((y[:, :PAIR] + bq) * HEAD_DIM ** (-0.5)).astype(BF16)
        k[at, :] = y[:, PAIR : 2 * PAIR].astype(BF16)
        v[at, :] = (y[:, 2 * PAIR :] + bv).astype(BF16)
        return 0

    lax.fori_loop(0, CUBE, project, 0)
    gather_events("p")

    attn = s["attn"]
    low_dst = attn.at[core, :, pair_at]

    def row_copy(m):
        at = pl.ds(pl.multiple_of((rank ^ m) * rows, rows), rows)
        return remote(low.at[at], low_dst, sems("torow"), m, me ^ m)

    def attend_step(step, _):
        far = CUBE - 1 - step
        i = cube ^ far
        at = pl.ds(pl.multiple_of(i * tile, tile), tile)
        outs_, logs = [], []
        for h in range(2):
            c = slice(h * HEAD_DIM, (h + 1) * HEAD_DIM)
            sc = dot(q[at, c], k[:, c], 1, 1)
            place = lax.broadcasted_iota(jnp.int32, sc.shape, 1)
            sc = jnp.where(place < length, sc, -1e30)
            top = jnp.max(sc, axis=1, keepdims=True)
            e = jnp.exp(sc - top)
            total = jnp.sum(e, axis=1, keepdims=True)
            outs_.append(dot(e.astype(BF16), v[:, c]) / total)
            logs.append(jnp.broadcast_to(top + jnp.log(total), (tile, HEAD_DIM)))
        mixed = jnp.concatenate(outs_, axis=1)
        o[at, :] = mixed
        low[at, :] = mixed.astype(BF16)
        lse[at, :] = jnp.concatenate(logs, axis=1)

        @pl.when(far > 0)
        def _():
            row_copy(2 * far).start()

        row_copy(2 * far + 1).start()
        for at_step in range(CUBE):
            if at_step in GATHER:

                @pl.when(step == at_step)
                def _():
                    gather_events(at_step)

        return 0

    lax.fori_loop(0, CUBE, attend_step, 0)
    attn[core, :, pair_at] = low[pl.ds(pl.multiple_of(rank * rows, rows), rows), :]
    gather_events("r")
    wait([row_copy(m) for m in range(1, BLOCK_DEVS)])
    swap_o.wait()

    x1, n1, r1, x1_low, slope, act = (s[name] for name in ("x1", "n1", "r1", "x1_low", "slope", "act"))
    part, got, df2 = (s[name] for name in ("part", "got", "df2"))
    p2, p3, got2, got3 = (s[name] for name in ("p2", "p3", "got2", "got3"))
    sums = s["sums"]

    def whole_o():
        return w_o[...].reshape(width, width)

    for m in range(2):
        part[0, m * rows : (m + 1) * rows, :] = dot(attn[m], whole_o())
    def trade_rows(buf, m):
        at = pl.ds(m * rows, rows)
        return remote(buf.at[0, at], buf.at[2, at], sems("rowx"), m, me ^ FAR)

    def pass_rows(buf, m):
        at = pl.ds(m * rows, rows)
        return remote(buf.at[2, at], buf.at[3, at], sems("rowp"), m, partner)

    def swap_rows(buf, m):
        at = pl.ds(m * rows, rows)
        return remote(buf.at[0, at], buf.at[1, at], sems("rows"), m, partner)

    load_t.wait()
    for m in range(2):
        at = slice(m * rows, (m + 1) * rows)
        nn, rs = norm_forward(tok[m].astype(F32) + part[0, at, :] + param[2:3, :])
        n1[at, :] = nn
        r1[at, :] = jnp.broadcast_to(rs, (rows, 128))
        y = nn * param[4:5, :] + param[5:6, :]
        x1[at, :] = y
        x1_low[0, at, :] = y.astype(BF16)
        trade_rows(x1_low, m).start()
        swap_rows(x1_low, m).start()
    gather_events("x")

    def hidden_units(a, j):
        cols = slice(j * chunk, (j + 1) * chunk)
        lines_ = slice(a * own, (a + 2) * own)
        w_ = w_i[:, :, :, :, :, :, cols].reshape(width, chunk)
        slope[j, lines_, :] = dot(x1_low[a : a + 2].reshape(2 * own, width), w_) + b_in[0:1, cols]

        def gelu_step(i, _):
            at = pl.ds(pl.multiple_of(a * own + i * 64, 64), 64)
            u = slope[j, at, :]
            phi = 0.5 + 0.5 * lax.erf(u * 0.7071067811865476)
            slope[j, at, :] = phi + u * (0.3989422804014327 * jnp.exp(-0.5 * u * u))
            act[at, cols] = (u * phi).astype(BF16)
            return 0

        lax.fori_loop(0, 2 * own // 64, gelu_step, 0)

    def pass_on(buf, m):
        trade_rows(buf, m).wait()
        pass_rows(buf, m).start()

    wait([swap_rows(x1_low, m) for m in range(2)])
    for j in range(2):
        gather_end(1 + j)
        hidden_units(0, j)
        pass_on(x1_low, j)
    gather_events("i")
    wait([pass_rows(x1_low, m) for m in range(2)])
    for j in range(2):
        hidden_units(2, j)
    gather_events("j")

    def near_copy(i):
        at = pl.ds(i * COLS, COLS)
        return remote(part.at[1, :, at], got.at[:, at], sems("near"), i, partner)

    def side_copy(i):
        at = pl.ds(i * COLS, COLS)
        return remote(p3.at[:, at], got3.at[:, at], sems("side"), i, partner)

    def far_copy(i):
        at = pl.ds(i * COLS, COLS)
        return remote(p2.at[:, at], got2.at[:, at], sems("far"), i, me ^ FAR)

    outs = width // COLS

    def partial_sums(terms):
        def send_far(i):
            cols = slice(i * COLS, (i + 1) * COLS)
            side_copy(i).wait()
            p2[:, cols] = (part[0, :, cols] + got3[:, cols].astype(F32)).astype(BF16)
            far_copy(i).start()

        for i in range(outs):
            cols = slice(i * COLS, (i + 1) * COLS)
            y = terms(2, i)
            part[0, :, cols] = y[:own]
            p3[:, cols] = y[own:].astype(BF16)
            side_copy(i).start()
            if i:
                send_far(i - 1)
        send_far(outs - 1)
        for i in range(outs):
            cols = slice(i * COLS, (i + 1) * COLS)
            y = terms(0, i)
            part[0, :, cols] = y[:own]
            part[1, :, cols] = y[own:]
            near_copy(i).start()

    def partial_end():
        wait([near_copy(i) for i in range(outs)])
        wait([far_copy(i) for i in range(outs)])

    def forward_terms(a, i):
        if a == 2 and i % 2 == 0:
            gather_end(3 + i // 2)
        w_ = w_u[:, :, :, :, i * COLS : (i + 1) * COLS].reshape(quarter, COLS)
        return dot(act[a * own : (a + 2) * own, :], w_)

    partial_sums(forward_terms)
    partial_end()

    for i in range(8):
        sums[i : i + 1, :] = jnp.zeros((1, width), F32)
    load_c.wait()
    for m in range(2):
        at = slice(m * rows, (m + 1) * rows)
        nn, rs = norm_forward(x1[at, :] + part[0, at, :] + got[at, :] + got2[at, :].astype(F32) + param[3:4, :])
        out[m] = (nn * param[6:7, :] + param[7:8, :]).astype(BF16)
        place = rank * rows + lax.broadcasted_iota(jnp.int32, (rows, 1), 0)
        dy = jnp.where(place < lengths[m], cot[m].astype(F32), 0.0)
        sums[6:7, :] += total_rows(dy * nn)
        sums[7:8, :] += total_rows(dy)
        d = norm_back(dy, nn, rs, param[6:7, :])
        x1[at, :] = d
        d_low = d.astype(BF16)
        df2[0, at, :] = d_low
        trade_rows(df2, m).start()
        swap_rows(df2, m).start()
        sums[3:4, :] += total_rows(d_low.astype(F32))
    stores = [load(out, out_h, 9)]

    fin = s["fin"]

    def unit(r, h_, a_, b_, t):
        return part_of(r + 1, h_, a_, b_, t) if r < 4 else part_o(h_, a_, b_, t)

    def buf(name, r):
        if r == 4:
            return s[name + "o"]
        return s[name + "i"].at[r] if r < 2 else s[name + "u"].at[r - 2]

    def reduce_copies(r, phase):
        name = ("ra", "rb", "rc")[phase]
        sem = (s[name + "_s"].at[r], s[name + "_r"].at[r])
        if phase == 2:
            if r < 4:
                return [remote(unit(r, 1 - z1, l1, l0, None), buf(name, r), sem, 0, me ^ 16)]
            return [
                remote(part_o(high ^ m, l1, l0, None), s["rco"].at[m - 1], sem, m, me ^ (8 * m))
                for m in range(1, highs)
            ]
        if phase == 0:
            regions = (every, 1 - l1, every, 0), (every, every, 1 - l0, 1)
            to = (me ^ 4, me ^ 2)
        else:
            regions = (every, l1, 1 - l0, 0), (every, 1 - l1, l0, 1)
            to = (me ^ 2, me ^ 4)
        return [remote(unit(r, *regions[t]), buf(name, r).at[t], sem, t, to[t]) for t in range(2)]

    def add_all(target, term):
        target[...] = target[...] + term[...]

    def reduce_add(r, phase):
        for h in range(2 if r < 4 else highs):
            if phase == 0:
                for b_ in range(2):
                    at = (h, every, b_) if r < 2 else (h, b_)
                    add_all(unit(r, h, l1, b_, 0), buf("ra", r).at[(0,) + at])
                    add_all(unit(r, h, b_, l0, 1), buf("ra", r).at[(1,) + at])
            else:
                for t in range(2):
                    add_all(unit(r, h, l1, l0, t), buf("rb", r).at[t, h])

    def reduce_last(r):
        if r == 4:
            total = part_o(high, l1, l0, None)[...].astype(F32)
            for m in range(1, highs):
                total = total + s["rco"][m - 1].astype(F32)
            gwo[...] = total
            return
        total = unit(r, z1, l1, l0, None)[...].astype(F32) + buf("rc", r)[...].astype(F32)
        if r < 2:
            fin[:, :, r * chunk : (r + 1) * chunk] = total.astype(BF16).reshape(QUAD, wr, chunk)
            start(fin_copies(r))
        else:
            gwout[:, (r - 2) * HALF : (r - 1) * HALF] = total

    def fin_copies(r):
        at = pl.ds(r * chunk, chunk)
        return [
            remote(fin.at[spot ^ m, :, at], s["fin_got"].at[m, :, at], (s["fin_s"].at[r], s["fin_r"].at[r]), m, me ^ mate(m))
            for m in range(1, QUAD)
        ]

    def reduce_events(name):
        for phase, r in REDUCE.get(name, ()):
            if phase > 0:
                wait(reduce_copies(r, phase - 1))
            if 0 < phase < 3:
                reduce_add(r, phase - 1)
            if phase == 3:
                reduce_last(r)
            else:
                start(reduce_copies(r, phase))

    du, gbin = s["du"], s["gbin"]

    def hidden_back(a, j):
        lines_ = slice(a * own, (a + 2) * own)
        cols = slice(j * chunk, (j + 1) * chunk)
        w_ = w_u[j].reshape(chunk, width)
        da = dot(df2[a : a + 2].reshape(2 * own, width), w_, 1, 1)
        du[lines_, cols] = (da * slope[j, lines_, :]).astype(BF16)

    wait([swap_rows(df2, m) for m in range(2)])
    for j in range(2):
        hidden_back(0, j)
        pass_on(df2, j)
    wait([pass_rows(df2, m) for m in range(2)])
    for j in range(2):
        hidden_back(2, j)

    def back_terms(a, i):
        return dot(du[a * own : (a + 2) * own, :], w_i[i // 2, i % 2].reshape(COLS, quarter), 1, 1)

    partial_sums(back_terms)
    x1_rows, df2_rows = x1_low[...].reshape(4 * own, width), df2[...].reshape(4 * own, width)
    for j in range(2):
        cols = slice(j * chunk, (j + 1) * chunk)
        w_i[:, :, :, :, :, :, cols] = dot(x1_rows, du[:, cols], 0, 0).astype(BF16).reshape(2, 2, 2, 2, 2, wr, chunk)
        reduce_events(f"w{j}")
    for j in range(2):
        cols = slice(j * HALF, (j + 1) * HALF)
        w_u[:, :, :, :, cols] = dot(act[...], df2_rows[:, cols], 0, 0).astype(BF16).reshape(2, 2, 2, fr, HALF)
        reduce_events(f"w{j + 2}")
    gbin[0:1, :] = total_rows(du[...].astype(F32))
    partial_end()

    dattn, dmid = s["dattn"], s["dmid"]
    for m in range(2):
        at = slice(m * rows, (m + 1) * rows)
        e = x1[at, :] + part[0, at, :] + got[at, :] + got2[at, :].astype(F32)
        nn, rs = n1[at, :], r1[at, 0:1]
        sums[4:5, :] += total_rows(e * nn)
        sums[5:6, :] += total_rows(e)
        d = norm_back(e, nn, rs, param[4:5, :])
        x1[at, :] = d
        d_low = d.astype(BF16)
        dmid[at, :] = d_low
        sums[2:3, :] += total_rows(d_low.astype(F32))
    for m in range(2):
        dattn[m] = dot(dmid[m * rows : (m + 1) * rows, :], whole_o(), 1, 1).astype(BF16)
    do = s["do"]

    def head_piece(m):
        at = pl.ds(pl.multiple_of((cube ^ (m // 2)) * PAIR, PAIR), PAIR)
        return dattn.at[core ^ (m % 2), :, at]

    def head_copy(m):
        return remote(head_piece(m), do.at[rank], sems("tohead"), m, me ^ m)

    start([head_copy(m) for m in range(BLOCK_DEVS - 1, 0, -1)])
    do[rank] = dattn[core, :, pair_at]
    g_o = dot(attn[0], dmid[0:rows, :], 0, 0) + dot(attn[1], dmid[rows:own, :], 0, 0)
    w_o[...] = g_o.astype(BF16).reshape(highs, 2, 2, 2, wr, width)
    swap_g = remote(w_o.at[:, :, :, 1 - core], s["o_got"], sems("swap"), 7, partner)
    swap_g.start()
    reduce_events("x")
    swap_g.wait()
    for h in range(highs):
        w_o[h, :, :, core] = (w_o[h, :, :, core].astype(F32) + s["o_got"][h].astype(F32)).astype(BF16)

    acc, g = slope, s["g"]
    acc[...] = jnp.zeros_like(acc)
    scale = HEAD_DIM ** (-0.5)
    block = acc.shape[2]

    def back_step(step, _):
        i = cube ^ step

        @pl.when(step > 0)
        def _():
            head_copy(2 * step).wait()

        head_copy(2 * step + 1).wait()
        at = pl.ds(pl.multiple_of(i * tile, tile), tile)
        outs_ = []
        d2 = do[pl.ds(2 * i, 2)].reshape(tile, PAIR)
        for h in range(2):
            c = slice(h * HEAD_DIM, (h + 1) * HEAD_DIM)
            d = d2[:, c]
            inner = jnp.sum(d.astype(F32) * o[at, c], axis=1, keepdims=True)
            norm = lse[at, h * HEAD_DIM : h * HEAD_DIM + 1]
            dq = None
            for b in range(4):
                keys = slice(b * block, (b + 1) * block)
                first = b % 2 * 2 * PAIR + h * HEAD_DIM
                sc = dot(q[at, c], k[keys, c], 1, 1)
                place = b * block + lax.broadcasted_iota(jnp.int32, sc.shape, 1)
                p = jnp.where(place < length, jnp.exp(sc - norm), 0.0)
                dp = dot(d, v[keys, c], 1, 1)
                ds = (p * (dp - inner)).astype(BF16)
                term = dot(ds, k[keys, c])
                dq = term if dq is None else dq + term
                acc[b // 2, first : first + HEAD_DIM, :] += dot(q[at, c], ds, 0, 0)
                acc[b // 2, first + PAIR : first + PAIR + HEAD_DIM, :] += dot(d, p.astype(BF16), 0, 0)
            outs_.append(dq)
        g[at, 0:PAIR] = (jnp.concatenate(outs_, axis=1).astype(BF16).astype(F32) * scale).astype(BF16)
        for at_step in range(CUBE):
            if at_step in REDUCE:

                @pl.when(step == at_step)
                def _():
                    reduce_events(at_step)

        return 0

    lax.fori_loop(0, CUBE, back_step, 0)
    for b in range(4):
        lines_ = slice(b * block, (b + 1) * block)
        first = b % 2 * 2 * PAIR
        g[lines_, PAIR : 3 * PAIR] = acc[b // 2, first : first + 2 * PAIR, :].T.astype(BF16)

    pg, pgot, pslot = s["pg"], s["pgot"], s["pslot"]
    step_width = width // highs

    def weight_step(i, _):
        cols = pl.ds(pl.multiple_of(i * step_width, step_width), step_width)
        block_ = dot(x_all[:, :, :, :, cols].reshape(CUBE * own, step_width), g[...], 0, 0).astype(BF16)
        pg[pl.ds(i * 4, 4)] = block_.reshape(4, 2, wr, 3 * PAIR)
        return 0

    lax.fori_loop(0, highs, weight_step, 0)
    swap_g = remote(pg.at[:, 1 - core], pgot, sems("swap"), 8, partner)
    swap_g.start()

    def spread_rows(i, _):
        at = pl.ds(pl.multiple_of(i * tile, tile), tile)
        x_all[i // 4, i // 2 % 2, i % 2] = dot(g[at, :], w_qkv(), 1, 1).astype(BF16)
        return 0

    lax.fori_loop(0, CUBE, spread_rows, 0)

    def region(t, i, phase, far):
        order = SUM_ORDERS[i]
        index = [slice(None)] * 3
        for done in order[:phase]:
            index[done] = bits[done]
        axis = order[phase]
        index[axis] = 1 - bits[axis] if far else bits[axis]
        return tuple(index) + (rows_of(t, i),)

    def row_sums(t, phase):
        sem = (s["xr_s"].at[t, phase], s["xr_r"].at[t, phase])
        return [
            remote(x_all.at[region(t, i, phase, True)], s[f"x{t}{phase}{i}"], sem, i, me ^ masks[order[phase]])
            for i, order in enumerate(SUM_ORDERS)
        ]

    def row_fold(t, phase):
        for i in range(3):
            at = region(t, i, phase, False)
            x_all[at] = x_all[at] + s[f"x{t}{phase}{i}"][...]

    start(row_sums(1, 0))
    start(row_sums(0, 0))

    db = total_rows(g[...].astype(F32))
    sums[0:1, pair_at] = db[:, 0:PAIR]
    sums[1:2, pair_at] = db[:, 2 * PAIR :]
    sent = []
    for a_ in range(2):
        line_sum = jnp.zeros((n, PAIR), F32)
        for i in range(4 * a_, 4 * a_ + 4):
            placed = jnp.where(owner, sums[i : i + 1, :], 0.0).astype(BF16)
            line_sum = line_sum + dot(placed, selector(i), 1, 1)
        sent.append(line_sum.astype(BF16))
    hidden = jnp.concatenate([gbin[0:1, i * fr : (i + 1) * fr] for i in range(quads)], axis=0)
    back_pick = (
        device_of(lax.broadcasted_iota(jnp.int32, (n, quads), 1), spot)
        == lax.broadcasted_iota(jnp.int32, (n, quads), 0)
    )
    sent.append(dot(back_pick.astype(BF16), hidden.astype(BF16)).astype(BF16))
    at_line = lax.broadcasted_iota(jnp.int32, (n * 16, n), 0) - 16 * lax.broadcasted_iota(jnp.int32, (n * 16, n), 1)
    wide = jnp.zeros((n * 16, PAIR), F32)
    for a_ in range(3):
        wide = wide + dot((at_line == a_).astype(BF16), sent[a_])
    lines_all[...] = wide.astype(BF16).reshape(chips, 2, 16, PAIR)
    swap_l = remote(lines_all.at[:, 1 - core], s["line_got"], sems("swap"), 11, partner)
    swap_l.start()
    swap_g.wait()
    for i in range(chips):
        pg[i, core] = (pg[i, core].astype(F32) + pgot[i].astype(F32)).astype(BF16)
    piece_sums = [
        remote(pg.at[chip ^ m, core], pslot.at[m], sems("psum"), m, me ^ (2 * m)) for m in range(1, chips)
    ]
    start(piece_sums)
    swap_l.wait()
    for i in range(chips):
        lines_all[i, core] = (lines_all[i, core].astype(F32) + s["line_got"][i].astype(F32)).astype(BF16)
    line_sums = [
        remote(lines_all.at[chip ^ m, core], s["line_slot"].at[m], sems("lsum"), m, me ^ (2 * m))
        for m in range(1, chips)
    ]
    start(line_sums)

    theirs_at = pl.ds(pl.multiple_of((1 - core) * rows, rows), rows)
    last = remote(x_all.at[bits[0], bits[1], bits[2], theirs_at], gtok.at[core], sems("swap"), 9, partner)
    def weight_results():
        wait(piece_sums)
        for m in range(chips):
            term = pg[chip, core].astype(F32) if m == 0 else pslot[m].astype(F32)
            at = pl.ds(pl.multiple_of((cube ^ (m % CUBE)) * PAIR, PAIR), PAIR)
            for i in range(3):
                value = term[:, i * PAIR : (i + 1) * PAIR]
                if m < CUBE:
                    gqkv[i, :, at] = value
                else:
                    gqkv[i, :, at] += value
        wait(line_sums)
        line_total = lines_all[chip, core].astype(F32)
        for m in range(1, chips):
            line_total = line_total + s["line_slot"][m].astype(F32)
        gline[...] = jnp.concatenate([line_total[i : i + 1, :] for i in range(3)], axis=1)
        for r in range(2):
            wait(fin_copies(r))
        for i in range(quads):
            at = slice(i * fr, (i + 1) * fr)
            for m in range(QUAD):
                value = fin[spot, :, at] if m == 0 else s["fin_got"][m, :, at]
                gwin[:, pl.ds(pl.multiple_of(device_of(i, spot ^ m) * fr, fr), fr)] = value.astype(F32)
        stores.extend([load(gqkv.at[i], ref, 10 + i) for i, ref in enumerate((gq_h, gk_h, gv_h))])
        stores.extend([load(gwo, gwo_h, 13), load(gwin, gwin_h, 14), load(gwout, gwout_h, 15), load(gline, gline_h, 16)])

    for phase in range(3):
        for t in (1, 0):
            wait(row_sums(t, phase))
            row_fold(t, phase)
            if phase < 2:
                start(row_sums(t, phase + 1))
            elif t == 1:
                last.start()
            reduce_events(f"d{phase}{t}")
        if phase == 1:
            weight_results()
    gtok[core] = (x1[own_rows, :] + x_all[bits[0], bits[1], bits[2], own_rows].astype(F32)).astype(BF16)
    last.wait()
    gtok[1 - core] = (x1[theirs_at, :] + gtok[1 - core].astype(F32)).astype(BF16)
    stores.append(load(gtok, gtok_h, 17))
    wait(stores)


ROW_ORDERS = ((0, 1, 2), (1, 2, 0), (2, 0, 1))
SUM_ORDERS = tuple(order[::-1] for order in ROW_ORDERS)
SPANS = (((0, 48), (48, 48), (96, 32)), ((0, 48), (48, 32), (80, 48)))
GATHER = {
    "t1": (("h", 0),),
    "t2": (("a", 0), ("h", 1), ("h", 2), ("h", 3), ("h", 4)),
    "p": (("b", 0),),
    2: (("a", 1), ("a", 2)),
    4: (("o", 0), ("b", 1)),
    6: (("b", 2),),
    7: (("a", 3), ("a", 4)),
    "x": (("b", 3),),
    "i": (("b", 4),),
}
REDUCE = {
    "w0": ((0, 0),),
    "w1": ((0, 1),),
    0: ((1, 0), (0, 2)),
    1: ((1, 1), (2, 0)),
    2: ((0, 3), (1, 2)),
    3: ((2, 1), (0, 4)),
    4: ((1, 3), (3, 0)),
    5: ((2, 2), (1, 4)),
    6: ((3, 1), (2, 3)),
    7: ((3, 2), (2, 4)),
    "d01": ((3, 3),),
    "d00": ((3, 4),),
}


def layer(n, seq_len, slot, tok, cot, wq, wk, wv, wo, w_in, w_out, line):
    _, rows, width = tok.shape
    wr, fr = wo.shape[0], w_out.shape[0]
    chips, highs = n // 2, n // 8
    own, total = 2 * rows, BLOCK_DEVS * rows
    quads = n // QUAD
    quarter = fr * quads
    chunk = quarter // 2
    outs = width // COLS
    groups = 5
    vm = pltpu.VMEM
    dma = pltpu.SemaphoreType.DMA
    shapes = {
        "x_all": vm((2, 2, 2, own, width), BF16),
        "p_all": vm((chips, 2, wr, 3 * PAIR), BF16),
        "w_o": vm((highs, 2, 2, 2, wr, width), BF16),
        "w_i": vm((2, 2, 2, 2, 2, wr, quarter), BF16),
        "w_u": vm((2, 2, 2, fr, width), BF16),
        "pieces": vm((CUBE, wr, 3 * PAIR), BF16),
        "w_loc": vm((QUAD, wr, quarter), BF16),
        "param": vm((8, width), F32),
        "b_in": vm((8, quarter), F32),
        "gbin": vm((8, quarter), F32),
        "sums": vm((8, width), F32),
        "q": vm((total, PAIR), BF16),
        "k": vm((total, PAIR), BF16),
        "v": vm((total, PAIR), BF16),
        "o": vm((total, PAIR), F32),
        "low": vm((total, PAIR), BF16),
        "lse": vm((total, PAIR), F32),
        "attn": vm((2, rows, width), BF16),
        "x1": vm((own, width), F32),
        "n1": vm((own, width), F32),
        "r1": vm((own, 128), F32),
        "x1_low": vm((4, own, width), BF16),
        "slope": vm((2, 4 * own, chunk), F32),
        "act": vm((4 * own, quarter), BF16),
        "part": vm((2, own, width), F32),
        "got": vm((own, width), F32),
        "df2": vm((4, own, width), BF16),
        "du": vm((4 * own, quarter), BF16),
        "dattn": vm((2, rows, width), BF16),
        "do": vm((BLOCK_DEVS, rows, PAIR), BF16),
        "g": vm((total, 3 * PAIR), BF16),
        "o_got": vm((highs, 2, 2, wr, width), BF16),
        "p2": vm((own, width), BF16),
        "p3": vm((own, width), BF16),
        "got2": vm((own, width), BF16),
        "got3": vm((own, width), BF16),
        "dmid": vm((own, width), BF16),
        "rai": vm((2, 2, 2, 2, 2, wr, chunk), BF16),
        "rau": vm((2, 2, 2, 2, fr // 2, HALF), BF16),
        "rbi": vm((2, 2, 2, 2, wr, chunk), BF16),
        "rbu": vm((2, 2, 2, fr // 2, HALF), BF16),
        "rci": vm((2, 2, 2, wr, chunk), BF16),
        "rcu": vm((2, fr, HALF), BF16),
        "rao": vm((2, highs, 2, wr, HALF), BF16),
        "rbo": vm((2, highs, wr, HALF), BF16),
        "rco": vm((highs - 1, wr, width), BF16),
        "line": vm((16, PAIR), BF16),
        "lines": vm((chips, 2, 16, PAIR), BF16),
        "line_got": vm((chips, 16, PAIR), BF16),
        "line_slot": vm((chips, 16, PAIR), BF16),
        "tok": vm((2, rows, width), BF16),
        "cot": vm((2, rows, width), BF16),
        "out": vm((2, rows, width), BF16),
        "gtok": vm((2, rows, width), BF16),
        "wqkv": vm((3, wr, width), BF16),
        "w_in": vm((wr, fr * n), BF16),
        "gqkv": vm((3, wr, width), F32),
        "gwo": vm((wr, width), F32),
        "gwin": vm((wr, fr * n), F32),
        "gwout": vm((fr, width), F32),
        "gline": vm((1, 3 * PAIR), F32),
        "fin": vm((QUAD, wr, quarter), BF16),
        "fin_got": vm((QUAD, wr, quarter), BF16),
        "pg": vm((chips, 2, wr, 3 * PAIR), BF16),
        "pgot": vm((chips, wr, 3 * PAIR), BF16),
        "pslot": vm((chips, wr, 3 * PAIR), BF16),
    }
    for t in range(2):
        for phase, lead in enumerate(((2, 2), (2,), ())):
            for i in range(3):
                shapes[f"x{t}{phase}{i}"] = vm(lead + (SPANS[t][i][1], width), BF16)
    counts = {
        "swap": (12,), "piece": (chips,), "line": (chips,), "lsum": (chips,), "cube": (2, 3, 3), "hi": (groups, highs), "ab": (groups, 2, 2),
        "torow": (BLOCK_DEVS,), "trade": (QUAD,), "rowx": (2,), "rowp": (2,), "rows": (2,), "near": (outs,), "side": (outs,),
        "far": (outs,), "tohead": (BLOCK_DEVS,), "ra": (groups, highs), "rb": (groups, highs),
        "rc": (groups, highs), "fin": (2, QUAD), "xr": (2, 3, 3), "psum": (chips,),
    }
    for name, count in counts.items():
        shapes[name + "_s"] = dma(count)
        shapes[name + "_r"] = dma(count)
    shapes["load"] = dma((18,))
    s = jax.ShapeDtypeStruct
    return pl.pallas_call(
        functools.partial(layer_kernel, n, tuple(shapes)),
        name="layer",
        out_shape=(
            s((2, rows, width), BF16),
            s((2, rows, width), BF16),
            s((wr, width), F32),
            s((wr, width), F32),
            s((wr, width), F32),
            s((wr, width), F32),
            s((wr, fr * n), F32),
            s((fr, width), F32),
            s((1, 3 * PAIR), F32),
        ),
        in_specs=[SMEM, SMEM] + [ANY] * 8 + [VMEM],
        out_specs=(ANY,) * 9,
        scratch_shapes=list(shapes.values()),
        compiler_params=pltpu.CompilerParams(collective_id=6, has_side_effects=True, vmem_limit_bytes=64 << 20),
    )(seq_len, slot, tok, cot, wq, wk, wv, wo, w_in, w_out, line)


def finish_kernel(wr, *refs):
    big, lines, outs, small = refs[:8], refs[8], refs[9:17], refs[17:26]
    held, sem = refs[26:34], refs[34]
    ins = [pltpu.make_async_copy(a, b, sem.at[0, i]) for i, (a, b) in enumerate(zip(big, held))]
    start(ins)
    copies = [pltpu.make_async_copy(a, b, sem.at[1, i]) for i, (a, b) in enumerate(zip(held, outs))]
    for i, ref in enumerate(small):
        ref[...] = lines[0, i * wr : i * wr + ref.shape[0]]
    for one, other in zip(ins, copies):
        one.wait()
        other.start()
    wait(copies)


def finish(wr, fr, *values):
    s = jax.ShapeDtypeStruct
    return pl.pallas_call(
        functools.partial(finish_kernel, wr),
        name="finish",
        out_shape=tuple(s(value.shape, value.dtype) for value in values[:8])
        + (s((wr,), F32),) * 8
        + (s((fr,), F32),),
        in_specs=[ANY] * 8 + [VMEM],
        out_specs=(ANY,) * 8 + (VMEM,) * 9,
        scratch_shapes=[pltpu.VMEM(value.shape, value.dtype) for value in values[:8]]
        + [pltpu.SemaphoreType.DMA((2, 8))],
    )(*values)


def on_device(
    n, tokens, cotangent, seq_lengths, slot_block, w_query, w_key, w_value, w_output, w_in, w_out,
    b_query, b_value, b_output, b_in, b_out, ln1_gain, ln1_bias, ln2_gain, ln2_bias,
):
    _, rows, width = tokens.shape
    wr = w_query.shape[0]
    fr = w_out.shape[0]
    ff = fr // wr
    chips = n // 2
    highs = n // 8
    device = lax.axis_index("fsdp")
    core, chip = device % 2, device // 2
    cube = chip % CUBE
    vectors = (b_query, b_value, b_output, b_out, ln1_gain, ln1_bias, ln2_gain, ln2_bias, b_in)
    if wr % 16 == 0 and 8 * wr + fr == 3 * PAIR and fr == PAIR:
        total = 3 * PAIR
        line = sum(
            jnp.pad(value.astype(F32)[None], ((0, 0), (i * wr, total - i * wr - value.shape[0])))
            for i, value in enumerate(vectors)
        )
        values = layer(
            n, seq_lengths, slot_block, tokens, cotangent, w_query, w_key, w_value, w_output, w_in, w_out, line
        )
        results = finish(wr, fr, *values)
        bq, bv, bo, bout, gain1, shift1, gain2, shift2, bin_ = results[8:]
        return results[:8] + (bq, bv, bo, bin_, bout, gain1, shift1, gain2, shift2)
    line = jnp.concatenate(vectors)
    lengths = jnp.sum(jnp.where(slot_block == device // BLOCK_DEVS, seq_lengths, 0), axis=1).astype(jnp.int32)
    live = lax.dynamic_slice(lengths, (core,), (1,))
    pad = -(-(wr + 1) // 16) * 16
    cols = jnp.stack([w_query, w_key, w_value]).reshape(3, wr, CUBE, PAIR).transpose(2, 1, 0, 3)
    cols = cols.reshape(CUBE, wr, 3 * PAIR)
    line = jnp.pad(line, (0, 3 * PAIR - line.shape[0]))
    tail = jnp.pad(line[None], ((0, pad - wr - 1), (0, 0)))
    pieces = jnp.concatenate([cols, jnp.broadcast_to(tail, (CUBE,) + tail.shape)], axis=1)
    in_loc = w_in.reshape(wr, chips, 2, ff, wr).transpose(2, 3, 0, 1, 4).reshape(2, ff, wr, HALF)
    w_loc = jnp.concatenate([w_output, w_out]).reshape(ff + 1, wr, 2, HALF).transpose(0, 2, 1, 3)
    x_all, p_all, w_all = gather(n, tokens, pieces, w_loc, in_loc)
    x = x_all.reshape(BLOCK_DEVS * rows, width)
    w_qkv = p_all[:, :, :wr].reshape(width, 3 * PAIR)
    lines = p_all[:, :, wr].reshape(n, 3 * PAIR)
    small = lines[:, : 8 * wr].reshape(n, 8, wr).transpose(1, 0, 2).reshape(8, width)
    bias_in = lax.dynamic_index_in_dim(lines.reshape(chips, 2, 3 * PAIR), core, 1, keepdims=False)
    bias_in = bias_in[:, 8 * wr : 8 * wr + fr].reshape(chips, ff, wr).transpose(1, 0, 2).reshape(ff, HALF)
    bias_qv = lax.dynamic_slice(small, (0, cube * PAIR), (2, PAIR)).astype(F32)
    q, k, v, o, low, lse = attend(live, x, w_qkv, bias_qv[0:1], bias_qv[1:2])
    attn = exchange(to_rows_kernel, n, low.reshape(BLOCK_DEVS, rows, PAIR), (2, rows, width), "to_rows", 1)
    out, dh, dattn, g_in, g_out, g_o, g_small, g_bin = rows_call(
        n, lengths, attn, tokens, cotangent, w_all, small, bias_in
    )
    do = exchange(to_heads_kernel, n, dattn, (BLOCK_DEVS, rows, PAIR), "to_heads", 2).reshape(-1, PAIR)
    dx, dw, db = attend_back(live, q, k, v, o, lse, do, x, w_qkv)
    unit = (wr, HALF)
    g = jnp.concatenate(
        [
            g_in.reshape((ff, highs, 2, 2, 2) + unit),
            g_out.reshape((ff, 2, highs, 2, 2) + unit).transpose(0, 2, 3, 4, 1, 5, 6),
        ]
    )
    one = g_o.reshape((2, highs, 2, 2, 2) + unit).transpose(4, 1, 2, 3, 0, 5, 6)
    r_w, r_in = scatter_w(n, g, one)
    wide = jnp.zeros((2, width), F32)
    wide = lax.dynamic_update_slice(wide, jnp.stack([db[0, :PAIR], db[0, 2 * PAIR :]]), (0, cube * PAIR))
    lines = (g_small + jnp.pad(wide, ((0, 6), (0, 0)))).reshape(8, n, wr).transpose(1, 0, 2).reshape(n, 8 * wr)
    hidden = g_bin.reshape(ff, chips, wr).transpose(1, 0, 2).reshape(chips, 1, fr)
    hidden = jnp.where(jnp.arange(2)[None, :, None] == core, hidden, 0.0).reshape(n, fr)
    lines = jnp.concatenate([lines, hidden], axis=1)
    lines = jnp.pad(lines, ((0, 0), (0, 3 * PAIR - lines.shape[1])))[:, None]
    parts = jnp.concatenate([dw.reshape(n, wr, 3 * PAIR), lines, jnp.zeros((n, pad - wr - 1, 3 * PAIR), F32)], axis=1)
    parts = parts.astype(BF16).reshape(chips, 2, pad, 3 * PAIR)
    gtok, red = scatter_x(n, dx.reshape(2, 2, 2, 2 * rows, width), dh, parts)
    red = jnp.stack([lax.dynamic_index_in_dim(red, cube ^ m, 0, keepdims=False) for m in range(CUBE)])
    g_qkv = red[:, :wr].reshape(CUBE, wr, 3, PAIR).transpose(2, 1, 0, 3).reshape(3, wr, width)
    line = jnp.sum(red[:, wr], axis=0)
    g_w_in = r_in.reshape(2, ff, wr, chips, wr).transpose(2, 3, 0, 1, 4).reshape(wr, fr * n)
    flat = r_w.transpose(0, 2, 1, 3).reshape(ff * 2 + 1, wr, width)
    biases = [line[i * wr : (i + 1) * wr] for i in range(8)]
    bq, bv, bo, bout, gain1, shift1, gain2, shift2 = biases
    return (
        out, gtok, g_qkv[0], g_qkv[1], g_qkv[2], flat[0], g_w_in, flat[1 + ff :].reshape(fr, width),
        bq, bv, bo, line[8 * wr : 8 * wr + fr], bout, gain1, shift1, gain2, shift2,
    )


def solution(mesh):
    n = mesh.shape["fsdp"]
    rows, vector, whole = P(None, "fsdp", None), P("fsdp"), P()
    matrix = P("fsdp", None)
    return jax.shard_map(
        functools.partial(on_device, n),
        mesh=mesh,
        in_specs=(rows, rows, whole, whole) + (matrix,) * 6 + (vector,) * 9,
        out_specs=(rows, rows) + (matrix,) * 6 + (vector,) * 9,
        check_vma=False,
    )
```
